256 devices in a mesh: fx: 32 (over z, y), fy: 4 (over x), fz: 2 (over core).
Axes of the slice: x: 4, y: 4, z: 8, core: 2. Of those that a mesh axis runs over, the one named last changes fastest.
Arguments:
- state: float32 [5, 16, 1024, 512], P(None, 'fz', 'fx', 'fy'), may hold values from -6 to 6
- kappa: float32 [16, 1024, 512], P('fz', 'fx', 'fy'), may hold values from 0.25 to 1
- mix: float32 [5, 5], replicated, may hold values from -0.16 to 0.16
- press_weight: float32 [5], replicated, may hold values from 0.5 to 1.5
- source_weight: float32 [5], replicated, may hold values from 0.05 to 0.2
- interp: float32 [128, 128], replicated, may hold values from -0.25 to 0.25
- block_inverse: float32 [512, 128, 128], P('fx'), as said below
- coupling: float32 [512, 128, 128], P('fx'), may hold values from -0.125 to 0.125
- front_order: int32 [32, 16], P('fx'), may hold values from 0 to 15, each once within a row
- face_owner: int32 [4096, 1], P(('fx', 'fy')), may hold values from 0 to 31; in each aligned block of 32 rows (0 to 31, 32 to 63, ...) at most 2 rows name the same one
- face_slot: int32 [4096], P(('fx', 'fy')), may hold values from 0 to 15
Outputs:
- state_out: float32 [5, 16, 1024, 512], P(None, 'fz', 'fx', 'fy')
- displacement: float32 [512, 128], P('fx')
The draws below stay inside these ranges and needn't reach their ends.
Inputs may be any that keep to these rules, and one draw needn't show every extreme that they name: `face_owner`: in the rows of one device no owner is named more than 2 times; every draw has some device naming one owner exactly 2 times. `front_order`: each row lists every block of one owner once. `block_inverse`: each block is the inverse of a stiffness block.
All inputs are finite; a program needn't handle non-finite values.
Results may differ from the reference program's by a relative error of at most 0.00021.
Values sent between devices are 32-bit elements; how exact they have to be, the bound alone decides.
A program may use at most 64 MiB of HBM per device.

```python
import math
import jax
import jax.numpy as jnp
import numpy as np
from jax import lax

NV = 5
CX = 32
CY = 128
EB = 128
EBD = 16
ITERS = 3
NZ = 16
NX = 1024
NY = 512
FACE_BLOCKS = 4096
STRUCT_BLOCKS = 512
CAP = 2
N_FX = 32
N_FY = 4


def draw_block_inverse(key, part):
    first_key, second_key = jax.random.split(jax.random.fold_in(key, 11))
    offdiag = jax.random.normal(first_key, (STRUCT_BLOCKS, EB, EB), jnp.float32) * (0.35 / math.sqrt(EB))
    diagonal = jax.random.uniform(second_key, (STRUCT_BLOCKS, EB), jnp.float32, 0.6, 1.2)
    identity = jnp.eye(EB, dtype=jnp.float32)
    return offdiag * (1.0 - identity) + identity * diagonal[:, :, None]


def plant(values, stream_key, least, largest):
    longest = values.shape.index(max(values.shape))
    spots = []
    for shift in (0, 1):
        where = [jax.random.randint(jax.random.fold_in(stream_key, axis), (), 0, length) for axis, length in enumerate(values.shape)]
        where[longest] = (where[longest] + shift) % values.shape[longest]
        spots.append(tuple(where))
    return values.at[spots[0]].set(least).at[spots[1]].set(largest)


def block_scale(own_key, dims, shards, smallest, top_value):
    def one(axis_at, blocks):
        steps = jax.random.uniform(jax.random.fold_in(jax.random.fold_in(own_key, 6), axis_at), (blocks,), jnp.float32, smallest / len(shards), top_value / len(shards))
        return jnp.repeat(jnp.exp(steps), dims[axis_at] // blocks).reshape((-1,) + (1,) * (len(dims) - axis_at - 1))

    loudness = one(*shards[0])
    for cut in shards[1:]:
        loudness = loudness * one(*cut)
    return loudness


def deal_out(key, own, number, rows, number_of, top, most, slope):
    order = jax.random.permutation(key, number_of)
    heavy_load, ordinary = load_shares(number_of, rows * top, most, slope, True), load_shares(number_of, rows * top, most, slope, False)
    places = jnp.arange(number_of)

    def named(tallies, rotation):
        used = int((tallies > 0).sum())
        fixed = max(1, used // 4)
        passed = fixed + (places - fixed + rotation * (used - fixed)) % max(1, number_of - fixed)
        return jnp.zeros((number_of,), jnp.int32).at[order[jnp.where(places < fixed, places, passed)]].set(jnp.asarray(tallies, jnp.int32))

    tallies = jnp.where(number % 4 == 0, named(heavy_load, number // 4), named(ordinary, number - number // 4 - 1))
    mixed = jax.random.permutation(jax.random.fold_in(own, 3), number_of)
    source_of, receiver = mixed[0:number_of // 2 * 2:2], mixed[1:number_of // 2 * 2:2]
    slack = jnp.minimum(tallies[source_of] - 1, most - tallies[receiver]) // 2
    slack = jnp.where((source_of == order[0]) | (receiver == order[0]) | (tallies[receiver] == 0), 0, jnp.maximum(slack, 0))
    passed = jax.random.randint(jax.random.fold_in(own, 4), (number_of // 2,), 0, 1 << 20) % (slack + 1)
    tallies = tallies.at[source_of].add(-passed).at[receiver].add(passed)
    items = jnp.searchsorted(jnp.cumsum(tallies), jnp.arange(rows * top), side="right").astype(jnp.int32)
    listing = items.reshape(top, rows).T
    listing = listing[jax.random.permutation(jax.random.fold_in(own, 1), rows)]
    rotation = jax.random.randint(jax.random.fold_in(own, 2), (rows, 1), 0, top)
    return jnp.take_along_axis(listing, (jnp.arange(top)[None, :] + rotation) % top, axis=1)


def load_shares(amount, total, bound, slope, full):
    loads = [(1 << 20) // math.isqrt(rank ** slope) + 1 for rank in range(1, amount + 1)]
    largest = bound if full else min(bound, max(-(-total // amount), total * loads[0] // sum(loads)))
    least = 1 if total - largest >= amount - 1 else 0
    counts, spare = [largest] + [least] * (amount - 1), total - largest - least * (amount - 1)
    while spare > 0:
        free = [i for i in range(1, amount) if counts[i] < largest] or [i for i in range(1, amount) if counts[i] < bound]
        pool, left = sum([loads[i] for i in free]), spare
        for i in free:
            extra = min(bound - counts[i], max(1, left * loads[i] // pool), spare)
            counts[i] = counts[i] + extra
            spare = spare - extra
    return np.array(counts)


def scatter_about(key, dims, spread, most, pieces=(), kind=jnp.bfloat16):
    result = spread * jax.random.normal(key, dims, jnp.float32)
    if pieces:
        result = result * block_scale(key, dims, pieces, -0.22, 0.18)
    return jnp.clip(result, -most, most).astype(kind)


def setup_inputs(seed: int = 0) -> dict:
    streams_of = jax.random.split(jax.random.key(seed), 12)
    state = scatter_about(streams_of[0], (NV, NZ, NX, NY), 1.0, 6.0, ((1, 2), (2, 32), (3, 4)), jnp.float32)
    kappa = jnp.clip(jnp.exp(math.log(1.0) - 1.3862944 * jax.random.uniform(streams_of[1], (NZ, NX, NY), jnp.float32) ** block_scale(streams_of[1], (NZ, NX, NY), ((0, 2), (1, 32), (2, 4)), -0.2, 0.2)), 0.25, 1.0)
    mix = scatter_about(streams_of[2], (NV, NV), 0.04, 0.16, (), jnp.float32)
    press_weight = jnp.clip(jax.random.uniform(streams_of[3], (NV,), jnp.float32, 0.5, 1.5), 0.5, 1.5)
    source_weight = jnp.clip(jax.random.uniform(streams_of[4], (NV,), jnp.float32, 0.05, 0.2), 0.05, 0.2)
    interp = scatter_about(streams_of[5], (CY, EB), (4 * CY) ** -0.5, 0.25, (), jnp.float32)
    block_inverse = draw_block_inverse(jax.random.fold_in(streams_of[11], 71), 0)
    coupling = scatter_about(streams_of[7], (STRUCT_BLOCKS, EB, EB), (16 * EB) ** -0.5, 0.125, ((0, 32),), jnp.float32)
    front_order = jax.vmap(lambda own: jax.random.permutation(own, EBD))(jax.random.split(streams_of[8], N_FX)).reshape((N_FX, EBD)).astype(jnp.int32)
    face_owner_keys = jax.random.split(jax.random.fold_in(streams_of[9], 1), FACE_BLOCKS // CX)
    face_owner_turns = jax.random.permutation(jax.random.fold_in(streams_of[9], 3), FACE_BLOCKS // CX)
    face_owner = jax.vmap(lambda own, number: deal_out(jax.random.fold_in(streams_of[9], 2), own, number, CX, N_FX, 1, CAP, 2))(face_owner_keys, face_owner_turns).reshape((FACE_BLOCKS, 1))
    face_slot = plant(jax.random.randint(streams_of[10], (FACE_BLOCKS,), 0, EBD), jax.random.fold_in(streams_of[10], 1), 0, EBD - 1).astype(jnp.int32)
    return {"state": state, "kappa": kappa, "mix": mix, "press_weight": press_weight, "source_weight": source_weight, "interp": interp, "block_inverse": block_inverse, "coupling": coupling, "front_order": front_order, "face_owner": face_owner, "face_slot": face_slot}


DIFFUSION = 0.16
HIGHEST = lax.Precision.HIGHEST


def sweep_core(padded, coeff, mix):
    centre = padded[:, 1:-1, 1:-1, 1:-1]
    beside = padded[:, 2:, 1:-1, 1:-1] + padded[:, :-2, 1:-1, 1:-1]
    beside = beside + padded[:, 1:-1, 2:, 1:-1] + padded[:, 1:-1, :-2, 1:-1]
    beside = beside + padded[:, 1:-1, 1:-1, 2:] + padded[:, 1:-1, 1:-1, :-2]
    mixed = jnp.einsum("cd,dzxy->czxy", mix, centre, precision=HIGHEST)
    return centre + DIFFUSION * coeff[None] * (beside - 6.0 * centre) + mixed


def frontal(block_loads, inverse, coupling, order):
    blocks_owner, block_dofs = block_loads.shape

    def advance(position, carry):
        previous, solved = carry
        target = order[position]
        right_side = block_loads[target] - jnp.dot(coupling[target], previous, precision=HIGHEST)
        current = jnp.dot(inverse[target], right_side, precision=HIGHEST)
        return current, solved.at[target].set(current)

    start = (jnp.zeros((block_dofs,), jnp.float32), jnp.zeros((blocks_owner, block_dofs), jnp.float32))
    return lax.fori_loop(0, blocks_owner, advance, start)[1]


def reference(state, kappa, mix, press_weight, source_weight, interp, block_inverse, coupling, front_order, face_owner, face_slot):
    target = face_owner[:, 0] * EBD + face_slot
    displacement = jnp.zeros((STRUCT_BLOCKS, EB), jnp.float32)
    profile = 1.0 - jnp.arange(NZ).astype(jnp.float32) / NZ
    for iteration in range(ITERS):
        for sweep_index in range(2):
            padded = jnp.pad(state, ((0, 0), (1, 1), (1, 1), (1, 1)))
            state = sweep_core(padded, kappa, mix)
        pressure = jnp.sum(press_weight[:, None, None] * state[:, 0], axis=0)
        face_blocks = pressure.reshape(N_FX, CX, N_FY, CY).transpose(0, 2, 1, 3).reshape(FACE_BLOCKS, CY)
        forces = jax.ops.segment_sum(face_blocks, target, num_segments=STRUCT_BLOCKS)
        block_loads = jnp.dot(forces, interp, precision=HIGHEST).reshape(N_FX, EBD, EB)
        solved = jax.vmap(frontal)(block_loads, block_inverse.reshape(N_FX, EBD, EB, EB), coupling.reshape(N_FX, EBD, EB, EB), front_order)
        displacement = solved.reshape(STRUCT_BLOCKS, EB)
        face_disp = jnp.dot(displacement, interp.T, precision=HIGHEST)[target]
        wall_disp = face_disp.reshape(N_FX, N_FY, CX, CY).transpose(0, 2, 1, 3).reshape(NX, NY)
        state = state + source_weight[:, None, None, None] * profile[None, :, None, None] * wall_disp[None, None]
    return state, displacement
```

```python
import functools

import jax
import jax.numpy as jnp
from jax import lax
from jax.experimental import pallas as pl
from jax.experimental.pallas import tpu as pltpu
from jax.sharding import PartitionSpec as P

ITERS = 3
DIFFUSION = 0.16
HIGHEST = lax.Precision.HIGHEST
MESH = pl.DeviceIdType.MESH
F32 = jnp.float32
BF16 = jnp.bfloat16

NV, NZL, CX, CY = 5, 8, 32, 128
NFX, NFY = 32, 4
RING_Z, RING_Y = 8, 4
EB, EBD, CAP = 128, 16, 2
FACES = NFX * NFY * CAP
NT = (((1,), (1,)), ((), ()))


def far_first(step, ring):
    return ring // 2 + (1 - 2 * (step % 2)) * ((step + 1) // 2)


def split(values):
    high = values.astype(BF16)
    return high, (values - high.astype(F32)).astype(BF16)


def pick(selector, values):
    high, low = split(values)
    return jnp.dot(selector, high, preferred_element_type=F32) + jnp.dot(selector, low, preferred_element_type=F32)


def kernel(
    state_in, kappa_in, mix, press_weight, source_weight, interp, inverse_in, coupling_in, order, owner, slot,
    state_out, disp_out,
    S, K, BI, CO, R, XS, XR, YS, YR, ZR, SF, RF, SD, RD, FP, FPT, AM, AT, FR, XV, DV, DR,
    load_sem, hsend, hrecv, fsend, frecv, dsend, drecv, osend, orecv,
):
    ix, iy, iz = lax.axis_index("fx"), lax.axis_index("fy"), lax.axis_index("fz")
    ring_z, ring_y = ix // RING_Y, ix % RING_Y
    on_wall = iz == 0
    is_solver = iy == ix % NFY

    def owner_at(step):
        z = (ring_z + far_first(step // RING_Y, RING_Z)) % RING_Z
        y = (ring_y + far_first(step % RING_Y, RING_Y)) % RING_Y
        return z * RING_Y + y

    def face_at(step):
        z = (ring_z + far_first(step // 16, RING_Z)) % RING_Z
        y = (ring_y + far_first((step // 4) % 4, RING_Y)) % RING_Y
        return z * RING_Y + y, (iy + far_first(step % 4, NFY)) % NFY

    def signal(barrier, device):
        pl.semaphore_signal(barrier, inc=1, device_id=device, device_id_type=MESH)

    loads = [
        pltpu.make_async_copy(state_in, S.at[0, :, pl.ds(1, NZL)], load_sem.at[0]),
        pltpu.make_async_copy(kappa_in, K, load_sem.at[1]),
        pltpu.make_async_copy(inverse_in, BI, load_sem.at[2]),
        pltpu.make_async_copy(coupling_in, CO, load_sem.at[3]),
    ]
    for load in loads:
        load.start()
    XR[...] = jnp.zeros_like(XR)
    YR[...] = jnp.zeros_like(YR)
    zero_plane = jnp.zeros((NV, CX, CY), F32)
    for buffer in range(2):
        S[buffer, :, 0] = zero_plane
        S[buffer, :, NZL + 1] = zero_plane

    barrier = pltpu.get_barrier_semaphore()
    neighbours = (
        (ix > 0, (ix - 1, iy, iz)),
        (ix < NFX - 1, (ix + 1, iy, iz)),
        (iy > 0, (ix, iy - 1, iz)),
        (iy < NFY - 1, (ix, iy + 1, iz)),
    )

    @pl.when(is_solver)
    def _():
        def to_faces(step, carry):
            to_x, to_y = face_at(step)

            @pl.when(jnp.logical_not(jnp.logical_and(jnp.logical_and(to_x == ix, to_y == iy), on_wall)))
            def _():
                signal(barrier, (to_x, to_y, 0))

            return carry

        lax.fori_loop(0, NFX * NFY, to_faces, 0)

    def to_solvers(step, carry):
        to = owner_at(step)

        @pl.when(jnp.logical_not(jnp.logical_and(to == ix, is_solver)))
        def _():
            signal(barrier, (to, to % NFY, iz))

        return carry

    lax.fori_loop(0, NFX, to_solvers, 0)
    expected = jnp.int32(1)
    signal(barrier, (ix, iy, 1 - iz))
    for present, device in neighbours:
        expected = expected + present.astype(jnp.int32)

        @pl.when(present)
        def _():
            signal(barrier, device)

    solver_count = is_solver.astype(jnp.int32)
    wall_count = on_wall.astype(jnp.int32)
    expected = expected + wall_count * (2 * NFX - solver_count) + solver_count * (NFX * NFY - 1)

    rows = lax.broadcasted_iota(jnp.int32, (CAP * NFX, CX), 0)
    faces = lax.broadcasted_iota(jnp.int32, (CAP * NFX, CX), 1)
    named = (owner[...] == rows // CAP).astype(F32)
    earlier = (
        lax.broadcasted_iota(jnp.int32, (CX, CX), 0) < lax.broadcasted_iota(jnp.int32, (CX, CX), 1)
    ).astype(BF16)
    rank = jnp.dot(named.astype(BF16), earlier, preferred_element_type=F32)
    chosen = jnp.where(rank == (rows % CAP).astype(F32), named, 0.0)
    AM[...] = chosen
    unit = (lax.broadcasted_iota(jnp.int32, (CX, CX), 0) == lax.broadcasted_iota(jnp.int32, (CX, CX), 1)).astype(F32)
    AT[...] = lax.dot_general(unit, chosen, NT, preferred_element_type=F32)
    slot_rows = jnp.sum(chosen * (slot[...] + 1).astype(F32), axis=1, keepdims=True)
    SF[...] = jnp.broadcast_to(slot_rows, (CAP * NFX, CY))

    pl.semaphore_wait(barrier, expected)

    def send_to_solvers(turn):
        def send(step, carry):
            to = owner_at(step // 2)
            to_z = step % 2
            here = jnp.logical_and(jnp.logical_and(to == ix, is_solver), to_z == iz)
            source = SF.at[pl.ds(CAP * to, CAP)]
            target = RF.at[turn, pl.ds(CAP * (ix * NFY + iy), CAP)]

            @pl.when(here)
            def _():
                pltpu.make_async_copy(source, target, frecv.at[turn]).start()

            @pl.when(jnp.logical_not(here))
            def _():
                pltpu.make_async_remote_copy(
                    source, target, fsend.at[turn], frecv.at[turn], device_id=(to, to % NFY, to_z), device_id_type=MESH
                ).start()

            return carry

        @pl.when(on_wall)
        def _():
            lax.fori_loop(0, 2 * NFX, send, 0)

    def sent_to_solvers(turn):
        @pl.when(on_wall)
        def _():
            @pl.when(is_solver)
            def _():
                rest = RF.at[turn, pl.ds(0, CAP * (2 * NFX - 1))]
                pltpu.make_async_copy(rest, rest, fsend.at[turn]).wait()

            @pl.when(jnp.logical_not(is_solver))
            def _():
                rest = RF.at[turn, pl.ds(0, CAP * 2 * NFX)]
                pltpu.make_async_copy(rest, rest, fsend.at[turn]).wait()

    def heard_from_faces(turn):
        whole = RF.at[turn]
        pltpu.make_async_copy(whole, whole, frecv.at[turn]).wait()

    def send_to_faces(turn):
        def send(step, carry):
            to_x, to_y = face_at(step)
            here = jnp.logical_and(to_x == ix, to_y == iy)
            source = SD.at[pl.ds(CAP * (to_x * NFY + to_y), CAP)]
            target = RD.at[turn, pl.ds(CAP * ix, CAP)]

            @pl.when(here)
            def _():
                pltpu.make_async_copy(source, target, drecv.at[turn]).start()

            @pl.when(jnp.logical_not(here))
            def _():
                pltpu.make_async_remote_copy(
                    source, target, dsend.at[turn], drecv.at[turn], device_id=(to_x, to_y, iz), device_id_type=MESH
                ).start()

            return carry

        lax.fori_loop(0, NFX * NFY, send, 0)

    def sent_to_faces(turn):
        rest = RF.at[turn, pl.ds(0, FACES - CAP)]
        pltpu.make_async_copy(rest, rest, dsend.at[turn]).wait()

    send_to_solvers(ITERS)

    for load in loads:
        load.wait()

    @pl.when(is_solver)
    def _():
        def products(k, carry):
            block = order[0, k]
            inverse = BI[block]
            force_part = lax.dot_general(interp[...], inverse, NT, precision=HIGHEST, preferred_element_type=F32)
            chain = jnp.dot(inverse, CO[block], precision=HIGHEST, preferred_element_type=F32)
            high, low = split(jnp.concatenate([force_part, -chain.T], axis=0))
            R[k] = jnp.concatenate([high, low], axis=1)
            return carry

        lax.fori_loop(0, EBD, products, 0)

    sent_to_solvers(ITERS)

    block_rows = lax.broadcasted_iota(jnp.int32, (EBD, EB), 0)
    block_lanes = lax.broadcasted_iota(jnp.int32, (EBD, EB), 1)
    placed = jnp.zeros((EBD, EB), F32)
    for k in range(EBD):
        placed = jnp.where(jnp.logical_and(block_rows == k, block_lanes == order[0, k]), 1.0, placed)

    @pl.when(is_solver)
    def _():
        heard_from_faces(ITERS)
        face_lanes = lax.broadcasted_iota(jnp.int32, (FACES, EB), 1) + 1
        slot_of = (RF[ITERS] == face_lanes.astype(F32)).astype(F32)
        FP[...] = lax.dot_general(placed, slot_of, NT, preferred_element_type=F32)
        FPT[...] = lax.dot_general(slot_of, placed, NT, preferred_element_type=F32)

    lane = lax.broadcasted_iota(jnp.int32, (CX, CY), 1)
    row = lax.broadcasted_iota(jnp.int32, (CX, CY), 0)

    def pack(src):
        def plane(z, carry):
            low, high = carry
            for c in range(NV):
                centre = src[c, z + 1]
                XS[0, c, pl.ds(z, 1), :] = centre[0:1]
                XS[1, c, pl.ds(z, 1), :] = centre[CX - 1 : CX]
                here = lane == c * NZL + z
                low = jnp.where(here, centre[:, 0:1], low)
                high = jnp.where(here, centre[:, CY - 1 : CY], high)
            return low, high

        nothing = jnp.zeros((CX, CY), F32)
        low, high = lax.fori_loop(0, NZL, plane, (nothing, nothing))
        YS[0] = low
        YS[1] = high

    def halo_copies(n, src):
        def remote(source, target, at, there, device):
            return pltpu.make_async_remote_copy(
                source, target, hsend.at[n, at], hrecv.at[n, there], device_id=device, device_id_type=MESH
            )

        (has_left, left), (has_right, right), (has_front, front), (has_back, back) = neighbours
        always = iz >= 0
        sends = (
            (has_left, remote(XS.at[0], XR.at[n, 1], 0, 1, left)),
            (has_right, remote(XS.at[1], XR.at[n, 0], 1, 0, right)),
            (has_front, remote(YS.at[0], YR.at[n, 1], 2, 3, front)),
            (has_back, remote(YS.at[1], YR.at[n, 0], 3, 2, back)),
            (always, remote(src.at[:, NZL - (NZL - 1) * iz], ZR.at[n], 4, 4, (ix, iy, 1 - iz))),
        )
        waits = (
            (has_left, remote(XS.at[0], XR.at[n, 0], 0, 0, left)),
            (has_right, remote(XS.at[1], XR.at[n, 1], 1, 1, right)),
            (has_front, remote(YS.at[0], YR.at[n, 0], 2, 2, front)),
            (has_back, remote(YS.at[1], YR.at[n, 1], 3, 3, back)),
            (always, remote(src.at[:, NZL - (NZL - 1) * iz], ZR.at[n], 4, 4, (ix, iy, 1 - iz))),
        )
        return sends, waits

    def sweep(n, src, dst):
        pack(src)
        sends, waits = halo_copies(n, src)
        for present, copy in sends:

            @pl.when(present)
            def _():
                copy.start()

        for present, copy in waits:

            @pl.when(present)
            def _():
                copy.wait_recv()

        for present, copy in sends:

            @pl.when(present)
            def _():
                copy.wait_send()

        src[:, (NZL + 1) * (1 - iz)] = ZR[n]

        def plane(z, carry):
            coeff = DIFFUSION * K[z]
            centres = [src[c, z + 1] for c in range(NV)]
            for c in range(NV):
                centre = centres[c]
                at = c * NZL + z
                beside = src[c, z] + src[c, z + 2]
                beside += jnp.where(row == 0, XR[n, 0, c, pl.ds(z, 1), :], pltpu.roll(centre, 1, 0))
                beside += jnp.where(row == CX - 1, XR[n, 1, c, pl.ds(z, 1), :], pltpu.roll(centre, CX - 1, 0))
                front = pltpu.roll(YR[n, 0], (CY - at) % CY, 1)
                back = pltpu.roll(YR[n, 1], CY - 1 - at, 1)
                beside += jnp.where(lane == 0, front, pltpu.roll(centre, 1, 1))
                beside += jnp.where(lane == CY - 1, back, pltpu.roll(centre, CY - 1, 1))
                total = centre + coeff * (beside - 6.0 * centre)
                for d in range(NV):
                    total += mix[c, d] * centres[d]
                dst[c, z + 1] = total
            return carry

        lax.fori_loop(0, NZL, plane, 0)

    def solve():
        for k in range(EBD):
            force = FR[pl.ds(k, 1), :]
            previous = XV[pl.ds(k - 1, 1), :] if k else jnp.zeros((1, EB), F32)
            both = jnp.concatenate([force, previous], axis=1)
            high = both.astype(BF16).astype(F32)
            at = lax.broadcasted_iota(jnp.int32, (8, 2 * EB), 0)
            left = jnp.where(at == 0, high, jnp.where(at == 1, both - high, 0.0)).astype(BF16)
            result = jnp.dot(left, R[k], preferred_element_type=F32)
            summed = result[:, :EB] + result[:, EB:]
            XV[pl.ds(k, 1), :] = summed[0:1] + summed[1:2]

    total_z = NZL * lax.axis_size("fz")

    def iteration(it, carry):
        sweep(2 * it, S.at[0], S.at[1])
        sweep(2 * it + 1, S.at[1], S.at[0])

        @pl.when(on_wall)
        def _():
            pressure = press_weight[0] * S[0, 0, 1]
            for c in range(1, NV):
                pressure += press_weight[c] * S[0, c, 1]
            SF[...] = pick(AM[...].astype(BF16), pressure)

        send_to_solvers(it)

        @pl.when(is_solver)
        def _():
            heard_from_faces(it)
            FR[...] = pick(FP[...].astype(BF16), RF[it])
            solve()
            facing = lax.dot_general(XV[...], interp[...], NT, precision=HIGHEST, preferred_element_type=F32)
            SD[...] = pick(FPT[...].astype(BF16), facing)
            send_to_faces(it)

        whole = RD.at[it]
        pltpu.make_async_copy(whole, whole, drecv.at[it]).wait()
        wall = pick(AT[...].astype(BF16), RD[it])

        def add(z, carry):
            height = (iz * NZL + z).astype(F32)
            raised = (1.0 - height / total_z) * wall
            for c in range(NV):
                S[0, c, z + 1] += source_weight[c] * raised
            return carry

        lax.fori_loop(0, NZL, add, 0)
        sent_to_solvers(it)

        @pl.when(is_solver)
        def _():
            sent_to_faces(it)

        return carry

    lax.fori_loop(0, ITERS, iteration, 0)

    out = pltpu.make_async_copy(S.at[0, :, pl.ds(1, NZL)], state_out, load_sem.at[0])
    out.start()

    def disp_copy(t, source, target):
        return pltpu.make_async_remote_copy(
            source, target, osend.at[t], orecv, device_id=(ix, (iy + t) % NFY, iz), device_id_type=MESH
        )

    @pl.when(is_solver)
    def _():
        back = lax.dot_general(placed, XV[...], (((0,), (0,)), ((), ())), precision=HIGHEST, preferred_element_type=F32)
        DV[...] = back[:EBD]
        for t in range(1, NFY):
            disp_copy(t, DV, DR).start()
        DR[...] = back[:EBD]
        for t in range(1, NFY):
            disp_copy(t, DV, DR).wait_send()

    @pl.when(jnp.logical_not(is_solver))
    def _():
        disp_copy(1, DV, DR).wait_recv()

    disp_out[...] = DR[...]
    out.wait()


def on_device(
    state, kappa, mix, press_weight, source_weight, interp, block_inverse, coupling, front_order, face_owner, face_slot
):
    anywhere = pl.BlockSpec(memory_space=pl.ANY)
    smem = pl.BlockSpec(memory_space=pltpu.SMEM)
    vmem = pl.BlockSpec(memory_space=pltpu.VMEM)
    dma = pltpu.SemaphoreType.DMA
    sweeps = 2 * ITERS
    return pl.pallas_call(
        kernel,
        out_shape=(
            jax.ShapeDtypeStruct(state.shape, F32),
            jax.ShapeDtypeStruct((EBD, EB), F32),
        ),
        in_specs=[anywhere, anywhere, smem, smem, smem, vmem, anywhere, anywhere, smem, vmem, vmem],
        out_specs=(anywhere, vmem),
        scratch_shapes=[
            pltpu.VMEM((2, NV, NZL + 2, CX, CY), F32),
            pltpu.VMEM((NZL, CX, CY), F32),
            pltpu.VMEM((EBD, EB, EB), F32),
            pltpu.VMEM((EBD, EB, EB), F32),
            pltpu.VMEM((EBD, 2 * EB, 2 * EB), BF16),
            pltpu.VMEM((2, NV, NZL, CY), F32),
            pltpu.VMEM((sweeps, 2, NV, NZL, CY), F32),
            pltpu.VMEM((2, CX, CY), F32),
            pltpu.VMEM((sweeps, 2, CX, CY), F32),
            pltpu.VMEM((sweeps, NV, CX, CY), F32),
            pltpu.VMEM((CAP * NFX, CY), F32),
            pltpu.VMEM((ITERS + 1, FACES, CY), F32),
            pltpu.VMEM((FACES, CY), F32),
            pltpu.VMEM((ITERS, CAP * NFX, CY), F32),
            pltpu.VMEM((EBD, FACES), F32),
            pltpu.VMEM((FACES, EBD), F32),
            pltpu.VMEM((CAP * NFX, CX), F32),
            pltpu.VMEM((CX, CAP * NFX), F32),
            pltpu.VMEM((EBD, EB), F32),
            pltpu.VMEM((EBD, EB), F32),
            pltpu.VMEM((EBD, EB), F32),
            pltpu.VMEM((EBD, EB), F32),
            dma((4,)),
            dma((sweeps, 5)),
            dma((sweeps, 5)),
            dma((ITERS + 1,)),
            dma((ITERS + 1,)),
            dma((ITERS,)),
            dma((ITERS,)),
            dma((NFY,)),
            dma,
        ],
        compiler_params=pltpu.CompilerParams(
            collective_id=0, has_side_effects=True, vmem_limit_bytes=40 * 1024 * 1024
        ),
    )(
        state, kappa, mix, press_weight, source_weight, interp, block_inverse, coupling, front_order,
        face_owner.reshape(1, -1), face_slot.reshape(1, -1),
    )


def solution(mesh):
    return jax.shard_map(
        on_device,
        mesh=mesh,
        in_specs=(
            P(None, "fz", "fx", "fy"),
            P("fz", "fx", "fy"),
            P(),
            P(),
            P(),
            P(),
            P("fx", None, None),
            P("fx", None, None),
            P("fx", None),
            P(("fx", "fy"), None),
            P(("fx", "fy")),
        ),
        out_specs=(P(None, "fz", "fx", "fy"), P("fx", None)),
        check_vma=False,
    )
```

```python
import jax
import jax.numpy as jnp
from jax import lax
from jax.experimental import pallas as pl
from jax.experimental.pallas import tpu as pltpu
from jax.sharding import PartitionSpec as P

ITERS = 3
DIFFUSION = 0.16
HIGHEST = lax.Precision.HIGHEST
MESH = pl.DeviceIdType.MESH
F32 = jnp.float32
BF16 = jnp.bfloat16

NV, NZL, CX, CY = 5, 8, 32, 128
NZ = 16
NFX, NFY = 32, 4
RING_Z, RING_Y = 8, 4
EB, EBD, CAP = 128, 16, 2
FACES = NFX * NFY * CAP
PAD = 8
CXE = CX + 2 * PAD
NT = (((1,), (1,)), ((), ()))
FAR_Y = (2, 1, 3, 0)


def far_first(step, ring):
    return ring // 2 + (1 - 2 * (step % 2)) * ((step + 1) // 2)


def split(values):
    high = values.astype(BF16)
    return high, (values - high.astype(F32)).astype(BF16)


def pick(selector, values):
    high, low = split(values)
    return jnp.dot(selector, high, preferred_element_type=F32) + jnp.dot(selector, low, preferred_element_type=F32)


def kernel(
    state_in, kappa_in, mix_in, press_in, source_in, interp_in, inverse_in, coupling_in, order_in, owner_in, slot_in,
    state_out, disp_out,
    mix, press_weight, source_weight, interp, order, owner, slot,
    S, K, KX, KE, BI, CO, R, XS, XR, YS, YR, YK, ZR, KZ, SL, SF, RF, SD, RD, FP, FPT, AM, AT, FR, XV, DV, DR,
    WN, LP, LE, QB, PB,
    load_sem, hsend, hrecv, fsend, frecv, dsend, drecv, osend, orecv, wsend, wrecv, rsend, rrecv,
):
    ix, iy, iz = lax.axis_index("fx"), lax.axis_index("fy"), lax.axis_index("fz")
    ring_z, ring_y = ix // RING_Y, ix % RING_Y
    on_wall = iz == 0
    off_wall = iz == 1
    is_solver = iy == ring_y
    not_solver = jnp.logical_not(is_solver)
    turned_y = {d: (ring_y + d) % RING_Y for d in FAR_Y}
    turned_x = {d: (iy + d) % NFY for d in FAR_Y}
    answer_x = ((iy + 2 - iz) % NFY, (iy + 3 * iz) % NFY)

    def row_base(step):
        return ((ring_z + far_first(step, RING_Z)) % RING_Z) * RING_Y

    def signal(barrier, device):
        pl.semaphore_signal(barrier, inc=1, device_id=device, device_id_type=MESH)

    loads = [
        pltpu.make_async_copy(source, target, load_sem.at[n])
        for n, (source, target) in enumerate(
            (
                (owner_in, owner),
                (slot_in, slot),
                (order_in, order),
                (kappa_in, K),
                (state_in, S.at[0, :, pl.ds(1, NZL)]),
                (inverse_in, BI),
                (coupling_in, CO),
                (interp_in, interp),
                (mix_in, mix),
                (press_in, press_weight),
                (source_in, source_weight),
            )
        )
    ]
    for load in loads:
        load.start()

    barrier = pltpu.get_barrier_semaphore()
    has_left, has_right, has_front, has_back = ix > 0, ix < NFX - 1, iy > 0, iy < NFY - 1
    sides = (
        (has_left, (ix - 1, iy, iz)),
        (has_right, (ix + 1, iy, iz)),
        (has_front, (ix, iy - 1, iz)),
        (has_back, (ix, iy + 1, iz)),
    )
    corners = (
        (jnp.logical_and(has_left, has_front), (ix - 1, iy - 1, iz)),
        (jnp.logical_and(has_left, has_back), (ix - 1, iy + 1, iz)),
        (jnp.logical_and(has_right, has_front), (ix + 1, iy - 1, iz)),
        (jnp.logical_and(has_right, has_back), (ix + 1, iy + 1, iz)),
    )
    other_core = (ix, iy, 1 - iz)

    @pl.when(is_solver)
    def _():
        def greet(step, carry):
            base = row_base(step)
            for dy in FAR_Y:
                for dx in FAR_Y:
                    signal(barrier, (base + turned_y[dy], turned_x[dx], 0))
            return carry

        lax.fori_loop(0, RING_Z - 1, greet, 0)
        for dy in FAR_Y:
            for dx in FAR_Y:
                if dy or dx:
                    signal(barrier, (ring_z * RING_Y + turned_y[dy], turned_x[dx], 0))

        @pl.when(off_wall)
        def _():
            signal(barrier, (ix, iy, 0))

    @pl.when(on_wall)
    def _():
        cores = {dy: (iy + turned_y[dy]) % 2 for dy in FAR_Y}

        def greet(step, carry):
            base = row_base(step)
            for dy in FAR_Y:
                signal(barrier, (base + turned_y[dy], turned_y[dy], cores[dy]))
            return carry

        lax.fori_loop(0, RING_Z - 1, greet, 0)
        for dy in FAR_Y[:3]:
            signal(barrier, (ring_z * RING_Y + turned_y[dy], turned_y[dy], cores[dy]))

        @pl.when(not_solver)
        def _():
            signal(barrier, (ix, ring_y, cores[0]))

    @pl.when(not_solver)
    def _():
        signal(barrier, (ix, ring_y, iz))

    for ref in (XR, YR, WN):
        ref[...] = jnp.zeros_like(ref)

    signal(barrier, other_core)
    solver_count = is_solver.astype(jnp.int32)
    wall_count = on_wall.astype(jnp.int32)
    expected = 1 + wall_count * (2 * NFX - solver_count) + solver_count * (2 * NFX - wall_count + NFY - 1)
    for present, device in sides + corners:
        expected = expected + present.astype(jnp.int32)

        @pl.when(present)
        def _():
            signal(barrier, device)

    zero_plane = jnp.zeros((NV, CX, CY), F32)
    for buffer in range(2):
        S[buffer, :, 0] = zero_plane
        S[buffer, :, NZL + 1] = zero_plane

    for load in loads[:3]:
        load.wait()
    rows = lax.broadcasted_iota(jnp.int32, (CAP * NFX, CX), 0)
    named = (owner[...] == rows // CAP).astype(F32)
    earlier = (
        lax.broadcasted_iota(jnp.int32, (CX, CX), 0) < lax.broadcasted_iota(jnp.int32, (CX, CX), 1)
    ).astype(BF16)
    rank = jnp.dot(named.astype(BF16), earlier, preferred_element_type=F32)
    chosen = jnp.where(rank == (rows % CAP).astype(F32), named, 0.0)
    AM[...] = chosen
    unit = (lax.broadcasted_iota(jnp.int32, (CX, CX), 0) == lax.broadcasted_iota(jnp.int32, (CX, CX), 1)).astype(F32)
    AT[...] = lax.dot_general(unit, chosen, NT, preferred_element_type=F32)
    slot_rows = jnp.sum(chosen * (slot[...] + 1).astype(F32), axis=1, keepdims=True)
    SL[...] = jnp.broadcast_to(slot_rows, (CAP * NFX, CY))
    block_rows = lax.broadcasted_iota(jnp.int32, (EBD, EB), 0)
    block_lanes = lax.broadcasted_iota(jnp.int32, (EBD, EB), 1)
    placed = jnp.zeros((EBD, EB), F32)
    for k in range(EBD):
        placed = jnp.where(jnp.logical_and(block_rows == k, block_lanes == order[0, k]), 1.0, placed)

    lane = lax.broadcasted_iota(jnp.int32, (CX, CY), 1)
    row = lax.broadcasted_iota(jnp.int32, (CX, CY), 0)
    for load in loads[3:5]:
        load.wait()

    def kappa_faces(z, carry):
        low, high = carry
        coeff = DIFFUSION * K[z]
        KX[z + 1, PAD : PAD + CX] = coeff
        XS[0, NV, pl.ds(z, 1), :] = coeff[0:1]
        XS[1, NV, pl.ds(z, 1), :] = coeff[CX - 1 : CX]
        here = lane == NV * NZL + z
        return jnp.where(here, coeff[:, 0:1], low), jnp.where(here, coeff[:, CY - 1 : CY], high)

    nothing = jnp.zeros((CX, CY), F32)
    YK[0], YK[1] = lax.fori_loop(0, NZL, kappa_faces, (nothing, nothing))

    def pack(src):
        def plane(z, carry):
            low, high = carry
            for c in range(NV):
                centre = src[c, z + 1]
                XS[0, c, pl.ds(z, 1), :] = centre[0:1]
                XS[1, c, pl.ds(z, 1), :] = centre[CX - 1 : CX]
                here = lane == c * NZL + z
                low = jnp.where(here, centre[:, 0:1], low)
                high = jnp.where(here, centre[:, CY - 1 : CY], high)
            return low, high

        YS[0], YS[1] = lax.fori_loop(0, NZL, plane, (YK[0], YK[1]))

    edge = NZL - (NZL - 1) * iz

    def halo_copies(n, src):
        def remote(source, target, at, there, device):
            return pltpu.make_async_remote_copy(
                source, target, hsend.at[n, at], hrecv.at[n, there], device_id=device, device_id_type=MESH
            )

        (_, left), (_, right), (_, front), (_, back) = sides
        always = iz >= 0
        plane = src.at[:, edge]
        sends = (
            (has_left, remote(XS.at[0], XR.at[n, 1], 0, 1, left)),
            (has_right, remote(XS.at[1], XR.at[n, 0], 1, 0, right)),
            (has_front, remote(YS.at[0], YR.at[n, 1], 2, 3, front)),
            (has_back, remote(YS.at[1], YR.at[n, 0], 3, 2, back)),
            (always, remote(plane, ZR.at[n], 4, 4, other_core)),
        )
        waits = (
            (has_left, remote(XS.at[0], XR.at[n, 0], 0, 0, left)),
            (has_right, remote(XS.at[1], XR.at[n, 1], 1, 1, right)),
            (has_front, remote(YS.at[0], YR.at[n, 0], 2, 2, front)),
            (has_back, remote(YS.at[1], YR.at[n, 1], 3, 3, back)),
            (always, remote(plane, ZR.at[n], 4, 4, other_core)),
        )
        return sends, waits

    def each(copies, action):
        for present, copy in copies:

            @pl.when(present)
            def _():
                action(copy)

    def start_halo(n, src):
        pack(src)
        each(halo_copies(n, src)[0], lambda copy: copy.start())

    def finish_halo(n, src):
        sends, waits = halo_copies(n, src)
        each(waits, lambda copy: copy.wait_recv())
        each(sends, lambda copy: copy.wait_send())
        src[:, (NZL + 1) * (1 - iz)] = ZR[n]

    def sweep(n, src, dst):
        def plane(z, carry):
            coeff = KX[z + 1, PAD : PAD + CX]
            centres = [src[c, z + 1] for c in range(NV)]
            for c in range(NV):
                centre = centres[c]
                at = c * NZL + z
                beside = src[c, z] + src[c, z + 2]
                beside += jnp.where(row == 0, XR[n, 0, c, pl.ds(z, 1), :], pltpu.roll(centre, 1, 0))
                beside += jnp.where(row == CX - 1, XR[n, 1, c, pl.ds(z, 1), :], pltpu.roll(centre, CX - 1, 0))
                front = pltpu.roll(YR[n, 0], (CY - at) % CY, 1)
                back = pltpu.roll(YR[n, 1], CY - 1 - at, 1)
                beside += jnp.where(lane == 0, front, pltpu.roll(centre, 1, 1))
                beside += jnp.where(lane == CY - 1, back, pltpu.roll(centre, CY - 1, 1))
                total = centre + coeff * (beside - 6.0 * centre)
                for d in range(NV):
                    total += mix[c, d] * centres[d]
                dst[c, z + 1] = total
            return carry

        lax.fori_loop(0, NZL, plane, 0)

    kappa_plane = pltpu.make_async_remote_copy(
        KX.at[edge], KZ, osend.at[0], orecv.at[0], device_id=other_core, device_id_type=MESH
    )

    def send_to_solvers(turn, rows_out):
        target = RF.at[turn, pl.ds(CAP * (ix * NFY + iy), CAP)]

        def send(to, y, core):
            pltpu.make_async_remote_copy(
                rows_out.at[pl.ds(CAP * to, CAP)], target, fsend.at[turn], frecv.at[turn],
                device_id=(to, y, core), device_id_type=MESH,
            ).start()

        def group(step, carry):
            base = row_base(step)
            for dy in FAR_Y:
                for core in range(2):
                    send(base + turned_y[dy], turned_y[dy], core)
            return carry

        @pl.when(on_wall)
        def _():
            lax.fori_loop(0, RING_Z - 1, group, 0)
            for dy in FAR_Y[:3]:
                for core in range(2):
                    send(ring_z * RING_Y + turned_y[dy], turned_y[dy], core)
            send(ix, ring_y, 1)

            @pl.when(not_solver)
            def _():
                send(ix, ring_y, 0)

            @pl.when(is_solver)
            def _():
                pltpu.make_async_copy(rows_out.at[pl.ds(CAP * ix, CAP)], target, frecv.at[turn]).start()

    def sent_to_solvers(turn):
        @pl.when(on_wall)
        def _():
            @pl.when(is_solver)
            def _():
                rest = RF.at[turn, pl.ds(0, CAP * (2 * NFX - 1))]
                pltpu.make_async_copy(rest, rest, fsend.at[turn]).wait()

            @pl.when(not_solver)
            def _():
                rest = RF.at[turn, pl.ds(0, CAP * 2 * NFX)]
                pltpu.make_async_copy(rest, rest, fsend.at[turn]).wait()

    def heard_from_faces(turn):
        whole = RF.at[turn]
        pltpu.make_async_copy(whole, whole, frecv.at[turn]).wait()

    def send_to_faces(turn):
        target = RD.at[turn, pl.ds(CAP * ix, CAP)]

        def send(to_x, to_y):
            pltpu.make_async_remote_copy(
                SD.at[pl.ds(CAP * (to_x * NFY + to_y), CAP)], target, dsend.at[turn], drecv.at[turn],
                device_id=(to_x, to_y, 0), device_id_type=MESH,
            ).start()

        def group(step, carry):
            base = row_base(step)
            for dy in FAR_Y:
                for x in answer_x:
                    send(base + turned_y[dy], x)
            return carry

        lax.fori_loop(0, RING_Z - 1, group, 0)
        for dy in FAR_Y[:3]:
            for x in answer_x:
                send(ring_z * RING_Y + turned_y[dy], x)
        send(ix, answer_x[0])

        @pl.when(off_wall)
        def _():
            send(ix, answer_x[1])

        @pl.when(on_wall)
        def _():
            pltpu.make_async_copy(SD.at[pl.ds(CAP * (ix * NFY + iy), CAP)], target, drecv.at[turn]).start()

    def sent_to_faces(turn):
        @pl.when(on_wall)
        def _():
            rest = RF.at[turn, pl.ds(0, CAP * (2 * NFX - 1))]
            pltpu.make_async_copy(rest, rest, dsend.at[turn]).wait()

        @pl.when(off_wall)
        def _():
            rest = RF.at[turn, pl.ds(0, CAP * 2 * NFX)]
            pltpu.make_async_copy(rest, rest, dsend.at[turn]).wait()

    for load in loads[5:]:
        load.wait()

    @pl.when(is_solver)
    def _():
        def products(k, carry):
            block = order[0, k]
            inverse = BI[block]
            force_part = lax.dot_general(interp[...], inverse, NT, precision=HIGHEST, preferred_element_type=F32)
            chain = jnp.dot(inverse, CO[block], precision=HIGHEST, preferred_element_type=F32)
            high, low = split(jnp.concatenate([force_part, -chain.T], axis=0))
            R[k] = jnp.concatenate([high, low], axis=1)
            return carry

        lax.fori_loop(0, EBD, products, 0)

    numbers = range(NV)
    source = [source_weight[c] for c in numbers]
    once = [source[c] + sum(mix[c, d] * source[d] for d in numbers) for c in numbers]
    twice = [once[c] + sum(mix[c, d] * once[d] for d in numbers) for c in numbers]
    press_source = sum(press_weight[c] * source[c] for c in numbers)
    press_once = sum(press_weight[c] * once[c] for c in numbers)
    press_twice = sum(press_weight[c] * twice[c] for c in numbers)

    pl.semaphore_wait(barrier, expected)
    start_halo(0, S.at[0])
    kappa_plane.start()
    send_to_solvers(ITERS, SL)
    finish_halo(0, S.at[0])
    sweep(0, S.at[0], S.at[1])
    start_halo(1, S.at[1])

    kappa_plane.wait()
    KX[(NZL + 1) * (1 - iz)] = KZ[...]
    KX[(NZL + 1) * iz] = jnp.zeros((CXE, CY), F32)
    tile_row = lax.broadcasted_iota(jnp.int32, (PAD, CY), 0)

    def kappa_edges(z, carry):
        KX[z + 1, 0:PAD] = jnp.where(tile_row == PAD - 1, XR[0, 0, NV, pl.ds(z, 1), :], 0.0)
        KX[z + 1, PAD + CX : CXE] = jnp.where(tile_row == 0, XR[0, 1, NV, pl.ds(z, 1), :], 0.0)
        at = NV * NZL + z
        front = pltpu.roll(YR[0, 0], CY - 1 - at, 1)
        back = pltpu.roll(YR[0, 1], (CY - at) % CY, 1)
        KE[z] = jnp.where(lane >= CY // 2, front, back)
        return carry

    lax.fori_loop(0, NZL, kappa_edges, 0)

    def wall_base():
        @pl.when(on_wall)
        def _():
            pressure = press_weight[0] * S[0, 0, 1]
            for c in range(1, NV):
                pressure += press_weight[c] * S[0, c, 1]
            PB[...] = pressure

    finish_halo(1, S.at[1])
    sweep(1, S.at[1], S.at[0])
    wall_base()
    sent_to_solvers(ITERS)

    @pl.when(on_wall)
    def _():
        SF[...] = pick(AM[...].astype(BF16), PB[...])

    send_to_solvers(0, SF)

    @pl.when(is_solver)
    def _():
        heard_from_faces(ITERS)
        face_lanes = lax.broadcasted_iota(jnp.int32, (FACES, EB), 1) + 1
        slot_of = (RF[ITERS] == face_lanes.astype(F32)).astype(F32)
        FP[...] = lax.dot_general(placed, slot_of, NT, preferred_element_type=F32)
        FPT[...] = lax.dot_general(slot_of, placed, NT, preferred_element_type=F32)

    def solve():
        for k in range(EBD):
            force = FR[pl.ds(k, 1), :]
            previous = XV[pl.ds(k - 1, 1), :] if k else jnp.zeros((1, EB), F32)
            both = jnp.concatenate([force, previous], axis=1)
            high = both.astype(BF16).astype(F32)
            at = lax.broadcasted_iota(jnp.int32, (8, 2 * EB), 0)
            left = jnp.where(at == 0, high, jnp.where(at == 1, both - high, 0.0)).astype(BF16)
            result = jnp.dot(left, R[k], preferred_element_type=F32)
            summed = result[:, :EB] + result[:, EB:]
            XV[pl.ds(k, 1), :] = summed[0:1] + summed[1:2]

    def wall_copies(it):
        def remote(n, opposite, source_row, side, target_row, count, device):
            copy = lambda here, there: pltpu.make_async_remote_copy(
                WN.at[it, 1, pl.ds(source_row, count)], WN.at[it, side, pl.ds(target_row, count)],
                wsend.at[it, here], wrecv.at[it, there], device_id=device, device_id_type=MESH,
            )
            return copy(n, opposite), copy(n, n)

        low, high = PAD, PAD + CX - 8
        (_, left), (_, right), (_, front), (_, back) = sides
        (lf, left_front), (lb, left_back), (rf, right_front), (rb, right_back) = corners
        return (
            (has_left, remote(0, 1, low, 1, PAD + CX, 8, left)),
            (has_right, remote(1, 0, high, 1, 0, 8, right)),
            (has_front, remote(2, 3, PAD, 2, PAD, CX, front)),
            (has_back, remote(3, 2, PAD, 0, PAD, CX, back)),
            (lf, remote(4, 7, low, 2, PAD + CX, 8, left_front)),
            (lb, remote(5, 6, low, 0, PAD + CX, 8, left_back)),
            (rf, remote(6, 5, high, 2, 0, 8, right_front)),
            (rb, remote(7, 4, high, 0, 0, 8, right_back)),
        )

    lane_e = lax.broadcasted_iota(jnp.int32, (CXE, CY), 1)
    inner = slice(PAD, PAD + CX)

    def spread(it):
        centre = WN[it, 1]
        beyond = jnp.where(lane_e >= CY // 2, WN[it, 0], WN[it, 2])
        up, down = pltpu.roll(centre, 1, 1), pltpu.roll(centre, CY - 1, 1)
        out_up, out_down = pltpu.roll(beyond, 1, 1), pltpu.roll(beyond, CY - 1, 1)
        lap = pltpu.roll(centre, 1, 0) + pltpu.roll(centre, CXE - 1, 0) - 4.0 * centre
        lap += jnp.where(lane_e == 0, out_up, up) + jnp.where(lane_e == CY - 1, out_down, down)
        lap_e = pltpu.roll(beyond, 1, 0) + pltpu.roll(beyond, CXE - 1, 0) - 4.0 * beyond
        lap_e += jnp.where(lane_e >= CY // 2, out_up + down, out_down + up)
        LP[0], LP[1] = lap, centre
        LE[0], LE[1] = lap_e[inner], beyond[inner]

    def ring_sum(wide, edge_columns, below, above, coeff):
        own = wide[inner]
        total = pltpu.roll(wide, 1, 0)[inner] + pltpu.roll(wide, CXE - 1, 0)[inner] + below + above - 6.0 * own
        total += jnp.where(lane == 0, pltpu.roll(edge_columns, 1, 1), pltpu.roll(own, 1, 1))
        total += jnp.where(lane == CY - 1, pltpu.roll(edge_columns, CY - 1, 1), pltpu.roll(own, CY - 1, 1))
        return coeff * total

    first_jump = (NZ - 1.0) / NZ - 2.0

    def wall_response(it):
        wide = KX[1] * (LP[0] + first_jump * LP[1])
        edges = KE[0] * (LE[0] + first_jump * LE[1])
        above = KX[2, inner] * ((NZ - 1.0) / NZ * LP[0, inner])
        bend = ring_sum(wide, edges, 0.0, above, KX[1, inner])
        return press_twice * LP[1, inner] + 2.0 * press_once * wide[inner] + press_source * bend

    def profile(plane):
        height = iz * NZL + plane - 1
        return 1.0 - height.astype(F32) / NZ, jnp.where(height == 0, first_jump, 0.0)

    def update():
        def first(plane, carry):
            share, jump = profile(plane)
            QB[plane] = KX[plane] * (share * LP[0] + jump * LP[1])
            return carry

        lax.fori_loop(0, NZL + 2, first, 0)

        def second(z, carry):
            share, jump = profile(z + 1)
            edges = KE[z] * (share * LE[0] + jump * LE[1])
            wide = QB[z + 1]
            bend = ring_sum(wide, edges, QB[z, inner], QB[z + 2, inner], KX[z + 1, inner])
            raised, slope = share * LP[1, inner], wide[inner]
            for c in range(NV):
                S[0, c, z + 1] += twice[c] * raised + 2.0 * once[c] * slope + source[c] * bend
            return carry

        lax.fori_loop(0, NZL, second, 0)

    def iteration(it, carry):
        more = it < ITERS - 1
        n = 2 * it + 2

        @pl.when(more)
        def _():
            start_halo(n, S.at[0])
            finish_halo(n, S.at[0])
            sweep(n, S.at[0], S.at[1])
            start_halo(n + 1, S.at[1])

        @pl.when(is_solver)
        def _():
            heard_from_faces(it)
            FR[...] = pick(FP[...].astype(BF16), RF[it])
            solve()
            facing = lax.dot_general(XV[...], interp[...], NT, precision=HIGHEST, preferred_element_type=F32)
            SD[...] = pick(FPT[...].astype(BF16), facing)
            send_to_faces(it)

        @pl.when(more)
        def _():
            finish_halo(n + 1, S.at[1])
            sweep(n + 1, S.at[1], S.at[0])
            wall_base()

        relay = pltpu.make_async_remote_copy(
            WN.at[it], WN.at[it], rsend.at[it], rrecv.at[it], device_id=other_core, device_id_type=MESH
        )

        @pl.when(on_wall)
        def _():
            sent_to_solvers(it)
            whole = RD.at[it]
            pltpu.make_async_copy(whole, whole, drecv.at[it]).wait()
            WN[it, 1, inner] = pick(AT[...].astype(BF16), RD[it])

            @pl.when(more)
            def _():
                copies = wall_copies(it)
                each(copies, lambda pair: pair[0].start())
                each(copies, lambda pair: pair[1].wait_recv())
                spread(it)
                SF[...] = pick(AM[...].astype(BF16), PB[...] + wall_response(it))
                send_to_solvers(it + 1, SF)
                each(copies, lambda pair: pair[0].wait_send())

            relay.start()

        @pl.when(off_wall)
        def _():
            relay.wait_recv()

        @pl.when(more)
        def _():
            @pl.when(off_wall)
            def _():
                spread(it)

            update()

        @pl.when(on_wall)
        def _():
            relay.wait_send()

        @pl.when(is_solver)
        def _():
            sent_to_faces(it)

        return carry

    lax.fori_loop(0, ITERS, iteration, 0)

    wall = WN[ITERS - 1, 1, inner]

    def add(z, carry):
        share, _ = profile(z + 1)
        raised = share * wall
        for c in range(NV):
            S[0, c, z + 1] += source[c] * raised
        return carry

    lax.fori_loop(0, NZL, add, 0)
    out = pltpu.make_async_copy(S.at[0, :, pl.ds(1, NZL)], state_out, load_sem.at[0])
    out.start()

    def disp_copy(t):
        return pltpu.make_async_remote_copy(
            DV, DR, osend.at[t], orecv.at[1], device_id=(ix, (iy + t) % NFY, iz), device_id_type=MESH
        )

    @pl.when(is_solver)
    def _():
        back = lax.dot_general(placed, XV[...], (((0,), (0,)), ((), ())), precision=HIGHEST, preferred_element_type=F32)
        DV[...] = back[:EBD]
        for t in range(1, NFY):
            disp_copy(t).start()
        DR[...] = back[:EBD]
        for t in range(1, NFY):
            disp_copy(t).wait_send()

    @pl.when(not_solver)
    def _():
        disp_copy(1).wait_recv()

    disp_out[...] = DR[...]
    out.wait()


def on_device(
    state, kappa, mix, press_weight, source_weight, interp, block_inverse, coupling, front_order, face_owner, face_slot
):
    hbm = pl.BlockSpec(memory_space=pltpu.HBM)
    vmem = pl.BlockSpec(memory_space=pltpu.VMEM)
    dma = pltpu.SemaphoreType.DMA
    sweeps = 2 * ITERS
    return pl.pallas_call(
        kernel,
        out_shape=(
            jax.ShapeDtypeStruct(state.shape, F32),
            jax.ShapeDtypeStruct((EBD, EB), F32),
        ),
        in_specs=[hbm] * 11,
        out_specs=(hbm, vmem),
        scratch_shapes=[
            pltpu.SMEM((NV, NV), F32),
            pltpu.SMEM((NV,), F32),
            pltpu.SMEM((NV,), F32),
            pltpu.VMEM((CY, EB), F32),
            pltpu.SMEM((1, EBD), jnp.int32),
            pltpu.VMEM((1, CX), jnp.int32),
            pltpu.VMEM((1, CX), jnp.int32),
            pltpu.VMEM((2, NV, NZL + 2, CX, CY), F32),
            pltpu.VMEM((NZL, CX, CY), F32),
            pltpu.VMEM((NZL + 2, CXE, CY), F32),
            pltpu.VMEM((NZL, CX, CY), F32),
            pltpu.VMEM((EBD, EB, EB), F32),
            pltpu.VMEM((EBD, EB, EB), F32),
            pltpu.VMEM((EBD, 2 * EB, 2 * EB), BF16),
            pltpu.VMEM((2, NV + 1, NZL, CY), F32),
            pltpu.VMEM((sweeps, 2, NV + 1, NZL, CY), F32),
            pltpu.VMEM((2, CX, CY), F32),
            pltpu.VMEM((sweeps, 2, CX, CY), F32),
            pltpu.VMEM((2, CX, CY), F32),
            pltpu.VMEM((sweeps, NV, CX, CY), F32),
            pltpu.VMEM((CXE, CY), F32),
            pltpu.VMEM((CAP * NFX, CY), F32),
            pltpu.VMEM((CAP * NFX, CY), F32),
            pltpu.VMEM((ITERS + 1, FACES, CY), F32),
            pltpu.VMEM((FACES, CY), F32),
            pltpu.VMEM((ITERS, CAP * NFX, CY), F32),
            pltpu.VMEM((EBD, FACES), F32),
            pltpu.VMEM((FACES, EBD), F32),
            pltpu.VMEM((CAP * NFX, CX), F32),
            pltpu.VMEM((CX, CAP * NFX), F32),
            pltpu.VMEM((EBD, EB), F32),
            pltpu.VMEM((EBD, EB), F32),
            pltpu.VMEM((EBD, EB), F32),
            pltpu.VMEM((EBD, EB), F32),
            pltpu.VMEM((ITERS, 3, CXE, CY), F32),
            pltpu.VMEM((2, CXE, CY), F32),
            pltpu.VMEM((2, CX, CY), F32),
            pltpu.VMEM((NZL + 2, CXE, CY), F32),
            pltpu.VMEM((CX, CY), F32),
            dma((11,)),
            dma((sweeps, 5)),
            dma((sweeps, 5)),
            dma((ITERS + 1,)),
            dma((ITERS + 1,)),
            dma((ITERS,)),
            dma((ITERS,)),
            dma((NFY,)),
            dma((2,)),
            dma((ITERS, 8)),
            dma((ITERS, 8)),
            dma((ITERS,)),
            dma((ITERS,)),
        ],
        compiler_params=pltpu.CompilerParams(
            collective_id=0, has_side_effects=True, vmem_limit_bytes=40 * 1024 * 1024
        ),
    )(
        state, kappa, mix, press_weight, source_weight, interp, block_inverse, coupling, front_order,
        face_owner.reshape(1, -1), face_slot.reshape(1, -1),
    )


def solution(mesh):
    return jax.shard_map(
        on_device,
        mesh=mesh,
        in_specs=(
            P(None, "fz", "fx", "fy"),
            P("fz", "fx", "fy"),
            P(),
            P(),
            P(),
            P(),
            P("fx", None, None),
            P("fx", None, None),
            P("fx", None),
            P(("fx", "fy"), None),
            P(("fx", "fy")),
        ),
        out_specs=(P(None, "fz", "fx", "fy"), P("fx", None)),
        check_vma=False,
    )
```

```python
import jax
import jax.numpy as jnp
from jax import lax
from jax.experimental import pallas as pl
from jax.experimental.pallas import tpu as pltpu
from jax.sharding import PartitionSpec as P

ITERS = 3
DIFFUSION = 0.16
HIGHEST = lax.Precision.HIGHEST
MESH = pl.DeviceIdType.MESH
F32 = jnp.float32
BF16 = jnp.bfloat16

NV, NZL, CX, CY = 5, 8, 32, 128
NZ = 16
NFX, NFY = 32, 4
RING_Z, RING_Y = 8, 4
EB, EBD, CAP = 128, 16, 2
FACES = NFX * NFY * CAP
PAD = 8
CXE = CX + 2 * PAD
NT = (((1,), (1,)), ((), ()))
FAR_Y = (2, 1, 3, 0)


def far_first(step, ring):
    return ring // 2 + (1 - 2 * (step % 2)) * ((step + 1) // 2)


def split(values):
    high = values.astype(BF16)
    return high, (values - high.astype(F32)).astype(BF16)


def pick(selector, values):
    high, low = split(values)
    return jnp.dot(selector, high, preferred_element_type=F32) + jnp.dot(selector, low, preferred_element_type=F32)


def kernel(
    state_in, kappa_in, mix_in, press_in, source_in, interp_in, inverse_in, coupling_in, order_in, owner_in, slot_in,
    state_out, raised_out, disp_out,
    mix, press_weight, source_weight, interp, order, owner, slot,
    S, K, KX, KE, BI, CO, R, XS, XR, YS, YR, YK, ZR, KZ, SL, SF, RF, SD, RD, FP, FPT, AM, AT, FR, XV, DV, DR,
    WN, LP, LE, QB, PB,
    load_sem, hsend, hrecv, fsend, frecv, dsend, drecv, osend, orecv, wsend, wrecv, rsend, rrecv,
):
    ix, iy, iz = lax.axis_index("fx"), lax.axis_index("fy"), lax.axis_index("fz")
    ring_z, ring_y = ix // RING_Y, ix % RING_Y
    on_wall = iz == 0
    off_wall = iz == 1
    is_solver = iy == ring_y
    not_solver = jnp.logical_not(is_solver)
    turned_y = {d: (ring_y + d) % RING_Y for d in FAR_Y}
    turned_x = {d: (iy + d) % NFY for d in FAR_Y}
    answer_x = ((iy + 2 - iz) % NFY, (iy + 3 * iz) % NFY)

    def row_base(step):
        return ((ring_z + far_first(step, RING_Z)) % RING_Z) * RING_Y

    def signal(barrier, device):
        pl.semaphore_signal(barrier, inc=1, device_id=device, device_id_type=MESH)

    loads = [
        pltpu.make_async_copy(source, target, load_sem.at[n])
        for n, (source, target) in enumerate(
            (
                (owner_in, owner),
                (slot_in, slot),
                (order_in, order),
                (kappa_in, K),
                (state_in, S.at[0, :, pl.ds(1, NZL)]),
                (inverse_in, BI),
                (coupling_in, CO),
                (interp_in, interp),
                (mix_in, mix),
                (press_in, press_weight),
                (source_in, source_weight),
            )
        )
    ]
    for load in loads:
        load.start()

    barrier = pltpu.get_barrier_semaphore()
    has_left, has_right, has_front, has_back = ix > 0, ix < NFX - 1, iy > 0, iy < NFY - 1
    sides = (
        (has_left, (ix - 1, iy, iz)),
        (has_right, (ix + 1, iy, iz)),
        (has_front, (ix, iy - 1, iz)),
        (has_back, (ix, iy + 1, iz)),
    )
    corners = (
        (jnp.logical_and(has_left, has_front), (ix - 1, iy - 1, iz)),
        (jnp.logical_and(has_left, has_back), (ix - 1, iy + 1, iz)),
        (jnp.logical_and(has_right, has_front), (ix + 1, iy - 1, iz)),
        (jnp.logical_and(has_right, has_back), (ix + 1, iy + 1, iz)),
    )
    other_core = (ix, iy, 1 - iz)

    @pl.when(is_solver)
    def _():
        def greet(step, carry):
            base = row_base(step)
            for dy in FAR_Y:
                for dx in FAR_Y:
                    signal(barrier, (base + turned_y[dy], turned_x[dx], 0))
            return carry

        lax.fori_loop(0, RING_Z - 1, greet, 0)
        for dy in FAR_Y:
            for dx in FAR_Y:
                if dy or dx:
                    signal(barrier, (ring_z * RING_Y + turned_y[dy], turned_x[dx], 0))

        @pl.when(off_wall)
        def _():
            signal(barrier, (ix, iy, 0))

    @pl.when(on_wall)
    def _():
        cores = {dy: (iy + turned_y[dy]) % 2 for dy in FAR_Y}

        def greet(step, carry):
            base = row_base(step)
            for dy in FAR_Y:
                signal(barrier, (base + turned_y[dy], turned_y[dy], cores[dy]))
            return carry

        lax.fori_loop(0, RING_Z - 1, greet, 0)
        for dy in FAR_Y[:3]:
            signal(barrier, (ring_z * RING_Y + turned_y[dy], turned_y[dy], cores[dy]))

        @pl.when(not_solver)
        def _():
            signal(barrier, (ix, ring_y, cores[0]))

    @pl.when(not_solver)
    def _():
        signal(barrier, (ix, ring_y, iz))

    for ref in (XR, YR, WN):
        ref[...] = jnp.zeros_like(ref)

    signal(barrier, other_core)
    solver_count = is_solver.astype(jnp.int32)
    wall_count = on_wall.astype(jnp.int32)
    expected = 1 + wall_count * (2 * NFX - solver_count) + solver_count * (2 * NFX - wall_count + NFY - 1)
    for present, device in sides + corners:
        expected = expected + present.astype(jnp.int32)

        @pl.when(present)
        def _():
            signal(barrier, device)

    zero_plane = jnp.zeros((NV, CX, CY), F32)
    for buffer in range(2):
        S[buffer, :, 0] = zero_plane
        S[buffer, :, NZL + 1] = zero_plane

    for load in loads[:3]:
        load.wait()
    rows = lax.broadcasted_iota(jnp.int32, (CAP * NFX, CX), 0)
    named = (owner[...] == rows // CAP).astype(F32)
    earlier = (
        lax.broadcasted_iota(jnp.int32, (CX, CX), 0) < lax.broadcasted_iota(jnp.int32, (CX, CX), 1)
    ).astype(BF16)
    rank = jnp.dot(named.astype(BF16), earlier, preferred_element_type=F32)
    chosen = jnp.where(rank == (rows % CAP).astype(F32), named, 0.0)
    AM[...] = chosen
    unit = (lax.broadcasted_iota(jnp.int32, (CX, CX), 0) == lax.broadcasted_iota(jnp.int32, (CX, CX), 1)).astype(F32)
    AT[...] = lax.dot_general(unit, chosen, NT, preferred_element_type=F32)
    slot_rows = jnp.sum(chosen * (slot[...] + 1).astype(F32), axis=1, keepdims=True)
    SL[...] = jnp.broadcast_to(slot_rows, (CAP * NFX, CY))
    block_rows = lax.broadcasted_iota(jnp.int32, (EBD, EB), 0)
    block_lanes = lax.broadcasted_iota(jnp.int32, (EBD, EB), 1)
    placed = jnp.zeros((EBD, EB), F32)
    for k in range(EBD):
        placed = jnp.where(jnp.logical_and(block_rows == k, block_lanes == order[0, k]), 1.0, placed)

    lane = lax.broadcasted_iota(jnp.int32, (CX, CY), 1)
    row = lax.broadcasted_iota(jnp.int32, (CX, CY), 0)
    for load in loads[3:5]:
        load.wait()

    def kappa_faces(z, carry):
        low, high = carry
        coeff = DIFFUSION * K[z]
        KX[z + 1, PAD : PAD + CX] = coeff
        XS[0, NV, pl.ds(z, 1), :] = coeff[0:1]
        XS[1, NV, pl.ds(z, 1), :] = coeff[CX - 1 : CX]
        here = lane == NV * NZL + z
        return jnp.where(here, coeff[:, 0:1], low), jnp.where(here, coeff[:, CY - 1 : CY], high)

    nothing = jnp.zeros((CX, CY), F32)
    YK[0], YK[1] = lax.fori_loop(0, NZL, kappa_faces, (nothing, nothing))

    def pack(src):
        def plane(z, carry):
            low, high = carry
            for c in range(NV):
                centre = src[c, z + 1]
                XS[0, c, pl.ds(z, 1), :] = centre[0:1]
                XS[1, c, pl.ds(z, 1), :] = centre[CX - 1 : CX]
                here = lane == c * NZL + z
                low = jnp.where(here, centre[:, 0:1], low)
                high = jnp.where(here, centre[:, CY - 1 : CY], high)
            return low, high

        YS[0], YS[1] = lax.fori_loop(0, NZL, plane, (YK[0], YK[1]))

    edge = NZL - (NZL - 1) * iz

    def halo_copies(n, src):
        def remote(source, target, at, there, device):
            return pltpu.make_async_remote_copy(
                source, target, hsend.at[n, at], hrecv.at[n, there], device_id=device, device_id_type=MESH
            )

        (_, left), (_, right), (_, front), (_, back) = sides
        always = iz >= 0
        plane = src.at[:, edge]
        sends = (
            (has_left, remote(XS.at[0], XR.at[n, 1], 0, 1, left)),
            (has_right, remote(XS.at[1], XR.at[n, 0], 1, 0, right)),
            (has_front, remote(YS.at[0], YR.at[n, 1], 2, 3, front)),
            (has_back, remote(YS.at[1], YR.at[n, 0], 3, 2, back)),
            (always, remote(plane, ZR.at[n], 4, 4, other_core)),
        )
        waits = (
            (has_left, remote(XS.at[0], XR.at[n, 0], 0, 0, left)),
            (has_right, remote(XS.at[1], XR.at[n, 1], 1, 1, right)),
            (has_front, remote(YS.at[0], YR.at[n, 0], 2, 2, front)),
            (has_back, remote(YS.at[1], YR.at[n, 1], 3, 3, back)),
            (always, remote(plane, ZR.at[n], 4, 4, other_core)),
        )
        return sends, waits

    def each(copies, action):
        for present, copy in copies:

            @pl.when(present)
            def _():
                action(copy)

    def start_halo(n, src):
        each(halo_copies(n, src)[0], lambda copy: copy.start())

    def finish_halo(n, src):
        sends, waits = halo_copies(n, src)
        each(waits, lambda copy: copy.wait_recv())
        each(sends, lambda copy: copy.wait_send())
        src[:, (NZL + 1) * (1 - iz)] = ZR[n]

    def sweep(n, src, dst):
        def plane(z, carry):
            coeff = KX[z + 1, PAD : PAD + CX]
            centres = [src[c, z + 1] for c in range(NV)]
            for c in range(NV):
                centre = centres[c]
                at = c * NZL + z
                beside = src[c, z] + src[c, z + 2]
                beside += jnp.where(row == 0, XR[n, 0, c, pl.ds(z, 1), :], pltpu.roll(centre, 1, 0))
                beside += jnp.where(row == CX - 1, XR[n, 1, c, pl.ds(z, 1), :], pltpu.roll(centre, CX - 1, 0))
                front = pltpu.roll(YR[n, 0], (CY - at) % CY, 1)
                back = pltpu.roll(YR[n, 1], CY - 1 - at, 1)
                beside += jnp.where(lane == 0, front, pltpu.roll(centre, 1, 1))
                beside += jnp.where(lane == CY - 1, back, pltpu.roll(centre, CY - 1, 1))
                total = centre + coeff * (beside - 6.0 * centre)
                for d in range(NV):
                    total += mix[c, d] * centres[d]
                dst[c, z + 1] = total
            return carry

        lax.fori_loop(0, NZL, plane, 0)

    kappa_plane = pltpu.make_async_remote_copy(
        KX.at[edge], KZ, osend.at[0], orecv.at[0], device_id=other_core, device_id_type=MESH
    )

    def send_to_solvers(turn, rows_out):
        target = RF.at[turn, pl.ds(CAP * (ix * NFY + iy), CAP)]

        def send(to, y, core):
            pltpu.make_async_remote_copy(
                rows_out.at[pl.ds(CAP * to, CAP)], target, fsend.at[turn], frecv.at[turn],
                device_id=(to, y, core), device_id_type=MESH,
            ).start()

        def group(step, carry):
            base = row_base(step)
            for dy in FAR_Y:
                for core in range(2):
                    send(base + turned_y[dy], turned_y[dy], core)
            return carry

        @pl.when(on_wall)
        def _():
            lax.fori_loop(0, RING_Z - 1, group, 0)
            for dy in FAR_Y[:3]:
                for core in range(2):
                    send(ring_z * RING_Y + turned_y[dy], turned_y[dy], core)
            send(ix, ring_y, 1)

            @pl.when(not_solver)
            def _():
                send(ix, ring_y, 0)

            @pl.when(is_solver)
            def _():
                pltpu.make_async_copy(rows_out.at[pl.ds(CAP * ix, CAP)], target, frecv.at[turn]).start()

    def sent_to_solvers(turn):
        @pl.when(on_wall)
        def _():
            @pl.when(is_solver)
            def _():
                rest = RF.at[turn, pl.ds(0, CAP * (2 * NFX - 1))]
                pltpu.make_async_copy(rest, rest, fsend.at[turn]).wait()

            @pl.when(not_solver)
            def _():
                rest = RF.at[turn, pl.ds(0, CAP * 2 * NFX)]
                pltpu.make_async_copy(rest, rest, fsend.at[turn]).wait()

    def heard_from_faces(turn):
        whole = RF.at[turn]
        pltpu.make_async_copy(whole, whole, frecv.at[turn]).wait()

    def send_to_faces(turn):
        target = RD.at[turn, pl.ds(CAP * ix, CAP)]

        def send(to_x, to_y):
            pltpu.make_async_remote_copy(
                SD.at[pl.ds(CAP * (to_x * NFY + to_y), CAP)], target, dsend.at[turn], drecv.at[turn],
                device_id=(to_x, to_y, 0), device_id_type=MESH,
            ).start()

        def group(step, carry):
            base = row_base(step)
            for dy in FAR_Y:
                for x in answer_x:
                    send(base + turned_y[dy], x)
            return carry

        lax.fori_loop(0, RING_Z - 1, group, 0)
        for dy in FAR_Y[:3]:
            for x in answer_x:
                send(ring_z * RING_Y + turned_y[dy], x)
        send(ix, answer_x[0])

        @pl.when(off_wall)
        def _():
            send(ix, answer_x[1])

        @pl.when(on_wall)
        def _():
            pltpu.make_async_copy(SD.at[pl.ds(CAP * (ix * NFY + iy), CAP)], target, drecv.at[turn]).start()

    def sent_to_faces(turn):
        @pl.when(on_wall)
        def _():
            rest = RF.at[turn, pl.ds(0, CAP * (2 * NFX - 1))]
            pltpu.make_async_copy(rest, rest, dsend.at[turn]).wait()

        @pl.when(off_wall)
        def _():
            rest = RF.at[turn, pl.ds(0, CAP * 2 * NFX)]
            pltpu.make_async_copy(rest, rest, dsend.at[turn]).wait()

    for load in loads[5:]:
        load.wait()

    @pl.when(is_solver)
    def _():
        def products(k, carry):
            block = order[0, k]
            inverse = BI[block]
            force_part = lax.dot_general(interp[...], inverse, NT, precision=HIGHEST, preferred_element_type=F32)
            chain = jnp.dot(inverse, CO[block], precision=HIGHEST, preferred_element_type=F32)
            high, low = split(jnp.concatenate([force_part, -chain.T], axis=0))
            R[k] = jnp.concatenate([high, low], axis=1)
            return carry

        lax.fori_loop(0, EBD, products, 0)

    numbers = range(NV)
    source = [source_weight[c] for c in numbers]
    once = [source[c] + sum(mix[c, d] * source[d] for d in numbers) for c in numbers]
    twice = [once[c] + sum(mix[c, d] * once[d] for d in numbers) for c in numbers]
    press_source = sum(press_weight[c] * source[c] for c in numbers)
    press_once = sum(press_weight[c] * once[c] for c in numbers)
    press_twice = sum(press_weight[c] * twice[c] for c in numbers)

    pack(S.at[0])
    pl.semaphore_wait(barrier, expected)
    start_halo(0, S.at[0])
    kappa_plane.start()
    send_to_solvers(ITERS, SL)
    finish_halo(0, S.at[0])
    sweep(0, S.at[0], S.at[1])
    pack(S.at[1])
    start_halo(1, S.at[1])

    kappa_plane.wait()
    KX[(NZL + 1) * (1 - iz)] = KZ[...]
    KX[(NZL + 1) * iz] = jnp.zeros((CXE, CY), F32)
    tile_row = lax.broadcasted_iota(jnp.int32, (PAD, CY), 0)

    def kappa_edges(z, carry):
        KX[z + 1, 0:PAD] = jnp.where(tile_row == PAD - 1, XR[0, 0, NV, pl.ds(z, 1), :], 0.0)
        KX[z + 1, PAD + CX : CXE] = jnp.where(tile_row == 0, XR[0, 1, NV, pl.ds(z, 1), :], 0.0)
        at = NV * NZL + z
        front = pltpu.roll(YR[0, 0], CY - 1 - at, 1)
        back = pltpu.roll(YR[0, 1], (CY - at) % CY, 1)
        KE[z] = jnp.where(lane >= CY // 2, front, back)
        return carry

    lax.fori_loop(0, NZL, kappa_edges, 0)

    def wall_base():
        @pl.when(on_wall)
        def _():
            pressure = press_weight[0] * S[0, 0, 1]
            for c in range(1, NV):
                pressure += press_weight[c] * S[0, c, 1]
            PB[...] = pressure

    finish_halo(1, S.at[1])
    sweep(1, S.at[1], S.at[0])
    wall_base()
    sent_to_solvers(ITERS)

    @pl.when(on_wall)
    def _():
        SF[...] = pick(AM[...].astype(BF16), PB[...])

    send_to_solvers(0, SF)

    @pl.when(is_solver)
    def _():
        heard_from_faces(ITERS)
        face_lanes = lax.broadcasted_iota(jnp.int32, (FACES, EB), 1) + 1
        slot_of = (RF[ITERS] == face_lanes.astype(F32)).astype(F32)
        FP[...] = lax.dot_general(placed, slot_of, NT, preferred_element_type=F32)
        FPT[...] = lax.dot_general(slot_of, placed, NT, preferred_element_type=F32)

    def solve():
        for k in range(EBD):
            force = FR[pl.ds(k, 1), :]
            previous = XV[pl.ds(k - 1, 1), :] if k else jnp.zeros((1, EB), F32)
            both = jnp.concatenate([force, previous], axis=1)
            high = both.astype(BF16).astype(F32)
            at = lax.broadcasted_iota(jnp.int32, (8, 2 * EB), 0)
            left = jnp.where(at == 0, high, jnp.where(at == 1, both - high, 0.0)).astype(BF16)
            result = jnp.dot(left, R[k], preferred_element_type=F32)
            summed = result[:, :EB] + result[:, EB:]
            XV[pl.ds(k, 1), :] = summed[0:1] + summed[1:2]

    def wall_copies(it):
        def remote(n, opposite, source_row, side, target_row, count, device):
            copy = lambda here, there: pltpu.make_async_remote_copy(
                WN.at[it, 1, pl.ds(source_row, count)], WN.at[it, side, pl.ds(target_row, count)],
                wsend.at[it, here], wrecv.at[it, there], device_id=device, device_id_type=MESH,
            )
            return copy(n, opposite), copy(n, n)

        low, high = PAD, PAD + CX - 8
        (_, left), (_, right), (_, front), (_, back) = sides
        (lf, left_front), (lb, left_back), (rf, right_front), (rb, right_back) = corners
        return (
            (has_left, remote(0, 1, low, 1, PAD + CX, 8, left)),
            (has_right, remote(1, 0, high, 1, 0, 8, right)),
            (has_front, remote(2, 3, PAD, 2, PAD, CX, front)),
            (has_back, remote(3, 2, PAD, 0, PAD, CX, back)),
            (lf, remote(4, 7, low, 2, PAD + CX, 8, left_front)),
            (lb, remote(5, 6, low, 0, PAD + CX, 8, left_back)),
            (rf, remote(6, 5, high, 2, 0, 8, right_front)),
            (rb, remote(7, 4, high, 0, 0, 8, right_back)),
        )

    lane_e = lax.broadcasted_iota(jnp.int32, (CXE, CY), 1)
    inner = slice(PAD, PAD + CX)

    def spread(it):
        centre = WN[it, 1]
        beyond = jnp.where(lane_e >= CY // 2, WN[it, 0], WN[it, 2])
        up, down = pltpu.roll(centre, 1, 1), pltpu.roll(centre, CY - 1, 1)
        out_up, out_down = pltpu.roll(beyond, 1, 1), pltpu.roll(beyond, CY - 1, 1)
        lap = pltpu.roll(centre, 1, 0) + pltpu.roll(centre, CXE - 1, 0) - 4.0 * centre
        lap += jnp.where(lane_e == 0, out_up, up) + jnp.where(lane_e == CY - 1, out_down, down)
        lap_e = pltpu.roll(beyond, 1, 0) + pltpu.roll(beyond, CXE - 1, 0) - 4.0 * beyond
        lap_e += jnp.where(lane_e >= CY // 2, out_up + down, out_down + up)
        LP[0], LP[1] = lap, centre
        LE[0], LE[1] = lap_e[inner], beyond[inner]

    def ring_sum(wide, edge_columns, below, above, coeff):
        own = wide[inner]
        total = pltpu.roll(wide, 1, 0)[inner] + pltpu.roll(wide, CXE - 1, 0)[inner] + below + above - 6.0 * own
        total += jnp.where(lane == 0, pltpu.roll(edge_columns, 1, 1), pltpu.roll(own, 1, 1))
        total += jnp.where(lane == CY - 1, pltpu.roll(edge_columns, CY - 1, 1), pltpu.roll(own, CY - 1, 1))
        return coeff * total

    first_jump = (NZ - 1.0) / NZ - 2.0

    def wall_response(it):
        wide = KX[1] * (LP[0] + first_jump * LP[1])
        edges = KE[0] * (LE[0] + first_jump * LE[1])
        above = KX[2, inner] * ((NZ - 1.0) / NZ * LP[0, inner])
        bend = ring_sum(wide, edges, 0.0, above, KX[1, inner])
        return press_twice * LP[1, inner] + 2.0 * press_once * wide[inner] + press_source * bend

    def profile(plane):
        height = iz * NZL + plane - 1
        return 1.0 - height.astype(F32) / NZ, jnp.where(height == 0, first_jump, 0.0)

    def update():
        def first(plane, carry):
            share, jump = profile(plane)
            QB[plane] = KX[plane] * (share * LP[0] + jump * LP[1])
            return carry

        lax.fori_loop(0, NZL + 2, first, 0)

        def second(z, carry):
            share, jump = profile(z + 1)
            edges = KE[z] * (share * LE[0] + jump * LE[1])
            wide = QB[z + 1]
            bend = ring_sum(wide, edges, QB[z, inner], QB[z + 2, inner], KX[z + 1, inner])
            raised, slope = share * LP[1, inner], wide[inner]
            for c in range(NV):
                S[0, c, z + 1] += twice[c] * raised + 2.0 * once[c] * slope + source[c] * bend
            return carry

        lax.fori_loop(0, NZL, second, 0)

    def answer(it):
        heard_from_faces(it)
        FR[...] = pick(FP[...].astype(BF16), RF[it])
        solve()
        facing = lax.dot_general(XV[...], interp[...], NT, precision=HIGHEST, preferred_element_type=F32)
        SD[...] = pick(FPT[...].astype(BF16), facing)
        send_to_faces(it)

    def hear_wall(it):
        sent_to_solvers(it)
        whole = RD.at[it]
        pltpu.make_async_copy(whole, whole, drecv.at[it]).wait()
        WN[it, 1, inner] = pick(AT[...].astype(BF16), RD[it])

    def relay(it, part):
        return pltpu.make_async_remote_copy(
            part, part, rsend.at[it], rrecv.at[it], device_id=other_core, device_id_type=MESH
        )

    def iteration(it, carry):
        n = 2 * it + 2
        pack(S.at[0])
        start_halo(n, S.at[0])
        finish_halo(n, S.at[0])
        sweep(n, S.at[0], S.at[1])
        pack(S.at[1])
        start_halo(n + 1, S.at[1])

        @pl.when(is_solver)
        def _():
            answer(it)

        finish_halo(n + 1, S.at[1])
        sweep(n + 1, S.at[1], S.at[0])
        wall_base()
        beside_wall = relay(it, WN.at[it])

        @pl.when(on_wall)
        def _():
            hear_wall(it)
            copies = wall_copies(it)
            each(copies, lambda pair: pair[0].start())
            each(copies, lambda pair: pair[1].wait_recv())
            spread(it)
            SF[...] = pick(AM[...].astype(BF16), PB[...] + wall_response(it))
            send_to_solvers(it + 1, SF)
            beside_wall.start()
            each(copies, lambda pair: pair[0].wait_send())

        @pl.when(off_wall)
        def _():
            beside_wall.wait_recv()
            spread(it)

        update()

        @pl.when(on_wall)
        def _():
            beside_wall.wait_send()

        @pl.when(is_solver)
        def _():
            sent_to_faces(it)

        return carry

    lax.fori_loop(0, ITERS - 1, iteration, 0)

    last = ITERS - 1
    out = pltpu.make_async_copy(S.at[0, :, pl.ds(1, NZL)], state_out, load_sem.at[0])
    out.start()

    def disp_copy(t):
        return pltpu.make_async_remote_copy(
            DV, DR, osend.at[t], orecv.at[1], device_id=(ix, (iy + t) % NFY, iz), device_id_type=MESH
        )

    @pl.when(is_solver)
    def _():
        answer(last)
        back = lax.dot_general(placed, XV[...], (((0,), (0,)), ((), ())), precision=HIGHEST, preferred_element_type=F32)
        DV[...] = back[:EBD]
        for t in range(1, NFY):
            disp_copy(t).start()
        disp_out[...] = back[:EBD]

    beside_wall = relay(last, WN.at[last, 1, pl.ds(PAD, CX)])

    @pl.when(on_wall)
    def _():
        hear_wall(last)
        beside_wall.start()

    @pl.when(off_wall)
    def _():
        beside_wall.wait_recv()

    for z in range(NZL):
        share, _ = profile(z + 1)
        raised_out[z] = share * WN[last, 1, inner]

    @pl.when(on_wall)
    def _():
        beside_wall.wait_send()

    @pl.when(is_solver)
    def _():
        sent_to_faces(last)
        for t in range(1, NFY):
            disp_copy(t).wait_send()

    @pl.when(not_solver)
    def _():
        disp_copy(1).wait_recv()
        disp_out[...] = DR[...]

    out.wait()


def on_device(
    state, kappa, mix, press_weight, source_weight, interp, block_inverse, coupling, front_order, face_owner, face_slot
):
    hbm = pl.BlockSpec(memory_space=pltpu.HBM)
    vmem = pl.BlockSpec(memory_space=pltpu.VMEM)
    dma = pltpu.SemaphoreType.DMA
    sweeps = 2 * ITERS
    before, raised, displacement = pl.pallas_call(
        kernel,
        out_shape=(
            jax.ShapeDtypeStruct(state.shape, F32),
            jax.ShapeDtypeStruct(kappa.shape, F32),
            jax.ShapeDtypeStruct((EBD, EB), F32),
        ),
        in_specs=[hbm] * 11,
        out_specs=(hbm, vmem, vmem),
        scratch_shapes=[
            pltpu.SMEM((NV, NV), F32),
            pltpu.SMEM((NV,), F32),
            pltpu.SMEM((NV,), F32),
            pltpu.VMEM((CY, EB), F32),
            pltpu.SMEM((1, EBD), jnp.int32),
            pltpu.VMEM((1, CX), jnp.int32),
            pltpu.VMEM((1, CX), jnp.int32),
            pltpu.VMEM((2, NV, NZL + 2, CX, CY), F32),
            pltpu.VMEM((NZL, CX, CY), F32),
            pltpu.VMEM((NZL + 2, CXE, CY), F32),
            pltpu.VMEM((NZL, CX, CY), F32),
            pltpu.VMEM((EBD, EB, EB), F32),
            pltpu.VMEM((EBD, EB, EB), F32),
            pltpu.VMEM((EBD, 2 * EB, 2 * EB), BF16),
            pltpu.VMEM((2, NV + 1, NZL, CY), F32),
            pltpu.VMEM((sweeps, 2, NV + 1, NZL, CY), F32),
            pltpu.VMEM((2, CX, CY), F32),
            pltpu.VMEM((sweeps, 2, CX, CY), F32),
            pltpu.VMEM((2, CX, CY), F32),
            pltpu.VMEM((sweeps, NV, CX, CY), F32),
            pltpu.VMEM((CXE, CY), F32),
            pltpu.VMEM((CAP * NFX, CY), F32),
            pltpu.VMEM((CAP * NFX, CY), F32),
            pltpu.VMEM((ITERS + 1, FACES, CY), F32),
            pltpu.VMEM((FACES, CY), F32),
            pltpu.VMEM((ITERS, CAP * NFX, CY), F32),
            pltpu.VMEM((EBD, FACES), F32),
            pltpu.VMEM((FACES, EBD), F32),
            pltpu.VMEM((CAP * NFX, CX), F32),
            pltpu.VMEM((CX, CAP * NFX), F32),
            pltpu.VMEM((EBD, EB), F32),
            pltpu.VMEM((EBD, EB), F32),
            pltpu.VMEM((EBD, EB), F32),
            pltpu.VMEM((EBD, EB), F32),
            pltpu.VMEM((ITERS, 3, CXE, CY), F32),
            pltpu.VMEM((2, CXE, CY), F32),
            pltpu.VMEM((2, CX, CY), F32),
            pltpu.VMEM((NZL + 2, CXE, CY), F32),
            pltpu.VMEM((CX, CY), F32),
            dma((11,)),
            dma((sweeps, 5)),
            dma((sweeps, 5)),
            dma((ITERS + 1,)),
            dma((ITERS + 1,)),
            dma((ITERS,)),
            dma((ITERS,)),
            dma((NFY,)),
            dma((2,)),
            dma((ITERS, 8)),
            dma((ITERS, 8)),
            dma((ITERS,)),
            dma((ITERS,)),
        ],
        compiler_params=pltpu.CompilerParams(
            collective_id=0, has_side_effects=True, vmem_limit_bytes=60 * 1024 * 1024
        ),
    )(
        state, kappa, mix, press_weight, source_weight, interp, block_inverse, coupling, front_order,
        face_owner.reshape(1, -1), face_slot.reshape(1, -1),
    )
    return before + source_weight[:, None, None, None] * raised[None], displacement


def solution(mesh):
    return jax.shard_map(
        on_device,
        mesh=mesh,
        in_specs=(
            P(None, "fz", "fx", "fy"),
            P("fz", "fx", "fy"),
            P(),
            P(),
            P(),
            P(),
            P("fx", None, None),
            P("fx", None, None),
            P("fx", None),
            P(("fx", "fy"), None),
            P(("fx", "fy")),
        ),
        out_specs=(P(None, "fz", "fx", "fy"), P("fx", None)),
        check_vma=False,
    )
```

```python
import jax
import jax.numpy as jnp
from jax import lax
from jax.experimental import pallas as pl
from jax.experimental.pallas import tpu as pltpu
from jax.sharding import PartitionSpec as P

ITERS = 3
DIFFUSION = 0.16
HIGHEST = lax.Precision.HIGHEST
MESH = pl.DeviceIdType.MESH
F32 = jnp.float32
BF16 = jnp.bfloat16

NV, NZL, CX, CY = 5, 8, 32, 128
NZ = 16
NFX, NFY = 32, 4
RING_Z, RING_Y = 8, 4
EB, EBD, CAP = 128, 16, 2
FACES = NFX * NFY * CAP
PAD = 8
CXE = CX + 2 * PAD
NT = (((1,), (1,)), ((), ()))
FAR_Y = (2, 1, 3, 0)
AROUND = 11


def far_first(step, ring):
    return ring // 2 + (1 - 2 * (step % 2)) * ((step + 1) // 2)


def split(values):
    high = values.astype(BF16)
    return high, (values - high.astype(F32)).astype(BF16)


def pick(selector, values):
    high, low = split(values)
    return jnp.dot(selector, high, preferred_element_type=F32) + jnp.dot(selector, low, preferred_element_type=F32)


def kernel(
    state_in, kappa_in, mix_in, press_in, source_in, interp_in, inverse_in, coupling_in, order_in, owner_in, slot_in,
    state_out, raised_out, disp_out,
    mix, press_weight, source_weight, interp, order, owner, slot,
    S, K, KX, KE, BI, CO, R, XS, XR, YS, YR, YK, ZR, KZ, SL, SF, CS, RF, RC, SD, RD, FP, FPT, AM, AT, FR, XV, DV, DR,
    WN, LP, LE, QB, PB, G, GW, IN, XO, XA,
    load_sem, hsend, hrecv, fsend, frecv, dsend, drecv, osend, orecv, wsend, wrecv, rsend, rrecv, csend, crecv, xsend, xrecv,
):
    ix, iy, iz = lax.axis_index("fx"), lax.axis_index("fy"), lax.axis_index("fz")
    ring_z, ring_y = ix // RING_Y, ix % RING_Y
    on_wall = iz == 0
    off_wall = iz == 1
    is_solver = iy == ring_y
    not_solver = jnp.logical_not(is_solver)
    turned_y = {d: (ring_y + d) % RING_Y for d in FAR_Y}
    turned_x = {d: (iy + d) % NFY for d in FAR_Y}
    answer_x = ((iy + 2 - iz) % NFY, (iy + 3 * iz) % NFY)

    def row_base(step):
        return ((ring_z + far_first(step, RING_Z)) % RING_Z) * RING_Y

    def signal(barrier, device):
        pl.semaphore_signal(barrier, inc=1, device_id=device, device_id_type=MESH)

    loads = [
        pltpu.make_async_copy(source, target, load_sem.at[n])
        for n, (source, target) in enumerate(
            (
                (owner_in, owner),
                (slot_in, slot),
                (order_in, order),
                (kappa_in, K),
                (state_in, S.at[0, :, pl.ds(1, NZL)]),
                (inverse_in, BI),
                (coupling_in, CO),
                (interp_in, interp),
                (mix_in, mix),
                (press_in, press_weight),
                (source_in, source_weight),
            )
        )
    ]
    for load in loads:
        load.start()

    barrier = pltpu.get_barrier_semaphore()
    has_left, has_right, has_front, has_back = ix > 0, ix < NFX - 1, iy > 0, iy < NFY - 1
    sides = (
        (has_left, (ix - 1, iy, iz)),
        (has_right, (ix + 1, iy, iz)),
        (has_front, (ix, iy - 1, iz)),
        (has_back, (ix, iy + 1, iz)),
    )
    corners = (
        (jnp.logical_and(has_left, has_front), (ix - 1, iy - 1, iz)),
        (jnp.logical_and(has_left, has_back), (ix - 1, iy + 1, iz)),
        (jnp.logical_and(has_right, has_front), (ix + 1, iy - 1, iz)),
        (jnp.logical_and(has_right, has_back), (ix + 1, iy + 1, iz)),
    )
    other_core = (ix, iy, 1 - iz)

    @pl.when(is_solver)
    def _():
        def greet(step, carry):
            base = row_base(step)
            for dy in FAR_Y:
                for dx in FAR_Y:
                    signal(barrier, (base + turned_y[dy], turned_x[dx], 0))
            return carry

        lax.fori_loop(0, RING_Z - 1, greet, 0)
        for dy in FAR_Y:
            for dx in FAR_Y:
                if dy or dx:
                    signal(barrier, (ring_z * RING_Y + turned_y[dy], turned_x[dx], 0))

        @pl.when(off_wall)
        def _():
            signal(barrier, (ix, iy, 0))

        def greet_solvers(step, carry):
            base = row_base(step)
            for dy in FAR_Y:
                signal(barrier, (base + turned_y[dy], turned_y[dy], iz))
            return carry

        lax.fori_loop(0, RING_Z - 1, greet_solvers, 0)
        for dy in FAR_Y[:3]:
            signal(barrier, (ring_z * RING_Y + turned_y[dy], turned_y[dy], iz))

    @pl.when(on_wall)
    def _():
        cores = {dy: (iy + turned_y[dy]) % 2 for dy in FAR_Y}

        def greet(step, carry):
            base = row_base(step)
            for dy in FAR_Y:
                signal(barrier, (base + turned_y[dy], turned_y[dy], cores[dy]))
            return carry

        lax.fori_loop(0, RING_Z - 1, greet, 0)
        for dy in FAR_Y[:3]:
            signal(barrier, (ring_z * RING_Y + turned_y[dy], turned_y[dy], cores[dy]))

        @pl.when(not_solver)
        def _():
            signal(barrier, (ix, ring_y, cores[0]))

    @pl.when(not_solver)
    def _():
        signal(barrier, (ix, ring_y, iz))

    for ref in (XR, YR, WN):
        ref[...] = jnp.zeros_like(ref)

    signal(barrier, other_core)
    solver_count = is_solver.astype(jnp.int32)
    wall_count = on_wall.astype(jnp.int32)
    expected = 1 + wall_count * (2 * NFX - solver_count) + solver_count * (2 * NFX - wall_count + NFY - 1 + NFX - 1)
    for present, device in sides + corners:
        expected = expected + present.astype(jnp.int32)

        @pl.when(present)
        def _():
            signal(barrier, device)

    zero_plane = jnp.zeros((NV, CX, CY), F32)
    for buffer in range(2):
        S[buffer, :, 0] = zero_plane
        S[buffer, :, NZL + 1] = zero_plane

    for load in loads[:3]:
        load.wait()
    rows = lax.broadcasted_iota(jnp.int32, (CAP * NFX, CX), 0)
    named = (owner[...] == rows // CAP).astype(F32)
    earlier = (
        lax.broadcasted_iota(jnp.int32, (CX, CX), 0) < lax.broadcasted_iota(jnp.int32, (CX, CX), 1)
    ).astype(BF16)
    rank = jnp.dot(named.astype(BF16), earlier, preferred_element_type=F32)
    chosen = jnp.where(rank == (rows % CAP).astype(F32), named, 0.0)
    AM[...] = chosen
    unit = (lax.broadcasted_iota(jnp.int32, (CX, CX), 0) == lax.broadcasted_iota(jnp.int32, (CX, CX), 1)).astype(F32)
    AT[...] = lax.dot_general(unit, chosen, NT, preferred_element_type=F32)
    slot_rows = jnp.sum(chosen * (slot[...] + 1).astype(F32), axis=1, keepdims=True)
    SL[...] = jnp.broadcast_to(slot_rows, (CAP * NFX, CY))
    target_of = jnp.sum(unit * (EBD * owner[...] + slot[...] + 1).astype(F32), axis=1, keepdims=True)
    WN[ITERS, 1, PAD : PAD + CX] = jnp.broadcast_to(target_of, (CX, CY))
    block_rows = lax.broadcasted_iota(jnp.int32, (EBD, EB), 0)
    block_lanes = lax.broadcasted_iota(jnp.int32, (EBD, EB), 1)
    placed = jnp.zeros((EBD, EB), F32)
    for k in range(EBD):
        placed = jnp.where(jnp.logical_and(block_rows == k, block_lanes == order[0, k]), 1.0, placed)

    lane = lax.broadcasted_iota(jnp.int32, (CX, CY), 1)
    row = lax.broadcasted_iota(jnp.int32, (CX, CY), 0)
    for load in loads[3:5]:
        load.wait()

    def kappa_faces(z, carry):
        low, high = carry
        coeff = DIFFUSION * K[z]
        KX[z + 1, PAD : PAD + CX] = coeff
        XS[0, NV, pl.ds(z, 1), :] = coeff[0:1]
        XS[1, NV, pl.ds(z, 1), :] = coeff[CX - 1 : CX]
        here = lane == NV * NZL + z
        return jnp.where(here, coeff[:, 0:1], low), jnp.where(here, coeff[:, CY - 1 : CY], high)

    nothing = jnp.zeros((CX, CY), F32)
    YK[0], YK[1] = lax.fori_loop(0, NZL, kappa_faces, (nothing, nothing))

    def pack(src):
        def plane(z, carry):
            low, high = carry
            for c in range(NV):
                centre = src[c, z + 1]
                XS[0, c, pl.ds(z, 1), :] = centre[0:1]
                XS[1, c, pl.ds(z, 1), :] = centre[CX - 1 : CX]
                here = lane == c * NZL + z
                low = jnp.where(here, centre[:, 0:1], low)
                high = jnp.where(here, centre[:, CY - 1 : CY], high)
            return low, high

        YS[0], YS[1] = lax.fori_loop(0, NZL, plane, (YK[0], YK[1]))

    edge = NZL - (NZL - 1) * iz

    def halo_copies(n, src):
        def remote(source, target, at, there, device):
            return pltpu.make_async_remote_copy(
                source, target, hsend.at[n, at], hrecv.at[n, there], device_id=device, device_id_type=MESH
            )

        (_, left), (_, right), (_, front), (_, back) = sides
        always = iz >= 0
        plane = src.at[:, edge]
        sends = (
            (has_left, remote(XS.at[0], XR.at[n, 1], 0, 1, left)),
            (has_right, remote(XS.at[1], XR.at[n, 0], 1, 0, right)),
            (has_front, remote(YS.at[0], YR.at[n, 1], 2, 3, front)),
            (has_back, remote(YS.at[1], YR.at[n, 0], 3, 2, back)),
            (always, remote(plane, ZR.at[n], 4, 4, other_core)),
        )
        waits = (
            (has_left, remote(XS.at[0], XR.at[n, 0], 0, 0, left)),
            (has_right, remote(XS.at[1], XR.at[n, 1], 1, 1, right)),
            (has_front, remote(YS.at[0], YR.at[n, 0], 2, 2, front)),
            (has_back, remote(YS.at[1], YR.at[n, 1], 3, 3, back)),
            (always, remote(plane, ZR.at[n], 4, 4, other_core)),
        )
        return sends, waits

    def each(copies, action):
        for present, copy in copies:

            @pl.when(present)
            def _():
                action(copy)

    def start_halo(n, src):
        each(halo_copies(n, src)[0], lambda copy: copy.start())

    def finish_halo(n, src):
        sends, waits = halo_copies(n, src)
        each(waits, lambda copy: copy.wait_recv())
        each(sends, lambda copy: copy.wait_send())
        src[:, (NZL + 1) * (1 - iz)] = ZR[n]

    def sweep(n, src, dst):
        def plane(z, carry):
            coeff = KX[z + 1, PAD : PAD + CX]
            centres = [src[c, z + 1] for c in range(NV)]
            for c in range(NV):
                centre = centres[c]
                at = c * NZL + z
                beside = src[c, z] + src[c, z + 2]
                beside += jnp.where(row == 0, XR[n, 0, c, pl.ds(z, 1), :], pltpu.roll(centre, 1, 0))
                beside += jnp.where(row == CX - 1, XR[n, 1, c, pl.ds(z, 1), :], pltpu.roll(centre, CX - 1, 0))
                front = pltpu.roll(YR[n, 0], (CY - at) % CY, 1)
                back = pltpu.roll(YR[n, 1], CY - 1 - at, 1)
                beside += jnp.where(lane == 0, front, pltpu.roll(centre, 1, 1))
                beside += jnp.where(lane == CY - 1, back, pltpu.roll(centre, CY - 1, 1))
                total = centre + coeff * (beside - 6.0 * centre)
                for d in range(NV):
                    total += mix[c, d] * centres[d]
                dst[c, z + 1] = total
            return carry

        lax.fori_loop(0, NZL, plane, 0)

    kappa_plane = pltpu.make_async_remote_copy(
        KX.at[edge], KZ, osend.at[0], orecv.at[0], device_id=other_core, device_id_type=MESH
    )

    def send_to_solvers(rows_of, target, sent, heard):
        def send(to, y, core):
            pltpu.make_async_remote_copy(
                rows_of(to), target, sent, heard, device_id=(to, y, core), device_id_type=MESH
            ).start()

        def group(step, carry):
            base = row_base(step)
            for dy in FAR_Y:
                for core in range(2):
                    send(base + turned_y[dy], turned_y[dy], core)
            return carry

        @pl.when(on_wall)
        def _():
            lax.fori_loop(0, RING_Z - 1, group, 0)
            for dy in FAR_Y[:3]:
                for core in range(2):
                    send(ring_z * RING_Y + turned_y[dy], turned_y[dy], core)
            send(ix, ring_y, 1)

            @pl.when(not_solver)
            def _():
                send(ix, ring_y, 0)

            @pl.when(is_solver)
            def _():
                pltpu.make_async_copy(rows_of(ix), target, heard).start()

    own_rows = pl.ds(CAP * (ix * NFY + iy), CAP)

    def send_rows(turn, rows_out):
        send_to_solvers(
            lambda to: rows_out.at[pl.ds(CAP * to, CAP)], RF.at[turn, own_rows], fsend.at[turn], frecv.at[turn]
        )

    def send_pressure(turn):
        @pl.when(on_wall)
        def _():
            SF[...] = pick(AM[...].astype(BF16), PB[...])

        send_rows(turn, SF)

    def sent_to_solvers(turn):
        @pl.when(on_wall)
        def _():
            @pl.when(is_solver)
            def _():
                rest = RF.at[turn, pl.ds(0, CAP * (2 * NFX - 1))]
                pltpu.make_async_copy(rest, rest, fsend.at[turn]).wait()

            @pl.when(not_solver)
            def _():
                rest = RF.at[turn, pl.ds(0, CAP * 2 * NFX)]
                pltpu.make_async_copy(rest, rest, fsend.at[turn]).wait()

    def heard_from_faces(turn):
        whole = RF.at[turn]
        pltpu.make_async_copy(whole, whole, frecv.at[turn]).wait()

    def send_to_faces(turn):
        target = RD.at[turn, pl.ds(CAP * ix, CAP)]

        def send(to_x, to_y):
            pltpu.make_async_remote_copy(
                SD.at[pl.ds(CAP * (to_x * NFY + to_y), CAP)], target, dsend.at[turn], drecv.at[turn],
                device_id=(to_x, to_y, 0), device_id_type=MESH,
            ).start()

        def group(step, carry):
            base = row_base(step)
            for dy in FAR_Y:
                for x in answer_x:
                    send(base + turned_y[dy], x)
            return carry

        lax.fori_loop(0, RING_Z - 1, group, 0)
        for dy in FAR_Y[:3]:
            for x in answer_x:
                send(ring_z * RING_Y + turned_y[dy], x)
        send(ix, answer_x[0])

        @pl.when(off_wall)
        def _():
            send(ix, answer_x[1])

        @pl.when(on_wall)
        def _():
            pltpu.make_async_copy(SD.at[pl.ds(CAP * (ix * NFY + iy), CAP)], target, drecv.at[turn]).start()

    def sent_to_faces(turn):
        @pl.when(on_wall)
        def _():
            rest = RF.at[turn, pl.ds(0, CAP * (2 * NFX - 1))]
            pltpu.make_async_copy(rest, rest, dsend.at[turn]).wait()

        @pl.when(off_wall)
        def _():
            rest = RF.at[turn, pl.ds(0, CAP * 2 * NFX)]
            pltpu.make_async_copy(rest, rest, dsend.at[turn]).wait()

    for load in loads[5:]:
        load.wait()

    @pl.when(is_solver)
    def _():
        def products(k, carry):
            block = order[0, k]
            inverse = BI[block]
            force_part = lax.dot_general(interp[...], inverse, NT, precision=HIGHEST, preferred_element_type=F32)
            chain = jnp.dot(inverse, CO[block], precision=HIGHEST, preferred_element_type=F32)
            high, low = split(jnp.concatenate([force_part, -chain.T], axis=0))
            R[k] = jnp.concatenate([high, low], axis=1)
            return carry

        lax.fori_loop(0, EBD, products, 0)

    numbers = range(NV)
    source = [source_weight[c] for c in numbers]
    once = [source[c] + sum(mix[c, d] * source[d] for d in numbers) for c in numbers]
    twice = [once[c] + sum(mix[c, d] * once[d] for d in numbers) for c in numbers]
    press_source = sum(press_weight[c] * source[c] for c in numbers)
    press_once = sum(press_weight[c] * once[c] for c in numbers)
    press_twice = sum(press_weight[c] * twice[c] for c in numbers)

    pack(S.at[0])
    pl.semaphore_wait(barrier, expected)
    start_halo(0, S.at[0])
    kappa_plane.start()
    send_rows(ITERS, SL)
    finish_halo(0, S.at[0])
    sweep(0, S.at[0], S.at[1])
    pack(S.at[1])
    start_halo(1, S.at[1])

    kappa_plane.wait()
    KX[(NZL + 1) * (1 - iz)] = KZ[...]
    KX[(NZL + 1) * iz] = jnp.zeros((CXE, CY), F32)
    tile_row = lax.broadcasted_iota(jnp.int32, (PAD, CY), 0)

    def kappa_edges(z, carry):
        KX[z + 1, 0:PAD] = jnp.where(tile_row == PAD - 1, XR[0, 0, NV, pl.ds(z, 1), :], 0.0)
        KX[z + 1, PAD + CX : CXE] = jnp.where(tile_row == 0, XR[0, 1, NV, pl.ds(z, 1), :], 0.0)
        at = NV * NZL + z
        front = pltpu.roll(YR[0, 0], CY - 1 - at, 1)
        back = pltpu.roll(YR[0, 1], (CY - at) % CY, 1)
        KE[z] = jnp.where(lane >= CY // 2, front, back)
        return carry

    lax.fori_loop(0, NZL, kappa_edges, 0)

    def wall_base():
        @pl.when(on_wall)
        def _():
            pressure = press_weight[0] * S[0, 0, 1]
            for c in range(1, NV):
                pressure += press_weight[c] * S[0, c, 1]
            PB[...] = pressure

    finish_halo(1, S.at[1])
    sweep(1, S.at[1], S.at[0])
    wall_base()
    sent_to_solvers(ITERS)

    send_pressure(0)

    @pl.when(is_solver)
    def _():
        heard_from_faces(ITERS)
        face_lanes = lax.broadcasted_iota(jnp.int32, (FACES, EB), 1) + 1
        slot_of = (RF[ITERS] == face_lanes.astype(F32)).astype(F32)
        FP[...] = lax.dot_general(placed, slot_of, NT, preferred_element_type=F32)
        FPT[...] = lax.dot_general(slot_of, placed, NT, preferred_element_type=F32)

    def solve():
        for k in range(EBD):
            force = FR[pl.ds(k, 1), :]
            previous = XV[pl.ds(k - 1, 1), :] if k else jnp.zeros((1, EB), F32)
            both = jnp.concatenate([force, previous], axis=1)
            high = both.astype(BF16).astype(F32)
            at = lax.broadcasted_iota(jnp.int32, (8, 2 * EB), 0)
            left = jnp.where(at == 0, high, jnp.where(at == 1, both - high, 0.0)).astype(BF16)
            result = jnp.dot(left, R[k], preferred_element_type=F32)
            summed = result[:, :EB] + result[:, EB:]
            XV[pl.ds(k, 1), :] = summed[0:1] + summed[1:2]

    def wall_copies(it):
        def remote(n, opposite, source_row, side, target_row, count, device):
            copy = lambda here, there: pltpu.make_async_remote_copy(
                WN.at[it, 1, pl.ds(source_row, count)], WN.at[it, side, pl.ds(target_row, count)],
                wsend.at[it, here], wrecv.at[it, there], device_id=device, device_id_type=MESH,
            )
            return copy(n, opposite), copy(n, n)

        low, high = PAD, PAD + CX - 8
        (_, left), (_, right), (_, front), (_, back) = sides
        (lf, left_front), (lb, left_back), (rf, right_front), (rb, right_back) = corners
        return (
            (has_left, remote(0, 1, low, 1, PAD + CX, 8, left)),
            (has_right, remote(1, 0, high, 1, 0, 8, right)),
            (has_front, remote(2, 3, PAD, 2, PAD, CX, front)),
            (has_back, remote(3, 2, PAD, 0, PAD, CX, back)),
            (lf, remote(4, 7, low, 2, PAD + CX, 8, left_front)),
            (lb, remote(5, 6, low, 0, PAD + CX, 8, left_back)),
            (rf, remote(6, 5, high, 2, 0, 8, right_front)),
            (rb, remote(7, 4, high, 0, 0, 8, right_back)),
        )

    lane_e = lax.broadcasted_iota(jnp.int32, (CXE, CY), 1)
    inner = slice(PAD, PAD + CX)

    def spread(it):
        centre = WN[it, 1]
        beyond = jnp.where(lane_e >= CY // 2, WN[it, 0], WN[it, 2])
        up, down = pltpu.roll(centre, 1, 1), pltpu.roll(centre, CY - 1, 1)
        out_up, out_down = pltpu.roll(beyond, 1, 1), pltpu.roll(beyond, CY - 1, 1)
        lap = pltpu.roll(centre, 1, 0) + pltpu.roll(centre, CXE - 1, 0) - 4.0 * centre
        lap += jnp.where(lane_e == 0, out_up, up) + jnp.where(lane_e == CY - 1, out_down, down)
        lap_e = pltpu.roll(beyond, 1, 0) + pltpu.roll(beyond, CXE - 1, 0) - 4.0 * beyond
        lap_e += jnp.where(lane_e >= CY // 2, out_up + down, out_down + up)
        LP[0], LP[1] = lap, centre
        LE[0], LE[1] = lap_e[inner], beyond[inner]

    def ring_sum(wide, edge_columns, below, above, coeff):
        own = wide[inner]
        total = pltpu.roll(wide, 1, 0)[inner] + pltpu.roll(wide, CXE - 1, 0)[inner] + below + above - 6.0 * own
        total += jnp.where(lane == 0, pltpu.roll(edge_columns, 1, 1), pltpu.roll(own, 1, 1))
        total += jnp.where(lane == CY - 1, pltpu.roll(edge_columns, CY - 1, 1), pltpu.roll(own, CY - 1, 1))
        return coeff * total

    first_jump = (NZ - 1.0) / NZ - 2.0

    def profile(plane):
        height = iz * NZL + plane - 1
        return 1.0 - height.astype(F32) / NZ, jnp.where(height == 0, first_jump, 0.0)

    def update():
        def first(plane, carry):
            share, jump = profile(plane)
            QB[plane] = KX[plane] * (share * LP[0] + jump * LP[1])
            return carry

        lax.fori_loop(0, NZL + 2, first, 0)

        def second(z, carry):
            share, jump = profile(z + 1)
            edges = KE[z] * (share * LE[0] + jump * LE[1])
            wide = QB[z + 1]
            bend = ring_sum(wide, edges, QB[z, inner], QB[z + 2, inner], KX[z + 1, inner])
            raised, slope = share * LP[1, inner], wide[inner]
            for c in range(NV):
                S[0, c, z + 1] += twice[c] * raised + 2.0 * once[c] * slope + source[c] * bend
            return carry

        lax.fori_loop(0, NZL, second, 0)

    def tell_faces():
        targets = (
            [pltpu.roll(WN[ITERS, 1], (CXE - d) % CXE, 0)[inner] for d in range(-2, 3)]
            + [pltpu.roll(WN[ITERS, 0], (CXE - d) % CXE, 0)[inner] for d in range(-1, 2)]
            + [pltpu.roll(WN[ITERS, 2], (CXE - d) % CXE, 0)[inner] for d in range(-1, 2)]
        )
        facts = targets + [
            jnp.broadcast_to(KE[0, :, CY - 1 : CY], (CX, CY)), jnp.broadcast_to(KE[0, :, 0:1], (CX, CY)),
        ]
        table = jnp.zeros((CX, CY), F32)
        for n, fact in enumerate(facts):
            table = jnp.where(lane == n, fact, table)
        wall_coeff = KX[1]
        selector = AM[...].astype(BF16)
        CS[0] = pick(selector, table)
        for n, d in enumerate((-1, 0, 1)):
            CS[n + 1] = pick(selector, pltpu.roll(wall_coeff, (CXE - d) % CXE, 0)[inner])
        CS[4] = pick(selector, KX[2, inner])

    def send_facts():
        send_to_solvers(lambda to: CS.at[:, pl.ds(CAP * to, CAP)], RC.at[:, own_rows], csend, crecv)

    def sent_facts():
        @pl.when(on_wall)
        def _():
            @pl.when(is_solver)
            def _():
                rest = RC.at[:, pl.ds(0, CAP * (2 * NFX - 1))]
                pltpu.make_async_copy(rest, rest, csend).wait()

            @pl.when(not_solver)
            def _():
                rest = RC.at[:, pl.ds(0, CAP * 2 * NFX)]
                pltpu.make_async_copy(rest, rest, csend).wait()

    def hear_facts():
        pltpu.make_async_copy(RC, RC, crecv).wait()
        names = lax.broadcasted_iota(jnp.int32, (FACES, NFX * EBD), 1) + 1
        names = names.astype(F32)
        for m in range(AROUND):
            G[m] = jnp.where(names == RC[0, :, m : m + 1], 1.0, 0.0).astype(BF16)

    def tell_solvers(it, facing):
        if it:
            rest = XA.at[0, pl.ds(0, (NFX - 1) * EBD)]
            pltpu.make_async_copy(rest, rest, xsend.at[it - 1]).wait()
        own = pick(placed.T[:EBD].astype(BF16), facing)
        XO[...] = own
        XA[it, pl.ds(EBD * ix, EBD)] = own

        def send(to, y):
            pltpu.make_async_remote_copy(
                XO, XA.at[it, pl.ds(EBD * ix, EBD)], xsend.at[it], xrecv.at[it],
                device_id=(to, y, iz), device_id_type=MESH,
            ).start()

        def group(step, carry):
            base = row_base(step)
            for dy in FAR_Y:
                send(base + turned_y[dy], turned_y[dy])
            return carry

        lax.fori_loop(0, RING_Z - 1, group, 0)
        for dy in FAR_Y[:3]:
            send(ring_z * RING_Y + turned_y[dy], turned_y[dy])

    def respond(it):
        rest = XA.at[it, pl.ds(0, (NFX - 1) * EBD)]
        pltpu.make_async_copy(rest, rest, xrecv.at[it]).wait()
        high, low = split(XA[it])
        both = jnp.concatenate([high, low], axis=1)
        for m in range(AROUND):
            found = jnp.dot(G[m], both, preferred_element_type=F32)
            GW[m] = found[:, :CY] + found[:, CY:]

        def chunk(n, carry):
            at = pl.ds(pl.multiple_of(n * CX, CX), CX)
            centre = {d: GW[d + 2, at] for d in range(-2, 3)}
            beyond = {d: jnp.where(lane >= CY // 2, GW[d + 6, at], GW[d + 9, at]) for d in range(-1, 2)}
            coeff = {d: RC[d + 2, at] for d in range(-1, 2)}

            def wide_sum(d):
                total = centre[d - 1] + centre[d + 1] - 4.0 * centre[d]
                total += jnp.where(lane == 0, pltpu.roll(beyond[d], 1, 1), pltpu.roll(centre[d], 1, 1))
                return total + jnp.where(
                    lane == CY - 1, pltpu.roll(beyond[d], CY - 1, 1), pltpu.roll(centre[d], CY - 1, 1)
                )

            sums = {d: wide_sum(d) for d in range(-1, 2)}
            slopes = {d: coeff[d] * (sums[d] + first_jump * centre[d]) for d in range(-1, 2)}
            above = RC[4, at] * ((NZ - 1.0) / NZ * sums[0])
            facts = RC[0, at]
            edge_coeff = jnp.where(lane >= CY // 2, facts[:, AROUND : AROUND + 1], facts[:, AROUND + 1 : AROUND + 2])
            edge_sum = beyond[-1] + beyond[1] - 4.0 * beyond[0]
            edge_sum += jnp.where(
                lane >= CY // 2,
                pltpu.roll(beyond[0], 1, 1) + pltpu.roll(centre[0], CY - 1, 1),
                pltpu.roll(beyond[0], CY - 1, 1) + pltpu.roll(centre[0], 1, 1),
            )
            edges = edge_coeff * (edge_sum + first_jump * beyond[0])
            bend = slopes[-1] + slopes[1] + above - 6.0 * slopes[0]
            bend += jnp.where(lane == 0, pltpu.roll(edges, 1, 1), pltpu.roll(slopes[0], 1, 1))
            bend += jnp.where(lane == CY - 1, pltpu.roll(edges, CY - 1, 1), pltpu.roll(slopes[0], CY - 1, 1))
            IN[at] = press_twice * centre[0] + 2.0 * press_once * slopes[0] + press_source * coeff[0] * bend
            return carry

        lax.fori_loop(0, FACES // CX, chunk, 0)

    def answer(it):
        heard_from_faces(it)
        if it:
            sent_to_faces(it - 1)
        rows_in = RF[it] + IN[...] if it else RF[it]
        FR[...] = pick(FP[...].astype(BF16), rows_in)
        solve()
        facing = lax.dot_general(XV[...], interp[...], NT, precision=HIGHEST, preferred_element_type=F32)
        if it < ITERS - 1:
            tell_solvers(it, facing)
        SD[...] = pick(FPT[...].astype(BF16), facing)
        send_to_faces(it)

    def hear_wall(it):
        whole = RD.at[it]
        pltpu.make_async_copy(whole, whole, drecv.at[it]).wait()
        WN[it, 1, inner] = pick(AT[...].astype(BF16), RD[it])

    def relay(it, part):
        return pltpu.make_async_remote_copy(
            part, part, rsend.at[it], rrecv.at[it], device_id=other_core, device_id_type=MESH
        )

    around_wall = wall_copies(ITERS)

    @pl.when(on_wall)
    def _():
        each(around_wall, lambda pair: pair[0].start())

    for it in range(ITERS - 1):
        n = 2 * it + 2
        pack(S.at[0])
        start_halo(n, S.at[0])
        if it == 0:

            @pl.when(on_wall)
            def _():
                each(around_wall, lambda pair: pair[1].wait_recv())
                tell_faces()
                each(around_wall, lambda pair: pair[0].wait_send())

            send_facts()
        else:

            @pl.when(is_solver)
            def _():
                answer(it)

        finish_halo(n, S.at[0])
        sweep(n, S.at[0], S.at[1])
        pack(S.at[1])
        start_halo(n + 1, S.at[1])
        if it == 0:

            @pl.when(is_solver)
            def _():
                answer(it)

        finish_halo(n + 1, S.at[1])
        sweep(n + 1, S.at[1], S.at[0])
        wall_base()
        sent_to_solvers(it)
        send_pressure(it + 1)
        if it == 0:

            @pl.when(is_solver)
            def _():
                hear_facts()

        copies = wall_copies(it)

        @pl.when(on_wall)
        def _():
            hear_wall(it)
            each(copies, lambda pair: pair[0].start())

        @pl.when(is_solver)
        def _():
            respond(it)

        beside_wall = relay(it, WN.at[it])

        @pl.when(on_wall)
        def _():
            each(copies, lambda pair: pair[1].wait_recv())
            beside_wall.start()

        @pl.when(off_wall)
        def _():
            beside_wall.wait_recv()

        spread(it)
        update()

        @pl.when(on_wall)
        def _():
            each(copies, lambda pair: pair[0].wait_send())
            beside_wall.wait_send()

    sent_facts()

    last = ITERS - 1
    out = pltpu.make_async_copy(S.at[0, :, pl.ds(1, NZL)], state_out, load_sem.at[0])
    out.start()

    def disp_copy(t):
        return pltpu.make_async_remote_copy(
            DV, DR, osend.at[t], orecv.at[1], device_id=(ix, (iy + t) % NFY, iz), device_id_type=MESH
        )

    @pl.when(is_solver)
    def _():
        answer(last)
        back = lax.dot_general(placed, XV[...], (((0,), (0,)), ((), ())), precision=HIGHEST, preferred_element_type=F32)
        DV[...] = back[:EBD]
        for t in range(1, NFY):
            disp_copy(t).start()
        disp_out[...] = back[:EBD]

    beside_wall = relay(last, WN.at[last, 1, pl.ds(PAD, CX)])

    @pl.when(on_wall)
    def _():
        sent_to_solvers(last)
        hear_wall(last)
        beside_wall.start()

    @pl.when(off_wall)
    def _():
        beside_wall.wait_recv()

    for z in range(NZL):
        share, _ = profile(z + 1)
        raised_out[z] = share * WN[last, 1, inner]

    @pl.when(on_wall)
    def _():
        beside_wall.wait_send()

    @pl.when(is_solver)
    def _():
        sent_to_faces(last)
        rest = XA.at[0, pl.ds(0, (NFX - 1) * EBD)]
        pltpu.make_async_copy(rest, rest, xsend.at[last - 1]).wait()
        for t in range(1, NFY):
            disp_copy(t).wait_send()

    @pl.when(not_solver)
    def _():
        disp_copy(1).wait_recv()
        disp_out[...] = DR[...]

    out.wait()


def on_device(
    state, kappa, mix, press_weight, source_weight, interp, block_inverse, coupling, front_order, face_owner, face_slot
):
    hbm = pl.BlockSpec(memory_space=pltpu.HBM)
    vmem = pl.BlockSpec(memory_space=pltpu.VMEM)
    dma = pltpu.SemaphoreType.DMA
    sweeps = 2 * ITERS
    before, raised, displacement = pl.pallas_call(
        kernel,
        out_shape=(
            jax.ShapeDtypeStruct(state.shape, F32),
            jax.ShapeDtypeStruct(kappa.shape, F32),
            jax.ShapeDtypeStruct((EBD, EB), F32),
        ),
        in_specs=[hbm] * 11,
        out_specs=(hbm, vmem, vmem),
        scratch_shapes=[
            pltpu.SMEM((NV, NV), F32),
            pltpu.SMEM((NV,), F32),
            pltpu.SMEM((NV,), F32),
            pltpu.VMEM((CY, EB), F32),
            pltpu.SMEM((1, EBD), jnp.int32),
            pltpu.VMEM((1, CX), jnp.int32),
            pltpu.VMEM((1, CX), jnp.int32),
            pltpu.VMEM((2, NV, NZL + 2, CX, CY), F32),
            pltpu.VMEM((NZL, CX, CY), F32),
            pltpu.VMEM((NZL + 2, CXE, CY), F32),
            pltpu.VMEM((NZL, CX, CY), F32),
            pltpu.VMEM((EBD, EB, EB), F32),
            pltpu.VMEM((EBD, EB, EB), F32),
            pltpu.VMEM((EBD, 2 * EB, 2 * EB), BF16),
            pltpu.VMEM((2, NV + 1, NZL, CY), F32),
            pltpu.VMEM((sweeps, 2, NV + 1, NZL, CY), F32),
            pltpu.VMEM((2, CX, CY), F32),
            pltpu.VMEM((sweeps, 2, CX, CY), F32),
            pltpu.VMEM((2, CX, CY), F32),
            pltpu.VMEM((sweeps, NV, CX, CY), F32),
            pltpu.VMEM((CXE, CY), F32),
            pltpu.VMEM((CAP * NFX, CY), F32),
            pltpu.VMEM((CAP * NFX, CY), F32),
            pltpu.VMEM((5, CAP * NFX, CY), F32),
            pltpu.VMEM((ITERS + 1, FACES, CY), F32),
            pltpu.VMEM((5, FACES, CY), F32),
            pltpu.VMEM((FACES, CY), F32),
            pltpu.VMEM((ITERS, CAP * NFX, CY), F32),
            pltpu.VMEM((EBD, FACES), F32),
            pltpu.VMEM((FACES, EBD), F32),
            pltpu.VMEM((CAP * NFX, CX), F32),
            pltpu.VMEM((CX, CAP * NFX), F32),
            pltpu.VMEM((EBD, EB), F32),
            pltpu.VMEM((EBD, EB), F32),
            pltpu.VMEM((EBD, EB), F32),
            pltpu.VMEM((EBD, EB), F32),
            pltpu.VMEM((ITERS + 1, 3, CXE, CY), F32),
            pltpu.VMEM((2, CXE, CY), F32),
            pltpu.VMEM((2, CX, CY), F32),
            pltpu.VMEM((NZL + 2, CXE, CY), F32),
            pltpu.VMEM((CX, CY), F32),
            pltpu.VMEM((AROUND, FACES, NFX * EBD), BF16),
            pltpu.VMEM((AROUND, FACES, CY), F32),
            pltpu.VMEM((FACES, CY), F32),
            pltpu.VMEM((EBD, EB), F32),
            pltpu.VMEM((ITERS - 1, NFX * EBD, EB), F32),
            dma((11,)),
            dma((sweeps, 5)),
            dma((sweeps, 5)),
            dma((ITERS + 1,)),
            dma((ITERS + 1,)),
            dma((ITERS,)),
            dma((ITERS,)),
            dma((NFY,)),
            dma((2,)),
            dma((ITERS + 1, 8)),
            dma((ITERS + 1, 8)),
            dma((ITERS,)),
            dma((ITERS,)),
            dma,
            dma,
            dma((ITERS - 1,)),
            dma((ITERS - 1,)),
        ],
        compiler_params=pltpu.CompilerParams(
            collective_id=0, has_side_effects=True, vmem_limit_bytes=60 * 1024 * 1024
        ),
    )(
        state, kappa, mix, press_weight, source_weight, interp, block_inverse, coupling, front_order,
        face_owner.reshape(1, -1), face_slot.reshape(1, -1),
    )
    return before + source_weight[:, None, None, None] * raised[None], displacement


def solution(mesh):
    return jax.shard_map(
        on_device,
        mesh=mesh,
        in_specs=(
            P(None, "fz", "fx", "fy"),
            P("fz", "fx", "fy"),
            P(),
            P(),
            P(),
            P(),
            P("fx", None, None),
            P("fx", None, None),
            P("fx", None),
            P(("fx", "fy"), None),
            P(("fx", "fy")),
        ),
        out_specs=(P(None, "fz", "fx", "fy"), P("fx", None)),
        check_vma=False,
    )
```

```python
import jax
import jax.numpy as jnp
from jax import lax
from jax.experimental import pallas as pl
from jax.experimental.pallas import tpu as pltpu
from jax.sharding import PartitionSpec as P

ITERS = 3
DIFFUSION = 0.16
HIGHEST = lax.Precision.HIGHEST
MESH = pl.DeviceIdType.MESH
F32 = jnp.float32
BF16 = jnp.bfloat16

NV, NZL, CX, CY = 5, 8, 32, 128
NZ = 16
NFX, NFY = 32, 4
RING_Z, RING_Y = 8, 4
EB, EBD, CAP = 128, 16, 2
FACES = NFX * NFY * CAP
PAD = 8
CXE = CX + 2 * PAD
NT = (((1,), (1,)), ((), ()))
FAR_Y = (2, 1, 3, 0)
AROUND = 11


def far_first(step, ring):
    return ring // 2 + (1 - 2 * (step % 2)) * ((step + 1) // 2)


def split(values):
    high = values.astype(BF16)
    return high, (values - high.astype(F32)).astype(BF16)


def pick(selector, values):
    high, low = split(values)
    return jnp.dot(selector, high, preferred_element_type=F32) + jnp.dot(selector, low, preferred_element_type=F32)


def kernel(
    state_in, kappa_in, mix_in, press_in, source_in, interp_in, inverse_in, coupling_in, order_in, owner_in, slot_in,
    state_out, raised_out, disp_out,
    mix, press_weight, source_weight, interp, order, owner, slot,
    S, K, KX, KE, BI, CO, R, XS, XR, YS, YR, YK, ZR, KZ, SL, SF, CS, RF, RC, SD, RD, FP, FPT, AM, AT, FR, XV, DV, DR,
    WN, LP, LE, QB, PB, G, GW, IN, XO, XA,
    load_sem, hsend, hrecv, fsend, frecv, dsend, drecv, osend, orecv, wsend, wrecv, rsend, rrecv, csend, crecv, xsend, xrecv,
):
    ix, iy, iz = lax.axis_index("fx"), lax.axis_index("fy"), lax.axis_index("fz")
    ring_z, ring_y = ix // RING_Y, ix % RING_Y
    on_wall = iz == 0
    off_wall = iz == 1
    home = (ring_y + ring_z) % NFY
    is_solver = iy == home
    not_solver = jnp.logical_not(is_solver)
    turned_y = {d: (ring_y + d) % RING_Y for d in FAR_Y}
    turned_x = {d: (iy + d) % NFY for d in FAR_Y}
    answer_x = ((iy + 2 - iz) % NFY, (iy + 3 * iz) % NFY)

    def row_base(step):
        return ((ring_z + far_first(step, RING_Z)) % RING_Z) * RING_Y

    def homes(z):
        return {d: (turned_y[d] + z) % NFY for d in FAR_Y}

    def owners_at(step):
        z = (ring_z + far_first(step, RING_Z)) % RING_Z
        return [(z * RING_Y + turned_y[d], home_y) for d, home_y in homes(z).items()]

    near_owners = [(ring_z * RING_Y + turned_y[d], home_y) for d, home_y in homes(ring_z).items()][:3]

    def signal(barrier, device):
        pl.semaphore_signal(barrier, inc=1, device_id=device, device_id_type=MESH)

    loads = [
        pltpu.make_async_copy(source, target, load_sem.at[n])
        for n, (source, target) in enumerate(
            (
                (owner_in, owner),
                (slot_in, slot),
                (order_in, order),
                (kappa_in, K),
                (state_in, S.at[0, :, pl.ds(1, NZL)]),
                (inverse_in, BI),
                (coupling_in, CO),
                (interp_in, interp),
                (mix_in, mix),
                (press_in, press_weight),
                (source_in, source_weight),
            )
        )
    ]
    for load in loads:
        load.start()

    barrier = pltpu.get_barrier_semaphore()
    has_left, has_right, has_front, has_back = ix > 0, ix < NFX - 1, iy > 0, iy < NFY - 1
    sides = (
        (has_left, (ix - 1, iy, iz)),
        (has_right, (ix + 1, iy, iz)),
        (has_front, (ix, iy - 1, iz)),
        (has_back, (ix, iy + 1, iz)),
    )
    corners = (
        (jnp.logical_and(has_left, has_front), (ix - 1, iy - 1, iz)),
        (jnp.logical_and(has_left, has_back), (ix - 1, iy + 1, iz)),
        (jnp.logical_and(has_right, has_front), (ix + 1, iy - 1, iz)),
        (jnp.logical_and(has_right, has_back), (ix + 1, iy + 1, iz)),
    )
    other_core = (ix, iy, 1 - iz)

    @pl.when(is_solver)
    def _():
        def greet(step, carry):
            base = row_base(step)
            for dy in FAR_Y:
                for dx in FAR_Y:
                    signal(barrier, (base + turned_y[dy], turned_x[dx], 0))
            return carry

        lax.fori_loop(0, RING_Z - 1, greet, 0)
        for dy in FAR_Y:
            for dx in FAR_Y:
                if dy or dx:
                    signal(barrier, (ring_z * RING_Y + turned_y[dy], turned_x[dx], 0))

        @pl.when(off_wall)
        def _():
            signal(barrier, (ix, iy, 0))

        def greet_solvers(step, carry):
            for to, home_y in owners_at(step):
                signal(barrier, (to, home_y, iz))
            return carry

        lax.fori_loop(0, RING_Z - 1, greet_solvers, 0)
        for to, home_y in near_owners:
            signal(barrier, (to, home_y, iz))

    @pl.when(on_wall)
    def _():
        def greet(step, carry):
            for to, home_y in owners_at(step):
                signal(barrier, (to, home_y, (iy + home_y) % 2))
            return carry

        lax.fori_loop(0, RING_Z - 1, greet, 0)
        for to, home_y in near_owners:
            signal(barrier, (to, home_y, (iy + home_y) % 2))

        @pl.when(not_solver)
        def _():
            signal(barrier, (ix, home, (iy + home) % 2))

    @pl.when(not_solver)
    def _():
        signal(barrier, (ix, home, iz))

    for ref in (XR, YR, WN):
        ref[...] = jnp.zeros_like(ref)

    signal(barrier, other_core)
    solver_count = is_solver.astype(jnp.int32)
    wall_count = on_wall.astype(jnp.int32)
    expected = 1 + wall_count * (2 * NFX - solver_count) + solver_count * (2 * NFX - wall_count + NFY - 1 + NFX - 1)
    for present, device in sides + corners:
        expected = expected + present.astype(jnp.int32)

        @pl.when(present)
        def _():
            signal(barrier, device)

    zero_plane = jnp.zeros((NV, CX, CY), F32)
    for buffer in range(2):
        S[buffer, :, 0] = zero_plane
        S[buffer, :, NZL + 1] = zero_plane

    for load in loads[:3]:
        load.wait()
    rows = lax.broadcasted_iota(jnp.int32, (CAP * NFX, CX), 0)
    named = (owner[...] == rows // CAP).astype(F32)
    earlier = (
        lax.broadcasted_iota(jnp.int32, (CX, CX), 0) < lax.broadcasted_iota(jnp.int32, (CX, CX), 1)
    ).astype(BF16)
    rank = jnp.dot(named.astype(BF16), earlier, preferred_element_type=F32)
    chosen = jnp.where(rank == (rows % CAP).astype(F32), named, 0.0)
    AM[...] = chosen
    unit = (lax.broadcasted_iota(jnp.int32, (CX, CX), 0) == lax.broadcasted_iota(jnp.int32, (CX, CX), 1)).astype(F32)
    AT[...] = lax.dot_general(unit, chosen, NT, preferred_element_type=F32)
    slot_rows = jnp.sum(chosen * (slot[...] + 1).astype(F32), axis=1, keepdims=True)
    SL[...] = jnp.broadcast_to(slot_rows, (CAP * NFX, CY))
    target_of = jnp.sum(unit * (EBD * owner[...] + slot[...] + 1).astype(F32), axis=1, keepdims=True)
    WN[ITERS, 1, PAD : PAD + CX] = jnp.broadcast_to(target_of, (CX, CY))
    block_rows = lax.broadcasted_iota(jnp.int32, (EBD, EB), 0)
    block_lanes = lax.broadcasted_iota(jnp.int32, (EBD, EB), 1)
    placed = jnp.zeros((EBD, EB), F32)
    for k in range(EBD):
        placed = jnp.where(jnp.logical_and(block_rows == k, block_lanes == order[0, k]), 1.0, placed)

    lane = lax.broadcasted_iota(jnp.int32, (CX, CY), 1)
    row = lax.broadcasted_iota(jnp.int32, (CX, CY), 0)
    for load in loads[3:5]:
        load.wait()

    def kappa_faces(z, carry):
        low, high = carry
        coeff = DIFFUSION * K[z]
        KX[z + 1, PAD : PAD + CX] = coeff
        XS[0, NV, pl.ds(z, 1), :] = coeff[0:1]
        XS[1, NV, pl.ds(z, 1), :] = coeff[CX - 1 : CX]
        here = lane == NV * NZL + z
        return jnp.where(here, coeff[:, 0:1], low), jnp.where(here, coeff[:, CY - 1 : CY], high)

    nothing = jnp.zeros((CX, CY), F32)
    YK[0], YK[1] = lax.fori_loop(0, NZL, kappa_faces, (nothing, nothing))

    def pack(src):
        def plane(z, carry):
            low, high = carry
            for c in range(NV):
                centre = src[c, z + 1]
                XS[0, c, pl.ds(z, 1), :] = centre[0:1]
                XS[1, c, pl.ds(z, 1), :] = centre[CX - 1 : CX]
                here = lane == c * NZL + z
                low = jnp.where(here, centre[:, 0:1], low)
                high = jnp.where(here, centre[:, CY - 1 : CY], high)
            return low, high

        YS[0], YS[1] = lax.fori_loop(0, NZL, plane, (YK[0], YK[1]))

    edge = NZL - (NZL - 1) * iz

    def halo_copies(n, src):
        def remote(source, target, at, there, device):
            return pltpu.make_async_remote_copy(
                source, target, hsend.at[n, at], hrecv.at[n, there], device_id=device, device_id_type=MESH
            )

        (_, left), (_, right), (_, front), (_, back) = sides
        always = iz >= 0
        plane = src.at[:, edge]
        sends = (
            (has_left, remote(XS.at[0], XR.at[n, 1], 0, 1, left)),
            (has_right, remote(XS.at[1], XR.at[n, 0], 1, 0, right)),
            (has_front, remote(YS.at[0], YR.at[n, 1], 2, 3, front)),
            (has_back, remote(YS.at[1], YR.at[n, 0], 3, 2, back)),
            (always, remote(plane, ZR.at[n], 4, 4, other_core)),
        )
        waits = (
            (has_left, remote(XS.at[0], XR.at[n, 0], 0, 0, left)),
            (has_right, remote(XS.at[1], XR.at[n, 1], 1, 1, right)),
            (has_front, remote(YS.at[0], YR.at[n, 0], 2, 2, front)),
            (has_back, remote(YS.at[1], YR.at[n, 1], 3, 3, back)),
            (always, remote(plane, ZR.at[n], 4, 4, other_core)),
        )
        return sends, waits

    def each(copies, action):
        for present, copy in copies:

            @pl.when(present)
            def _():
                action(copy)

    def start_halo(n, src):
        each(halo_copies(n, src)[0], lambda copy: copy.start())

    def finish_halo(n, src):
        sends, waits = halo_copies(n, src)
        each(waits, lambda copy: copy.wait_recv())
        each(sends, lambda copy: copy.wait_send())
        src[:, (NZL + 1) * (1 - iz)] = ZR[n]

    def sweep(n, src, dst):
        def plane(z, carry):
            coeff = KX[z + 1, PAD : PAD + CX]
            centres = [src[c, z + 1] for c in range(NV)]
            for c in range(NV):
                centre = centres[c]
                at = c * NZL + z
                beside = src[c, z] + src[c, z + 2]
                beside += jnp.where(row == 0, XR[n, 0, c, pl.ds(z, 1), :], pltpu.roll(centre, 1, 0))
                beside += jnp.where(row == CX - 1, XR[n, 1, c, pl.ds(z, 1), :], pltpu.roll(centre, CX - 1, 0))
                front = pltpu.roll(YR[n, 0], (CY - at) % CY, 1)
                back = pltpu.roll(YR[n, 1], CY - 1 - at, 1)
                beside += jnp.where(lane == 0, front, pltpu.roll(centre, 1, 1))
                beside += jnp.where(lane == CY - 1, back, pltpu.roll(centre, CY - 1, 1))
                total = centre + coeff * (beside - 6.0 * centre)
                for d in range(NV):
                    total += mix[c, d] * centres[d]
                dst[c, z + 1] = total
            return carry

        lax.fori_loop(0, NZL, plane, 0)

    kappa_plane = pltpu.make_async_remote_copy(
        KX.at[edge], KZ, osend.at[0], orecv.at[0], device_id=other_core, device_id_type=MESH
    )

    def send_to_solvers(rows_of, target, sent, heard):
        def send(to, y, core):
            pltpu.make_async_remote_copy(
                rows_of(to), target, sent, heard, device_id=(to, y, core), device_id_type=MESH
            ).start()

        def group(step, carry):
            for to, home_y in owners_at(step):
                for core in range(2):
                    send(to, home_y, core)
            return carry

        @pl.when(on_wall)
        def _():
            lax.fori_loop(0, RING_Z - 1, group, 0)
            for to, home_y in near_owners:
                for core in range(2):
                    send(to, home_y, core)
            send(ix, home, 1)

            @pl.when(not_solver)
            def _():
                send(ix, home, 0)

            @pl.when(is_solver)
            def _():
                pltpu.make_async_copy(rows_of(ix), target, heard).start()

    own_rows = pl.ds(CAP * (ix * NFY + iy), CAP)

    def send_rows(turn, rows_out):
        send_to_solvers(
            lambda to: rows_out.at[pl.ds(CAP * to, CAP)], RF.at[turn, own_rows], fsend.at[turn], frecv.at[turn]
        )

    def send_pressure(turn):
        @pl.when(on_wall)
        def _():
            SF[...] = pick(AM[...].astype(BF16), PB[...])

        send_rows(turn, SF)

    def sent_to_solvers(turn):
        @pl.when(on_wall)
        def _():
            @pl.when(is_solver)
            def _():
                rest = RF.at[turn, pl.ds(0, CAP * (2 * NFX - 1))]
                pltpu.make_async_copy(rest, rest, fsend.at[turn]).wait()

            @pl.when(not_solver)
            def _():
                rest = RF.at[turn, pl.ds(0, CAP * 2 * NFX)]
                pltpu.make_async_copy(rest, rest, fsend.at[turn]).wait()

    def heard_from_faces(turn):
        whole = RF.at[turn]
        pltpu.make_async_copy(whole, whole, frecv.at[turn]).wait()

    def send_to_faces(turn):
        target = RD.at[turn, pl.ds(CAP * ix, CAP)]

        def send(to_x, to_y):
            pltpu.make_async_remote_copy(
                SD.at[pl.ds(CAP * (to_x * NFY + to_y), CAP)], target, dsend.at[turn], drecv.at[turn],
                device_id=(to_x, to_y, 0), device_id_type=MESH,
            ).start()

        def group(step, carry):
            base = row_base(step)
            for dy in FAR_Y:
                for x in answer_x:
                    send(base + turned_y[dy], x)
            return carry

        lax.fori_loop(0, RING_Z - 1, group, 0)
        for dy in FAR_Y[:3]:
            for x in answer_x:
                send(ring_z * RING_Y + turned_y[dy], x)
        send(ix, answer_x[0])

        @pl.when(off_wall)
        def _():
            send(ix, answer_x[1])

        @pl.when(on_wall)
        def _():
            pltpu.make_async_copy(SD.at[pl.ds(CAP * (ix * NFY + iy), CAP)], target, drecv.at[turn]).start()

    def sent_to_faces(turn):
        @pl.when(on_wall)
        def _():
            rest = RF.at[turn, pl.ds(0, CAP * (2 * NFX - 1))]
            pltpu.make_async_copy(rest, rest, dsend.at[turn]).wait()

        @pl.when(off_wall)
        def _():
            rest = RF.at[turn, pl.ds(0, CAP * 2 * NFX)]
            pltpu.make_async_copy(rest, rest, dsend.at[turn]).wait()

    for load in loads[5:]:
        load.wait()

    @pl.when(is_solver)
    def _():
        def products(k, carry):
            block = order[0, k]
            inverse = BI[block]
            force_part = lax.dot_general(interp[...], inverse, NT, precision=HIGHEST, preferred_element_type=F32)
            chain = jnp.dot(inverse, CO[block], precision=HIGHEST, preferred_element_type=F32)
            high, low = split(jnp.concatenate([force_part, -chain.T], axis=0))
            R[k] = jnp.concatenate([high, low], axis=1)
            return carry

        lax.fori_loop(0, EBD, products, 0)

    numbers = range(NV)
    source = [source_weight[c] for c in numbers]
    once = [source[c] + sum(mix[c, d] * source[d] for d in numbers) for c in numbers]
    twice = [once[c] + sum(mix[c, d] * once[d] for d in numbers) for c in numbers]
    press_source = sum(press_weight[c] * source[c] for c in numbers)
    press_once = sum(press_weight[c] * once[c] for c in numbers)
    press_twice = sum(press_weight[c] * twice[c] for c in numbers)

    pack(S.at[0])
    pl.semaphore_wait(barrier, expected)
    start_halo(0, S.at[0])
    kappa_plane.start()
    send_rows(ITERS, SL)
    finish_halo(0, S.at[0])
    sweep(0, S.at[0], S.at[1])
    pack(S.at[1])
    start_halo(1, S.at[1])

    kappa_plane.wait()
    KX[(NZL + 1) * (1 - iz)] = KZ[...]
    KX[(NZL + 1) * iz] = jnp.zeros((CXE, CY), F32)
    tile_row = lax.broadcasted_iota(jnp.int32, (PAD, CY), 0)

    def kappa_edges(z, carry):
        KX[z + 1, 0:PAD] = jnp.where(tile_row == PAD - 1, XR[0, 0, NV, pl.ds(z, 1), :], 0.0)
        KX[z + 1, PAD + CX : CXE] = jnp.where(tile_row == 0, XR[0, 1, NV, pl.ds(z, 1), :], 0.0)
        at = NV * NZL + z
        front = pltpu.roll(YR[0, 0], CY - 1 - at, 1)
        back = pltpu.roll(YR[0, 1], (CY - at) % CY, 1)
        KE[z] = jnp.where(lane >= CY // 2, front, back)
        return carry

    lax.fori_loop(0, NZL, kappa_edges, 0)

    def wall_base():
        @pl.when(on_wall)
        def _():
            pressure = press_weight[0] * S[0, 0, 1]
            for c in range(1, NV):
                pressure += press_weight[c] * S[0, c, 1]
            PB[...] = pressure

    finish_halo(1, S.at[1])
    sweep(1, S.at[1], S.at[0])
    wall_base()
    sent_to_solvers(ITERS)

    send_pressure(0)

    @pl.when(is_solver)
    def _():
        heard_from_faces(ITERS)
        face_lanes = lax.broadcasted_iota(jnp.int32, (FACES, EB), 1) + 1
        slot_of = (RF[ITERS] == face_lanes.astype(F32)).astype(F32)
        FP[...] = lax.dot_general(placed, slot_of, NT, preferred_element_type=F32)
        FPT[...] = lax.dot_general(slot_of, placed, NT, preferred_element_type=F32)

    def solve():
        for k in range(EBD):
            force = FR[pl.ds(k, 1), :]
            previous = XV[pl.ds(k - 1, 1), :] if k else jnp.zeros((1, EB), F32)
            both = jnp.concatenate([force, previous], axis=1)
            high = both.astype(BF16).astype(F32)
            at = lax.broadcasted_iota(jnp.int32, (8, 2 * EB), 0)
            left = jnp.where(at == 0, high, jnp.where(at == 1, both - high, 0.0)).astype(BF16)
            result = jnp.dot(left, R[k], preferred_element_type=F32)
            summed = result[:, :EB] + result[:, EB:]
            XV[pl.ds(k, 1), :] = summed[0:1] + summed[1:2]

    def wall_copies(it):
        def remote(n, opposite, source_row, side, target_row, count, device):
            copy = lambda here, there: pltpu.make_async_remote_copy(
                WN.at[it, 1, pl.ds(source_row, count)], WN.at[it, side, pl.ds(target_row, count)],
                wsend.at[it, here], wrecv.at[it, there], device_id=device, device_id_type=MESH,
            )
            return copy(n, opposite), copy(n, n)

        low, high = PAD, PAD + CX - 8
        (_, left), (_, right), (_, front), (_, back) = sides
        (lf, left_front), (lb, left_back), (rf, right_front), (rb, right_back) = corners
        return (
            (has_left, remote(0, 1, low, 1, PAD + CX, 8, left)),
            (has_right, remote(1, 0, high, 1, 0, 8, right)),
            (has_front, remote(2, 3, PAD, 2, PAD, CX, front)),
            (has_back, remote(3, 2, PAD, 0, PAD, CX, back)),
            (lf, remote(4, 7, low, 2, PAD + CX, 8, left_front)),
            (lb, remote(5, 6, low, 0, PAD + CX, 8, left_back)),
            (rf, remote(6, 5, high, 2, 0, 8, right_front)),
            (rb, remote(7, 4, high, 0, 0, 8, right_back)),
        )

    lane_e = lax.broadcasted_iota(jnp.int32, (CXE, CY), 1)
    inner = slice(PAD, PAD + CX)

    def spread(it):
        centre = WN[it, 1]
        beyond = jnp.where(lane_e >= CY // 2, WN[it, 0], WN[it, 2])
        up, down = pltpu.roll(centre, 1, 1), pltpu.roll(centre, CY - 1, 1)
        out_up, out_down = pltpu.roll(beyond, 1, 1), pltpu.roll(beyond, CY - 1, 1)
        lap = pltpu.roll(centre, 1, 0) + pltpu.roll(centre, CXE - 1, 0) - 4.0 * centre
        lap += jnp.where(lane_e == 0, out_up, up) + jnp.where(lane_e == CY - 1, out_down, down)
        lap_e = pltpu.roll(beyond, 1, 0) + pltpu.roll(beyond, CXE - 1, 0) - 4.0 * beyond
        lap_e += jnp.where(lane_e >= CY // 2, out_up + down, out_down + up)
        LP[0], LP[1] = lap, centre
        LE[0], LE[1] = lap_e[inner], beyond[inner]

    def ring_sum(wide, edge_columns, below, above, coeff):
        own = wide[inner]
        total = pltpu.roll(wide, 1, 0)[inner] + pltpu.roll(wide, CXE - 1, 0)[inner] + below + above - 6.0 * own
        total += jnp.where(lane == 0, pltpu.roll(edge_columns, 1, 1), pltpu.roll(own, 1, 1))
        total += jnp.where(lane == CY - 1, pltpu.roll(edge_columns, CY - 1, 1), pltpu.roll(own, CY - 1, 1))
        return coeff * total

    first_jump = (NZ - 1.0) / NZ - 2.0

    def profile(plane):
        height = iz * NZL + plane - 1
        return 1.0 - height.astype(F32) / NZ, jnp.where(height == 0, first_jump, 0.0)

    def update():
        def first(plane, carry):
            share, jump = profile(plane)
            QB[plane] = KX[plane] * (share * LP[0] + jump * LP[1])
            return carry

        lax.fori_loop(0, NZL + 2, first, 0)

        def second(z, carry):
            share, jump = profile(z + 1)
            edges = KE[z] * (share * LE[0] + jump * LE[1])
            wide = QB[z + 1]
            bend = ring_sum(wide, edges, QB[z, inner], QB[z + 2, inner], KX[z + 1, inner])
            raised, slope = share * LP[1, inner], wide[inner]
            for c in range(NV):
                S[0, c, z + 1] += twice[c] * raised + 2.0 * once[c] * slope + source[c] * bend
            return carry

        lax.fori_loop(0, NZL, second, 0)

    def tell_faces():
        targets = (
            [pltpu.roll(WN[ITERS, 1], (CXE - d) % CXE, 0)[inner] for d in range(-2, 3)]
            + [pltpu.roll(WN[ITERS, 0], (CXE - d) % CXE, 0)[inner] for d in range(-1, 2)]
            + [pltpu.roll(WN[ITERS, 2], (CXE - d) % CXE, 0)[inner] for d in range(-1, 2)]
        )
        facts = targets + [
            jnp.broadcast_to(KE[0, :, CY - 1 : CY], (CX, CY)), jnp.broadcast_to(KE[0, :, 0:1], (CX, CY)),
        ]
        table = jnp.zeros((CX, CY), F32)
        for n, fact in enumerate(facts):
            table = jnp.where(lane == n, fact, table)
        wall_coeff = KX[1]
        selector = AM[...].astype(BF16)
        CS[0] = pick(selector, table)
        for n, d in enumerate((-1, 0, 1)):
            CS[n + 1] = pick(selector, pltpu.roll(wall_coeff, (CXE - d) % CXE, 0)[inner])
        CS[4] = pick(selector, KX[2, inner])

    def send_facts():
        send_to_solvers(lambda to: CS.at[:, pl.ds(CAP * to, CAP)], RC.at[:, own_rows], csend, crecv)

    def sent_facts():
        @pl.when(on_wall)
        def _():
            @pl.when(is_solver)
            def _():
                rest = RC.at[:, pl.ds(0, CAP * (2 * NFX - 1))]
                pltpu.make_async_copy(rest, rest, csend).wait()

            @pl.when(not_solver)
            def _():
                rest = RC.at[:, pl.ds(0, CAP * 2 * NFX)]
                pltpu.make_async_copy(rest, rest, csend).wait()

    def hear_facts():
        pltpu.make_async_copy(RC, RC, crecv).wait()
        names = lax.broadcasted_iota(jnp.int32, (FACES, NFX * EBD), 1) + 1
        names = names.astype(F32)
        for m in range(AROUND):
            G[m] = jnp.where(names == RC[0, :, m : m + 1], 1.0, 0.0).astype(BF16)

    def tell_solvers(it, facing):
        if it:
            rest = XA.at[0, pl.ds(0, (NFX - 1) * EBD)]
            pltpu.make_async_copy(rest, rest, xsend.at[it - 1]).wait()
        own = pick(placed.T[:EBD].astype(BF16), facing)
        XO[...] = own
        XA[it, pl.ds(EBD * ix, EBD)] = own

        def send(to, y):
            pltpu.make_async_remote_copy(
                XO, XA.at[it, pl.ds(EBD * ix, EBD)], xsend.at[it], xrecv.at[it],
                device_id=(to, y, iz), device_id_type=MESH,
            ).start()

        def group(step, carry):
            for to, home_y in owners_at(step):
                send(to, home_y)
            return carry

        lax.fori_loop(0, RING_Z - 1, group, 0)
        for to, home_y in near_owners:
            send(to, home_y)

    def respond(it):
        rest = XA.at[it, pl.ds(0, (NFX - 1) * EBD)]
        pltpu.make_async_copy(rest, rest, xrecv.at[it]).wait()
        high, low = split(XA[it])
        both = jnp.concatenate([high, low], axis=1)
        for m in range(AROUND):
            found = jnp.dot(G[m], both, preferred_element_type=F32)
            GW[m] = found[:, :CY] + found[:, CY:]

        def chunk(n, carry):
            at = pl.ds(pl.multiple_of(n * CX, CX), CX)
            centre = {d: GW[d + 2, at] for d in range(-2, 3)}
            beyond = {d: jnp.where(lane >= CY // 2, GW[d + 6, at], GW[d + 9, at]) for d in range(-1, 2)}
            coeff = {d: RC[d + 2, at] for d in range(-1, 2)}

            def wide_sum(d):
                total = centre[d - 1] + centre[d + 1] - 4.0 * centre[d]
                total += jnp.where(lane == 0, pltpu.roll(beyond[d], 1, 1), pltpu.roll(centre[d], 1, 1))
                return total + jnp.where(
                    lane == CY - 1, pltpu.roll(beyond[d], CY - 1, 1), pltpu.roll(centre[d], CY - 1, 1)
                )

            sums = {d: wide_sum(d) for d in range(-1, 2)}
            slopes = {d: coeff[d] * (sums[d] + first_jump * centre[d]) for d in range(-1, 2)}
            above = RC[4, at] * ((NZ - 1.0) / NZ * sums[0])
            facts = RC[0, at]
            edge_coeff = jnp.where(lane >= CY // 2, facts[:, AROUND : AROUND + 1], facts[:, AROUND + 1 : AROUND + 2])
            edge_sum = beyond[-1] + beyond[1] - 4.0 * beyond[0]
            edge_sum += jnp.where(
                lane >= CY // 2,
                pltpu.roll(beyond[0], 1, 1) + pltpu.roll(centre[0], CY - 1, 1),
                pltpu.roll(beyond[0], CY - 1, 1) + pltpu.roll(centre[0], 1, 1),
            )
            edges = edge_coeff * (edge_sum + first_jump * beyond[0])
            bend = slopes[-1] + slopes[1] + above - 6.0 * slopes[0]
            bend += jnp.where(lane == 0, pltpu.roll(edges, 1, 1), pltpu.roll(slopes[0], 1, 1))
            bend += jnp.where(lane == CY - 1, pltpu.roll(edges, CY - 1, 1), pltpu.roll(slopes[0], CY - 1, 1))
            IN[at] = press_twice * centre[0] + 2.0 * press_once * slopes[0] + press_source * coeff[0] * bend
            return carry

        lax.fori_loop(0, FACES // CX, chunk, 0)

    def answer(it):
        heard_from_faces(it)
        if it:
            sent_to_faces(it - 1)
        rows_in = RF[it] + IN[...] if it else RF[it]
        FR[...] = pick(FP[...].astype(BF16), rows_in)
        solve()
        facing = lax.dot_general(XV[...], interp[...], NT, precision=HIGHEST, preferred_element_type=F32)
        if 0 < it < ITERS - 1:
            tell_solvers(it, facing)
        SD[...] = pick(FPT[...].astype(BF16), facing)
        send_to_faces(it)
        if it == 0:
            tell_solvers(it, facing)

    def hear_wall(it):
        whole = RD.at[it]
        pltpu.make_async_copy(whole, whole, drecv.at[it]).wait()
        WN[it, 1, inner] = pick(AT[...].astype(BF16), RD[it])

    def relay(it, part):
        return pltpu.make_async_remote_copy(
            part, part, rsend.at[it], rrecv.at[it], device_id=other_core, device_id_type=MESH
        )

    around_wall = wall_copies(ITERS)

    @pl.when(on_wall)
    def _():
        each(around_wall, lambda pair: pair[0].start())

    for it in range(ITERS - 1):
        n = 2 * it + 2
        pack(S.at[0])
        start_halo(n, S.at[0])
        if it == 0:

            @pl.when(on_wall)
            def _():
                each(around_wall, lambda pair: pair[1].wait_recv())
                tell_faces()
                each(around_wall, lambda pair: pair[0].wait_send())

            send_facts()
        else:

            @pl.when(is_solver)
            def _():
                answer(it)

        finish_halo(n, S.at[0])
        sweep(n, S.at[0], S.at[1])
        pack(S.at[1])
        start_halo(n + 1, S.at[1])
        if it == 0:

            @pl.when(is_solver)
            def _():
                answer(it)

        finish_halo(n + 1, S.at[1])
        sweep(n + 1, S.at[1], S.at[0])
        wall_base()
        sent_to_solvers(it)
        send_pressure(it + 1)
        if it == 0:

            @pl.when(is_solver)
            def _():
                hear_facts()

        copies = wall_copies(it)

        @pl.when(on_wall)
        def _():
            hear_wall(it)
            each(copies, lambda pair: pair[0].start())

        @pl.when(is_solver)
        def _():
            respond(it)

        beside_wall = relay(it, WN.at[it])

        @pl.when(on_wall)
        def _():
            each(copies, lambda pair: pair[1].wait_recv())
            beside_wall.start()

        @pl.when(off_wall)
        def _():
            beside_wall.wait_recv()

        spread(it)
        update()

        @pl.when(on_wall)
        def _():
            each(copies, lambda pair: pair[0].wait_send())
            beside_wall.wait_send()

    sent_facts()

    last = ITERS - 1
    out = pltpu.make_async_copy(S.at[0, :, pl.ds(1, NZL)], state_out, load_sem.at[0])
    out.start()

    def disp_copy(t):
        return pltpu.make_async_remote_copy(
            DV, DR, osend.at[t], orecv.at[1], device_id=(ix, (iy + t) % NFY, iz), device_id_type=MESH
        )

    @pl.when(is_solver)
    def _():
        answer(last)
        back = lax.dot_general(placed, XV[...], (((0,), (0,)), ((), ())), precision=HIGHEST, preferred_element_type=F32)
        DV[...] = back[:EBD]
        for t in range(1, NFY):
            disp_copy(t).start()
        disp_out[...] = back[:EBD]

    beside_wall = relay(last, WN.at[last, 1, pl.ds(PAD, CX)])

    @pl.when(on_wall)
    def _():
        sent_to_solvers(last)
        hear_wall(last)
        beside_wall.start()

    @pl.when(off_wall)
    def _():
        beside_wall.wait_recv()

    for z in range(NZL):
        share, _ = profile(z + 1)
        raised_out[z] = share * WN[last, 1, inner]

    @pl.when(on_wall)
    def _():
        beside_wall.wait_send()

    @pl.when(is_solver)
    def _():
        sent_to_faces(last)
        rest = XA.at[0, pl.ds(0, (NFX - 1) * EBD)]
        pltpu.make_async_copy(rest, rest, xsend.at[last - 1]).wait()
        for t in range(1, NFY):
            disp_copy(t).wait_send()

    @pl.when(not_solver)
    def _():
        disp_copy(1).wait_recv()
        disp_out[...] = DR[...]

    out.wait()


def on_device(
    state, kappa, mix, press_weight, source_weight, interp, block_inverse, coupling, front_order, face_owner, face_slot
):
    hbm = pl.BlockSpec(memory_space=pltpu.HBM)
    vmem = pl.BlockSpec(memory_space=pltpu.VMEM)
    dma = pltpu.SemaphoreType.DMA
    sweeps = 2 * ITERS
    before, raised, displacement = pl.pallas_call(
        kernel,
        out_shape=(
            jax.ShapeDtypeStruct(state.shape, F32),
            jax.ShapeDtypeStruct(kappa.shape, F32),
            jax.ShapeDtypeStruct((EBD, EB), F32),
        ),
        in_specs=[hbm] * 11,
        out_specs=(hbm, vmem, vmem),
        scratch_shapes=[
            pltpu.SMEM((NV, NV), F32),
            pltpu.SMEM((NV,), F32),
            pltpu.SMEM((NV,), F32),
            pltpu.VMEM((CY, EB), F32),
            pltpu.SMEM((1, EBD), jnp.int32),
            pltpu.VMEM((1, CX), jnp.int32),
            pltpu.VMEM((1, CX), jnp.int32),
            pltpu.VMEM((2, NV, NZL + 2, CX, CY), F32),
            pltpu.VMEM((NZL, CX, CY), F32),
            pltpu.VMEM((NZL + 2, CXE, CY), F32),
            pltpu.VMEM((NZL, CX, CY), F32),
            pltpu.VMEM((EBD, EB, EB), F32),
            pltpu.VMEM((EBD, EB, EB), F32),
            pltpu.VMEM((EBD, 2 * EB, 2 * EB), BF16),
            pltpu.VMEM((2, NV + 1, NZL, CY), F32),
            pltpu.VMEM((sweeps, 2, NV + 1, NZL, CY), F32),
            pltpu.VMEM((2, CX, CY), F32),
            pltpu.VMEM((sweeps, 2, CX, CY), F32),
            pltpu.VMEM((2, CX, CY), F32),
            pltpu.VMEM((sweeps, NV, CX, CY), F32),
            pltpu.VMEM((CXE, CY), F32),
            pltpu.VMEM((CAP * NFX, CY), F32),
            pltpu.VMEM((CAP * NFX, CY), F32),
            pltpu.VMEM((5, CAP * NFX, CY), F32),
            pltpu.VMEM((ITERS + 1, FACES, CY), F32),
            pltpu.VMEM((5, FACES, CY), F32),
            pltpu.VMEM((FACES, CY), F32),
            pltpu.VMEM((ITERS, CAP * NFX, CY), F32),
            pltpu.VMEM((EBD, FACES), F32),
            pltpu.VMEM((FACES, EBD), F32),
            pltpu.VMEM((CAP * NFX, CX), F32),
            pltpu.VMEM((CX, CAP * NFX), F32),
            pltpu.VMEM((EBD, EB), F32),
            pltpu.VMEM((EBD, EB), F32),
            pltpu.VMEM((EBD, EB), F32),
            pltpu.VMEM((EBD, EB), F32),
            pltpu.VMEM((ITERS + 1, 3, CXE, CY), F32),
            pltpu.VMEM((2, CXE, CY), F32),
            pltpu.VMEM((2, CX, CY), F32),
            pltpu.VMEM((NZL + 2, CXE, CY), F32),
            pltpu.VMEM((CX, CY), F32),
            pltpu.VMEM((AROUND, FACES, NFX * EBD), BF16),
            pltpu.VMEM((AROUND, FACES, CY), F32),
            pltpu.VMEM((FACES, CY), F32),
            pltpu.VMEM((EBD, EB), F32),
            pltpu.VMEM((ITERS - 1, NFX * EBD, EB), F32),
            dma((11,)),
            dma((sweeps, 5)),
            dma((sweeps, 5)),
            dma((ITERS + 1,)),
            dma((ITERS + 1,)),
            dma((ITERS,)),
            dma((ITERS,)),
            dma((NFY,)),
            dma((2,)),
            dma((ITERS + 1, 8)),
            dma((ITERS + 1, 8)),
            dma((ITERS,)),
            dma((ITERS,)),
            dma,
            dma,
            dma((ITERS - 1,)),
            dma((ITERS - 1,)),
        ],
        compiler_params=pltpu.CompilerParams(
            collective_id=0, has_side_effects=True, vmem_limit_bytes=60 * 1024 * 1024
        ),
    )(
        state, kappa, mix, press_weight, source_weight, interp, block_inverse, coupling, front_order,
        face_owner.reshape(1, -1), face_slot.reshape(1, -1),
    )
    return before + source_weight[:, None, None, None] * raised[None], displacement


def solution(mesh):
    return jax.shard_map(
        on_device,
        mesh=mesh,
        in_specs=(
            P(None, "fz", "fx", "fy"),
            P("fz", "fx", "fy"),
            P(),
            P(),
            P(),
            P(),
            P("fx", None, None),
            P("fx", None, None),
            P("fx", None),
            P(("fx", "fy"), None),
            P(("fx", "fy")),
        ),
        out_specs=(P(None, "fz", "fx", "fy"), P("fx", None)),
        check_vma=False,
    )
```

```python
import jax
import jax.numpy as jnp
from jax import lax
from jax.experimental import pallas as pl
from jax.experimental.pallas import tpu as pltpu
from jax.sharding import PartitionSpec as P

ITERS = 3
DIFFUSION = 0.16
HIGHEST = lax.Precision.HIGHEST
MESH = pl.DeviceIdType.MESH
F32 = jnp.float32
BF16 = jnp.bfloat16

NV, NZL, CX, CY = 5, 8, 32, 128
NZ = 16
NFX, NFY = 32, 4
RING_Z, RING_Y = 8, 4
EB, EBD, CAP = 128, 16, 2
FACES = NFX * NFY * CAP
PAD = 8
CXE = CX + 2 * PAD
NT = (((1,), (1,)), ((), ()))
FAR_Y = (2, 1, 3, 0)
AROUND = 11


def far_first(step, ring):
    return ring // 2 + (1 - 2 * (step % 2)) * ((step + 1) // 2)


def split(values):
    high = values.astype(BF16)
    return high, (values - high.astype(F32)).astype(BF16)


def pick(selector, values):
    high, low = split(values)
    return jnp.dot(selector, high, preferred_element_type=F32) + jnp.dot(selector, low, preferred_element_type=F32)


def kernel(
    state_in, kappa_in, mix_in, press_in, source_in, interp_in, inverse_in, coupling_in, order_in, owner_in, slot_in,
    state_out, raised_out, disp_out,
    mix, press_weight, source_weight, interp, order, owner, slot,
    S, K, KX, KE, BI, CO, R, XS, XR, YS, YR, YK, ZR, KZ, SL, SF, CS, RF, RC, SD, RD, FP, FPT, AM, AT, FR, XV, DV, DR,
    WN, LP, LE, QB, PB, G, GW, IN, XO, XA,
    load_sem, hsend, hrecv, fsend, frecv, dsend, drecv, osend, orecv, wsend, wrecv, rsend, rrecv, csend, crecv, xsend, xrecv,
):
    ix, iy, iz = lax.axis_index("fx"), lax.axis_index("fy"), lax.axis_index("fz")
    ring_z, ring_y = ix // RING_Y, ix % RING_Y
    on_wall = iz == 0
    off_wall = iz == 1
    home = (ring_y + ring_z) % NFY
    is_solver = iy == home
    not_solver = jnp.logical_not(is_solver)
    turned_y = {d: (ring_y + d) % RING_Y for d in FAR_Y}
    turned_x = {d: (iy + d) % NFY for d in FAR_Y}
    answer_x = ((iy + 2 - iz) % NFY, (iy + 3 * iz) % NFY)

    def row_base(step):
        return ((ring_z + far_first(step, RING_Z)) % RING_Z) * RING_Y

    def homes(z):
        return {d: (turned_y[d] + z) % NFY for d in FAR_Y}

    def owners_at(step):
        z = (ring_z + far_first(step, RING_Z)) % RING_Z
        return [(z * RING_Y + turned_y[d], home_y) for d, home_y in homes(z).items()]

    near_owners = [(ring_z * RING_Y + turned_y[d], home_y) for d, home_y in homes(ring_z).items()][:3]

    def signal(barrier, device):
        pl.semaphore_signal(barrier, inc=1, device_id=device, device_id_type=MESH)

    loads = [
        pltpu.make_async_copy(source, target, load_sem.at[n])
        for n, (source, target) in enumerate(
            (
                (owner_in, owner),
                (slot_in, slot),
                (order_in, order),
                (kappa_in, K),
                (state_in, S.at[0, :, pl.ds(1, NZL)]),
                (inverse_in, BI),
                (coupling_in, CO),
                (interp_in, interp),
                (mix_in, mix),
                (press_in, press_weight),
                (source_in, source_weight),
            )
        )
    ]
    for load in loads:
        load.start()

    barrier = pltpu.get_barrier_semaphore()
    has_left, has_right, has_front, has_back = ix > 0, ix < NFX - 1, iy > 0, iy < NFY - 1
    sides = (
        (has_left, (ix - 1, iy, iz)),
        (has_right, (ix + 1, iy, iz)),
        (has_front, (ix, iy - 1, iz)),
        (has_back, (ix, iy + 1, iz)),
    )
    corners = (
        (jnp.logical_and(has_left, has_front), (ix - 1, iy - 1, iz)),
        (jnp.logical_and(has_left, has_back), (ix - 1, iy + 1, iz)),
        (jnp.logical_and(has_right, has_front), (ix + 1, iy - 1, iz)),
        (jnp.logical_and(has_right, has_back), (ix + 1, iy + 1, iz)),
    )
    other_core = (ix, iy, 1 - iz)

    @pl.when(is_solver)
    def _():
        def greet(step, carry):
            base = row_base(step)
            for dy in FAR_Y:
                for dx in FAR_Y:
                    signal(barrier, (base + turned_y[dy], turned_x[dx], 0))
            return carry

        lax.fori_loop(0, RING_Z - 1, greet, 0)
        for dy in FAR_Y:
            for dx in FAR_Y:
                if dy or dx:
                    signal(barrier, (ring_z * RING_Y + turned_y[dy], turned_x[dx], 0))

        @pl.when(off_wall)
        def _():
            signal(barrier, (ix, iy, 0))

        def greet_solvers(step, carry):
            for to, home_y in owners_at(step):
                signal(barrier, (to, home_y, iz))
            return carry

        lax.fori_loop(0, RING_Z - 1, greet_solvers, 0)
        for to, home_y in near_owners:
            signal(barrier, (to, home_y, iz))

    @pl.when(on_wall)
    def _():
        def greet(step, carry):
            for to, home_y in owners_at(step):
                signal(barrier, (to, home_y, (iy + home_y) % 2))
            return carry

        lax.fori_loop(0, RING_Z - 1, greet, 0)
        for to, home_y in near_owners:
            signal(barrier, (to, home_y, (iy + home_y) % 2))

        @pl.when(not_solver)
        def _():
            signal(barrier, (ix, home, (iy + home) % 2))

    @pl.when(not_solver)
    def _():
        signal(barrier, (ix, home, iz))

    for ref in (XR, YR, WN):
        ref[...] = jnp.zeros_like(ref)

    signal(barrier, other_core)
    solver_count = is_solver.astype(jnp.int32)
    wall_count = on_wall.astype(jnp.int32)
    expected = 1 + wall_count * (2 * NFX - solver_count) + solver_count * (2 * NFX - wall_count + NFY - 1 + NFX - 1)
    for present, device in sides + corners:
        expected = expected + present.astype(jnp.int32)

        @pl.when(present)
        def _():
            signal(barrier, device)

    zero_plane = jnp.zeros((NV, CX, CY), F32)
    for buffer in range(2):
        S[buffer, :, 0] = zero_plane
        S[buffer, :, NZL + 1] = zero_plane

    for load in loads[:3]:
        load.wait()
    rows = lax.broadcasted_iota(jnp.int32, (CAP * NFX, CX), 0)
    named = (owner[...] == rows // CAP).astype(F32)
    earlier = (
        lax.broadcasted_iota(jnp.int32, (CX, CX), 0) < lax.broadcasted_iota(jnp.int32, (CX, CX), 1)
    ).astype(BF16)
    rank = jnp.dot(named.astype(BF16), earlier, preferred_element_type=F32)
    chosen = jnp.where(rank == (rows % CAP).astype(F32), named, 0.0)
    AM[...] = chosen
    unit = (lax.broadcasted_iota(jnp.int32, (CX, CX), 0) == lax.broadcasted_iota(jnp.int32, (CX, CX), 1)).astype(F32)
    AT[...] = lax.dot_general(unit, chosen, NT, preferred_element_type=F32)
    slot_rows = jnp.sum(chosen * (slot[...] + 1).astype(F32), axis=1, keepdims=True)
    SL[...] = jnp.broadcast_to(slot_rows, (CAP * NFX, CY))
    target_of = jnp.sum(unit * (EBD * owner[...] + slot[...] + 1).astype(F32), axis=1, keepdims=True)
    WN[ITERS, 1, PAD : PAD + CX] = jnp.broadcast_to(target_of, (CX, CY))
    block_rows = lax.broadcasted_iota(jnp.int32, (EBD, EB), 0)
    block_lanes = lax.broadcasted_iota(jnp.int32, (EBD, EB), 1)
    placed = jnp.zeros((EBD, EB), F32)
    for k in range(EBD):
        placed = jnp.where(jnp.logical_and(block_rows == k, block_lanes == order[0, k]), 1.0, placed)

    lane = lax.broadcasted_iota(jnp.int32, (CX, CY), 1)
    row = lax.broadcasted_iota(jnp.int32, (CX, CY), 0)
    for load in loads[3:5]:
        load.wait()

    pair = lane // 2

    def put_ends(ends, centre, at):
        return jnp.where(pair == at, pltpu.roll(centre, 2 * at + 1, 1), ends)

    def take_ends(n):
        return jnp.where(lane % 2 == 0, pltpu.roll(YR[n, 1], CY - 1, 1), pltpu.roll(YR[n, 0], 1, 1))

    def kappa_faces(z, ends):
        coeff = DIFFUSION * K[z]
        KX[z + 1, PAD : PAD + CX] = coeff
        XS[0, NV, pl.ds(z, 1), :] = coeff[0:1]
        XS[1, NV, pl.ds(z, 1), :] = coeff[CX - 1 : CX]
        return put_ends(ends, coeff, NV * NZL + z)

    YK[...] = lax.fori_loop(0, NZL, kappa_faces, jnp.zeros((CX, CY), F32))

    def pack(src):
        def plane(z, ends):
            for c in range(NV):
                centre = src[c, z + 1]
                XS[0, c, pl.ds(z, 1), :] = centre[0:1]
                XS[1, c, pl.ds(z, 1), :] = centre[CX - 1 : CX]
                ends = put_ends(ends, centre, c * NZL + z)
            return ends

        YS[...] = lax.fori_loop(0, NZL, plane, YK[...])

    edge = NZL - (NZL - 1) * iz

    def halo_copies(n, src):
        def remote(source, target, at, there, device):
            return pltpu.make_async_remote_copy(
                source, target, hsend.at[n, at], hrecv.at[n, there], device_id=device, device_id_type=MESH
            )

        (_, left), (_, right), (_, front), (_, back) = sides
        always = iz >= 0
        plane = src.at[:, edge]
        sends = (
            (has_left, remote(XS.at[0], XR.at[n, 1], 0, 1, left)),
            (has_right, remote(XS.at[1], XR.at[n, 0], 1, 0, right)),
            (has_front, remote(YS, YR.at[n, 1], 2, 3, front)),
            (has_back, remote(YS, YR.at[n, 0], 3, 2, back)),
            (always, remote(plane, ZR.at[n], 4, 4, other_core)),
        )
        waits = (
            (has_left, remote(XS.at[0], XR.at[n, 0], 0, 0, left)),
            (has_right, remote(XS.at[1], XR.at[n, 1], 1, 1, right)),
            (has_front, remote(YS, YR.at[n, 0], 2, 2, front)),
            (has_back, remote(YS, YR.at[n, 1], 3, 3, back)),
            (always, remote(plane, ZR.at[n], 4, 4, other_core)),
        )
        return sends, waits

    def each(copies, action):
        for present, copy in copies:

            @pl.when(present)
            def _():
                action(copy)

    def start_halo(n, src):
        each(halo_copies(n, src)[0], lambda copy: copy.start())

    def finish_halo(n, src):
        _, waits = halo_copies(n, src)
        each(waits, lambda copy: copy.wait_recv())
        src[:, (NZL + 1) * (1 - iz)] = ZR[n]

    def sweep(n, src, dst):
        outer = take_ends(n)

        def plane(z, carry):
            coeff = KX[z + 1, PAD : PAD + CX]
            centres = [src[c, z + 1] for c in range(NV)]
            for c in range(NV):
                centre = centres[c]
                at = c * NZL + z
                beside = src[c, z] + src[c, z + 2]
                beside += jnp.where(row == 0, XR[n, 0, c, pl.ds(z, 1), :], pltpu.roll(centre, 1, 0))
                beside += jnp.where(row == CX - 1, XR[n, 1, c, pl.ds(z, 1), :], pltpu.roll(centre, CX - 1, 0))
                ends = pltpu.roll(outer, CY - 1 - 2 * at, 1)
                beside += jnp.where(lane == 0, ends, pltpu.roll(centre, 1, 1))
                beside += jnp.where(lane == CY - 1, ends, pltpu.roll(centre, CY - 1, 1))
                total = centre + coeff * (beside - 6.0 * centre)
                for d in range(NV):
                    total += mix[c, d] * centres[d]
                dst[c, z + 1] = total
            return carry

        lax.fori_loop(0, NZL, plane, 0)
        each(halo_copies(n, src)[0], lambda copy: copy.wait_send())

    kappa_plane = pltpu.make_async_remote_copy(
        KX.at[edge], KZ, osend.at[0], orecv.at[0], device_id=other_core, device_id_type=MESH
    )

    def send_to_solvers(rows_of, target, sent, heard):
        def send(to, y, core):
            pltpu.make_async_remote_copy(
                rows_of(to), target, sent, heard, device_id=(to, y, core), device_id_type=MESH
            ).start()

        def group(step, carry):
            for to, home_y in owners_at(step):
                for core in range(2):
                    send(to, home_y, core)
            return carry

        @pl.when(on_wall)
        def _():
            lax.fori_loop(0, RING_Z - 1, group, 0)
            for to, home_y in near_owners:
                for core in range(2):
                    send(to, home_y, core)
            send(ix, home, 1)

            @pl.when(not_solver)
            def _():
                send(ix, home, 0)

            @pl.when(is_solver)
            def _():
                pltpu.make_async_copy(rows_of(ix), target, heard).start()

    own_rows = pl.ds(CAP * (ix * NFY + iy), CAP)

    def send_rows(turn, rows_out):
        send_to_solvers(
            lambda to: rows_out.at[pl.ds(CAP * to, CAP)], RF.at[turn, own_rows], fsend.at[turn], frecv.at[turn]
        )

    def send_pressure(turn):
        @pl.when(on_wall)
        def _():
            SF[...] = pick(AM[...].astype(BF16), PB[...])

        send_rows(turn, SF)

    def sent_to_solvers(turn):
        @pl.when(on_wall)
        def _():
            @pl.when(is_solver)
            def _():
                rest = RF.at[turn, pl.ds(0, CAP * (2 * NFX - 1))]
                pltpu.make_async_copy(rest, rest, fsend.at[turn]).wait()

            @pl.when(not_solver)
            def _():
                rest = RF.at[turn, pl.ds(0, CAP * 2 * NFX)]
                pltpu.make_async_copy(rest, rest, fsend.at[turn]).wait()

    def heard_from_faces(turn):
        whole = RF.at[turn]
        pltpu.make_async_copy(whole, whole, frecv.at[turn]).wait()

    def send_to_faces(turn):
        target = RD.at[turn, pl.ds(CAP * ix, CAP)]

        def send(to_x, to_y):
            pltpu.make_async_remote_copy(
                SD.at[pl.ds(CAP * (to_x * NFY + to_y), CAP)], target, dsend.at[turn], drecv.at[turn],
                device_id=(to_x, to_y, 0), device_id_type=MESH,
            ).start()

        def group(step, carry):
            base = row_base(step)
            for dy in FAR_Y:
                for x in answer_x:
                    send(base + turned_y[dy], x)
            return carry

        lax.fori_loop(0, RING_Z - 1, group, 0)
        for dy in FAR_Y[:3]:
            for x in answer_x:
                send(ring_z * RING_Y + turned_y[dy], x)
        send(ix, answer_x[0])

        @pl.when(off_wall)
        def _():
            send(ix, answer_x[1])

        @pl.when(on_wall)
        def _():
            pltpu.make_async_copy(SD.at[pl.ds(CAP * (ix * NFY + iy), CAP)], target, drecv.at[turn]).start()

    def sent_to_faces(turn):
        @pl.when(on_wall)
        def _():
            rest = RF.at[turn, pl.ds(0, CAP * (2 * NFX - 1))]
            pltpu.make_async_copy(rest, rest, dsend.at[turn]).wait()

        @pl.when(off_wall)
        def _():
            rest = RF.at[turn, pl.ds(0, CAP * 2 * NFX)]
            pltpu.make_async_copy(rest, rest, dsend.at[turn]).wait()

    for load in loads[5:]:
        load.wait()

    @pl.when(is_solver)
    def _():
        def products(k, carry):
            block = order[0, k]
            inverse = BI[block]
            force_part = lax.dot_general(interp[...], inverse, NT, precision=HIGHEST, preferred_element_type=F32)
            chain = jnp.dot(inverse, CO[block], precision=HIGHEST, preferred_element_type=F32)
            high, low = split(jnp.concatenate([force_part, -chain.T], axis=0))
            R[k] = jnp.concatenate([high, low], axis=1)
            return carry

        lax.fori_loop(0, EBD, products, 0)

    numbers = range(NV)
    source = [source_weight[c] for c in numbers]
    once = [source[c] + sum(mix[c, d] * source[d] for d in numbers) for c in numbers]
    twice = [once[c] + sum(mix[c, d] * once[d] for d in numbers) for c in numbers]
    press_source = sum(press_weight[c] * source[c] for c in numbers)
    press_once = sum(press_weight[c] * once[c] for c in numbers)
    press_twice = sum(press_weight[c] * twice[c] for c in numbers)

    pack(S.at[0])
    pl.semaphore_wait(barrier, expected)
    start_halo(0, S.at[0])
    kappa_plane.start()
    send_rows(ITERS, SL)
    finish_halo(0, S.at[0])
    sweep(0, S.at[0], S.at[1])
    pack(S.at[1])
    start_halo(1, S.at[1])

    kappa_plane.wait()
    KX[(NZL + 1) * (1 - iz)] = KZ[...]
    KX[(NZL + 1) * iz] = jnp.zeros((CXE, CY), F32)
    tile_row = lax.broadcasted_iota(jnp.int32, (PAD, CY), 0)

    ends = take_ends(0)

    def kappa_edges(z, carry):
        KX[z + 1, 0:PAD] = jnp.where(tile_row == PAD - 1, XR[0, 0, NV, pl.ds(z, 1), :], 0.0)
        KX[z + 1, PAD + CX : CXE] = jnp.where(tile_row == 0, XR[0, 1, NV, pl.ds(z, 1), :], 0.0)
        at = 2 * (NV * NZL + z)
        front = pltpu.roll(ends, CY - 2 - at, 1)
        back = pltpu.roll(ends, CY - at, 1)
        KE[z] = jnp.where(lane >= CY // 2, front, back)
        return carry

    lax.fori_loop(0, NZL, kappa_edges, 0)

    def wall_base():
        @pl.when(on_wall)
        def _():
            pressure = press_weight[0] * S[0, 0, 1]
            for c in range(1, NV):
                pressure += press_weight[c] * S[0, c, 1]
            PB[...] = pressure

    finish_halo(1, S.at[1])
    sweep(1, S.at[1], S.at[0])
    wall_base()
    sent_to_solvers(ITERS)

    send_pressure(0)

    @pl.when(is_solver)
    def _():
        heard_from_faces(ITERS)
        face_lanes = lax.broadcasted_iota(jnp.int32, (FACES, EB), 1) + 1
        slot_of = (RF[ITERS] == face_lanes.astype(F32)).astype(F32)
        FP[...] = lax.dot_general(placed, slot_of, NT, preferred_element_type=F32)
        FPT[...] = lax.dot_general(slot_of, placed, NT, preferred_element_type=F32)

    def solve():
        for k in range(EBD):
            force = FR[pl.ds(k, 1), :]
            previous = XV[pl.ds(k - 1, 1), :] if k else jnp.zeros((1, EB), F32)
            both = jnp.concatenate([force, previous], axis=1)
            high = both.astype(BF16).astype(F32)
            at = lax.broadcasted_iota(jnp.int32, (8, 2 * EB), 0)
            left = jnp.where(at == 0, high, jnp.where(at == 1, both - high, 0.0)).astype(BF16)
            result = jnp.dot(left, R[k], preferred_element_type=F32)
            summed = result[:, :EB] + result[:, EB:]
            XV[pl.ds(k, 1), :] = summed[0:1] + summed[1:2]

    def wall_copies(it):
        def remote(n, opposite, source_row, side, target_row, count, device):
            copy = lambda here, there: pltpu.make_async_remote_copy(
                WN.at[it, 1, pl.ds(source_row, count)], WN.at[it, side, pl.ds(target_row, count)],
                wsend.at[it, here], wrecv.at[it, there], device_id=device, device_id_type=MESH,
            )
            return copy(n, opposite), copy(n, n)

        low, high = PAD, PAD + CX - 8
        (_, left), (_, right), (_, front), (_, back) = sides
        (lf, left_front), (lb, left_back), (rf, right_front), (rb, right_back) = corners
        return (
            (has_left, remote(0, 1, low, 1, PAD + CX, 8, left)),
            (has_right, remote(1, 0, high, 1, 0, 8, right)),
            (has_front, remote(2, 3, PAD, 2, PAD, CX, front)),
            (has_back, remote(3, 2, PAD, 0, PAD, CX, back)),
            (lf, remote(4, 7, low, 2, PAD + CX, 8, left_front)),
            (lb, remote(5, 6, low, 0, PAD + CX, 8, left_back)),
            (rf, remote(6, 5, high, 2, 0, 8, right_front)),
            (rb, remote(7, 4, high, 0, 0, 8, right_back)),
        )

    lane_e = lax.broadcasted_iota(jnp.int32, (CXE, CY), 1)
    inner = slice(PAD, PAD + CX)

    def spread(it):
        centre = WN[it, 1]
        beyond = jnp.where(lane_e >= CY // 2, WN[it, 0], WN[it, 2])
        up, down = pltpu.roll(centre, 1, 1), pltpu.roll(centre, CY - 1, 1)
        out_up, out_down = pltpu.roll(beyond, 1, 1), pltpu.roll(beyond, CY - 1, 1)
        lap = pltpu.roll(centre, 1, 0) + pltpu.roll(centre, CXE - 1, 0) - 4.0 * centre
        lap += jnp.where(lane_e == 0, out_up, up) + jnp.where(lane_e == CY - 1, out_down, down)
        lap_e = pltpu.roll(beyond, 1, 0) + pltpu.roll(beyond, CXE - 1, 0) - 4.0 * beyond
        lap_e += jnp.where(lane_e >= CY // 2, out_up + down, out_down + up)
        LP[0], LP[1] = lap, centre
        LE[0], LE[1] = lap_e[inner], beyond[inner]

    def ring_sum(wide, edge_columns, below, above, coeff):
        own = wide[inner]
        total = pltpu.roll(wide, 1, 0)[inner] + pltpu.roll(wide, CXE - 1, 0)[inner] + below + above - 6.0 * own
        total += jnp.where(lane == 0, pltpu.roll(edge_columns, 1, 1), pltpu.roll(own, 1, 1))
        total += jnp.where(lane == CY - 1, pltpu.roll(edge_columns, CY - 1, 1), pltpu.roll(own, CY - 1, 1))
        return coeff * total

    first_jump = (NZ - 1.0) / NZ - 2.0

    def profile(plane):
        height = iz * NZL + plane - 1
        return 1.0 - height.astype(F32) / NZ, jnp.where(height == 0, first_jump, 0.0)

    def update():
        def first(plane, carry):
            share, jump = profile(plane)
            QB[plane] = KX[plane] * (share * LP[0] + jump * LP[1])
            return carry

        lax.fori_loop(0, NZL + 2, first, 0)

        def second(z, carry):
            share, jump = profile(z + 1)
            edges = KE[z] * (share * LE[0] + jump * LE[1])
            wide = QB[z + 1]
            bend = ring_sum(wide, edges, QB[z, inner], QB[z + 2, inner], KX[z + 1, inner])
            raised, slope = share * LP[1, inner], wide[inner]
            for c in range(NV):
                S[0, c, z + 1] += twice[c] * raised + 2.0 * once[c] * slope + source[c] * bend
            return carry

        lax.fori_loop(0, NZL, second, 0)

    def tell_faces():
        targets = (
            [pltpu.roll(WN[ITERS, 1], (CXE - d) % CXE, 0)[inner] for d in range(-2, 3)]
            + [pltpu.roll(WN[ITERS, 0], (CXE - d) % CXE, 0)[inner] for d in range(-1, 2)]
            + [pltpu.roll(WN[ITERS, 2], (CXE - d) % CXE, 0)[inner] for d in range(-1, 2)]
        )
        facts = targets + [
            jnp.broadcast_to(KE[0, :, CY - 1 : CY], (CX, CY)), jnp.broadcast_to(KE[0, :, 0:1], (CX, CY)),
        ]
        table = jnp.zeros((CX, CY), F32)
        for n, fact in enumerate(facts):
            table = jnp.where(lane == n, fact, table)
        wall_coeff = KX[1]
        selector = AM[...].astype(BF16)
        CS[0] = pick(selector, table)
        for n, d in enumerate((-1, 0, 1)):
            CS[n + 1] = pick(selector, pltpu.roll(wall_coeff, (CXE - d) % CXE, 0)[inner])
        CS[4] = pick(selector, KX[2, inner])

    def send_facts():
        send_to_solvers(lambda to: CS.at[:, pl.ds(CAP * to, CAP)], RC.at[:, own_rows], csend, crecv)

    def sent_facts():
        @pl.when(on_wall)
        def _():
            @pl.when(is_solver)
            def _():
                rest = RC.at[:, pl.ds(0, CAP * (2 * NFX - 1))]
                pltpu.make_async_copy(rest, rest, csend).wait()

            @pl.when(not_solver)
            def _():
                rest = RC.at[:, pl.ds(0, CAP * 2 * NFX)]
                pltpu.make_async_copy(rest, rest, csend).wait()

    def hear_facts():
        pltpu.make_async_copy(RC, RC, crecv).wait()
        names = lax.broadcasted_iota(jnp.int32, (FACES, NFX * EBD), 1) + 1
        names = names.astype(F32)
        for m in range(AROUND):
            G[m] = jnp.where(names == RC[0, :, m : m + 1], 1.0, 0.0).astype(BF16)

    def tell_solvers(it, facing):
        if it:
            rest = XA.at[0, pl.ds(0, (NFX - 1) * EBD)]
            pltpu.make_async_copy(rest, rest, xsend.at[it - 1]).wait()
        own = pick(placed.T[:EBD].astype(BF16), facing)
        XO[...] = own
        XA[it, pl.ds(EBD * ix, EBD)] = own

        def send(to, y):
            pltpu.make_async_remote_copy(
                XO, XA.at[it, pl.ds(EBD * ix, EBD)], xsend.at[it], xrecv.at[it],
                device_id=(to, y, iz), device_id_type=MESH,
            ).start()

        def group(step, carry):
            for to, home_y in owners_at(step):
                send(to, home_y)
            return carry

        lax.fori_loop(0, RING_Z - 1, group, 0)
        for to, home_y in near_owners:
            send(to, home_y)

    def respond(it):
        rest = XA.at[it, pl.ds(0, (NFX - 1) * EBD)]
        pltpu.make_async_copy(rest, rest, xrecv.at[it]).wait()
        high, low = split(XA[it])
        both = jnp.concatenate([high, low], axis=1)
        for m in range(AROUND):
            found = jnp.dot(G[m], both, preferred_element_type=F32)
            GW[m] = found[:, :CY] + found[:, CY:]

        def chunk(n, carry):
            at = pl.ds(pl.multiple_of(n * CX, CX), CX)
            centre = {d: GW[d + 2, at] for d in range(-2, 3)}
            beyond = {d: jnp.where(lane >= CY // 2, GW[d + 6, at], GW[d + 9, at]) for d in range(-1, 2)}
            coeff = {d: RC[d + 2, at] for d in range(-1, 2)}

            def wide_sum(d):
                total = centre[d - 1] + centre[d + 1] - 4.0 * centre[d]
                total += jnp.where(lane == 0, pltpu.roll(beyond[d], 1, 1), pltpu.roll(centre[d], 1, 1))
                return total + jnp.where(
                    lane == CY - 1, pltpu.roll(beyond[d], CY - 1, 1), pltpu.roll(centre[d], CY - 1, 1)
                )

            sums = {d: wide_sum(d) for d in range(-1, 2)}
            slopes = {d: coeff[d] * (sums[d] + first_jump * centre[d]) for d in range(-1, 2)}
            above = RC[4, at] * ((NZ - 1.0) / NZ * sums[0])
            facts = RC[0, at]
            edge_coeff = jnp.where(lane >= CY // 2, facts[:, AROUND : AROUND + 1], facts[:, AROUND + 1 : AROUND + 2])
            edge_sum = beyond[-1] + beyond[1] - 4.0 * beyond[0]
            edge_sum += jnp.where(
                lane >= CY // 2,
                pltpu.roll(beyond[0], 1, 1) + pltpu.roll(centre[0], CY - 1, 1),
                pltpu.roll(beyond[0], CY - 1, 1) + pltpu.roll(centre[0], 1, 1),
            )
            edges = edge_coeff * (edge_sum + first_jump * beyond[0])
            bend = slopes[-1] + slopes[1] + above - 6.0 * slopes[0]
            bend += jnp.where(lane == 0, pltpu.roll(edges, 1, 1), pltpu.roll(slopes[0], 1, 1))
            bend += jnp.where(lane == CY - 1, pltpu.roll(edges, CY - 1, 1), pltpu.roll(slopes[0], CY - 1, 1))
            IN[at] = press_twice * centre[0] + 2.0 * press_once * slopes[0] + press_source * coeff[0] * bend
            return carry

        lax.fori_loop(0, FACES // CX, chunk, 0)

    def answer(it):
        heard_from_faces(it)
        if it:
            sent_to_faces(it - 1)
        rows_in = RF[it] + IN[...] if it else RF[it]
        FR[...] = pick(FP[...].astype(BF16), rows_in)
        solve()
        facing = lax.dot_general(XV[...], interp[...], NT, precision=HIGHEST, preferred_element_type=F32)
        if 0 < it < ITERS - 1:
            tell_solvers(it, facing)
        SD[...] = pick(FPT[...].astype(BF16), facing)
        send_to_faces(it)
        if it == 0:
            tell_solvers(it, facing)

    def hear_wall(it):
        whole = RD.at[it]
        pltpu.make_async_copy(whole, whole, drecv.at[it]).wait()
        WN[it, 1, inner] = pick(AT[...].astype(BF16), RD[it])

    def relay(it, part):
        return pltpu.make_async_remote_copy(
            part, part, rsend.at[it], rrecv.at[it], device_id=other_core, device_id_type=MESH
        )

    around_wall = wall_copies(ITERS)

    @pl.when(on_wall)
    def _():
        each(around_wall, lambda pair: pair[0].start())

    for it in range(ITERS - 1):
        n = 2 * it + 2
        pack(S.at[0])
        start_halo(n, S.at[0])
        if it == 0:

            @pl.when(on_wall)
            def _():
                each(around_wall, lambda pair: pair[1].wait_recv())
                tell_faces()
                each(around_wall, lambda pair: pair[0].wait_send())

            send_facts()
        else:

            @pl.when(is_solver)
            def _():
                answer(it)

        finish_halo(n, S.at[0])
        sweep(n, S.at[0], S.at[1])
        pack(S.at[1])
        start_halo(n + 1, S.at[1])
        if it == 0:

            @pl.when(is_solver)
            def _():
                answer(it)

        finish_halo(n + 1, S.at[1])
        sweep(n + 1, S.at[1], S.at[0])
        wall_base()
        sent_to_solvers(it)
        send_pressure(it + 1)
        if it == 0:

            @pl.when(is_solver)
            def _():
                hear_facts()

        copies = wall_copies(it)

        @pl.when(on_wall)
        def _():
            hear_wall(it)
            each(copies, lambda pair: pair[0].start())

        @pl.when(is_solver)
        def _():
            respond(it)

        beside_wall = relay(it, WN.at[it])

        @pl.when(on_wall)
        def _():
            each(copies, lambda pair: pair[1].wait_recv())
            beside_wall.start()

        @pl.when(off_wall)
        def _():
            beside_wall.wait_recv()

        spread(it)
        update()

        @pl.when(on_wall)
        def _():
            each(copies, lambda pair: pair[0].wait_send())
            beside_wall.wait_send()

    sent_facts()

    last = ITERS - 1
    out = pltpu.make_async_copy(S.at[0, :, pl.ds(1, NZL)], state_out, load_sem.at[0])
    out.start()

    def disp_copy(t):
        return pltpu.make_async_remote_copy(
            DV, DR, osend.at[t], orecv.at[1], device_id=(ix, (iy + t) % NFY, iz), device_id_type=MESH
        )

    @pl.when(is_solver)
    def _():
        answer(last)
        back = lax.dot_general(placed, XV[...], (((0,), (0,)), ((), ())), precision=HIGHEST, preferred_element_type=F32)
        DV[...] = back[:EBD]
        for t in range(1, NFY):
            disp_copy(t).start()
        disp_out[...] = back[:EBD]

    beside_wall = relay(last, WN.at[last, 1, pl.ds(PAD, CX)])

    @pl.when(on_wall)
    def _():
        sent_to_solvers(last)
        hear_wall(last)
        beside_wall.start()

    @pl.when(off_wall)
    def _():
        beside_wall.wait_recv()

    for z in range(NZL):
        share, _ = profile(z + 1)
        raised_out[z] = share * WN[last, 1, inner]

    @pl.when(on_wall)
    def _():
        beside_wall.wait_send()

    @pl.when(is_solver)
    def _():
        sent_to_faces(last)
        rest = XA.at[0, pl.ds(0, (NFX - 1) * EBD)]
        pltpu.make_async_copy(rest, rest, xsend.at[last - 1]).wait()
        for t in range(1, NFY):
            disp_copy(t).wait_send()

    @pl.when(not_solver)
    def _():
        disp_copy(1).wait_recv()
        disp_out[...] = DR[...]

    out.wait()


def last_add(before, raised, source_in, displacement, state_out, disp_out, T, A, D, source_weight, load_sem, out_sem):
    weights = pltpu.make_async_copy(source_in, source_weight, load_sem.at[NV])
    heights = pltpu.make_async_copy(raised, A, load_sem.at[NV + 1])
    small_in = pltpu.make_async_copy(displacement, D, load_sem.at[NV + 2])
    loads = [pltpu.make_async_copy(before.at[c], T.at[c], load_sem.at[c]) for c in range(NV)]
    stores = [pltpu.make_async_copy(T.at[c], state_out.at[c], out_sem.at[c]) for c in range(NV)]
    small_out = pltpu.make_async_copy(D, disp_out, out_sem.at[NV])
    for copy in [weights, heights] + loads + [small_in]:
        copy.start()
    weights.wait()
    heights.wait()
    for c in range(NV):
        loads[c].wait()

        def plane(z, carry):
            T[c, z] += source_weight[c] * A[z]
            return carry

        lax.fori_loop(0, NZL, plane, 0)
        stores[c].start()
    small_in.wait()
    small_out.start()
    for copy in stores + [small_out]:
        copy.wait()


def on_device(
    state, kappa, mix, press_weight, source_weight, interp, block_inverse, coupling, front_order, face_owner, face_slot
):
    hbm = pl.BlockSpec(memory_space=pltpu.HBM)
    vmem = pl.BlockSpec(memory_space=pltpu.VMEM)
    dma = pltpu.SemaphoreType.DMA
    sweeps = 2 * ITERS
    before, raised, displacement = pl.pallas_call(
        kernel,
        out_shape=(
            jax.ShapeDtypeStruct(state.shape, F32),
            jax.ShapeDtypeStruct(kappa.shape, F32),
            jax.ShapeDtypeStruct((EBD, EB), F32),
        ),
        in_specs=[hbm] * 11,
        out_specs=(hbm, vmem, vmem),
        scratch_shapes=[
            pltpu.SMEM((NV, NV), F32),
            pltpu.SMEM((NV,), F32),
            pltpu.SMEM((NV,), F32),
            pltpu.VMEM((CY, EB), F32),
            pltpu.SMEM((1, EBD), jnp.int32),
            pltpu.VMEM((1, CX), jnp.int32),
            pltpu.VMEM((1, CX), jnp.int32),
            pltpu.VMEM((2, NV, NZL + 2, CX, CY), F32),
            pltpu.VMEM((NZL, CX, CY), F32),
            pltpu.VMEM((NZL + 2, CXE, CY), F32),
            pltpu.VMEM((NZL, CX, CY), F32),
            pltpu.VMEM((EBD, EB, EB), F32),
            pltpu.VMEM((EBD, EB, EB), F32),
            pltpu.VMEM((EBD, 2 * EB, 2 * EB), BF16),
            pltpu.VMEM((2, NV + 1, NZL, CY), F32),
            pltpu.VMEM((sweeps, 2, NV + 1, NZL, CY), F32),
            pltpu.VMEM((CX, CY), F32),
            pltpu.VMEM((sweeps, 2, CX, CY), F32),
            pltpu.VMEM((CX, CY), F32),
            pltpu.VMEM((sweeps, NV, CX, CY), F32),
            pltpu.VMEM((CXE, CY), F32),
            pltpu.VMEM((CAP * NFX, CY), F32),
            pltpu.VMEM((CAP * NFX, CY), F32),
            pltpu.VMEM((5, CAP * NFX, CY), F32),
            pltpu.VMEM((ITERS + 1, FACES, CY), F32),
            pltpu.VMEM((5, FACES, CY), F32),
            pltpu.VMEM((FACES, CY), F32),
            pltpu.VMEM((ITERS, CAP * NFX, CY), F32),
            pltpu.VMEM((EBD, FACES), F32),
            pltpu.VMEM((FACES, EBD), F32),
            pltpu.VMEM((CAP * NFX, CX), F32),
            pltpu.VMEM((CX, CAP * NFX), F32),
            pltpu.VMEM((EBD, EB), F32),
            pltpu.VMEM((EBD, EB), F32),
            pltpu.VMEM((EBD, EB), F32),
            pltpu.VMEM((EBD, EB), F32),
            pltpu.VMEM((ITERS + 1, 3, CXE, CY), F32),
            pltpu.VMEM((2, CXE, CY), F32),
            pltpu.VMEM((2, CX, CY), F32),
            pltpu.VMEM((NZL + 2, CXE, CY), F32),
            pltpu.VMEM((CX, CY), F32),
            pltpu.VMEM((AROUND, FACES, NFX * EBD), BF16),
            pltpu.VMEM((AROUND, FACES, CY), F32),
            pltpu.VMEM((FACES, CY), F32),
            pltpu.VMEM((EBD, EB), F32),
            pltpu.VMEM((ITERS - 1, NFX * EBD, EB), F32),
            dma((11,)),
            dma((sweeps, 5)),
            dma((sweeps, 5)),
            dma((ITERS + 1,)),
            dma((ITERS + 1,)),
            dma((ITERS,)),
            dma((ITERS,)),
            dma((NFY,)),
            dma((2,)),
            dma((ITERS + 1, 8)),
            dma((ITERS + 1, 8)),
            dma((ITERS,)),
            dma((ITERS,)),
            dma,
            dma,
            dma((ITERS - 1,)),
            dma((ITERS - 1,)),
        ],
        compiler_params=pltpu.CompilerParams(
            collective_id=0, has_side_effects=True, vmem_limit_bytes=60 * 1024 * 1024
        ),
    )(
        state, kappa, mix, press_weight, source_weight, interp, block_inverse, coupling, front_order,
        face_owner.reshape(1, -1), face_slot.reshape(1, -1),
    )
    return pl.pallas_call(
        last_add,
        out_shape=(
            jax.ShapeDtypeStruct(state.shape, F32),
            jax.ShapeDtypeStruct((EBD, EB), F32),
        ),
        in_specs=[hbm] * 4,
        out_specs=(hbm, hbm),
        scratch_shapes=[
            pltpu.VMEM((NV, NZL, CX, CY), F32),
            pltpu.VMEM((NZL, CX, CY), F32),
            pltpu.VMEM((EBD, EB), F32),
            pltpu.SMEM((NV,), F32),
            dma((NV + 3,)),
            dma((NV + 1,)),
        ],
        compiler_params=pltpu.CompilerParams(vmem_limit_bytes=60 * 1024 * 1024),
    )(before, raised, source_weight, displacement)


def solution(mesh):
    return jax.shard_map(
        on_device,
        mesh=mesh,
        in_specs=(
            P(None, "fz", "fx", "fy"),
            P("fz", "fx", "fy"),
            P(),
            P(),
            P(),
            P(),
            P("fx", None, None),
            P("fx", None, None),
            P("fx", None),
            P(("fx", "fy"), None),
            P(("fx", "fy")),
        ),
        out_specs=(P(None, "fz", "fx", "fy"), P("fx", None)),
        check_vma=False,
    )
```

```python
import jax
import jax.numpy as jnp
from jax import lax
from jax.experimental import pallas as pl
from jax.experimental.pallas import tpu as pltpu
from jax.sharding import PartitionSpec as P

ITERS = 3
DIFFUSION = 0.16
HIGHEST = lax.Precision.HIGHEST
MESH = pl.DeviceIdType.MESH
F32 = jnp.float32
BF16 = jnp.bfloat16

NV, NZL, CX, CY = 5, 8, 32, 128
NZ = 16
NFX, NFY = 32, 4
RING_Z, RING_Y = 8, 4
EB, EBD, CAP = 128, 16, 2
PAIRS = EBD // 2
FACES = NFX * NFY * CAP
PAD = 8
CXE = CX + 2 * PAD
NT = (((1,), (1,)), ((), ()))
FAR_Y = (2, 1, 3, 0)
AROUND = 11


def far_first(step, ring):
    return ring // 2 + (1 - 2 * (step % 2)) * ((step + 1) // 2)


def split(values):
    high = values.astype(BF16)
    return high, (values - high.astype(F32)).astype(BF16)


def pick(selector, values):
    high, low = split(values)
    return jnp.dot(selector, high, preferred_element_type=F32) + jnp.dot(selector, low, preferred_element_type=F32)


def kernel(
    state_in, kappa_in, mix_in, press_in, source_in, interp_in, inverse_in, coupling_in, order_in, owner_in, slot_in,
    state_out, raised_out, disp_out,
    mix, press_weight, source_weight, interp, order, owner, slot,
    S, K, KX, KE, BI, CO, R, RO, RN, XS, XR, YS, YR, YK, ZR, KZ, SL, SF, CS, RF, RC, SD, RD, FP, FPT, AM, AT, FR, XV, DV, DR,
    WN, LP, LE, QB, PB, G, GW, IN, XO, XA,
    load_sem, hsend, hrecv, fsend, frecv, dsend, drecv, osend, orecv, wsend, wrecv, rsend, rrecv, csend, crecv, xsend, xrecv,
):
    ix, iy, iz = lax.axis_index("fx"), lax.axis_index("fy"), lax.axis_index("fz")
    ring_z, ring_y = ix // RING_Y, ix % RING_Y
    on_wall = iz == 0
    off_wall = iz == 1
    home = (ring_y + ring_z) % NFY
    is_solver = iy == home
    not_solver = jnp.logical_not(is_solver)
    turned_y = {d: (ring_y + d) % RING_Y for d in FAR_Y}
    turned_x = {d: (iy + d) % NFY for d in FAR_Y}
    answer_x = ((iy + 2 - iz) % NFY, (iy + 3 * iz) % NFY)

    def row_base(step):
        return ((ring_z + far_first(step, RING_Z)) % RING_Z) * RING_Y

    def homes(z):
        return {d: (turned_y[d] + z) % NFY for d in FAR_Y}

    def owners_at(step):
        z = (ring_z + far_first(step, RING_Z)) % RING_Z
        return [(z * RING_Y + turned_y[d], home_y) for d, home_y in homes(z).items()]

    near_owners = [(ring_z * RING_Y + turned_y[d], home_y) for d, home_y in homes(ring_z).items()][:3]

    def signal(barrier, device):
        pl.semaphore_signal(barrier, inc=1, device_id=device, device_id_type=MESH)

    loads = [
        pltpu.make_async_copy(source, target, load_sem.at[n])
        for n, (source, target) in enumerate(
            (
                (owner_in, owner),
                (slot_in, slot),
                (order_in, order),
                (kappa_in, K),
                (state_in, S.at[0, :, pl.ds(1, NZL)]),
                (inverse_in, BI),
                (coupling_in, CO),
                (interp_in, interp),
                (mix_in, mix),
                (press_in, press_weight),
                (source_in, source_weight),
            )
        )
    ]
    for load in loads:
        load.start()

    barrier = pltpu.get_barrier_semaphore()
    has_left, has_right, has_front, has_back = ix > 0, ix < NFX - 1, iy > 0, iy < NFY - 1
    sides = (
        (has_left, (ix - 1, iy, iz)),
        (has_right, (ix + 1, iy, iz)),
        (has_front, (ix, iy - 1, iz)),
        (has_back, (ix, iy + 1, iz)),
    )
    corners = (
        (jnp.logical_and(has_left, has_front), (ix - 1, iy - 1, iz)),
        (jnp.logical_and(has_left, has_back), (ix - 1, iy + 1, iz)),
        (jnp.logical_and(has_right, has_front), (ix + 1, iy - 1, iz)),
        (jnp.logical_and(has_right, has_back), (ix + 1, iy + 1, iz)),
    )
    other_core = (ix, iy, 1 - iz)

    @pl.when(is_solver)
    def _():
        def greet(step, carry):
            base = row_base(step)
            for dy in FAR_Y:
                for dx in FAR_Y:
                    signal(barrier, (base + turned_y[dy], turned_x[dx], 0))
            return carry

        lax.fori_loop(0, RING_Z - 1, greet, 0)
        for dy in FAR_Y:
            for dx in FAR_Y:
                if dy or dx:
                    signal(barrier, (ring_z * RING_Y + turned_y[dy], turned_x[dx], 0))

        @pl.when(off_wall)
        def _():
            signal(barrier, (ix, iy, 0))

        def greet_solvers(step, carry):
            for to, home_y in owners_at(step):
                signal(barrier, (to, home_y, iz))
            return carry

        lax.fori_loop(0, RING_Z - 1, greet_solvers, 0)
        for to, home_y in near_owners:
            signal(barrier, (to, home_y, iz))

    @pl.when(on_wall)
    def _():
        def greet(step, carry):
            for to, home_y in owners_at(step):
                signal(barrier, (to, home_y, (iy + home_y) % 2))
            return carry

        lax.fori_loop(0, RING_Z - 1, greet, 0)
        for to, home_y in near_owners:
            signal(barrier, (to, home_y, (iy + home_y) % 2))

        @pl.when(not_solver)
        def _():
            signal(barrier, (ix, home, (iy + home) % 2))

    @pl.when(not_solver)
    def _():
        signal(barrier, (ix, home, iz))

    for ref in (XR, YR, WN):
        ref[...] = jnp.zeros_like(ref)

    signal(barrier, other_core)
    solver_count = is_solver.astype(jnp.int32)
    wall_count = on_wall.astype(jnp.int32)
    expected = 1 + wall_count * (2 * NFX - solver_count) + solver_count * (2 * NFX - wall_count + NFY - 1 + NFX - 1)
    for present, device in sides + corners:
        expected = expected + present.astype(jnp.int32)

        @pl.when(present)
        def _():
            signal(barrier, device)

    zero_plane = jnp.zeros((NV, CX, CY), F32)
    for buffer in range(2):
        S[buffer, :, 0] = zero_plane
        S[buffer, :, NZL + 1] = zero_plane

    for load in loads[:3]:
        load.wait()
    rows = lax.broadcasted_iota(jnp.int32, (CAP * NFX, CX), 0)
    named = (owner[...] == rows // CAP).astype(F32)
    earlier = (
        lax.broadcasted_iota(jnp.int32, (CX, CX), 0) < lax.broadcasted_iota(jnp.int32, (CX, CX), 1)
    ).astype(BF16)
    rank = jnp.dot(named.astype(BF16), earlier, preferred_element_type=F32)
    chosen = jnp.where(rank == (rows % CAP).astype(F32), named, 0.0)
    AM[...] = chosen
    unit = (lax.broadcasted_iota(jnp.int32, (CX, CX), 0) == lax.broadcasted_iota(jnp.int32, (CX, CX), 1)).astype(F32)
    AT[...] = lax.dot_general(unit, chosen, NT, preferred_element_type=F32)
    slot_rows = jnp.sum(chosen * (slot[...] + 1).astype(F32), axis=1, keepdims=True)
    SL[...] = jnp.broadcast_to(slot_rows, (CAP * NFX, CY))
    target_of = jnp.sum(unit * (EBD * owner[...] + slot[...] + 1).astype(F32), axis=1, keepdims=True)
    WN[ITERS, 1, PAD : PAD + CX] = jnp.broadcast_to(target_of, (CX, CY))
    block_rows = lax.broadcasted_iota(jnp.int32, (EBD, EB), 0)
    block_lanes = lax.broadcasted_iota(jnp.int32, (EBD, EB), 1)
    placed = jnp.zeros((EBD, EB), F32)
    for k in range(EBD):
        placed = jnp.where(jnp.logical_and(block_rows == k, block_lanes == order[0, k]), 1.0, placed)

    lane = lax.broadcasted_iota(jnp.int32, (CX, CY), 1)
    row = lax.broadcasted_iota(jnp.int32, (CX, CY), 0)
    for load in loads[3:5]:
        load.wait()

    pair = lane // 2

    def put_ends(ends, centre, at):
        return jnp.where(pair == at, pltpu.roll(centre, 2 * at + 1, 1), ends)

    def take_ends(n):
        return jnp.where(lane % 2 == 0, pltpu.roll(YR[n, 1], CY - 1, 1), pltpu.roll(YR[n, 0], 1, 1))

    def kappa_faces(z, ends):
        coeff = DIFFUSION * K[z]
        KX[z + 1, PAD : PAD + CX] = coeff
        XS[0, NV, pl.ds(z, 1), :] = coeff[0:1]
        XS[1, NV, pl.ds(z, 1), :] = coeff[CX - 1 : CX]
        return put_ends(ends, coeff, NV * NZL + z)

    YK[...] = lax.fori_loop(0, NZL, kappa_faces, jnp.zeros((CX, CY), F32))

    def pack(src):
        def plane(z, ends):
            for c in range(NV):
                centre = src[c, z + 1]
                XS[0, c, pl.ds(z, 1), :] = centre[0:1]
                XS[1, c, pl.ds(z, 1), :] = centre[CX - 1 : CX]
                ends = put_ends(ends, centre, c * NZL + z)
            return ends

        YS[...] = lax.fori_loop(0, NZL, plane, YK[...])

    edge = NZL - (NZL - 1) * iz

    def halo_copies(n, src):
        def remote(source, target, at, there, device):
            return pltpu.make_async_remote_copy(
                source, target, hsend.at[n, at], hrecv.at[n, there], device_id=device, device_id_type=MESH
            )

        (_, left), (_, right), (_, front), (_, back) = sides
        always = iz >= 0
        plane = src.at[:, edge]
        sends = (
            (has_left, remote(XS.at[0], XR.at[n, 1], 0, 1, left)),
            (has_right, remote(XS.at[1], XR.at[n, 0], 1, 0, right)),
            (has_front, remote(YS, YR.at[n, 1], 2, 3, front)),
            (has_back, remote(YS, YR.at[n, 0], 3, 2, back)),
            (always, remote(plane, ZR.at[n], 4, 4, other_core)),
        )
        waits = (
            (has_left, remote(XS.at[0], XR.at[n, 0], 0, 0, left)),
            (has_right, remote(XS.at[1], XR.at[n, 1], 1, 1, right)),
            (has_front, remote(YS, YR.at[n, 0], 2, 2, front)),
            (has_back, remote(YS, YR.at[n, 1], 3, 3, back)),
            (always, remote(plane, ZR.at[n], 4, 4, other_core)),
        )
        return sends, waits

    def each(copies, action):
        for present, copy in copies:

            @pl.when(present)
            def _():
                action(copy)

    def start_halo(n, src):
        each(halo_copies(n, src)[0], lambda copy: copy.start())

    def finish_halo(n, src):
        _, waits = halo_copies(n, src)
        each(waits, lambda copy: copy.wait_recv())
        src[:, (NZL + 1) * (1 - iz)] = ZR[n]

    def sweep(n, src, dst, first=0, end=NZL):
        outer = take_ends(n)

        def plane(z, carry):
            coeff = KX[z + 1, PAD : PAD + CX]
            centres = [src[c, z + 1] for c in range(NV)]
            for c in range(NV):
                centre = centres[c]
                at = c * NZL + z
                beside = src[c, z] + src[c, z + 2]
                beside += jnp.where(row == 0, XR[n, 0, c, pl.ds(z, 1), :], pltpu.roll(centre, 1, 0))
                beside += jnp.where(row == CX - 1, XR[n, 1, c, pl.ds(z, 1), :], pltpu.roll(centre, CX - 1, 0))
                ends = pltpu.roll(outer, CY - 1 - 2 * at, 1)
                beside += jnp.where(lane == 0, ends, pltpu.roll(centre, 1, 1))
                beside += jnp.where(lane == CY - 1, ends, pltpu.roll(centre, CY - 1, 1))
                total = centre + coeff * (beside - 6.0 * centre)
                for d in range(NV):
                    total += mix[c, d] * centres[d]
                dst[c, z + 1] = total
            return carry

        lax.fori_loop(first, end, plane, 0)
        if end == NZL:
            each(halo_copies(n, src)[0], lambda copy: copy.wait_send())

    kappa_plane = pltpu.make_async_remote_copy(
        KX.at[edge], KZ, osend.at[0], orecv.at[0], device_id=other_core, device_id_type=MESH
    )

    def send_to_solvers(rows_of, target, sent, heard):
        def send(to, y, core):
            pltpu.make_async_remote_copy(
                rows_of(to), target, sent, heard, device_id=(to, y, core), device_id_type=MESH
            ).start()

        def group(step, carry):
            for to, home_y in owners_at(step):
                for core in range(2):
                    send(to, home_y, core)
            return carry

        @pl.when(on_wall)
        def _():
            lax.fori_loop(0, RING_Z - 1, group, 0)
            for to, home_y in near_owners:
                for core in range(2):
                    send(to, home_y, core)
            send(ix, home, 1)

            @pl.when(not_solver)
            def _():
                send(ix, home, 0)

            @pl.when(is_solver)
            def _():
                pltpu.make_async_copy(rows_of(ix), target, heard).start()

    own_rows = pl.ds(CAP * (ix * NFY + iy), CAP)

    def send_rows(turn, rows_out):
        send_to_solvers(
            lambda to: rows_out.at[pl.ds(CAP * to, CAP)], RF.at[turn, own_rows], fsend.at[turn], frecv.at[turn]
        )

    def send_pressure(turn):
        @pl.when(on_wall)
        def _():
            SF[...] = pick(AM[...].astype(BF16), PB[...])

        send_rows(turn, SF)

    def sent_to_solvers(turn):
        @pl.when(on_wall)
        def _():
            @pl.when(is_solver)
            def _():
                rest = RF.at[turn, pl.ds(0, CAP * (2 * NFX - 1))]
                pltpu.make_async_copy(rest, rest, fsend.at[turn]).wait()

            @pl.when(not_solver)
            def _():
                rest = RF.at[turn, pl.ds(0, CAP * 2 * NFX)]
                pltpu.make_async_copy(rest, rest, fsend.at[turn]).wait()

    def heard_from_faces(turn):
        whole = RF.at[turn]
        pltpu.make_async_copy(whole, whole, frecv.at[turn]).wait()

    def send_to_faces(turn):
        target = RD.at[turn, pl.ds(CAP * ix, CAP)]

        def send(to_x, to_y):
            pltpu.make_async_remote_copy(
                SD.at[pl.ds(CAP * (to_x * NFY + to_y), CAP)], target, dsend.at[turn], drecv.at[turn],
                device_id=(to_x, to_y, 0), device_id_type=MESH,
            ).start()

        def group(step, carry):
            base = row_base(step)
            for dy in FAR_Y:
                for x in answer_x:
                    send(base + turned_y[dy], x)
            return carry

        lax.fori_loop(0, RING_Z - 1, group, 0)
        for dy in FAR_Y[:3]:
            for x in answer_x:
                send(ring_z * RING_Y + turned_y[dy], x)
        send(ix, answer_x[0])

        @pl.when(off_wall)
        def _():
            send(ix, answer_x[1])

        @pl.when(on_wall)
        def _():
            pltpu.make_async_copy(SD.at[pl.ds(CAP * (ix * NFY + iy), CAP)], target, drecv.at[turn]).start()

    def sent_to_faces(turn):
        @pl.when(on_wall)
        def _():
            rest = RF.at[turn, pl.ds(0, CAP * (2 * NFX - 1))]
            pltpu.make_async_copy(rest, rest, dsend.at[turn]).wait()

        @pl.when(off_wall)
        def _():
            rest = RF.at[turn, pl.ds(0, CAP * 2 * NFX)]
            pltpu.make_async_copy(rest, rest, dsend.at[turn]).wait()

    for load in loads[5:]:
        load.wait()

    @pl.when(is_solver)
    def _():
        def parts(k):
            block = order[0, k]
            inverse = BI[block]
            force_part = lax.dot_general(interp[...], inverse, NT, precision=HIGHEST, preferred_element_type=F32)
            chain = jnp.dot(inverse, CO[block], precision=HIGHEST, preferred_element_type=F32)
            return force_part, -chain.T

        def both_parts(matrix):
            high, low = split(matrix)
            return jnp.concatenate([high, low], axis=1)

        def products(m, carry):
            force, chain = parts(2 * m)
            next_force, next_chain = parts(2 * m + 1)
            passed = jnp.dot(force, next_chain, precision=HIGHEST, preferred_element_type=F32)
            leap = jnp.dot(chain, next_chain, precision=HIGHEST, preferred_element_type=F32)
            R[m] = both_parts(jnp.concatenate([force, chain], axis=0))
            RO[m] = both_parts(jnp.concatenate([next_force, passed], axis=0))
            RN[m] = both_parts(leap)
            return carry

        lax.fori_loop(0, PAIRS, products, 0)

    numbers = range(NV)
    source = [source_weight[c] for c in numbers]
    once = [source[c] + sum(mix[c, d] * source[d] for d in numbers) for c in numbers]
    twice = [once[c] + sum(mix[c, d] * once[d] for d in numbers) for c in numbers]
    press_source = sum(press_weight[c] * source[c] for c in numbers)
    press_once = sum(press_weight[c] * once[c] for c in numbers)
    press_twice = sum(press_weight[c] * twice[c] for c in numbers)

    inner = slice(PAD, PAD + CX)

    def wall_copies(it):
        def remote(n, opposite, source_row, side, target_row, count, device):
            copy = lambda here, there: pltpu.make_async_remote_copy(
                WN.at[it, 1, pl.ds(source_row, count)], WN.at[it, side, pl.ds(target_row, count)],
                wsend.at[it, here], wrecv.at[it, there], device_id=device, device_id_type=MESH,
            )
            return copy(n, opposite), copy(n, n)

        low, high = PAD, PAD + CX - 8
        (_, left), (_, right), (_, front), (_, back) = sides
        (lf, left_front), (lb, left_back), (rf, right_front), (rb, right_back) = corners
        return (
            (has_left, remote(0, 1, low, 1, PAD + CX, 8, left)),
            (has_right, remote(1, 0, high, 1, 0, 8, right)),
            (has_front, remote(2, 3, PAD, 2, PAD, CX, front)),
            (has_back, remote(3, 2, PAD, 0, PAD, CX, back)),
            (lf, remote(4, 7, low, 2, PAD + CX, 8, left_front)),
            (lb, remote(5, 6, low, 0, PAD + CX, 8, left_back)),
            (rf, remote(6, 5, high, 2, 0, 8, right_front)),
            (rb, remote(7, 4, high, 0, 0, 8, right_back)),
        )

    def tell_faces():
        targets = (
            [pltpu.roll(WN[ITERS, 1], (CXE - d) % CXE, 0)[inner] for d in range(-2, 3)]
            + [pltpu.roll(WN[ITERS, 0], (CXE - d) % CXE, 0)[inner] for d in range(-1, 2)]
            + [pltpu.roll(WN[ITERS, 2], (CXE - d) % CXE, 0)[inner] for d in range(-1, 2)]
        )
        facts = targets + [
            jnp.broadcast_to(KE[0, :, CY - 1 : CY], (CX, CY)), jnp.broadcast_to(KE[0, :, 0:1], (CX, CY)),
        ]
        table = jnp.zeros((CX, CY), F32)
        for n, fact in enumerate(facts):
            table = jnp.where(lane == n, fact, table)
        wall_coeff = KX[1]
        selector = AM[...].astype(BF16)
        CS[0] = pick(selector, table)
        for n, d in enumerate((-1, 0, 1)):
            CS[n + 1] = pick(selector, pltpu.roll(wall_coeff, (CXE - d) % CXE, 0)[inner])
        CS[4] = pick(selector, KX[2, inner])

    def send_facts():
        send_to_solvers(lambda to: CS.at[:, pl.ds(CAP * to, CAP)], RC.at[:, own_rows], csend, crecv)

    around_wall = wall_copies(ITERS)
    pack(S.at[0])
    pl.semaphore_wait(barrier, expected)
    start_halo(0, S.at[0])

    @pl.when(on_wall)
    def _():
        each(around_wall, lambda pair: pair[0].start())

    kappa_plane.start()
    send_rows(ITERS, SL)
    finish_halo(0, S.at[0])
    sweep(0, S.at[0], S.at[1])
    pack(S.at[1])
    start_halo(1, S.at[1])

    kappa_plane.wait()
    KX[(NZL + 1) * (1 - iz)] = KZ[...]
    KX[(NZL + 1) * iz] = jnp.zeros((CXE, CY), F32)
    tile_row = lax.broadcasted_iota(jnp.int32, (PAD, CY), 0)

    ends = take_ends(0)

    def kappa_edges(z, carry):
        KX[z + 1, 0:PAD] = jnp.where(tile_row == PAD - 1, XR[0, 0, NV, pl.ds(z, 1), :], 0.0)
        KX[z + 1, PAD + CX : CXE] = jnp.where(tile_row == 0, XR[0, 1, NV, pl.ds(z, 1), :], 0.0)
        at = 2 * (NV * NZL + z)
        front = pltpu.roll(ends, CY - 2 - at, 1)
        back = pltpu.roll(ends, CY - at, 1)
        KE[z] = jnp.where(lane >= CY // 2, front, back)
        return carry

    lax.fori_loop(0, NZL, kappa_edges, 0)

    @pl.when(on_wall)
    def _():
        each(around_wall, lambda pair: pair[1].wait_recv())
        tell_faces()
        each(around_wall, lambda pair: pair[0].wait_send())

    send_facts()

    def wall_base():
        @pl.when(on_wall)
        def _():
            pressure = press_weight[0] * S[0, 0, 1]
            for c in range(1, NV):
                pressure += press_weight[c] * S[0, c, 1]
            PB[...] = pressure

    finish_halo(1, S.at[1])
    sweep(1, S.at[1], S.at[0], 0, 1)
    wall_base()
    send_pressure(0)
    sweep(1, S.at[1], S.at[0], 1, NZL)
    sent_to_solvers(ITERS)

    @pl.when(is_solver)
    def _():
        heard_from_faces(ITERS)
        face_lanes = lax.broadcasted_iota(jnp.int32, (FACES, EB), 1) + 1
        slot_of = (RF[ITERS] == face_lanes.astype(F32)).astype(F32)
        FP[...] = lax.dot_general(placed, slot_of, NT, preferred_element_type=F32)
        FPT[...] = lax.dot_general(slot_of, placed, NT, preferred_element_type=F32)

    def times(row_in, matrix):
        width = row_in.shape[1]
        high = row_in.astype(BF16).astype(F32)
        at = lax.broadcasted_iota(jnp.int32, (8, width), 0)
        left = jnp.where(at == 0, high, jnp.where(at == 1, row_in - high, 0.0)).astype(BF16)
        result = jnp.dot(left, matrix, preferred_element_type=F32)
        summed = result[:, :EB] + result[:, EB:]
        return summed[0:1] + summed[1:2]

    def solve():
        force = [FR[pl.ds(k, 1), :] for k in range(EBD)]
        odd = [times(jnp.concatenate([force[2 * m + 1], force[2 * m]], axis=1), RO[m]) for m in range(PAIRS)]
        for m in range(PAIRS):
            if m:
                odd[m] += times(odd[m - 1], RN[m])
            XV[pl.ds(2 * m + 1, 1), :] = odd[m]
            previous = odd[m - 1] if m else jnp.zeros((1, EB), F32)
            XV[pl.ds(2 * m, 1), :] = times(jnp.concatenate([force[2 * m], previous], axis=1), R[m])

    lane_e = lax.broadcasted_iota(jnp.int32, (CXE, CY), 1)

    def spread(it):
        centre = WN[it, 1]
        beyond = jnp.where(lane_e >= CY // 2, WN[it, 0], WN[it, 2])
        up, down = pltpu.roll(centre, 1, 1), pltpu.roll(centre, CY - 1, 1)
        out_up, out_down = pltpu.roll(beyond, 1, 1), pltpu.roll(beyond, CY - 1, 1)
        lap = pltpu.roll(centre, 1, 0) + pltpu.roll(centre, CXE - 1, 0) - 4.0 * centre
        lap += jnp.where(lane_e == 0, out_up, up) + jnp.where(lane_e == CY - 1, out_down, down)
        lap_e = pltpu.roll(beyond, 1, 0) + pltpu.roll(beyond, CXE - 1, 0) - 4.0 * beyond
        lap_e += jnp.where(lane_e >= CY // 2, out_up + down, out_down + up)
        LP[0], LP[1] = lap, centre
        LE[0], LE[1] = lap_e[inner], beyond[inner]

    def ring_sum(wide, edge_columns, below, above, coeff):
        own = wide[inner]
        total = pltpu.roll(wide, 1, 0)[inner] + pltpu.roll(wide, CXE - 1, 0)[inner] + below + above - 6.0 * own
        total += jnp.where(lane == 0, pltpu.roll(edge_columns, 1, 1), pltpu.roll(own, 1, 1))
        total += jnp.where(lane == CY - 1, pltpu.roll(edge_columns, CY - 1, 1), pltpu.roll(own, CY - 1, 1))
        return coeff * total

    first_jump = (NZ - 1.0) / NZ - 2.0

    def profile(plane):
        height = iz * NZL + plane - 1
        return 1.0 - height.astype(F32) / NZ, jnp.where(height == 0, first_jump, 0.0)

    def update():
        def first(plane, carry):
            share, jump = profile(plane)
            QB[plane] = KX[plane] * (share * LP[0] + jump * LP[1])
            return carry

        lax.fori_loop(0, NZL + 2, first, 0)

        def second(z, carry):
            share, jump = profile(z + 1)
            edges = KE[z] * (share * LE[0] + jump * LE[1])
            wide = QB[z + 1]
            bend = ring_sum(wide, edges, QB[z, inner], QB[z + 2, inner], KX[z + 1, inner])
            raised, slope = share * LP[1, inner], wide[inner]
            for c in range(NV):
                S[0, c, z + 1] += twice[c] * raised + 2.0 * once[c] * slope + source[c] * bend
            return carry

        lax.fori_loop(0, NZL, second, 0)

    def sent_facts():
        @pl.when(on_wall)
        def _():
            @pl.when(is_solver)
            def _():
                rest = RC.at[:, pl.ds(0, CAP * (2 * NFX - 1))]
                pltpu.make_async_copy(rest, rest, csend).wait()

            @pl.when(not_solver)
            def _():
                rest = RC.at[:, pl.ds(0, CAP * 2 * NFX)]
                pltpu.make_async_copy(rest, rest, csend).wait()

    def hear_facts():
        pltpu.make_async_copy(RC, RC, crecv).wait()
        names = lax.broadcasted_iota(jnp.int32, (FACES, NFX * EBD), 1) + 1
        names = names.astype(F32)
        for m in range(AROUND):
            G[m] = jnp.where(names == RC[0, :, m : m + 1], 1.0, 0.0).astype(BF16)

    def tell_solvers(it, facing):
        if it:
            rest = XA.at[0, pl.ds(0, (NFX - 1) * EBD)]
            pltpu.make_async_copy(rest, rest, xsend.at[it - 1]).wait()
        own = pick(placed.T[:EBD].astype(BF16), facing)
        XO[...] = own
        XA[it, pl.ds(EBD * ix, EBD)] = own

        def send(to, y):
            pltpu.make_async_remote_copy(
                XO, XA.at[it, pl.ds(EBD * ix, EBD)], xsend.at[it], xrecv.at[it],
                device_id=(to, y, iz), device_id_type=MESH,
            ).start()

        def group(step, carry):
            for to, home_y in owners_at(step):
                send(to, home_y)
            return carry

        lax.fori_loop(0, RING_Z - 1, group, 0)
        for to, home_y in near_owners:
            send(to, home_y)

    def respond(it):
        rest = XA.at[it, pl.ds(0, (NFX - 1) * EBD)]
        pltpu.make_async_copy(rest, rest, xrecv.at[it]).wait()
        high, low = split(XA[it])
        both = jnp.concatenate([high, low], axis=1)
        for m in range(AROUND):
            found = jnp.dot(G[m], both, preferred_element_type=F32)
            GW[m] = found[:, :CY] + found[:, CY:]

        def chunk(n, carry):
            at = pl.ds(pl.multiple_of(n * CX, CX), CX)
            centre = {d: GW[d + 2, at] for d in range(-2, 3)}
            beyond = {d: jnp.where(lane >= CY // 2, GW[d + 6, at], GW[d + 9, at]) for d in range(-1, 2)}
            coeff = {d: RC[d + 2, at] for d in range(-1, 2)}

            def wide_sum(d):
                total = centre[d - 1] + centre[d + 1] - 4.0 * centre[d]
                total += jnp.where(lane == 0, pltpu.roll(beyond[d], 1, 1), pltpu.roll(centre[d], 1, 1))
                return total + jnp.where(
                    lane == CY - 1, pltpu.roll(beyond[d], CY - 1, 1), pltpu.roll(centre[d], CY - 1, 1)
                )

            sums = {d: wide_sum(d) for d in range(-1, 2)}
            slopes = {d: coeff[d] * (sums[d] + first_jump * centre[d]) for d in range(-1, 2)}
            above = RC[4, at] * ((NZ - 1.0) / NZ * sums[0])
            facts = RC[0, at]
            edge_coeff = jnp.where(lane >= CY // 2, facts[:, AROUND : AROUND + 1], facts[:, AROUND + 1 : AROUND + 2])
            edge_sum = beyond[-1] + beyond[1] - 4.0 * beyond[0]
            edge_sum += jnp.where(
                lane >= CY // 2,
                pltpu.roll(beyond[0], 1, 1) + pltpu.roll(centre[0], CY - 1, 1),
                pltpu.roll(beyond[0], CY - 1, 1) + pltpu.roll(centre[0], 1, 1),
            )
            edges = edge_coeff * (edge_sum + first_jump * beyond[0])
            bend = slopes[-1] + slopes[1] + above - 6.0 * slopes[0]
            bend += jnp.where(lane == 0, pltpu.roll(edges, 1, 1), pltpu.roll(slopes[0], 1, 1))
            bend += jnp.where(lane == CY - 1, pltpu.roll(edges, CY - 1, 1), pltpu.roll(slopes[0], CY - 1, 1))
            IN[at] = press_twice * centre[0] + 2.0 * press_once * slopes[0] + press_source * coeff[0] * bend
            return carry

        lax.fori_loop(0, FACES // CX, chunk, 0)

    def answer(it):
        heard_from_faces(it)
        if it:
            sent_to_faces(it - 1)
        rows_in = RF[it] + IN[...] if it else RF[it]
        FR[...] = pick(FP[...].astype(BF16), rows_in)
        solve()
        facing = lax.dot_general(XV[...], interp[...], NT, precision=HIGHEST, preferred_element_type=F32)
        if 0 < it < ITERS - 1:
            tell_solvers(it, facing)
        SD[...] = pick(FPT[...].astype(BF16), facing)
        send_to_faces(it)
        if it == 0:
            tell_solvers(it, facing)

    def hear_wall(it):
        whole = RD.at[it]
        pltpu.make_async_copy(whole, whole, drecv.at[it]).wait()
        WN[it, 1, inner] = pick(AT[...].astype(BF16), RD[it])

    def relay(it, part):
        return pltpu.make_async_remote_copy(
            part, part, rsend.at[it], rrecv.at[it], device_id=other_core, device_id_type=MESH
        )

    for it in range(ITERS - 1):
        n = 2 * it + 2
        pack(S.at[0])
        start_halo(n, S.at[0])
        if it:

            @pl.when(is_solver)
            def _():
                answer(it)

        finish_halo(n, S.at[0])
        sweep(n, S.at[0], S.at[1])
        pack(S.at[1])
        start_halo(n + 1, S.at[1])
        if it == 0:

            @pl.when(is_solver)
            def _():
                answer(it)

        finish_halo(n + 1, S.at[1])
        sweep(n + 1, S.at[1], S.at[0], 0, 1)
        wall_base()
        sent_to_solvers(it)
        send_pressure(it + 1)
        sweep(n + 1, S.at[1], S.at[0], 1, NZL)
        if it == 0:

            @pl.when(is_solver)
            def _():
                hear_facts()

        copies = wall_copies(it)

        @pl.when(on_wall)
        def _():
            hear_wall(it)
            each(copies, lambda pair: pair[0].start())

        @pl.when(is_solver)
        def _():
            respond(it)

        beside_wall = relay(it, WN.at[it])

        @pl.when(on_wall)
        def _():
            each(copies, lambda pair: pair[1].wait_recv())
            beside_wall.start()

        @pl.when(off_wall)
        def _():
            beside_wall.wait_recv()

        spread(it)
        update()

        @pl.when(on_wall)
        def _():
            each(copies, lambda pair: pair[0].wait_send())
            beside_wall.wait_send()

    sent_facts()

    last = ITERS - 1
    out = pltpu.make_async_copy(S.at[0, :, pl.ds(1, NZL)], state_out, load_sem.at[0])
    out.start()

    def disp_copy(t):
        return pltpu.make_async_remote_copy(
            DV, DR, osend.at[t], orecv.at[1], device_id=(ix, (iy + t) % NFY, iz), device_id_type=MESH
        )

    @pl.when(is_solver)
    def _():
        answer(last)
        back = lax.dot_general(placed, XV[...], (((0,), (0,)), ((), ())), precision=HIGHEST, preferred_element_type=F32)
        DV[...] = back[:EBD]
        for t in range(1, NFY):
            disp_copy(t).start()
        disp_out[...] = back[:EBD]

    beside_wall = relay(last, WN.at[last, 1, pl.ds(PAD, CX)])

    @pl.when(on_wall)
    def _():
        sent_to_solvers(last)
        hear_wall(last)
        beside_wall.start()

    @pl.when(off_wall)
    def _():
        beside_wall.wait_recv()

    for z in range(NZL):
        share, _ = profile(z + 1)
        raised_out[z] = share * WN[last, 1, inner]

    @pl.when(on_wall)
    def _():
        beside_wall.wait_send()

    @pl.when(is_solver)
    def _():
        sent_to_faces(last)
        rest = XA.at[0, pl.ds(0, (NFX - 1) * EBD)]
        pltpu.make_async_copy(rest, rest, xsend.at[last - 1]).wait()
        for t in range(1, NFY):
            disp_copy(t).wait_send()

    @pl.when(not_solver)
    def _():
        disp_copy(1).wait_recv()
        disp_out[...] = DR[...]

    out.wait()


def last_add(before, raised, source_in, displacement, state_out, disp_out, T, A, D, source_weight, load_sem, out_sem):
    weights = pltpu.make_async_copy(source_in, source_weight, load_sem.at[NV])
    heights = pltpu.make_async_copy(raised, A, load_sem.at[NV + 1])
    small_in = pltpu.make_async_copy(displacement, D, load_sem.at[NV + 2])
    loads = [pltpu.make_async_copy(before.at[c], T.at[c], load_sem.at[c]) for c in range(NV)]
    stores = [pltpu.make_async_copy(T.at[c], state_out.at[c], out_sem.at[c]) for c in range(NV)]
    small_out = pltpu.make_async_copy(D, disp_out, out_sem.at[NV])
    for copy in [weights, heights] + loads + [small_in]:
        copy.start()
    weights.wait()
    heights.wait()
    for c in range(NV):
        loads[c].wait()

        def plane(z, carry):
            T[c, z] += source_weight[c] * A[z]
            return carry

        lax.fori_loop(0, NZL, plane, 0)
        stores[c].start()
    small_in.wait()
    small_out.start()
    for copy in stores + [small_out]:
        copy.wait()


def on_device(
    state, kappa, mix, press_weight, source_weight, interp, block_inverse, coupling, front_order, face_owner, face_slot
):
    hbm = pl.BlockSpec(memory_space=pltpu.HBM)
    vmem = pl.BlockSpec(memory_space=pltpu.VMEM)
    dma = pltpu.SemaphoreType.DMA
    sweeps = 2 * ITERS
    before, raised, displacement = pl.pallas_call(
        kernel,
        out_shape=(
            jax.ShapeDtypeStruct(state.shape, F32),
            jax.ShapeDtypeStruct(kappa.shape, F32),
            jax.ShapeDtypeStruct((EBD, EB), F32),
        ),
        in_specs=[hbm] * 11,
        out_specs=(hbm, vmem, vmem),
        scratch_shapes=[
            pltpu.SMEM((NV, NV), F32),
            pltpu.SMEM((NV,), F32),
            pltpu.SMEM((NV,), F32),
            pltpu.VMEM((CY, EB), F32),
            pltpu.SMEM((1, EBD), jnp.int32),
            pltpu.VMEM((1, CX), jnp.int32),
            pltpu.VMEM((1, CX), jnp.int32),
            pltpu.VMEM((2, NV, NZL + 2, CX, CY), F32),
            pltpu.VMEM((NZL, CX, CY), F32),
            pltpu.VMEM((NZL + 2, CXE, CY), F32),
            pltpu.VMEM((NZL, CX, CY), F32),
            pltpu.VMEM((EBD, EB, EB), F32),
            pltpu.VMEM((EBD, EB, EB), F32),
            pltpu.VMEM((PAIRS, 2 * EB, 2 * EB), BF16),
            pltpu.VMEM((PAIRS, 2 * EB, 2 * EB), BF16),
            pltpu.VMEM((PAIRS, EB, 2 * EB), BF16),
            pltpu.VMEM((2, NV + 1, NZL, CY), F32),
            pltpu.VMEM((sweeps, 2, NV + 1, NZL, CY), F32),
            pltpu.VMEM((CX, CY), F32),
            pltpu.VMEM((sweeps, 2, CX, CY), F32),
            pltpu.VMEM((CX, CY), F32),
            pltpu.VMEM((sweeps, NV, CX, CY), F32),
            pltpu.VMEM((CXE, CY), F32),
            pltpu.VMEM((CAP * NFX, CY), F32),
            pltpu.VMEM((CAP * NFX, CY), F32),
            pltpu.VMEM((5, CAP * NFX, CY), F32),
            pltpu.VMEM((ITERS + 1, FACES, CY), F32),
            pltpu.VMEM((5, FACES, CY), F32),
            pltpu.VMEM((FACES, CY), F32),
            pltpu.VMEM((ITERS, CAP * NFX, CY), F32),
            pltpu.VMEM((EBD, FACES), F32),
            pltpu.VMEM((FACES, EBD), F32),
            pltpu.VMEM((CAP * NFX, CX), F32),
            pltpu.VMEM((CX, CAP * NFX), F32),
            pltpu.VMEM((EBD, EB), F32),
            pltpu.VMEM((EBD, EB), F32),
            pltpu.VMEM((EBD, EB), F32),
            pltpu.VMEM((EBD, EB), F32),
            pltpu.VMEM((ITERS + 1, 3, CXE, CY), F32),
            pltpu.VMEM((2, CXE, CY), F32),
            pltpu.VMEM((2, CX, CY), F32),
            pltpu.VMEM((NZL + 2, CXE, CY), F32),
            pltpu.VMEM((CX, CY), F32),
            pltpu.VMEM((AROUND, FACES, NFX * EBD), BF16),
            pltpu.VMEM((AROUND, FACES, CY), F32),
            pltpu.VMEM((FACES, CY), F32),
            pltpu.VMEM((EBD, EB), F32),
            pltpu.VMEM((ITERS - 1, NFX * EBD, EB), F32),
            dma((11,)),
            dma((sweeps, 5)),
            dma((sweeps, 5)),
            dma((ITERS + 1,)),
            dma((ITERS + 1,)),
            dma((ITERS,)),
            dma((ITERS,)),
            dma((NFY,)),
            dma((2,)),
            dma((ITERS + 1, 8)),
            dma((ITERS + 1, 8)),
            dma((ITERS,)),
            dma((ITERS,)),
            dma,
            dma,
            dma((ITERS - 1,)),
            dma((ITERS - 1,)),
        ],
        compiler_params=pltpu.CompilerParams(
            collective_id=0, has_side_effects=True, vmem_limit_bytes=60 * 1024 * 1024
        ),
    )(
        state, kappa, mix, press_weight, source_weight, interp, block_inverse, coupling, front_order,
        face_owner.reshape(1, -1), face_slot.reshape(1, -1),
    )
    return pl.pallas_call(
        last_add,
        out_shape=(
            jax.ShapeDtypeStruct(state.shape, F32),
            jax.ShapeDtypeStruct((EBD, EB), F32),
        ),
        in_specs=[hbm] * 4,
        out_specs=(hbm, hbm),
        scratch_shapes=[
            pltpu.VMEM((NV, NZL, CX, CY), F32),
            pltpu.VMEM((NZL, CX, CY), F32),
            pltpu.VMEM((EBD, EB), F32),
            pltpu.SMEM((NV,), F32),
            dma((NV + 3,)),
            dma((NV + 1,)),
        ],
        compiler_params=pltpu.CompilerParams(vmem_limit_bytes=60 * 1024 * 1024),
    )(before, raised, source_weight, displacement)


def solution(mesh):
    return jax.shard_map(
        on_device,
        mesh=mesh,
        in_specs=(
            P(None, "fz", "fx", "fy"),
            P("fz", "fx", "fy"),
            P(),
            P(),
            P(),
            P(),
            P("fx", None, None),
            P("fx", None, None),
            P("fx", None),
            P(("fx", "fy"), None),
            P(("fx", "fy")),
        ),
        out_specs=(P(None, "fz", "fx", "fy"), P("fx", None)),
        check_vma=False,
    )
```

```python
import jax
import jax.numpy as jnp
from jax import lax
from jax.experimental import pallas as pl
from jax.experimental.pallas import tpu as pltpu
from jax.sharding import PartitionSpec as P

ITERS = 3
DIFFUSION = 0.16
HIGHEST = lax.Precision.HIGHEST
MESH = pl.DeviceIdType.MESH
F32 = jnp.float32
BF16 = jnp.bfloat16

NV, NZL, CX, CY = 5, 8, 32, 128
NZ = 16
NFX, NFY = 32, 4
RING_Z, RING_Y = 8, 4
EB, EBD, CAP = 128, 16, 2
PAIRS = EBD // 2
FACES = NFX * NFY * CAP
PAD = 8
CXE = CX + 2 * PAD
NT = (((1,), (1,)), ((), ()))
FAR_Y = (2, 1, 3, 0)
AROUND = 11


def far_first(step, ring):
    return ring // 2 + (1 - 2 * (step % 2)) * ((step + 1) // 2)


def split(values):
    high = values.astype(BF16)
    return high, (values - high.astype(F32)).astype(BF16)


def pick(selector, values):
    high, low = split(values)
    return jnp.dot(selector, high, preferred_element_type=F32) + jnp.dot(selector, low, preferred_element_type=F32)


def kernel(
    state_in, kappa_in, mix_in, press_in, source_in, interp_in, inverse_in, coupling_in, order_in, owner_in, slot_in,
    state_out, raised_out, disp_out,
    mix, press_weight, source_weight, interp, order, owner, slot,
    S, K, KX, KE, BI, CO, R, RO, RN, XS, XR, YS, YR, YK, ZR, KZ, SL, SF, CS, RF, RC, SD, RD, FP, FPT, AM, AT, FR, XV, DV, DR,
    WN, LP, LE, QB, PB, G, GW, IN, XO, XA,
    load_sem, hsend, hrecv, fsend, frecv, dsend, drecv, osend, orecv, wsend, wrecv, rsend, rrecv, csend, crecv, xsend, xrecv,
):
    ix, iy, iz = lax.axis_index("fx"), lax.axis_index("fy"), lax.axis_index("fz")
    ring_z, ring_y = ix // RING_Y, ix % RING_Y
    on_wall = iz == 0
    off_wall = iz == 1
    home = (ring_y + ring_z) % NFY
    is_solver = iy == home
    not_solver = jnp.logical_not(is_solver)
    turned_y = {d: (ring_y + d) % RING_Y for d in FAR_Y}
    turned_x = {d: (iy + d) % NFY for d in FAR_Y}
    answer_x = ((iy + 2 - iz) % NFY, (iy + 3 * iz) % NFY)

    def row_base(step):
        return ((ring_z + far_first(step, RING_Z)) % RING_Z) * RING_Y

    def homes(z):
        return {d: (turned_y[d] + z) % NFY for d in FAR_Y}

    def owners_at(step):
        z = (ring_z + far_first(step, RING_Z)) % RING_Z
        return [(z * RING_Y + turned_y[d], home_y) for d, home_y in homes(z).items()]

    near_owners = [(ring_z * RING_Y + turned_y[d], home_y) for d, home_y in homes(ring_z).items()][:3]

    def signal(barrier, device):
        pl.semaphore_signal(barrier, inc=1, device_id=device, device_id_type=MESH)

    loads = [
        pltpu.make_async_copy(source, target, load_sem.at[n])
        for n, (source, target) in enumerate(
            (
                (owner_in, owner),
                (slot_in, slot),
                (order_in, order),
                (kappa_in, K),
                (state_in, S.at[0, :, pl.ds(1, NZL)]),
                (inverse_in, BI),
                (coupling_in, CO),
                (interp_in, interp),
                (mix_in, mix),
                (press_in, press_weight),
                (source_in, source_weight),
            )
        )
    ]
    for load in loads:
        load.start()

    barrier = pltpu.get_barrier_semaphore()
    has_left, has_right, has_front, has_back = ix > 0, ix < NFX - 1, iy > 0, iy < NFY - 1
    sides = (
        (has_left, (ix - 1, iy, iz)),
        (has_right, (ix + 1, iy, iz)),
        (has_front, (ix, iy - 1, iz)),
        (has_back, (ix, iy + 1, iz)),
    )
    corners = (
        (jnp.logical_and(has_left, has_front), (ix - 1, iy - 1, iz)),
        (jnp.logical_and(has_left, has_back), (ix - 1, iy + 1, iz)),
        (jnp.logical_and(has_right, has_front), (ix + 1, iy - 1, iz)),
        (jnp.logical_and(has_right, has_back), (ix + 1, iy + 1, iz)),
    )
    other_core = (ix, iy, 1 - iz)

    @pl.when(is_solver)
    def _():
        def greet(step, carry):
            base = row_base(step)
            for dy in FAR_Y:
                for dx in FAR_Y:
                    signal(barrier, (base + turned_y[dy], turned_x[dx], 0))
            return carry

        lax.fori_loop(0, RING_Z - 1, greet, 0)
        for dy in FAR_Y:
            for dx in FAR_Y:
                if dy or dx:
                    signal(barrier, (ring_z * RING_Y + turned_y[dy], turned_x[dx], 0))

        @pl.when(off_wall)
        def _():
            signal(barrier, (ix, iy, 0))

        def greet_solvers(step, carry):
            for to, home_y in owners_at(step):
                signal(barrier, (to, home_y, iz))
            return carry

        lax.fori_loop(0, RING_Z - 1, greet_solvers, 0)
        for to, home_y in near_owners:
            signal(barrier, (to, home_y, iz))

    @pl.when(on_wall)
    def _():
        def greet(step, carry):
            for to, home_y in owners_at(step):
                signal(barrier, (to, home_y, (iy + home_y) % 2))
            return carry

        lax.fori_loop(0, RING_Z - 1, greet, 0)
        for to, home_y in near_owners:
            signal(barrier, (to, home_y, (iy + home_y) % 2))

        @pl.when(not_solver)
        def _():
            signal(barrier, (ix, home, (iy + home) % 2))

    @pl.when(not_solver)
    def _():
        signal(barrier, (ix, home, iz))

    for ref in (XR, YR, WN):
        ref[...] = jnp.zeros_like(ref)

    signal(barrier, other_core)
    solver_count = is_solver.astype(jnp.int32)
    wall_count = on_wall.astype(jnp.int32)
    expected = 1 + wall_count * (2 * NFX - solver_count) + solver_count * (2 * NFX - wall_count + NFY - 1 + NFX - 1)
    for present, device in sides + corners:
        expected = expected + present.astype(jnp.int32)

        @pl.when(present)
        def _():
            signal(barrier, device)

    zero_plane = jnp.zeros((NV, CX, CY), F32)
    for buffer in range(2):
        S[buffer, :, 0] = zero_plane
        S[buffer, :, NZL + 1] = zero_plane

    for load in loads[:3]:
        load.wait()
    rows = lax.broadcasted_iota(jnp.int32, (CAP * NFX, CX), 0)
    named = (owner[...] == rows // CAP).astype(F32)
    earlier = (
        lax.broadcasted_iota(jnp.int32, (CX, CX), 0) < lax.broadcasted_iota(jnp.int32, (CX, CX), 1)
    ).astype(BF16)
    rank = jnp.dot(named.astype(BF16), earlier, preferred_element_type=F32)
    chosen = jnp.where(rank == (rows % CAP).astype(F32), named, 0.0)
    AM[...] = chosen
    unit = (lax.broadcasted_iota(jnp.int32, (CX, CX), 0) == lax.broadcasted_iota(jnp.int32, (CX, CX), 1)).astype(F32)
    AT[...] = lax.dot_general(unit, chosen, NT, preferred_element_type=F32)
    slot_rows = jnp.sum(chosen * (slot[...] + 1).astype(F32), axis=1, keepdims=True)
    SL[...] = jnp.broadcast_to(slot_rows, (CAP * NFX, CY))
    target_of = jnp.sum(unit * (EBD * owner[...] + slot[...] + 1).astype(F32), axis=1, keepdims=True)
    WN[ITERS, 1, PAD : PAD + CX] = jnp.broadcast_to(target_of, (CX, CY))
    block_rows = lax.broadcasted_iota(jnp.int32, (EBD, EB), 0)
    block_lanes = lax.broadcasted_iota(jnp.int32, (EBD, EB), 1)
    placed = jnp.zeros((EBD, EB), F32)
    for k in range(EBD):
        placed = jnp.where(jnp.logical_and(block_rows == k, block_lanes == order[0, k]), 1.0, placed)

    lane = lax.broadcasted_iota(jnp.int32, (CX, CY), 1)
    row = lax.broadcasted_iota(jnp.int32, (CX, CY), 0)
    for load in loads[3:5]:
        load.wait()

    pair = lane // 2

    def put_ends(ends, centre, at):
        return jnp.where(pair == at, pltpu.roll(centre, 2 * at + 1, 1), ends)

    def take_ends(n):
        return jnp.where(lane % 2 == 0, pltpu.roll(YR[n, 1], CY - 1, 1), pltpu.roll(YR[n, 0], 1, 1))

    def kappa_faces(z, ends):
        coeff = DIFFUSION * K[z]
        KX[z + 1, PAD : PAD + CX] = coeff
        XS[0, NV, pl.ds(z, 1), :] = coeff[0:1]
        XS[1, NV, pl.ds(z, 1), :] = coeff[CX - 1 : CX]
        return put_ends(ends, coeff, NV * NZL + z)

    YK[...] = lax.fori_loop(0, NZL, kappa_faces, jnp.zeros((CX, CY), F32))

    def pack(src):
        def plane(z, ends):
            for c in range(NV):
                centre = src[c, z + 1]
                XS[0, c, pl.ds(z, 1), :] = centre[0:1]
                XS[1, c, pl.ds(z, 1), :] = centre[CX - 1 : CX]
                ends = put_ends(ends, centre, c * NZL + z)
            return ends

        YS[...] = lax.fori_loop(0, NZL, plane, YK[...])

    edge = NZL - (NZL - 1) * iz

    def halo_copies(n, src):
        def remote(source, target, at, there, device):
            return pltpu.make_async_remote_copy(
                source, target, hsend.at[n, at], hrecv.at[n, there], device_id=device, device_id_type=MESH
            )

        (_, left), (_, right), (_, front), (_, back) = sides
        always = iz >= 0
        plane = src.at[:, edge]
        sends = (
            (has_left, remote(XS.at[0], XR.at[n, 1], 0, 1, left)),
            (has_right, remote(XS.at[1], XR.at[n, 0], 1, 0, right)),
            (has_front, remote(YS, YR.at[n, 1], 2, 3, front)),
            (has_back, remote(YS, YR.at[n, 0], 3, 2, back)),
            (always, remote(plane, ZR.at[n], 4, 4, other_core)),
        )
        waits = (
            (has_left, remote(XS.at[0], XR.at[n, 0], 0, 0, left)),
            (has_right, remote(XS.at[1], XR.at[n, 1], 1, 1, right)),
            (has_front, remote(YS, YR.at[n, 0], 2, 2, front)),
            (has_back, remote(YS, YR.at[n, 1], 3, 3, back)),
            (always, remote(plane, ZR.at[n], 4, 4, other_core)),
        )
        return sends, waits

    def each(copies, action):
        for present, copy in copies:

            @pl.when(present)
            def _():
                action(copy)

    def start_halo(n, src):
        each(halo_copies(n, src)[0], lambda copy: copy.start())

    def finish_halo(n, src):
        _, waits = halo_copies(n, src)
        each(waits, lambda copy: copy.wait_recv())
        src[:, (NZL + 1) * (1 - iz)] = ZR[n]

    def sweep(n, src, dst, first=0, end=NZL):
        outer = take_ends(n)

        def plane(z, carry):
            coeff = KX[z + 1, PAD : PAD + CX]
            centres = [src[c, z + 1] for c in range(NV)]
            for c in range(NV):
                centre = centres[c]
                at = c * NZL + z
                beside = src[c, z] + src[c, z + 2]
                beside += jnp.where(row == 0, XR[n, 0, c, pl.ds(z, 1), :], pltpu.roll(centre, 1, 0))
                beside += jnp.where(row == CX - 1, XR[n, 1, c, pl.ds(z, 1), :], pltpu.roll(centre, CX - 1, 0))
                ends = pltpu.roll(outer, CY - 1 - 2 * at, 1)
                beside += jnp.where(lane == 0, ends, pltpu.roll(centre, 1, 1))
                beside += jnp.where(lane == CY - 1, ends, pltpu.roll(centre, CY - 1, 1))
                total = centre + coeff * (beside - 6.0 * centre)
                for d in range(NV):
                    total += mix[c, d] * centres[d]
                dst[c, z + 1] = total
            return carry

        lax.fori_loop(first, end, plane, 0)
        if end == NZL:
            each(halo_copies(n, src)[0], lambda copy: copy.wait_send())

    kappa_plane = pltpu.make_async_remote_copy(
        KX.at[edge], KZ, osend.at[0], orecv.at[0], device_id=other_core, device_id_type=MESH
    )

    def send_to_solvers(rows_of, target, sent, heard):
        def send(to, y, core):
            pltpu.make_async_remote_copy(
                rows_of(to), target, sent, heard, device_id=(to, y, core), device_id_type=MESH
            ).start()

        def group(step, carry):
            for to, home_y in owners_at(step):
                for core in range(2):
                    send(to, home_y, core)
            return carry

        @pl.when(on_wall)
        def _():
            lax.fori_loop(0, RING_Z - 1, group, 0)
            for to, home_y in near_owners:
                for core in range(2):
                    send(to, home_y, core)
            send(ix, home, 1)

            @pl.when(not_solver)
            def _():
                send(ix, home, 0)

            @pl.when(is_solver)
            def _():
                pltpu.make_async_copy(rows_of(ix), target, heard).start()

    own_rows = pl.ds(CAP * (ix * NFY + iy), CAP)

    def send_rows(turn, rows_out):
        send_to_solvers(
            lambda to: rows_out.at[pl.ds(CAP * to, CAP)], RF.at[turn, own_rows], fsend.at[turn], frecv.at[turn]
        )

    def send_pressure(turn):
        @pl.when(on_wall)
        def _():
            SF[...] = pick(AM[...].astype(BF16), PB[...])

        send_rows(turn, SF)

    def sent_to_solvers(turn):
        @pl.when(on_wall)
        def _():
            @pl.when(is_solver)
            def _():
                rest = RF.at[turn, pl.ds(0, CAP * (2 * NFX - 1))]
                pltpu.make_async_copy(rest, rest, fsend.at[turn]).wait()

            @pl.when(not_solver)
            def _():
                rest = RF.at[turn, pl.ds(0, CAP * 2 * NFX)]
                pltpu.make_async_copy(rest, rest, fsend.at[turn]).wait()

    def heard_from_faces(turn):
        whole = RF.at[turn]
        pltpu.make_async_copy(whole, whole, frecv.at[turn]).wait()

    def send_to_faces(turn):
        target = RD.at[turn, pl.ds(CAP * ix, CAP)]

        def send(to_x, to_y):
            pltpu.make_async_remote_copy(
                SD.at[pl.ds(CAP * (to_x * NFY + to_y), CAP)], target, dsend.at[turn], drecv.at[turn],
                device_id=(to_x, to_y, 0), device_id_type=MESH,
            ).start()

        def group(step, carry):
            base = row_base(step)
            for dy in FAR_Y:
                for x in answer_x:
                    send(base + turned_y[dy], x)
            return carry

        lax.fori_loop(0, RING_Z - 1, group, 0)
        for dy in FAR_Y[:3]:
            for x in answer_x:
                send(ring_z * RING_Y + turned_y[dy], x)
        send(ix, answer_x[0])

        @pl.when(off_wall)
        def _():
            send(ix, answer_x[1])

        @pl.when(on_wall)
        def _():
            pltpu.make_async_copy(SD.at[pl.ds(CAP * (ix * NFY + iy), CAP)], target, drecv.at[turn]).start()

    def sent_to_faces(turn):
        @pl.when(on_wall)
        def _():
            rest = RF.at[turn, pl.ds(0, CAP * (2 * NFX - 1))]
            pltpu.make_async_copy(rest, rest, dsend.at[turn]).wait()

        @pl.when(off_wall)
        def _():
            rest = RF.at[turn, pl.ds(0, CAP * 2 * NFX)]
            pltpu.make_async_copy(rest, rest, dsend.at[turn]).wait()

    for load in loads[5:]:
        load.wait()

    @pl.when(is_solver)
    def _():
        def parts(k):
            block = order[0, k]
            inverse = BI[block]
            force_part = lax.dot_general(interp[...], inverse, NT, precision=HIGHEST, preferred_element_type=F32)
            chain = jnp.dot(inverse, CO[block], precision=HIGHEST, preferred_element_type=F32)
            return force_part, -chain.T

        def both_parts(matrix):
            high, low = split(matrix)
            return jnp.concatenate([high, low], axis=1)

        def products(m, carry):
            force, chain = parts(2 * m)
            next_force, next_chain = parts(2 * m + 1)
            passed = jnp.dot(force, next_chain, precision=HIGHEST, preferred_element_type=F32)
            leap = jnp.dot(chain, next_chain, precision=HIGHEST, preferred_element_type=F32)
            R[m] = both_parts(jnp.concatenate([force, chain], axis=0))
            RO[m] = both_parts(jnp.concatenate([next_force, passed], axis=0))
            RN[m] = both_parts(leap)
            return carry

        lax.fori_loop(0, PAIRS, products, 0)

    numbers = range(NV)
    source = [source_weight[c] for c in numbers]
    once = [source[c] + sum(mix[c, d] * source[d] for d in numbers) for c in numbers]
    twice = [once[c] + sum(mix[c, d] * once[d] for d in numbers) for c in numbers]
    press_source = sum(press_weight[c] * source[c] for c in numbers)
    press_once = sum(press_weight[c] * once[c] for c in numbers)
    press_twice = sum(press_weight[c] * twice[c] for c in numbers)

    inner = slice(PAD, PAD + CX)

    def wall_copies(it):
        def remote(n, opposite, source_row, side, target_row, count, device):
            copy = lambda here, there: pltpu.make_async_remote_copy(
                WN.at[it, 1, pl.ds(source_row, count)], WN.at[it, side, pl.ds(target_row, count)],
                wsend.at[it, here], wrecv.at[it, there], device_id=device, device_id_type=MESH,
            )
            return copy(n, opposite), copy(n, n)

        low, high = PAD, PAD + CX - 8
        (_, left), (_, right), (_, front), (_, back) = sides
        (lf, left_front), (lb, left_back), (rf, right_front), (rb, right_back) = corners
        return (
            (has_left, remote(0, 1, low, 1, PAD + CX, 8, left)),
            (has_right, remote(1, 0, high, 1, 0, 8, right)),
            (has_front, remote(2, 3, PAD, 2, PAD, CX, front)),
            (has_back, remote(3, 2, PAD, 0, PAD, CX, back)),
            (lf, remote(4, 7, low, 2, PAD + CX, 8, left_front)),
            (lb, remote(5, 6, low, 0, PAD + CX, 8, left_back)),
            (rf, remote(6, 5, high, 2, 0, 8, right_front)),
            (rb, remote(7, 4, high, 0, 0, 8, right_back)),
        )

    def tell_faces():
        targets = (
            [pltpu.roll(WN[ITERS, 1], (CXE - d) % CXE, 0)[inner] for d in range(-2, 3)]
            + [pltpu.roll(WN[ITERS, 0], (CXE - d) % CXE, 0)[inner] for d in range(-1, 2)]
            + [pltpu.roll(WN[ITERS, 2], (CXE - d) % CXE, 0)[inner] for d in range(-1, 2)]
        )
        facts = targets + [
            jnp.broadcast_to(KE[0, :, CY - 1 : CY], (CX, CY)), jnp.broadcast_to(KE[0, :, 0:1], (CX, CY)),
        ]
        table = jnp.zeros((CX, CY), F32)
        for n, fact in enumerate(facts):
            table = jnp.where(lane == n, fact, table)
        wall_coeff = KX[1]
        selector = AM[...].astype(BF16)
        CS[0] = pick(selector, table)
        for n, d in enumerate((-1, 0, 1)):
            CS[n + 1] = pick(selector, pltpu.roll(wall_coeff, (CXE - d) % CXE, 0)[inner])
        CS[4] = pick(selector, KX[2, inner])

    half = FACES // 2
    facts_core = ix // (NFX // 2)
    facts_here = jnp.logical_and(is_solver, facts_core == iz)

    def send_facts():
        def send(to, home_y):
            pltpu.make_async_remote_copy(
                CS.at[:, pl.ds(CAP * to, CAP)], RC.at[:, own_rows], csend, crecv.at[0],
                device_id=(to, home_y, facts_core), device_id_type=MESH,
            ).start()

        def group(step, carry):
            for to, home_y in owners_at(step):
                send(to, home_y)
            return carry

        @pl.when(on_wall)
        def _():
            lax.fori_loop(0, RING_Z - 1, group, 0)
            for to, home_y in near_owners:
                send(to, home_y)

            @pl.when(facts_here)
            def _():
                pltpu.make_async_copy(CS.at[:, pl.ds(CAP * ix, CAP)], RC.at[:, own_rows], crecv.at[0]).start()

            @pl.when(jnp.logical_not(facts_here))
            def _():
                send(ix, home)

    share_facts = pltpu.make_async_remote_copy(
        RC.at[:, pl.ds(half * iz, half)], RC.at[:, pl.ds(half * iz, half)], csend, crecv.at[1],
        device_id=other_core, device_id_type=MESH,
    )

    around_wall = wall_copies(ITERS)
    pack(S.at[0])
    pl.semaphore_wait(barrier, expected)
    start_halo(0, S.at[0])

    @pl.when(on_wall)
    def _():
        each(around_wall, lambda pair: pair[0].start())

    kappa_plane.start()
    send_rows(ITERS, SL)
    finish_halo(0, S.at[0])
    sweep(0, S.at[0], S.at[1])
    pack(S.at[1])
    start_halo(1, S.at[1])

    kappa_plane.wait()
    KX[(NZL + 1) * (1 - iz)] = KZ[...]
    KX[(NZL + 1) * iz] = jnp.zeros((CXE, CY), F32)
    tile_row = lax.broadcasted_iota(jnp.int32, (PAD, CY), 0)

    ends = take_ends(0)

    def kappa_edges(z, carry):
        KX[z + 1, 0:PAD] = jnp.where(tile_row == PAD - 1, XR[0, 0, NV, pl.ds(z, 1), :], 0.0)
        KX[z + 1, PAD + CX : CXE] = jnp.where(tile_row == 0, XR[0, 1, NV, pl.ds(z, 1), :], 0.0)
        at = 2 * (NV * NZL + z)
        front = pltpu.roll(ends, CY - 2 - at, 1)
        back = pltpu.roll(ends, CY - at, 1)
        KE[z] = jnp.where(lane >= CY // 2, front, back)
        return carry

    lax.fori_loop(0, NZL, kappa_edges, 0)

    def wall_base():
        @pl.when(on_wall)
        def _():
            pressure = press_weight[0] * S[0, 0, 1]
            for c in range(1, NV):
                pressure += press_weight[c] * S[0, c, 1]
            PB[...] = pressure

    finish_halo(1, S.at[1])
    sweep(1, S.at[1], S.at[0], 0, 1)
    wall_base()
    send_pressure(0)
    sweep(1, S.at[1], S.at[0], 1, NZL)
    sent_to_solvers(ITERS)

    @pl.when(on_wall)
    def _():
        each(around_wall, lambda pair: pair[1].wait_recv())
        tell_faces()
        each(around_wall, lambda pair: pair[0].wait_send())

    send_facts()


    @pl.when(is_solver)
    def _():
        heard_from_faces(ITERS)
        face_lanes = lax.broadcasted_iota(jnp.int32, (FACES, EB), 1) + 1
        slot_of = (RF[ITERS] == face_lanes.astype(F32)).astype(F32)
        FP[...] = lax.dot_general(placed, slot_of, NT, preferred_element_type=F32)
        FPT[...] = lax.dot_general(slot_of, placed, NT, preferred_element_type=F32)

    def times(row_in, matrix):
        width = row_in.shape[1]
        high = row_in.astype(BF16).astype(F32)
        at = lax.broadcasted_iota(jnp.int32, (8, width), 0)
        left = jnp.where(at == 0, high, jnp.where(at == 1, row_in - high, 0.0)).astype(BF16)
        result = jnp.dot(left, matrix, preferred_element_type=F32)
        summed = result[:, :EB] + result[:, EB:]
        return summed[0:1] + summed[1:2]

    def solve():
        force = [FR[pl.ds(k, 1), :] for k in range(EBD)]
        odd = [times(jnp.concatenate([force[2 * m + 1], force[2 * m]], axis=1), RO[m]) for m in range(PAIRS)]
        for m in range(PAIRS):
            if m:
                odd[m] += times(odd[m - 1], RN[m])
            XV[pl.ds(2 * m + 1, 1), :] = odd[m]
            previous = odd[m - 1] if m else jnp.zeros((1, EB), F32)
            XV[pl.ds(2 * m, 1), :] = times(jnp.concatenate([force[2 * m], previous], axis=1), R[m])

    lane_e = lax.broadcasted_iota(jnp.int32, (CXE, CY), 1)

    def spread(it):
        centre = WN[it, 1]
        beyond = jnp.where(lane_e >= CY // 2, WN[it, 0], WN[it, 2])
        up, down = pltpu.roll(centre, 1, 1), pltpu.roll(centre, CY - 1, 1)
        out_up, out_down = pltpu.roll(beyond, 1, 1), pltpu.roll(beyond, CY - 1, 1)
        lap = pltpu.roll(centre, 1, 0) + pltpu.roll(centre, CXE - 1, 0) - 4.0 * centre
        lap += jnp.where(lane_e == 0, out_up, up) + jnp.where(lane_e == CY - 1, out_down, down)
        lap_e = pltpu.roll(beyond, 1, 0) + pltpu.roll(beyond, CXE - 1, 0) - 4.0 * beyond
        lap_e += jnp.where(lane_e >= CY // 2, out_up + down, out_down + up)
        LP[0], LP[1] = lap, centre
        LE[0], LE[1] = lap_e[inner], beyond[inner]

    def ring_sum(wide, edge_columns, below, above, coeff):
        own = wide[inner]
        total = pltpu.roll(wide, 1, 0)[inner] + pltpu.roll(wide, CXE - 1, 0)[inner] + below + above - 6.0 * own
        total += jnp.where(lane == 0, pltpu.roll(edge_columns, 1, 1), pltpu.roll(own, 1, 1))
        total += jnp.where(lane == CY - 1, pltpu.roll(edge_columns, CY - 1, 1), pltpu.roll(own, CY - 1, 1))
        return coeff * total

    first_jump = (NZ - 1.0) / NZ - 2.0

    def profile(plane):
        height = iz * NZL + plane - 1
        return 1.0 - height.astype(F32) / NZ, jnp.where(height == 0, first_jump, 0.0)

    def update():
        def first(plane, carry):
            share, jump = profile(plane)
            QB[plane] = KX[plane] * (share * LP[0] + jump * LP[1])
            return carry

        lax.fori_loop(0, NZL + 2, first, 0)

        def second(z, carry):
            share, jump = profile(z + 1)
            edges = KE[z] * (share * LE[0] + jump * LE[1])
            wide = QB[z + 1]
            bend = ring_sum(wide, edges, QB[z, inner], QB[z + 2, inner], KX[z + 1, inner])
            raised, slope = share * LP[1, inner], wide[inner]
            for c in range(NV):
                S[0, c, z + 1] += twice[c] * raised + 2.0 * once[c] * slope + source[c] * bend
            return carry

        lax.fori_loop(0, NZL, second, 0)

    def sent_facts():
        @pl.when(on_wall)
        def _():
            @pl.when(facts_here)
            def _():
                rest = RC.at[:, pl.ds(0, CAP * (NFX - 1))]
                pltpu.make_async_copy(rest, rest, csend).wait()

            @pl.when(jnp.logical_not(facts_here))
            def _():
                rest = RC.at[:, pl.ds(0, CAP * NFX)]
                pltpu.make_async_copy(rest, rest, csend).wait()

    def pass_facts():
        mine = RC.at[:, pl.ds(half * iz, half)]
        pltpu.make_async_copy(mine, mine, crecv.at[0]).wait()
        share_facts.start()

    def hear_facts():
        share_facts.wait()
        names = lax.broadcasted_iota(jnp.int32, (FACES, NFX * EBD), 1) + 1
        names = names.astype(F32)
        for m in range(AROUND):
            G[m] = jnp.where(names == RC[0, :, m : m + 1], 1.0, 0.0).astype(BF16)

    def tell_solvers(it, facing):
        if it:
            rest = XA.at[0, pl.ds(0, (NFX - 1) * EBD)]
            pltpu.make_async_copy(rest, rest, xsend.at[it - 1]).wait()
        own = pick(placed.T[:EBD].astype(BF16), facing)
        XO[...] = own
        XA[it, pl.ds(EBD * ix, EBD)] = own

        def send(to, y):
            pltpu.make_async_remote_copy(
                XO, XA.at[it, pl.ds(EBD * ix, EBD)], xsend.at[it], xrecv.at[it],
                device_id=(to, y, iz), device_id_type=MESH,
            ).start()

        def group(step, carry):
            for to, home_y in owners_at(step):
                send(to, home_y)
            return carry

        lax.fori_loop(0, RING_Z - 1, group, 0)
        for to, home_y in near_owners:
            send(to, home_y)

    def respond(it):
        rest = XA.at[it, pl.ds(0, (NFX - 1) * EBD)]
        pltpu.make_async_copy(rest, rest, xrecv.at[it]).wait()
        high, low = split(XA[it])
        both = jnp.concatenate([high, low], axis=1)
        for m in range(AROUND):
            found = jnp.dot(G[m], both, preferred_element_type=F32)
            GW[m] = found[:, :CY] + found[:, CY:]

        def chunk(n, carry):
            at = pl.ds(pl.multiple_of(n * CX, CX), CX)
            centre = {d: GW[d + 2, at] for d in range(-2, 3)}
            beyond = {d: jnp.where(lane >= CY // 2, GW[d + 6, at], GW[d + 9, at]) for d in range(-1, 2)}
            coeff = {d: RC[d + 2, at] for d in range(-1, 2)}

            def wide_sum(d):
                total = centre[d - 1] + centre[d + 1] - 4.0 * centre[d]
                total += jnp.where(lane == 0, pltpu.roll(beyond[d], 1, 1), pltpu.roll(centre[d], 1, 1))
                return total + jnp.where(
                    lane == CY - 1, pltpu.roll(beyond[d], CY - 1, 1), pltpu.roll(centre[d], CY - 1, 1)
                )

            sums = {d: wide_sum(d) for d in range(-1, 2)}
            slopes = {d: coeff[d] * (sums[d] + first_jump * centre[d]) for d in range(-1, 2)}
            above = RC[4, at] * ((NZ - 1.0) / NZ * sums[0])
            facts = RC[0, at]
            edge_coeff = jnp.where(lane >= CY // 2, facts[:, AROUND : AROUND + 1], facts[:, AROUND + 1 : AROUND + 2])
            edge_sum = beyond[-1] + beyond[1] - 4.0 * beyond[0]
            edge_sum += jnp.where(
                lane >= CY // 2,
                pltpu.roll(beyond[0], 1, 1) + pltpu.roll(centre[0], CY - 1, 1),
                pltpu.roll(beyond[0], CY - 1, 1) + pltpu.roll(centre[0], 1, 1),
            )
            edges = edge_coeff * (edge_sum + first_jump * beyond[0])
            bend = slopes[-1] + slopes[1] + above - 6.0 * slopes[0]
            bend += jnp.where(lane == 0, pltpu.roll(edges, 1, 1), pltpu.roll(slopes[0], 1, 1))
            bend += jnp.where(lane == CY - 1, pltpu.roll(edges, CY - 1, 1), pltpu.roll(slopes[0], CY - 1, 1))
            IN[at] = press_twice * centre[0] + 2.0 * press_once * slopes[0] + press_source * coeff[0] * bend
            return carry

        lax.fori_loop(0, FACES // CX, chunk, 0)

    def answer(it):
        heard_from_faces(it)
        if it:
            sent_to_faces(it - 1)
        rows_in = RF[it] + IN[...] if it else RF[it]
        FR[...] = pick(FP[...].astype(BF16), rows_in)
        solve()
        facing = lax.dot_general(XV[...], interp[...], NT, precision=HIGHEST, preferred_element_type=F32)
        if 0 < it < ITERS - 1:
            tell_solvers(it, facing)
        SD[...] = pick(FPT[...].astype(BF16), facing)
        send_to_faces(it)
        if it == 0:
            tell_solvers(it, facing)

    def hear_wall(it):
        whole = RD.at[it]
        pltpu.make_async_copy(whole, whole, drecv.at[it]).wait()
        WN[it, 1, inner] = pick(AT[...].astype(BF16), RD[it])

    def relay(it, part):
        return pltpu.make_async_remote_copy(
            part, part, rsend.at[it], rrecv.at[it], device_id=other_core, device_id_type=MESH
        )

    for it in range(ITERS - 1):
        n = 2 * it + 2
        pack(S.at[0])
        start_halo(n, S.at[0])
        if it:

            @pl.when(is_solver)
            def _():
                answer(it)

        finish_halo(n, S.at[0])
        sweep(n, S.at[0], S.at[1])
        pack(S.at[1])
        start_halo(n + 1, S.at[1])
        if it == 0:
            sent_facts()

            @pl.when(is_solver)
            def _():
                answer(it)
                pass_facts()

        finish_halo(n + 1, S.at[1])
        sweep(n + 1, S.at[1], S.at[0], 0, 1)
        wall_base()
        sent_to_solvers(it)
        send_pressure(it + 1)
        sweep(n + 1, S.at[1], S.at[0], 1, NZL)
        if it == 0:

            @pl.when(is_solver)
            def _():
                hear_facts()

        copies = wall_copies(it)

        @pl.when(on_wall)
        def _():
            hear_wall(it)
            each(copies, lambda pair: pair[0].start())

        @pl.when(is_solver)
        def _():
            respond(it)

        beside_wall = relay(it, WN.at[it])

        @pl.when(on_wall)
        def _():
            each(copies, lambda pair: pair[1].wait_recv())
            beside_wall.start()

        @pl.when(off_wall)
        def _():
            beside_wall.wait_recv()

        spread(it)
        update()

        @pl.when(on_wall)
        def _():
            each(copies, lambda pair: pair[0].wait_send())
            beside_wall.wait_send()

    last = ITERS - 1
    out = pltpu.make_async_copy(S.at[0, :, pl.ds(1, NZL)], state_out, load_sem.at[0])
    out.start()

    def disp_copy(t):
        return pltpu.make_async_remote_copy(
            DV, DR, osend.at[t], orecv.at[1], device_id=(ix, (iy + t) % NFY, iz), device_id_type=MESH
        )

    @pl.when(is_solver)
    def _():
        answer(last)
        back = lax.dot_general(placed, XV[...], (((0,), (0,)), ((), ())), precision=HIGHEST, preferred_element_type=F32)
        DV[...] = back[:EBD]
        for t in range(1, NFY):
            disp_copy(t).start()
        disp_out[...] = back[:EBD]

    beside_wall = relay(last, WN.at[last, 1, pl.ds(PAD, CX)])

    @pl.when(on_wall)
    def _():
        sent_to_solvers(last)
        hear_wall(last)
        beside_wall.start()

    @pl.when(off_wall)
    def _():
        beside_wall.wait_recv()

    for z in range(NZL):
        share, _ = profile(z + 1)
        raised_out[z] = share * WN[last, 1, inner]

    @pl.when(on_wall)
    def _():
        beside_wall.wait_send()

    @pl.when(is_solver)
    def _():
        sent_to_faces(last)
        rest = XA.at[0, pl.ds(0, (NFX - 1) * EBD)]
        pltpu.make_async_copy(rest, rest, xsend.at[last - 1]).wait()
        for t in range(1, NFY):
            disp_copy(t).wait_send()

    @pl.when(not_solver)
    def _():
        disp_copy(1).wait_recv()
        disp_out[...] = DR[...]

    out.wait()


def last_add(before, raised, source_in, displacement, state_out, disp_out, T, A, D, source_weight, load_sem, out_sem):
    weights = pltpu.make_async_copy(source_in, source_weight, load_sem.at[NV])
    heights = pltpu.make_async_copy(raised, A, load_sem.at[NV + 1])
    small_in = pltpu.make_async_copy(displacement, D, load_sem.at[NV + 2])
    loads = [pltpu.make_async_copy(before.at[c], T.at[c], load_sem.at[c]) for c in range(NV)]
    stores = [pltpu.make_async_copy(T.at[c], state_out.at[c], out_sem.at[c]) for c in range(NV)]
    small_out = pltpu.make_async_copy(D, disp_out, out_sem.at[NV])
    for copy in [weights, heights] + loads + [small_in]:
        copy.start()
    weights.wait()
    heights.wait()
    for c in range(NV):
        loads[c].wait()

        def plane(z, carry):
            T[c, z] += source_weight[c] * A[z]
            return carry

        lax.fori_loop(0, NZL, plane, 0)
        stores[c].start()
    small_in.wait()
    small_out.start()
    for copy in stores + [small_out]:
        copy.wait()


def on_device(
    state, kappa, mix, press_weight, source_weight, interp, block_inverse, coupling, front_order, face_owner, face_slot
):
    hbm = pl.BlockSpec(memory_space=pltpu.HBM)
    vmem = pl.BlockSpec(memory_space=pltpu.VMEM)
    dma = pltpu.SemaphoreType.DMA
    sweeps = 2 * ITERS
    before, raised, displacement = pl.pallas_call(
        kernel,
        out_shape=(
            jax.ShapeDtypeStruct(state.shape, F32),
            jax.ShapeDtypeStruct(kappa.shape, F32),
            jax.ShapeDtypeStruct((EBD, EB), F32),
        ),
        in_specs=[hbm] * 11,
        out_specs=(hbm, vmem, vmem),
        scratch_shapes=[
            pltpu.SMEM((NV, NV), F32),
            pltpu.SMEM((NV,), F32),
            pltpu.SMEM((NV,), F32),
            pltpu.VMEM((CY, EB), F32),
            pltpu.SMEM((1, EBD), jnp.int32),
            pltpu.VMEM((1, CX), jnp.int32),
            pltpu.VMEM((1, CX), jnp.int32),
            pltpu.VMEM((2, NV, NZL + 2, CX, CY), F32),
            pltpu.VMEM((NZL, CX, CY), F32),
            pltpu.VMEM((NZL + 2, CXE, CY), F32),
            pltpu.VMEM((NZL, CX, CY), F32),
            pltpu.VMEM((EBD, EB, EB), F32),
            pltpu.VMEM((EBD, EB, EB), F32),
            pltpu.VMEM((PAIRS, 2 * EB, 2 * EB), BF16),
            pltpu.VMEM((PAIRS, 2 * EB, 2 * EB), BF16),
            pltpu.VMEM((PAIRS, EB, 2 * EB), BF16),
            pltpu.VMEM((2, NV + 1, NZL, CY), F32),
            pltpu.VMEM((sweeps, 2, NV + 1, NZL, CY), F32),
            pltpu.VMEM((CX, CY), F32),
            pltpu.VMEM((sweeps, 2, CX, CY), F32),
            pltpu.VMEM((CX, CY), F32),
            pltpu.VMEM((sweeps, NV, CX, CY), F32),
            pltpu.VMEM((CXE, CY), F32),
            pltpu.VMEM((CAP * NFX, CY), F32),
            pltpu.VMEM((CAP * NFX, CY), F32),
            pltpu.VMEM((5, CAP * NFX, CY), F32),
            pltpu.VMEM((ITERS + 1, FACES, CY), F32),
            pltpu.VMEM((5, FACES, CY), F32),
            pltpu.VMEM((FACES, CY), F32),
            pltpu.VMEM((ITERS, CAP * NFX, CY), F32),
            pltpu.VMEM((EBD, FACES), F32),
            pltpu.VMEM((FACES, EBD), F32),
            pltpu.VMEM((CAP * NFX, CX), F32),
            pltpu.VMEM((CX, CAP * NFX), F32),
            pltpu.VMEM((EBD, EB), F32),
            pltpu.VMEM((EBD, EB), F32),
            pltpu.VMEM((EBD, EB), F32),
            pltpu.VMEM((EBD, EB), F32),
            pltpu.VMEM((ITERS + 1, 3, CXE, CY), F32),
            pltpu.VMEM((2, CXE, CY), F32),
            pltpu.VMEM((2, CX, CY), F32),
            pltpu.VMEM((NZL + 2, CXE, CY), F32),
            pltpu.VMEM((CX, CY), F32),
            pltpu.VMEM((AROUND, FACES, NFX * EBD), BF16),
            pltpu.VMEM((AROUND, FACES, CY), F32),
            pltpu.VMEM((FACES, CY), F32),
            pltpu.VMEM((EBD, EB), F32),
            pltpu.VMEM((ITERS - 1, NFX * EBD, EB), F32),
            dma((11,)),
            dma((sweeps, 5)),
            dma((sweeps, 5)),
            dma((ITERS + 1,)),
            dma((ITERS + 1,)),
            dma((ITERS,)),
            dma((ITERS,)),
            dma((NFY,)),
            dma((2,)),
            dma((ITERS + 1, 8)),
            dma((ITERS + 1, 8)),
            dma((ITERS,)),
            dma((ITERS,)),
            dma,
            dma((2,)),
            dma((ITERS - 1,)),
            dma((ITERS - 1,)),
        ],
        compiler_params=pltpu.CompilerParams(
            collective_id=0, has_side_effects=True, vmem_limit_bytes=60 * 1024 * 1024
        ),
    )(
        state, kappa, mix, press_weight, source_weight, interp, block_inverse, coupling, front_order,
        face_owner.reshape(1, -1), face_slot.reshape(1, -1),
    )
    return pl.pallas_call(
        last_add,
        out_shape=(
            jax.ShapeDtypeStruct(state.shape, F32),
            jax.ShapeDtypeStruct((EBD, EB), F32),
        ),
        in_specs=[hbm] * 4,
        out_specs=(hbm, hbm),
        scratch_shapes=[
            pltpu.VMEM((NV, NZL, CX, CY), F32),
            pltpu.VMEM((NZL, CX, CY), F32),
            pltpu.VMEM((EBD, EB), F32),
            pltpu.SMEM((NV,), F32),
            dma((NV + 3,)),
            dma((NV + 1,)),
        ],
        compiler_params=pltpu.CompilerParams(vmem_limit_bytes=60 * 1024 * 1024),
    )(before, raised, source_weight, displacement)


def solution(mesh):
    return jax.shard_map(
        on_device,
        mesh=mesh,
        in_specs=(
            P(None, "fz", "fx", "fy"),
            P("fz", "fx", "fy"),
            P(),
            P(),
            P(),
            P(),
            P("fx", None, None),
            P("fx", None, None),
            P("fx", None),
            P(("fx", "fy"), None),
            P(("fx", "fy")),
        ),
        out_specs=(P(None, "fz", "fx", "fy"), P("fx", None)),
        check_vma=False,
    )
```

```python
import jax
import jax.numpy as jnp
from jax import lax
from jax.experimental import pallas as pl
from jax.experimental.pallas import tpu as pltpu
from jax.sharding import PartitionSpec as P

ITERS = 3
DIFFUSION = 0.16
HIGHEST = lax.Precision.HIGHEST
MESH = pl.DeviceIdType.MESH
F32 = jnp.float32
BF16 = jnp.bfloat16

NV, NZL, CX, CY = 5, 8, 32, 128
NZ = 16
NFX, NFY = 32, 4
RING_Z, RING_Y = 8, 4
EB, EBD, CAP = 128, 16, 2
PAIRS = EBD // 2
FACES = NFX * NFY * CAP
PAD = 8
CXE = CX + 2 * PAD
NT = (((1,), (1,)), ((), ()))
FAR_Y = (2, 1, 3, 0)
AROUND = 11


def far_first(step, ring):
    return ring // 2 + (1 - 2 * (step % 2)) * ((step + 1) // 2)


def split(values):
    high = values.astype(BF16)
    return high, (values - high.astype(F32)).astype(BF16)


def pick(selector, values):
    high, low = split(values)
    return jnp.dot(selector, high, preferred_element_type=F32) + jnp.dot(selector, low, preferred_element_type=F32)


def kernel(
    state_in, kappa_in, mix_in, press_in, source_in, interp_in, inverse_in, coupling_in, order_in, owner_in, slot_in,
    state_out, raised_out, disp_out,
    mix, press_weight, source_weight, interp, order, owner, slot,
    S, K, KX, KE, BI, CO, R, RO, RN, XS, XR, YS, YR, YK, ZR, KZ, SL, SF, CS, RF, RC, SD, RD, FP, FPT, AM, AT, FR, XV, DV, DR,
    WN, LP, LE, QB, PB, G, GW, IN, XO, XA,
    load_sem, hsend, hrecv, fsend, frecv, dsend, drecv, osend, orecv, wsend, wrecv, rsend, rrecv, csend, crecv, xsend, xrecv,
):
    ix, iy, iz = lax.axis_index("fx"), lax.axis_index("fy"), lax.axis_index("fz")
    ring_z, ring_y = ix // RING_Y, ix % RING_Y
    on_wall = iz == 0
    off_wall = iz == 1
    home = (ring_y + ring_z) % NFY
    is_solver = iy == home
    not_solver = jnp.logical_not(is_solver)
    turned_y = {d: (ring_y + d) % RING_Y for d in FAR_Y}
    turned_x = {d: (iy + d) % NFY for d in FAR_Y}
    answer_x = ((iy + 2 - iz) % NFY, (iy + 3 * iz) % NFY)

    def row_base(step):
        return ((ring_z + far_first(step, RING_Z)) % RING_Z) * RING_Y

    def homes(z):
        return {d: (turned_y[d] + z) % NFY for d in FAR_Y}

    def owners_at(step):
        z = (ring_z + far_first(step, RING_Z)) % RING_Z
        return [(z * RING_Y + turned_y[d], home_y) for d, home_y in homes(z).items()]

    near_owners = [(ring_z * RING_Y + turned_y[d], home_y) for d, home_y in homes(ring_z).items()][:3]

    def signal(barrier, device):
        pl.semaphore_signal(barrier, inc=1, device_id=device, device_id_type=MESH)

    loads = [
        pltpu.make_async_copy(source, target, load_sem.at[n])
        for n, (source, target) in enumerate(
            (
                (owner_in, owner),
                (slot_in, slot),
                (order_in, order),
                (kappa_in, K),
                (state_in, S.at[0, :, pl.ds(1, NZL)]),
                (inverse_in, BI),
                (coupling_in, CO),
                (interp_in, interp),
                (mix_in, mix),
                (press_in, press_weight),
                (source_in, source_weight),
            )
        )
    ]
    for load in loads:
        load.start()

    barrier = pltpu.get_barrier_semaphore()
    has_left, has_right, has_front, has_back = ix > 0, ix < NFX - 1, iy > 0, iy < NFY - 1
    sides = (
        (has_left, (ix - 1, iy, iz)),
        (has_right, (ix + 1, iy, iz)),
        (has_front, (ix, iy - 1, iz)),
        (has_back, (ix, iy + 1, iz)),
    )
    corners = (
        (jnp.logical_and(has_left, has_front), (ix - 1, iy - 1, iz)),
        (jnp.logical_and(has_left, has_back), (ix - 1, iy + 1, iz)),
        (jnp.logical_and(has_right, has_front), (ix + 1, iy - 1, iz)),
        (jnp.logical_and(has_right, has_back), (ix + 1, iy + 1, iz)),
    )
    other_core = (ix, iy, 1 - iz)

    @pl.when(is_solver)
    def _():
        def greet(step, carry):
            base = row_base(step)
            for dy in FAR_Y:
                for dx in FAR_Y:
                    signal(barrier, (base + turned_y[dy], turned_x[dx], 0))
            return carry

        lax.fori_loop(0, RING_Z - 1, greet, 0)
        for dy in FAR_Y:
            for dx in FAR_Y:
                if dy or dx:
                    signal(barrier, (ring_z * RING_Y + turned_y[dy], turned_x[dx], 0))

        @pl.when(off_wall)
        def _():
            signal(barrier, (ix, iy, 0))

        def greet_solvers(step, carry):
            for to, home_y in owners_at(step):
                signal(barrier, (to, home_y, iz))
            return carry

        lax.fori_loop(0, RING_Z - 1, greet_solvers, 0)
        for to, home_y in near_owners:
            signal(barrier, (to, home_y, iz))

    @pl.when(on_wall)
    def _():
        def greet(step, carry):
            for to, home_y in owners_at(step):
                signal(barrier, (to, home_y, (iy + home_y) % 2))
            return carry

        lax.fori_loop(0, RING_Z - 1, greet, 0)
        for to, home_y in near_owners:
            signal(barrier, (to, home_y, (iy + home_y) % 2))

        @pl.when(not_solver)
        def _():
            signal(barrier, (ix, home, (iy + home) % 2))

    @pl.when(not_solver)
    def _():
        signal(barrier, (ix, home, iz))

    for ref in (XR, YR, WN):
        ref[...] = jnp.zeros_like(ref)

    signal(barrier, other_core)
    solver_count = is_solver.astype(jnp.int32)
    wall_count = on_wall.astype(jnp.int32)
    expected = 1 + wall_count * (2 * NFX - solver_count) + solver_count * (2 * NFX - wall_count + NFY - 1 + NFX - 1)
    for present, device in sides + corners:
        expected = expected + present.astype(jnp.int32)

        @pl.when(present)
        def _():
            signal(barrier, device)

    zero_plane = jnp.zeros((NV, CX, CY), F32)
    for buffer in range(2):
        S[buffer, :, 0] = zero_plane
        S[buffer, :, NZL + 1] = zero_plane

    for load in loads[:3]:
        load.wait()
    rows = lax.broadcasted_iota(jnp.int32, (CAP * NFX, CX), 0)
    named = (owner[...] == rows // CAP).astype(F32)
    earlier = (
        lax.broadcasted_iota(jnp.int32, (CX, CX), 0) < lax.broadcasted_iota(jnp.int32, (CX, CX), 1)
    ).astype(BF16)
    rank = jnp.dot(named.astype(BF16), earlier, preferred_element_type=F32)
    chosen = jnp.where(rank == (rows % CAP).astype(F32), named, 0.0)
    AM[...] = chosen
    unit = (lax.broadcasted_iota(jnp.int32, (CX, CX), 0) == lax.broadcasted_iota(jnp.int32, (CX, CX), 1)).astype(F32)
    AT[...] = lax.dot_general(unit, chosen, NT, preferred_element_type=F32)
    slot_rows = jnp.sum(chosen * (slot[...] + 1).astype(F32), axis=1, keepdims=True)
    SL[...] = jnp.broadcast_to(slot_rows, (CAP * NFX, CY))
    target_of = jnp.sum(unit * (EBD * owner[...] + slot[...] + 1).astype(F32), axis=1, keepdims=True)
    WN[ITERS, 1, PAD : PAD + CX] = jnp.broadcast_to(target_of, (CX, CY))
    block_rows = lax.broadcasted_iota(jnp.int32, (EBD, EB), 0)
    block_lanes = lax.broadcasted_iota(jnp.int32, (EBD, EB), 1)
    placed = jnp.zeros((EBD, EB), F32)
    for k in range(EBD):
        placed = jnp.where(jnp.logical_and(block_rows == k, block_lanes == order[0, k]), 1.0, placed)

    lane = lax.broadcasted_iota(jnp.int32, (CX, CY), 1)
    row = lax.broadcasted_iota(jnp.int32, (CX, CY), 0)
    for load in loads[3:5]:
        load.wait()

    pair = lane // 2

    def put_ends(ends, centre, at):
        return jnp.where(pair == at, pltpu.roll(centre, 2 * at + 1, 1), ends)

    def take_ends(n):
        return jnp.where(lane % 2 == 0, pltpu.roll(YR[n, 1], CY - 1, 1), pltpu.roll(YR[n, 0], 1, 1))

    def kappa_faces(z, ends):
        coeff = DIFFUSION * K[z]
        KX[z + 1, PAD : PAD + CX] = coeff
        XS[0, NV, pl.ds(z, 1), :] = coeff[0:1]
        XS[1, NV, pl.ds(z, 1), :] = coeff[CX - 1 : CX]
        return put_ends(ends, coeff, NV * NZL + z)

    YK[...] = lax.fori_loop(0, NZL, kappa_faces, jnp.zeros((CX, CY), F32))

    def pack(src):
        def plane(z, ends):
            for c in range(NV):
                centre = src[c, z + 1]
                XS[0, c, pl.ds(z, 1), :] = centre[0:1]
                XS[1, c, pl.ds(z, 1), :] = centre[CX - 1 : CX]
                ends = put_ends(ends, centre, c * NZL + z)
            return ends

        YS[...] = lax.fori_loop(0, NZL, plane, YK[...])

    edge = NZL - (NZL - 1) * iz

    def halo_copies(n, src):
        def remote(source, target, at, there, device):
            return pltpu.make_async_remote_copy(
                source, target, hsend.at[n, at], hrecv.at[n, there], device_id=device, device_id_type=MESH
            )

        (_, left), (_, right), (_, front), (_, back) = sides
        always = iz >= 0
        plane = src.at[:, edge]
        sends = (
            (has_left, remote(XS.at[0], XR.at[n, 1], 0, 1, left)),
            (has_right, remote(XS.at[1], XR.at[n, 0], 1, 0, right)),
            (has_front, remote(YS, YR.at[n, 1], 2, 3, front)),
            (has_back, remote(YS, YR.at[n, 0], 3, 2, back)),
            (always, remote(plane, ZR.at[n], 4, 4, other_core)),
        )
        waits = (
            (has_left, remote(XS.at[0], XR.at[n, 0], 0, 0, left)),
            (has_right, remote(XS.at[1], XR.at[n, 1], 1, 1, right)),
            (has_front, remote(YS, YR.at[n, 0], 2, 2, front)),
            (has_back, remote(YS, YR.at[n, 1], 3, 3, back)),
            (always, remote(plane, ZR.at[n], 4, 4, other_core)),
        )
        return sends, waits

    def each(copies, action):
        for present, copy in copies:

            @pl.when(present)
            def _():
                action(copy)

    def start_halo(n, src):
        each(halo_copies(n, src)[0], lambda copy: copy.start())

    def finish_halo(n, src):
        _, waits = halo_copies(n, src)
        each(waits, lambda copy: copy.wait_recv())
        src[:, (NZL + 1) * (1 - iz)] = ZR[n]

    def sweep(n, src, dst, first=0, end=NZL):
        outer = take_ends(n)

        def plane(z, carry):
            coeff = KX[z + 1, PAD : PAD + CX]
            centres = [src[c, z + 1] for c in range(NV)]
            for c in range(NV):
                centre = centres[c]
                at = c * NZL + z
                beside = src[c, z] + src[c, z + 2]
                beside += jnp.where(row == 0, XR[n, 0, c, pl.ds(z, 1), :], pltpu.roll(centre, 1, 0))
                beside += jnp.where(row == CX - 1, XR[n, 1, c, pl.ds(z, 1), :], pltpu.roll(centre, CX - 1, 0))
                ends = pltpu.roll(outer, CY - 1 - 2 * at, 1)
                beside += jnp.where(lane == 0, ends, pltpu.roll(centre, 1, 1))
                beside += jnp.where(lane == CY - 1, ends, pltpu.roll(centre, CY - 1, 1))
                total = centre + coeff * (beside - 6.0 * centre)
                for d in range(NV):
                    total += mix[c, d] * centres[d]
                dst[c, z + 1] = total
            return carry

        lax.fori_loop(first, end, plane, 0)
        if end == NZL:
            each(halo_copies(n, src)[0], lambda copy: copy.wait_send())

    kappa_plane = pltpu.make_async_remote_copy(
        KX.at[edge], KZ, osend.at[0], orecv.at[0], device_id=other_core, device_id_type=MESH
    )

    def send_to_solvers(rows_of, target, sent, heard):
        def send(to, y, core):
            pltpu.make_async_remote_copy(
                rows_of(to), target, sent, heard, device_id=(to, y, core), device_id_type=MESH
            ).start()

        def group(step, carry):
            for to, home_y in owners_at(step):
                for core in range(2):
                    send(to, home_y, core)
            return carry

        @pl.when(on_wall)
        def _():
            lax.fori_loop(0, RING_Z - 1, group, 0)
            for to, home_y in near_owners:
                for core in range(2):
                    send(to, home_y, core)
            send(ix, home, 1)

            @pl.when(not_solver)
            def _():
                send(ix, home, 0)

            @pl.when(is_solver)
            def _():
                pltpu.make_async_copy(rows_of(ix), target, heard).start()

    own_rows = pl.ds(CAP * (ix * NFY + iy), CAP)

    def send_rows(turn, rows_out):
        send_to_solvers(
            lambda to: rows_out.at[pl.ds(CAP * to, CAP)], RF.at[turn, own_rows], fsend.at[turn], frecv.at[turn]
        )

    def send_pressure(turn):
        @pl.when(on_wall)
        def _():
            SF[...] = pick(AM[...].astype(BF16), PB[...])

        send_rows(turn, SF)

    def sent_to_solvers(turn):
        @pl.when(on_wall)
        def _():
            @pl.when(is_solver)
            def _():
                rest = RF.at[turn, pl.ds(0, CAP * (2 * NFX - 1))]
                pltpu.make_async_copy(rest, rest, fsend.at[turn]).wait()

            @pl.when(not_solver)
            def _():
                rest = RF.at[turn, pl.ds(0, CAP * 2 * NFX)]
                pltpu.make_async_copy(rest, rest, fsend.at[turn]).wait()

    def heard_from_faces(turn):
        whole = RF.at[turn]
        pltpu.make_async_copy(whole, whole, frecv.at[turn]).wait()

    def send_to_faces(turn):
        target = RD.at[turn, pl.ds(CAP * ix, CAP)]

        def send(to_x, to_y):
            pltpu.make_async_remote_copy(
                SD.at[pl.ds(CAP * (to_x * NFY + to_y), CAP)], target, dsend.at[turn], drecv.at[turn],
                device_id=(to_x, to_y, 0), device_id_type=MESH,
            ).start()

        def group(step, carry):
            base = row_base(step)
            for dy in FAR_Y:
                for x in answer_x:
                    send(base + turned_y[dy], x)
            return carry

        lax.fori_loop(0, RING_Z - 1, group, 0)
        for dy in FAR_Y[:3]:
            for x in answer_x:
                send(ring_z * RING_Y + turned_y[dy], x)
        send(ix, answer_x[0])

        @pl.when(off_wall)
        def _():
            send(ix, answer_x[1])

        @pl.when(on_wall)
        def _():
            pltpu.make_async_copy(SD.at[pl.ds(CAP * (ix * NFY + iy), CAP)], target, drecv.at[turn]).start()

    def sent_to_faces(turn):
        @pl.when(on_wall)
        def _():
            rest = RF.at[turn, pl.ds(0, CAP * (2 * NFX - 1))]
            pltpu.make_async_copy(rest, rest, dsend.at[turn]).wait()

        @pl.when(off_wall)
        def _():
            rest = RF.at[turn, pl.ds(0, CAP * 2 * NFX)]
            pltpu.make_async_copy(rest, rest, dsend.at[turn]).wait()

    for load in loads[5:]:
        load.wait()

    @pl.when(is_solver)
    def _():
        def parts(k):
            block = order[0, k]
            inverse = BI[block]
            force_part = lax.dot_general(interp[...], inverse, NT, precision=HIGHEST, preferred_element_type=F32)
            chain = jnp.dot(inverse, CO[block], precision=HIGHEST, preferred_element_type=F32)
            return force_part, -chain.T

        def both_parts(matrix):
            high, low = split(matrix)
            return jnp.concatenate([high, low], axis=1)

        def products(m, carry):
            force, chain = parts(2 * m)
            next_force, next_chain = parts(2 * m + 1)
            passed = jnp.dot(force, next_chain, precision=HIGHEST, preferred_element_type=F32)
            leap = jnp.dot(chain, next_chain, precision=HIGHEST, preferred_element_type=F32)
            R[m] = both_parts(jnp.concatenate([force, chain], axis=0))
            RO[m] = both_parts(jnp.concatenate([next_force, passed], axis=0))
            RN[m] = both_parts(leap)
            return carry

        lax.fori_loop(0, PAIRS, products, 0)

    numbers = range(NV)
    source = [source_weight[c] for c in numbers]
    once = [source[c] + sum(mix[c, d] * source[d] for d in numbers) for c in numbers]
    twice = [once[c] + sum(mix[c, d] * once[d] for d in numbers) for c in numbers]
    press_source = sum(press_weight[c] * source[c] for c in numbers)
    press_once = sum(press_weight[c] * once[c] for c in numbers)
    press_twice = sum(press_weight[c] * twice[c] for c in numbers)

    inner = slice(PAD, PAD + CX)

    def wall_copies(it):
        def remote(n, opposite, source_row, side, target_row, count, device):
            copy = lambda here, there: pltpu.make_async_remote_copy(
                WN.at[it, 1, pl.ds(source_row, count)], WN.at[it, side, pl.ds(target_row, count)],
                wsend.at[it, here], wrecv.at[it, there], device_id=device, device_id_type=MESH,
            )
            return copy(n, opposite), copy(n, n)

        low, high = PAD, PAD + CX - 8
        (_, left), (_, right), (_, front), (_, back) = sides
        (lf, left_front), (lb, left_back), (rf, right_front), (rb, right_back) = corners
        return (
            (has_left, remote(0, 1, low, 1, PAD + CX, 8, left)),
            (has_right, remote(1, 0, high, 1, 0, 8, right)),
            (has_front, remote(2, 3, PAD, 2, PAD, CX, front)),
            (has_back, remote(3, 2, PAD, 0, PAD, CX, back)),
            (lf, remote(4, 7, low, 2, PAD + CX, 8, left_front)),
            (lb, remote(5, 6, low, 0, PAD + CX, 8, left_back)),
            (rf, remote(6, 5, high, 2, 0, 8, right_front)),
            (rb, remote(7, 4, high, 0, 0, 8, right_back)),
        )

    def tell_faces():
        targets = (
            [pltpu.roll(WN[ITERS, 1], (CXE - d) % CXE, 0)[inner] for d in range(-2, 3)]
            + [pltpu.roll(WN[ITERS, 0], (CXE - d) % CXE, 0)[inner] for d in range(-1, 2)]
            + [pltpu.roll(WN[ITERS, 2], (CXE - d) % CXE, 0)[inner] for d in range(-1, 2)]
        )
        facts = targets + [
            jnp.broadcast_to(KE[0, :, CY - 1 : CY], (CX, CY)), jnp.broadcast_to(KE[0, :, 0:1], (CX, CY)),
        ]
        table = jnp.zeros((CX, CY), F32)
        for n, fact in enumerate(facts):
            table = jnp.where(lane == n, fact, table)
        wall_coeff = KX[1]
        selector = AM[...].astype(BF16)
        CS[0] = pick(selector, table)
        for n, d in enumerate((-1, 0, 1)):
            CS[n + 1] = pick(selector, pltpu.roll(wall_coeff, (CXE - d) % CXE, 0)[inner])
        CS[4] = pick(selector, KX[2, inner])

    half = FACES // 2
    facts_core = ix // (NFX // 2)
    facts_here = jnp.logical_and(is_solver, facts_core == iz)

    def send_facts():
        def send(to, home_y):
            pltpu.make_async_remote_copy(
                CS.at[:, pl.ds(CAP * to, CAP)], RC.at[:, own_rows], csend, crecv.at[0],
                device_id=(to, home_y, facts_core), device_id_type=MESH,
            ).start()

        def group(step, carry):
            for to, home_y in owners_at(step):
                send(to, home_y)
            return carry

        @pl.when(on_wall)
        def _():
            lax.fori_loop(0, RING_Z - 1, group, 0)
            for to, home_y in near_owners:
                send(to, home_y)

            @pl.when(facts_here)
            def _():
                pltpu.make_async_copy(CS.at[:, pl.ds(CAP * ix, CAP)], RC.at[:, own_rows], crecv.at[0]).start()

            @pl.when(jnp.logical_not(facts_here))
            def _():
                send(ix, home)

    share_facts = pltpu.make_async_remote_copy(
        RC.at[:, pl.ds(half * iz, half)], RC.at[:, pl.ds(half * iz, half)], csend, crecv.at[1],
        device_id=other_core, device_id_type=MESH,
    )

    around_wall = wall_copies(ITERS)
    pack(S.at[0])
    pl.semaphore_wait(barrier, expected)
    start_halo(0, S.at[0])

    @pl.when(on_wall)
    def _():
        each(around_wall, lambda pair: pair[0].start())

    kappa_plane.start()
    send_rows(ITERS, SL)
    finish_halo(0, S.at[0])
    sweep(0, S.at[0], S.at[1])
    pack(S.at[1])
    start_halo(1, S.at[1])

    kappa_plane.wait()
    KX[(NZL + 1) * (1 - iz)] = KZ[...]
    KX[(NZL + 1) * iz] = jnp.zeros((CXE, CY), F32)
    tile_row = lax.broadcasted_iota(jnp.int32, (PAD, CY), 0)

    ends = take_ends(0)

    def kappa_edges(z, carry):
        KX[z + 1, 0:PAD] = jnp.where(tile_row == PAD - 1, XR[0, 0, NV, pl.ds(z, 1), :], 0.0)
        KX[z + 1, PAD + CX : CXE] = jnp.where(tile_row == 0, XR[0, 1, NV, pl.ds(z, 1), :], 0.0)
        at = 2 * (NV * NZL + z)
        front = pltpu.roll(ends, CY - 2 - at, 1)
        back = pltpu.roll(ends, CY - at, 1)
        KE[z] = jnp.where(lane >= CY // 2, front, back)
        return carry

    lax.fori_loop(0, NZL, kappa_edges, 0)

    def wall_base():
        @pl.when(on_wall)
        def _():
            pressure = press_weight[0] * S[0, 0, 1]
            for c in range(1, NV):
                pressure += press_weight[c] * S[0, c, 1]
            PB[...] = pressure

    finish_halo(1, S.at[1])
    sweep(1, S.at[1], S.at[0], 0, 1)
    wall_base()
    send_pressure(0)
    sweep(1, S.at[1], S.at[0], 1, NZL)
    sent_to_solvers(ITERS)


    @pl.when(is_solver)
    def _():
        heard_from_faces(ITERS)
        face_lanes = lax.broadcasted_iota(jnp.int32, (FACES, EB), 1) + 1
        slot_of = (RF[ITERS] == face_lanes.astype(F32)).astype(F32)
        FP[...] = lax.dot_general(placed, slot_of, NT, preferred_element_type=F32)
        FPT[...] = lax.dot_general(slot_of, placed, NT, preferred_element_type=F32)

    def times(row_in, matrix):
        width = row_in.shape[1]
        high = row_in.astype(BF16).astype(F32)
        at = lax.broadcasted_iota(jnp.int32, (8, width), 0)
        left = jnp.where(at == 0, high, jnp.where(at == 1, row_in - high, 0.0)).astype(BF16)
        result = jnp.dot(left, matrix, preferred_element_type=F32)
        summed = result[:, :EB] + result[:, EB:]
        return summed[0:1] + summed[1:2]

    def solve():
        force = [FR[pl.ds(k, 1), :] for k in range(EBD)]
        odd = [times(jnp.concatenate([force[2 * m + 1], force[2 * m]], axis=1), RO[m]) for m in range(PAIRS)]
        for m in range(PAIRS):
            if m:
                odd[m] += times(odd[m - 1], RN[m])
            XV[pl.ds(2 * m + 1, 1), :] = odd[m]
            previous = odd[m - 1] if m else jnp.zeros((1, EB), F32)
            XV[pl.ds(2 * m, 1), :] = times(jnp.concatenate([force[2 * m], previous], axis=1), R[m])

    lane_e = lax.broadcasted_iota(jnp.int32, (CXE, CY), 1)

    def spread(it):
        centre = WN[it, 1]
        beyond = jnp.where(lane_e >= CY // 2, WN[it, 0], WN[it, 2])
        up, down = pltpu.roll(centre, 1, 1), pltpu.roll(centre, CY - 1, 1)
        out_up, out_down = pltpu.roll(beyond, 1, 1), pltpu.roll(beyond, CY - 1, 1)
        lap = pltpu.roll(centre, 1, 0) + pltpu.roll(centre, CXE - 1, 0) - 4.0 * centre
        lap += jnp.where(lane_e == 0, out_up, up) + jnp.where(lane_e == CY - 1, out_down, down)
        lap_e = pltpu.roll(beyond, 1, 0) + pltpu.roll(beyond, CXE - 1, 0) - 4.0 * beyond
        lap_e += jnp.where(lane_e >= CY // 2, out_up + down, out_down + up)
        LP[0], LP[1] = lap, centre
        LE[0], LE[1] = lap_e[inner], beyond[inner]

    def ring_sum(wide, edge_columns, below, above, coeff):
        own = wide[inner]
        total = pltpu.roll(wide, 1, 0)[inner] + pltpu.roll(wide, CXE - 1, 0)[inner] + below + above - 6.0 * own
        total += jnp.where(lane == 0, pltpu.roll(edge_columns, 1, 1), pltpu.roll(own, 1, 1))
        total += jnp.where(lane == CY - 1, pltpu.roll(edge_columns, CY - 1, 1), pltpu.roll(own, CY - 1, 1))
        return coeff * total

    first_jump = (NZ - 1.0) / NZ - 2.0

    def profile(plane):
        height = iz * NZL + plane - 1
        return 1.0 - height.astype(F32) / NZ, jnp.where(height == 0, first_jump, 0.0)

    def update():
        def first(plane, carry):
            share, jump = profile(plane)
            QB[plane] = KX[plane] * (share * LP[0] + jump * LP[1])
            return carry

        lax.fori_loop(0, NZL + 2, first, 0)

        def second(z, carry):
            share, jump = profile(z + 1)
            edges = KE[z] * (share * LE[0] + jump * LE[1])
            wide = QB[z + 1]
            bend = ring_sum(wide, edges, QB[z, inner], QB[z + 2, inner], KX[z + 1, inner])
            raised, slope = share * LP[1, inner], wide[inner]
            for c in range(NV):
                S[0, c, z + 1] += twice[c] * raised + 2.0 * once[c] * slope + source[c] * bend
            return carry

        lax.fori_loop(0, NZL, second, 0)

    def sent_facts():
        @pl.when(on_wall)
        def _():
            @pl.when(facts_here)
            def _():
                rest = RC.at[:, pl.ds(0, CAP * (NFX - 1))]
                pltpu.make_async_copy(rest, rest, csend).wait()

            @pl.when(jnp.logical_not(facts_here))
            def _():
                rest = RC.at[:, pl.ds(0, CAP * NFX)]
                pltpu.make_async_copy(rest, rest, csend).wait()

    def pass_facts():
        mine = RC.at[:, pl.ds(half * iz, half)]
        pltpu.make_async_copy(mine, mine, crecv.at[0]).wait()
        share_facts.start()

    def hear_facts():
        share_facts.wait()
        names = lax.broadcasted_iota(jnp.int32, (FACES, NFX * EBD), 1) + 1
        names = names.astype(F32)
        for m in range(AROUND):
            G[m] = jnp.where(names == RC[0, :, m : m + 1], 1.0, 0.0).astype(BF16)

    def tell_solvers(it, facing):
        if it:
            rest = XA.at[0, pl.ds(0, (NFX - 1) * EBD)]
            pltpu.make_async_copy(rest, rest, xsend.at[it - 1]).wait()
        own = pick(placed.T[:EBD].astype(BF16), facing)
        XO[...] = own
        XA[it, pl.ds(EBD * ix, EBD)] = own

        def send(to, y):
            pltpu.make_async_remote_copy(
                XO, XA.at[it, pl.ds(EBD * ix, EBD)], xsend.at[it], xrecv.at[it],
                device_id=(to, y, iz), device_id_type=MESH,
            ).start()

        def group(step, carry):
            for to, home_y in owners_at(step):
                send(to, home_y)
            return carry

        lax.fori_loop(0, RING_Z - 1, group, 0)
        for to, home_y in near_owners:
            send(to, home_y)

    def respond(it):
        rest = XA.at[it, pl.ds(0, (NFX - 1) * EBD)]
        pltpu.make_async_copy(rest, rest, xrecv.at[it]).wait()
        high, low = split(XA[it])
        both = jnp.concatenate([high, low], axis=1)
        for m in range(AROUND):
            found = jnp.dot(G[m], both, preferred_element_type=F32)
            GW[m] = found[:, :CY] + found[:, CY:]

        def chunk(n, carry):
            at = pl.ds(pl.multiple_of(n * CX, CX), CX)
            centre = {d: GW[d + 2, at] for d in range(-2, 3)}
            beyond = {d: jnp.where(lane >= CY // 2, GW[d + 6, at], GW[d + 9, at]) for d in range(-1, 2)}
            coeff = {d: RC[d + 2, at] for d in range(-1, 2)}

            def wide_sum(d):
                total = centre[d - 1] + centre[d + 1] - 4.0 * centre[d]
                total += jnp.where(lane == 0, pltpu.roll(beyond[d], 1, 1), pltpu.roll(centre[d], 1, 1))
                return total + jnp.where(
                    lane == CY - 1, pltpu.roll(beyond[d], CY - 1, 1), pltpu.roll(centre[d], CY - 1, 1)
                )

            sums = {d: wide_sum(d) for d in range(-1, 2)}
            slopes = {d: coeff[d] * (sums[d] + first_jump * centre[d]) for d in range(-1, 2)}
            above = RC[4, at] * ((NZ - 1.0) / NZ * sums[0])
            facts = RC[0, at]
            edge_coeff = jnp.where(lane >= CY // 2, facts[:, AROUND : AROUND + 1], facts[:, AROUND + 1 : AROUND + 2])
            edge_sum = beyond[-1] + beyond[1] - 4.0 * beyond[0]
            edge_sum += jnp.where(
                lane >= CY // 2,
                pltpu.roll(beyond[0], 1, 1) + pltpu.roll(centre[0], CY - 1, 1),
                pltpu.roll(beyond[0], CY - 1, 1) + pltpu.roll(centre[0], 1, 1),
            )
            edges = edge_coeff * (edge_sum + first_jump * beyond[0])
            bend = slopes[-1] + slopes[1] + above - 6.0 * slopes[0]
            bend += jnp.where(lane == 0, pltpu.roll(edges, 1, 1), pltpu.roll(slopes[0], 1, 1))
            bend += jnp.where(lane == CY - 1, pltpu.roll(edges, CY - 1, 1), pltpu.roll(slopes[0], CY - 1, 1))
            IN[at] = press_twice * centre[0] + 2.0 * press_once * slopes[0] + press_source * coeff[0] * bend
            return carry

        lax.fori_loop(0, FACES // CX, chunk, 0)

    def answer(it):
        heard_from_faces(it)
        if it:
            sent_to_faces(it - 1)
        rows_in = RF[it] + IN[...] if it else RF[it]
        FR[...] = pick(FP[...].astype(BF16), rows_in)
        solve()
        facing = lax.dot_general(XV[...], interp[...], NT, precision=HIGHEST, preferred_element_type=F32)
        if 0 < it < ITERS - 1:
            tell_solvers(it, facing)
        SD[...] = pick(FPT[...].astype(BF16), facing)
        send_to_faces(it)
        if it == 0:
            tell_solvers(it, facing)

    def hear_wall(it):
        whole = RD.at[it]
        pltpu.make_async_copy(whole, whole, drecv.at[it]).wait()
        WN[it, 1, inner] = pick(AT[...].astype(BF16), RD[it])

    def relay(it, part):
        return pltpu.make_async_remote_copy(
            part, part, rsend.at[it], rrecv.at[it], device_id=other_core, device_id_type=MESH
        )

    for it in range(ITERS - 1):
        n = 2 * it + 2
        pack(S.at[0])
        start_halo(n, S.at[0])
        if it == 0:

            @pl.when(on_wall)
            def _():
                each(around_wall, lambda pair: pair[1].wait_recv())
                tell_faces()
                each(around_wall, lambda pair: pair[0].wait_send())

            send_facts()
        else:

            @pl.when(is_solver)
            def _():
                answer(it)

        finish_halo(n, S.at[0])
        sweep(n, S.at[0], S.at[1])
        pack(S.at[1])
        start_halo(n + 1, S.at[1])
        if it == 0:
            sent_facts()

            @pl.when(is_solver)
            def _():
                answer(it)
                pass_facts()

        finish_halo(n + 1, S.at[1])
        sweep(n + 1, S.at[1], S.at[0], 0, 1)
        wall_base()
        sent_to_solvers(it)
        send_pressure(it + 1)
        sweep(n + 1, S.at[1], S.at[0], 1, NZL)
        if it == 0:

            @pl.when(is_solver)
            def _():
                hear_facts()

        copies = wall_copies(it)

        @pl.when(on_wall)
        def _():
            hear_wall(it)
            each(copies, lambda pair: pair[0].start())

        @pl.when(is_solver)
        def _():
            respond(it)

        beside_wall = relay(it, WN.at[it])

        @pl.when(on_wall)
        def _():
            each(copies, lambda pair: pair[1].wait_recv())
            beside_wall.start()

        @pl.when(off_wall)
        def _():
            beside_wall.wait_recv()

        spread(it)
        update()

        @pl.when(on_wall)
        def _():
            each(copies, lambda pair: pair[0].wait_send())
            beside_wall.wait_send()

    last = ITERS - 1
    out = pltpu.make_async_copy(S.at[0, :, pl.ds(1, NZL)], state_out, load_sem.at[0])
    out.start()

    def disp_copy(t):
        return pltpu.make_async_remote_copy(
            DV, DR, osend.at[t], orecv.at[1], device_id=(ix, (iy + t) % NFY, iz), device_id_type=MESH
        )

    @pl.when(is_solver)
    def _():
        answer(last)
        back = lax.dot_general(placed, XV[...], (((0,), (0,)), ((), ())), precision=HIGHEST, preferred_element_type=F32)
        DV[...] = back[:EBD]
        for t in range(1, NFY):
            disp_copy(t).start()
        disp_out[...] = back[:EBD]

    beside_wall = relay(last, WN.at[last, 1, pl.ds(PAD, CX)])

    @pl.when(on_wall)
    def _():
        sent_to_solvers(last)
        hear_wall(last)
        beside_wall.start()

    @pl.when(off_wall)
    def _():
        beside_wall.wait_recv()

    for z in range(NZL):
        share, _ = profile(z + 1)
        raised_out[z] = share * WN[last, 1, inner]

    @pl.when(on_wall)
    def _():
        beside_wall.wait_send()

    @pl.when(is_solver)
    def _():
        sent_to_faces(last)
        rest = XA.at[0, pl.ds(0, (NFX - 1) * EBD)]
        pltpu.make_async_copy(rest, rest, xsend.at[last - 1]).wait()
        for t in range(1, NFY):
            disp_copy(t).wait_send()

    @pl.when(not_solver)
    def _():
        disp_copy(1).wait_recv()
        disp_out[...] = DR[...]

    out.wait()


def last_add(before, raised, source_in, displacement, state_out, disp_out, T, A, D, source_weight, load_sem, out_sem):
    weights = pltpu.make_async_copy(source_in, source_weight, load_sem.at[NV])
    heights = pltpu.make_async_copy(raised, A, load_sem.at[NV + 1])
    small_in = pltpu.make_async_copy(displacement, D, load_sem.at[NV + 2])
    loads = [pltpu.make_async_copy(before.at[c], T.at[c], load_sem.at[c]) for c in range(NV)]
    stores = [pltpu.make_async_copy(T.at[c], state_out.at[c], out_sem.at[c]) for c in range(NV)]
    small_out = pltpu.make_async_copy(D, disp_out, out_sem.at[NV])
    for copy in [weights, heights] + loads + [small_in]:
        copy.start()
    weights.wait()
    heights.wait()
    for c in range(NV):
        loads[c].wait()

        def plane(z, carry):
            T[c, z] += source_weight[c] * A[z]
            return carry

        lax.fori_loop(0, NZL, plane, 0)
        stores[c].start()
    small_in.wait()
    small_out.start()
    for copy in stores + [small_out]:
        copy.wait()


def on_device(
    state, kappa, mix, press_weight, source_weight, interp, block_inverse, coupling, front_order, face_owner, face_slot
):
    hbm = pl.BlockSpec(memory_space=pltpu.HBM)
    vmem = pl.BlockSpec(memory_space=pltpu.VMEM)
    dma = pltpu.SemaphoreType.DMA
    sweeps = 2 * ITERS
    before, raised, displacement = pl.pallas_call(
        kernel,
        out_shape=(
            jax.ShapeDtypeStruct(state.shape, F32),
            jax.ShapeDtypeStruct(kappa.shape, F32),
            jax.ShapeDtypeStruct((EBD, EB), F32),
        ),
        in_specs=[hbm] * 11,
        out_specs=(hbm, vmem, vmem),
        scratch_shapes=[
            pltpu.SMEM((NV, NV), F32),
            pltpu.SMEM((NV,), F32),
            pltpu.SMEM((NV,), F32),
            pltpu.VMEM((CY, EB), F32),
            pltpu.SMEM((1, EBD), jnp.int32),
            pltpu.VMEM((1, CX), jnp.int32),
            pltpu.VMEM((1, CX), jnp.int32),
            pltpu.VMEM((2, NV, NZL + 2, CX, CY), F32),
            pltpu.VMEM((NZL, CX, CY), F32),
            pltpu.VMEM((NZL + 2, CXE, CY), F32),
            pltpu.VMEM((NZL, CX, CY), F32),
            pltpu.VMEM((EBD, EB, EB), F32),
            pltpu.VMEM((EBD, EB, EB), F32),
            pltpu.VMEM((PAIRS, 2 * EB, 2 * EB), BF16),
            pltpu.VMEM((PAIRS, 2 * EB, 2 * EB), BF16),
            pltpu.VMEM((PAIRS, EB, 2 * EB), BF16),
            pltpu.VMEM((2, NV + 1, NZL, CY), F32),
            pltpu.VMEM((sweeps, 2, NV + 1, NZL, CY), F32),
            pltpu.VMEM((CX, CY), F32),
            pltpu.VMEM((sweeps, 2, CX, CY), F32),
            pltpu.VMEM((CX, CY), F32),
            pltpu.VMEM((sweeps, NV, CX, CY), F32),
            pltpu.VMEM((CXE, CY), F32),
            pltpu.VMEM((CAP * NFX, CY), F32),
            pltpu.VMEM((CAP * NFX, CY), F32),
            pltpu.VMEM((5, CAP * NFX, CY), F32),
            pltpu.VMEM((ITERS + 1, FACES, CY), F32),
            pltpu.VMEM((5, FACES, CY), F32),
            pltpu.VMEM((FACES, CY), F32),
            pltpu.VMEM((ITERS, CAP * NFX, CY), F32),
            pltpu.VMEM((EBD, FACES), F32),
            pltpu.VMEM((FACES, EBD), F32),
            pltpu.VMEM((CAP * NFX, CX), F32),
            pltpu.VMEM((CX, CAP * NFX), F32),
            pltpu.VMEM((EBD, EB), F32),
            pltpu.VMEM((EBD, EB), F32),
            pltpu.VMEM((EBD, EB), F32),
            pltpu.VMEM((EBD, EB), F32),
            pltpu.VMEM((ITERS + 1, 3, CXE, CY), F32),
            pltpu.VMEM((2, CXE, CY), F32),
            pltpu.VMEM((2, CX, CY), F32),
            pltpu.VMEM((NZL + 2, CXE, CY), F32),
            pltpu.VMEM((CX, CY), F32),
            pltpu.VMEM((AROUND, FACES, NFX * EBD), BF16),
            pltpu.VMEM((AROUND, FACES, CY), F32),
            pltpu.VMEM((FACES, CY), F32),
            pltpu.VMEM((EBD, EB), F32),
            pltpu.VMEM((ITERS - 1, NFX * EBD, EB), F32),
            dma((11,)),
            dma((sweeps, 5)),
            dma((sweeps, 5)),
            dma((ITERS + 1,)),
            dma((ITERS + 1,)),
            dma((ITERS,)),
            dma((ITERS,)),
            dma((NFY,)),
            dma((2,)),
            dma((ITERS + 1, 8)),
            dma((ITERS + 1, 8)),
            dma((ITERS,)),
            dma((ITERS,)),
            dma,
            dma((2,)),
            dma((ITERS - 1,)),
            dma((ITERS - 1,)),
        ],
        compiler_params=pltpu.CompilerParams(
            collective_id=0, has_side_effects=True, vmem_limit_bytes=60 * 1024 * 1024
        ),
    )(
        state, kappa, mix, press_weight, source_weight, interp, block_inverse, coupling, front_order,
        face_owner.reshape(1, -1), face_slot.reshape(1, -1),
    )
    return pl.pallas_call(
        last_add,
        out_shape=(
            jax.ShapeDtypeStruct(state.shape, F32),
            jax.ShapeDtypeStruct((EBD, EB), F32),
        ),
        in_specs=[hbm] * 4,
        out_specs=(hbm, hbm),
        scratch_shapes=[
            pltpu.VMEM((NV, NZL, CX, CY), F32),
            pltpu.VMEM((NZL, CX, CY), F32),
            pltpu.VMEM((EBD, EB), F32),
            pltpu.SMEM((NV,), F32),
            dma((NV + 3,)),
            dma((NV + 1,)),
        ],
        compiler_params=pltpu.CompilerParams(vmem_limit_bytes=60 * 1024 * 1024),
    )(before, raised, source_weight, displacement)


def solution(mesh):
    return jax.shard_map(
        on_device,
        mesh=mesh,
        in_specs=(
            P(None, "fz", "fx", "fy"),
            P("fz", "fx", "fy"),
            P(),
            P(),
            P(),
            P(),
            P("fx", None, None),
            P("fx", None, None),
            P("fx", None),
            P(("fx", "fy"), None),
            P(("fx", "fy")),
        ),
        out_specs=(P(None, "fz", "fx", "fy"), P("fx", None)),
        check_vma=False,
    )
```

```python
import jax
import jax.numpy as jnp
from jax import lax
from jax.experimental import pallas as pl
from jax.experimental.pallas import tpu as pltpu
from jax.sharding import PartitionSpec as P

ITERS = 3
DIFFUSION = 0.16
HIGHEST = lax.Precision.HIGHEST
MESH = pl.DeviceIdType.MESH
F32 = jnp.float32
BF16 = jnp.bfloat16

NV, NZL, CX, CY = 5, 8, 32, 128
NZ = 16
NFX, NFY = 32, 4
RING_Z, RING_Y = 8, 4
EB, EBD, CAP = 128, 16, 2
PAIRS = EBD // 2
FACES = NFX * NFY * CAP
PAD = 8
CXE = CX + 2 * PAD
NT = (((1,), (1,)), ((), ()))
FAR_Y = (2, 1, 3, 0)
AROUND = 11


def far_first(step, ring):
    return ring // 2 + (1 - 2 * (step % 2)) * ((step + 1) // 2)


def split(values):
    high = values.astype(BF16)
    return high, (values - high.astype(F32)).astype(BF16)


def pick(selector, values):
    high, low = split(values)
    return jnp.dot(selector, high, preferred_element_type=F32) + jnp.dot(selector, low, preferred_element_type=F32)


def kernel(
    state_in, kappa_in, mix_in, press_in, source_in, interp_in, inverse_in, coupling_in, order_in, owner_in, slot_in,
    state_out, raised_out, disp_out,
    mix, press_weight, source_weight, interp, order, owner, slot,
    S, K, KX, KE, BI, CO, R, RO, RN, XS, XR, YS, YR, YK, ZR, KZ, SL, SF, CS, RF, RC, SD, RD, FP, FPT, AM, AT, FR, XV, DV, DR,
    WN, LP, LE, QB, PB, G, GW, IN, XO, XA,
    load_sem, hsend, hrecv, fsend, frecv, dsend, drecv, osend, orecv, wsend, wrecv, rsend, rrecv, csend, crecv, xsend, xrecv,
):
    ix, iy, iz = lax.axis_index("fx"), lax.axis_index("fy"), lax.axis_index("fz")
    ring_z, ring_y = ix // RING_Y, ix % RING_Y
    on_wall = iz == 0
    off_wall = iz == 1
    home = (ring_y + ring_z) % NFY
    is_solver = iy == home
    not_solver = jnp.logical_not(is_solver)
    turned_y = {d: (ring_y + d) % RING_Y for d in FAR_Y}
    turned_x = {d: (iy + d) % NFY for d in FAR_Y}
    answer_x = ((iy + 2 - iz) % NFY, (iy + 3 * iz) % NFY)

    def row_base(step):
        return ((ring_z + far_first(step, RING_Z)) % RING_Z) * RING_Y

    def homes(z):
        return {d: (turned_y[d] + z) % NFY for d in FAR_Y}

    def owners_at(step):
        z = (ring_z + far_first(step, RING_Z)) % RING_Z
        return [(z * RING_Y + turned_y[d], home_y) for d, home_y in homes(z).items()]

    near_owners = [(ring_z * RING_Y + turned_y[d], home_y) for d, home_y in homes(ring_z).items()][:3]

    def signal(barrier, device):
        pl.semaphore_signal(barrier, inc=1, device_id=device, device_id_type=MESH)

    loads = [
        pltpu.make_async_copy(source, target, load_sem.at[n])
        for n, (source, target) in enumerate(
            (
                (owner_in, owner),
                (slot_in, slot),
                (order_in, order),
                (kappa_in, K),
                (state_in, S.at[0, :, pl.ds(1, NZL)]),
                (inverse_in, BI),
                (coupling_in, CO),
                (interp_in, interp),
                (mix_in, mix),
                (press_in, press_weight),
                (source_in, source_weight),
            )
        )
    ]
    for load in loads:
        load.start()

    barrier = pltpu.get_barrier_semaphore()
    has_left, has_right, has_front, has_back = ix > 0, ix < NFX - 1, iy > 0, iy < NFY - 1
    sides = (
        (has_left, (ix - 1, iy, iz)),
        (has_right, (ix + 1, iy, iz)),
        (has_front, (ix, iy - 1, iz)),
        (has_back, (ix, iy + 1, iz)),
    )
    corners = (
        (jnp.logical_and(has_left, has_front), (ix - 1, iy - 1, iz)),
        (jnp.logical_and(has_left, has_back), (ix - 1, iy + 1, iz)),
        (jnp.logical_and(has_right, has_front), (ix + 1, iy - 1, iz)),
        (jnp.logical_and(has_right, has_back), (ix + 1, iy + 1, iz)),
    )
    other_core = (ix, iy, 1 - iz)

    @pl.when(is_solver)
    def _():
        def greet(step, carry):
            base = row_base(step)
            for dy in FAR_Y:
                for dx in FAR_Y:
                    signal(barrier, (base + turned_y[dy], turned_x[dx], 0))
            return carry

        lax.fori_loop(0, RING_Z - 1, greet, 0)
        for dy in FAR_Y:
            for dx in FAR_Y:
                if dy or dx:
                    signal(barrier, (ring_z * RING_Y + turned_y[dy], turned_x[dx], 0))

        @pl.when(off_wall)
        def _():
            signal(barrier, (ix, iy, 0))

        def greet_solvers(step, carry):
            for to, home_y in owners_at(step):
                signal(barrier, (to, home_y, iz))
            return carry

        lax.fori_loop(0, RING_Z - 1, greet_solvers, 0)
        for to, home_y in near_owners:
            signal(barrier, (to, home_y, iz))

    @pl.when(on_wall)
    def _():
        def greet(step, carry):
            for to, home_y in owners_at(step):
                signal(barrier, (to, home_y, (iy + home_y) % 2))
            return carry

        lax.fori_loop(0, RING_Z - 1, greet, 0)
        for to, home_y in near_owners:
            signal(barrier, (to, home_y, (iy + home_y) % 2))

        @pl.when(not_solver)
        def _():
            signal(barrier, (ix, home, (iy + home) % 2))

    @pl.when(not_solver)
    def _():
        signal(barrier, (ix, home, iz))

    for ref in (XR, YR, WN):
        ref[...] = jnp.zeros_like(ref)

    signal(barrier, other_core)
    solver_count = is_solver.astype(jnp.int32)
    wall_count = on_wall.astype(jnp.int32)
    expected = 1 + wall_count * (2 * NFX - solver_count) + solver_count * (2 * NFX - wall_count + NFY - 1 + NFX - 1)
    for present, device in sides + corners:
        expected = expected + present.astype(jnp.int32)

        @pl.when(present)
        def _():
            signal(barrier, device)

    zero_plane = jnp.zeros((NV, CX, CY), F32)
    for buffer in range(2):
        S[buffer, :, 0] = zero_plane
        S[buffer, :, NZL + 1] = zero_plane

    for load in loads[:3]:
        load.wait()
    rows = lax.broadcasted_iota(jnp.int32, (CAP * NFX, CX), 0)
    named = (owner[...] == rows // CAP).astype(F32)
    earlier = (
        lax.broadcasted_iota(jnp.int32, (CX, CX), 0) < lax.broadcasted_iota(jnp.int32, (CX, CX), 1)
    ).astype(BF16)
    rank = jnp.dot(named.astype(BF16), earlier, preferred_element_type=F32)
    chosen = jnp.where(rank == (rows % CAP).astype(F32), named, 0.0)
    AM[...] = chosen
    unit = (lax.broadcasted_iota(jnp.int32, (CX, CX), 0) == lax.broadcasted_iota(jnp.int32, (CX, CX), 1)).astype(F32)
    AT[...] = lax.dot_general(unit, chosen, NT, preferred_element_type=F32)
    slot_rows = jnp.sum(chosen * (slot[...] + 1).astype(F32), axis=1, keepdims=True)
    SL[...] = jnp.broadcast_to(slot_rows, (CAP * NFX, CY))
    target_of = jnp.sum(unit * (EBD * owner[...] + slot[...] + 1).astype(F32), axis=1, keepdims=True)
    WN[ITERS, 1, PAD : PAD + CX] = jnp.broadcast_to(target_of, (CX, CY))
    block_rows = lax.broadcasted_iota(jnp.int32, (EBD, EB), 0)
    block_lanes = lax.broadcasted_iota(jnp.int32, (EBD, EB), 1)
    placed = jnp.zeros((EBD, EB), F32)
    for k in range(EBD):
        placed = jnp.where(jnp.logical_and(block_rows == k, block_lanes == order[0, k]), 1.0, placed)

    lane = lax.broadcasted_iota(jnp.int32, (CX, CY), 1)
    row = lax.broadcasted_iota(jnp.int32, (CX, CY), 0)
    for load in loads[3:5]:
        load.wait()

    pair = lane // 2

    def put_ends(ends, centre, at):
        return jnp.where(pair == at, pltpu.roll(centre, 2 * at + 1, 1), ends)

    def take_ends(n):
        return jnp.where(lane % 2 == 0, pltpu.roll(YR[n, 1], CY - 1, 1), pltpu.roll(YR[n, 0], 1, 1))

    def kappa_faces(z, ends):
        coeff = DIFFUSION * K[z]
        KX[z + 1, PAD : PAD + CX] = coeff
        XS[0, NV, pl.ds(z, 1), :] = coeff[0:1]
        XS[1, NV, pl.ds(z, 1), :] = coeff[CX - 1 : CX]
        return put_ends(ends, coeff, NV * NZL + z)

    YK[...] = lax.fori_loop(0, NZL, kappa_faces, jnp.zeros((CX, CY), F32))

    def pack(src):
        def plane(z, ends):
            for c in range(NV):
                centre = src[c, z + 1]
                XS[0, c, pl.ds(z, 1), :] = centre[0:1]
                XS[1, c, pl.ds(z, 1), :] = centre[CX - 1 : CX]
                ends = put_ends(ends, centre, c * NZL + z)
            return ends

        YS[...] = lax.fori_loop(0, NZL, plane, YK[...])

    edge = NZL - (NZL - 1) * iz

    def halo_copies(n, src):
        def remote(source, target, at, there, device):
            return pltpu.make_async_remote_copy(
                source, target, hsend.at[n, at], hrecv.at[n, there], device_id=device, device_id_type=MESH
            )

        (_, left), (_, right), (_, front), (_, back) = sides
        always = iz >= 0
        plane = src.at[:, edge]
        sends = (
            (has_left, remote(XS.at[0], XR.at[n, 1], 0, 1, left)),
            (has_right, remote(XS.at[1], XR.at[n, 0], 1, 0, right)),
            (has_front, remote(YS, YR.at[n, 1], 2, 3, front)),
            (has_back, remote(YS, YR.at[n, 0], 3, 2, back)),
            (always, remote(plane, ZR.at[n], 4, 4, other_core)),
        )
        waits = (
            (has_left, remote(XS.at[0], XR.at[n, 0], 0, 0, left)),
            (has_right, remote(XS.at[1], XR.at[n, 1], 1, 1, right)),
            (has_front, remote(YS, YR.at[n, 0], 2, 2, front)),
            (has_back, remote(YS, YR.at[n, 1], 3, 3, back)),
            (always, remote(plane, ZR.at[n], 4, 4, other_core)),
        )
        return sends, waits

    def each(copies, action):
        for present, copy in copies:

            @pl.when(present)
            def _():
                action(copy)

    def start_halo(n, src):
        each(halo_copies(n, src)[0], lambda copy: copy.start())

    def finish_halo(n, src):
        _, waits = halo_copies(n, src)
        each(waits, lambda copy: copy.wait_recv())
        src[:, (NZL + 1) * (1 - iz)] = ZR[n]

    def sweep(n, src, dst, first=0, end=NZL):
        outer = take_ends(n)

        def plane(z, carry):
            coeff = KX[z + 1, PAD : PAD + CX]
            centres = [src[c, z + 1] for c in range(NV)]
            for c in range(NV):
                centre = centres[c]
                at = c * NZL + z
                beside = src[c, z] + src[c, z + 2]
                beside += jnp.where(row == 0, XR[n, 0, c, pl.ds(z, 1), :], pltpu.roll(centre, 1, 0))
                beside += jnp.where(row == CX - 1, XR[n, 1, c, pl.ds(z, 1), :], pltpu.roll(centre, CX - 1, 0))
                ends = pltpu.roll(outer, CY - 1 - 2 * at, 1)
                beside += jnp.where(lane == 0, ends, pltpu.roll(centre, 1, 1))
                beside += jnp.where(lane == CY - 1, ends, pltpu.roll(centre, CY - 1, 1))
                total = centre + coeff * (beside - 6.0 * centre)
                for d in range(NV):
                    total += mix[c, d] * centres[d]
                dst[c, z + 1] = total
            return carry

        lax.fori_loop(first, end, plane, 0)
        if end == NZL:
            each(halo_copies(n, src)[0], lambda copy: copy.wait_send())

    kappa_plane = pltpu.make_async_remote_copy(
        KX.at[edge], KZ, osend.at[0], orecv.at[0], device_id=other_core, device_id_type=MESH
    )

    def send_to_solvers(rows_of, target, sent, heard):
        def send(to, y, core):
            pltpu.make_async_remote_copy(
                rows_of(to), target, sent, heard, device_id=(to, y, core), device_id_type=MESH
            ).start()

        def group(step, carry):
            for to, home_y in owners_at(step):
                for core in range(2):
                    send(to, home_y, core)
            return carry

        @pl.when(on_wall)
        def _():
            lax.fori_loop(0, RING_Z - 1, group, 0)
            for to, home_y in near_owners:
                for core in range(2):
                    send(to, home_y, core)
            send(ix, home, 1)

            @pl.when(not_solver)
            def _():
                send(ix, home, 0)

            @pl.when(is_solver)
            def _():
                pltpu.make_async_copy(rows_of(ix), target, heard).start()

    own_rows = pl.ds(CAP * (ix * NFY + iy), CAP)

    def send_rows(turn, rows_out):
        send_to_solvers(
            lambda to: rows_out.at[pl.ds(CAP * to, CAP)], RF.at[turn, own_rows], fsend.at[turn], frecv.at[turn]
        )

    def send_pressure(turn):
        @pl.when(on_wall)
        def _():
            SF[...] = pick(AM[...].astype(BF16), PB[...])

        send_rows(turn, SF)

    def sent_to_solvers(turn):
        @pl.when(on_wall)
        def _():
            @pl.when(is_solver)
            def _():
                rest = RF.at[turn, pl.ds(0, CAP * (2 * NFX - 1))]
                pltpu.make_async_copy(rest, rest, fsend.at[turn]).wait()

            @pl.when(not_solver)
            def _():
                rest = RF.at[turn, pl.ds(0, CAP * 2 * NFX)]
                pltpu.make_async_copy(rest, rest, fsend.at[turn]).wait()

    def heard_from_faces(turn):
        whole = RF.at[turn]
        pltpu.make_async_copy(whole, whole, frecv.at[turn]).wait()

    def send_to_faces(turn):
        target = RD.at[turn, pl.ds(CAP * ix, CAP)]

        def send(to_x, to_y):
            pltpu.make_async_remote_copy(
                SD.at[pl.ds(CAP * (to_x * NFY + to_y), CAP)], target, dsend.at[turn], drecv.at[turn],
                device_id=(to_x, to_y, 0), device_id_type=MESH,
            ).start()

        def group(step, carry):
            base = row_base(step)
            for dy in FAR_Y:
                for x in answer_x:
                    send(base + turned_y[dy], x)
            return carry

        lax.fori_loop(0, RING_Z - 1, group, 0)
        for dy in FAR_Y[:3]:
            for x in answer_x:
                send(ring_z * RING_Y + turned_y[dy], x)
        send(ix, answer_x[0])

        @pl.when(off_wall)
        def _():
            send(ix, answer_x[1])

        @pl.when(on_wall)
        def _():
            pltpu.make_async_copy(SD.at[pl.ds(CAP * (ix * NFY + iy), CAP)], target, drecv.at[turn]).start()

    def sent_to_faces(turn):
        @pl.when(on_wall)
        def _():
            rest = RF.at[turn, pl.ds(0, CAP * (2 * NFX - 1))]
            pltpu.make_async_copy(rest, rest, dsend.at[turn]).wait()

        @pl.when(off_wall)
        def _():
            rest = RF.at[turn, pl.ds(0, CAP * 2 * NFX)]
            pltpu.make_async_copy(rest, rest, dsend.at[turn]).wait()

    for load in loads[5:]:
        load.wait()

    @pl.when(is_solver)
    def _():
        def parts(k):
            block = order[0, k]
            inverse = BI[block]
            force_part = lax.dot_general(interp[...], inverse, NT, precision=HIGHEST, preferred_element_type=F32)
            chain = jnp.dot(inverse, CO[block], precision=HIGHEST, preferred_element_type=F32)
            return force_part, -chain.T

        def both_parts(matrix):
            high, low = split(matrix)
            return jnp.concatenate([high, low], axis=1)

        def products(m, carry):
            force, chain = parts(2 * m)
            next_force, next_chain = parts(2 * m + 1)
            passed = jnp.dot(force, next_chain, precision=HIGHEST, preferred_element_type=F32)
            leap = jnp.dot(chain, next_chain, precision=HIGHEST, preferred_element_type=F32)
            R[m] = both_parts(jnp.concatenate([force, chain], axis=0))
            RO[m] = both_parts(jnp.concatenate([next_force, passed], axis=0))
            RN[m] = both_parts(leap)
            return carry

        lax.fori_loop(0, PAIRS, products, 0)

    numbers = range(NV)
    source = [source_weight[c] for c in numbers]
    once = [source[c] + sum(mix[c, d] * source[d] for d in numbers) for c in numbers]
    twice = [once[c] + sum(mix[c, d] * once[d] for d in numbers) for c in numbers]
    press_source = sum(press_weight[c] * source[c] for c in numbers)
    press_once = sum(press_weight[c] * once[c] for c in numbers)
    press_twice = sum(press_weight[c] * twice[c] for c in numbers)

    inner = slice(PAD, PAD + CX)

    def wall_copies(it):
        def remote(n, opposite, source_row, side, target_row, count, device):
            copy = lambda here, there: pltpu.make_async_remote_copy(
                WN.at[it, 1, pl.ds(source_row, count)], WN.at[it, side, pl.ds(target_row, count)],
                wsend.at[it, here], wrecv.at[it, there], device_id=device, device_id_type=MESH,
            )
            return copy(n, opposite), copy(n, n)

        low, high = PAD, PAD + CX - 8
        (_, left), (_, right), (_, front), (_, back) = sides
        (lf, left_front), (lb, left_back), (rf, right_front), (rb, right_back) = corners
        return (
            (has_left, remote(0, 1, low, 1, PAD + CX, 8, left)),
            (has_right, remote(1, 0, high, 1, 0, 8, right)),
            (has_front, remote(2, 3, PAD, 2, PAD, CX, front)),
            (has_back, remote(3, 2, PAD, 0, PAD, CX, back)),
            (lf, remote(4, 7, low, 2, PAD + CX, 8, left_front)),
            (lb, remote(5, 6, low, 0, PAD + CX, 8, left_back)),
            (rf, remote(6, 5, high, 2, 0, 8, right_front)),
            (rb, remote(7, 4, high, 0, 0, 8, right_back)),
        )

    def tell_faces():
        targets = (
            [pltpu.roll(WN[ITERS, 1], (CXE - d) % CXE, 0)[inner] for d in range(-2, 3)]
            + [pltpu.roll(WN[ITERS, 0], (CXE - d) % CXE, 0)[inner] for d in range(-1, 2)]
            + [pltpu.roll(WN[ITERS, 2], (CXE - d) % CXE, 0)[inner] for d in range(-1, 2)]
        )
        facts = targets + [
            jnp.broadcast_to(KE[0, :, CY - 1 : CY], (CX, CY)), jnp.broadcast_to(KE[0, :, 0:1], (CX, CY)),
        ]
        table = jnp.zeros((CX, CY), F32)
        for n, fact in enumerate(facts):
            table = jnp.where(lane == n, fact, table)
        wall_coeff = KX[1]
        selector = AM[...].astype(BF16)
        CS[0] = pick(selector, table)
        for n, d in enumerate((-1, 0, 1)):
            CS[n + 1] = pick(selector, pltpu.roll(wall_coeff, (CXE - d) % CXE, 0)[inner])
        CS[4] = pick(selector, KX[2, inner])

    half = FACES // 2
    facts_core = ix // (NFX // 2)
    facts_here = jnp.logical_and(is_solver, facts_core == iz)

    def send_facts():
        def send(to, home_y):
            pltpu.make_async_remote_copy(
                CS.at[:, pl.ds(CAP * to, CAP)], RC.at[:, own_rows], csend, crecv.at[0],
                device_id=(to, home_y, facts_core), device_id_type=MESH,
            ).start()

        def group(step, carry):
            for to, home_y in owners_at(step):
                send(to, home_y)
            return carry

        @pl.when(on_wall)
        def _():
            lax.fori_loop(0, RING_Z - 1, group, 0)
            for to, home_y in near_owners:
                send(to, home_y)

            @pl.when(facts_here)
            def _():
                pltpu.make_async_copy(CS.at[:, pl.ds(CAP * ix, CAP)], RC.at[:, own_rows], crecv.at[0]).start()

            @pl.when(jnp.logical_not(facts_here))
            def _():
                send(ix, home)

    share_facts = pltpu.make_async_remote_copy(
        RC.at[:, pl.ds(half * iz, half)], RC.at[:, pl.ds(half * iz, half)], csend, crecv.at[1],
        device_id=other_core, device_id_type=MESH,
    )

    around_wall = wall_copies(ITERS)
    pack(S.at[0])
    pl.semaphore_wait(barrier, expected)
    start_halo(0, S.at[0])

    @pl.when(on_wall)
    def _():
        each(around_wall, lambda pair: pair[0].start())

    kappa_plane.start()
    send_rows(ITERS, SL)
    finish_halo(0, S.at[0])
    sweep(0, S.at[0], S.at[1])
    pack(S.at[1])
    start_halo(1, S.at[1])

    kappa_plane.wait()
    KX[(NZL + 1) * (1 - iz)] = KZ[...]
    KX[(NZL + 1) * iz] = jnp.zeros((CXE, CY), F32)
    tile_row = lax.broadcasted_iota(jnp.int32, (PAD, CY), 0)

    ends = take_ends(0)

    def kappa_edges(z, carry):
        KX[z + 1, 0:PAD] = jnp.where(tile_row == PAD - 1, XR[0, 0, NV, pl.ds(z, 1), :], 0.0)
        KX[z + 1, PAD + CX : CXE] = jnp.where(tile_row == 0, XR[0, 1, NV, pl.ds(z, 1), :], 0.0)
        at = 2 * (NV * NZL + z)
        front = pltpu.roll(ends, CY - 2 - at, 1)
        back = pltpu.roll(ends, CY - at, 1)
        KE[z] = jnp.where(lane >= CY // 2, front, back)
        return carry

    lax.fori_loop(0, NZL, kappa_edges, 0)

    def wall_base():
        @pl.when(on_wall)
        def _():
            pressure = press_weight[0] * S[0, 0, 1]
            for c in range(1, NV):
                pressure += press_weight[c] * S[0, c, 1]
            PB[...] = pressure

    finish_halo(1, S.at[1])
    sweep(1, S.at[1], S.at[0], 0, 1)
    wall_base()
    send_pressure(0)
    sweep(1, S.at[1], S.at[0], 1, NZL)
    sent_to_solvers(ITERS)


    @pl.when(is_solver)
    def _():
        heard_from_faces(ITERS)
        face_lanes = lax.broadcasted_iota(jnp.int32, (FACES, EB), 1) + 1
        slot_of = (RF[ITERS] == face_lanes.astype(F32)).astype(F32)
        FP[...] = lax.dot_general(placed, slot_of, NT, preferred_element_type=F32)
        FPT[...] = lax.dot_general(slot_of, placed, NT, preferred_element_type=F32)

    def times(row_in, matrix):
        width = row_in.shape[1]
        high = row_in.astype(BF16).astype(F32)
        at = lax.broadcasted_iota(jnp.int32, (8, width), 0)
        left = jnp.where(at == 0, high, jnp.where(at == 1, row_in - high, 0.0)).astype(BF16)
        result = jnp.dot(left, matrix, preferred_element_type=F32)
        summed = result[:, :EB] + result[:, EB:]
        return summed[0:1] + summed[1:2]

    def solve():
        force = [FR[pl.ds(k, 1), :] for k in range(EBD)]
        odd = [times(jnp.concatenate([force[2 * m + 1], force[2 * m]], axis=1), RO[m]) for m in range(PAIRS)]
        for m in range(PAIRS):
            if m:
                odd[m] += times(odd[m - 1], RN[m])
            XV[pl.ds(2 * m + 1, 1), :] = odd[m]
            previous = odd[m - 1] if m else jnp.zeros((1, EB), F32)
            XV[pl.ds(2 * m, 1), :] = times(jnp.concatenate([force[2 * m], previous], axis=1), R[m])

    lane_e = lax.broadcasted_iota(jnp.int32, (CXE, CY), 1)

    def spread(it):
        centre = WN[it, 1]
        beyond = jnp.where(lane_e >= CY // 2, WN[it, 0], WN[it, 2])
        up, down = pltpu.roll(centre, 1, 1), pltpu.roll(centre, CY - 1, 1)
        out_up, out_down = pltpu.roll(beyond, 1, 1), pltpu.roll(beyond, CY - 1, 1)
        lap = pltpu.roll(centre, 1, 0) + pltpu.roll(centre, CXE - 1, 0) - 4.0 * centre
        lap += jnp.where(lane_e == 0, out_up, up) + jnp.where(lane_e == CY - 1, out_down, down)
        lap_e = pltpu.roll(beyond, 1, 0) + pltpu.roll(beyond, CXE - 1, 0) - 4.0 * beyond
        lap_e += jnp.where(lane_e >= CY // 2, out_up + down, out_down + up)
        LP[0], LP[1] = lap, centre
        LE[0], LE[1] = lap_e[inner], beyond[inner]

    def ring_sum(wide, edge_columns, below, above, coeff):
        own = wide[inner]
        total = pltpu.roll(wide, 1, 0)[inner] + pltpu.roll(wide, CXE - 1, 0)[inner] + below + above - 6.0 * own
        total += jnp.where(lane == 0, pltpu.roll(edge_columns, 1, 1), pltpu.roll(own, 1, 1))
        total += jnp.where(lane == CY - 1, pltpu.roll(edge_columns, CY - 1, 1), pltpu.roll(own, CY - 1, 1))
        return coeff * total

    first_jump = (NZ - 1.0) / NZ - 2.0

    def profile(plane):
        height = iz * NZL + plane - 1
        return 1.0 - height.astype(F32) / NZ, jnp.where(height == 0, first_jump, 0.0)

    def update():
        def first(plane, carry):
            share, jump = profile(plane)
            QB[plane] = KX[plane] * (share * LP[0] + jump * LP[1])
            return carry

        lax.fori_loop(0, NZL + 2, first, 0)

        def second(z, carry):
            share, jump = profile(z + 1)
            edges = KE[z] * (share * LE[0] + jump * LE[1])
            wide = QB[z + 1]
            bend = ring_sum(wide, edges, QB[z, inner], QB[z + 2, inner], KX[z + 1, inner])
            raised, slope = share * LP[1, inner], wide[inner]
            for c in range(NV):
                S[0, c, z + 1] += twice[c] * raised + 2.0 * once[c] * slope + source[c] * bend
            return carry

        lax.fori_loop(0, NZL, second, 0)

    def sent_facts():
        @pl.when(on_wall)
        def _():
            @pl.when(facts_here)
            def _():
                rest = RC.at[:, pl.ds(0, CAP * (NFX - 1))]
                pltpu.make_async_copy(rest, rest, csend).wait()

            @pl.when(jnp.logical_not(facts_here))
            def _():
                rest = RC.at[:, pl.ds(0, CAP * NFX)]
                pltpu.make_async_copy(rest, rest, csend).wait()

    def pass_facts():
        mine = RC.at[:, pl.ds(half * iz, half)]
        pltpu.make_async_copy(mine, mine, crecv.at[0]).wait()
        share_facts.start()

    def hear_facts():
        share_facts.wait()
        names = lax.broadcasted_iota(jnp.int32, (FACES, NFX * EBD), 1) + 1
        names = names.astype(F32)
        for m in range(AROUND):
            G[m] = jnp.where(names == RC[0, :, m : m + 1], 1.0, 0.0).astype(BF16)

    def tell_solvers(it, facing):
        if it:
            rest = XA.at[0, pl.ds(0, (NFX - 1) * EBD)]
            pltpu.make_async_copy(rest, rest, xsend.at[it - 1]).wait()
        own = pick(placed.T[:EBD].astype(BF16), facing)
        XO[...] = own
        XA[it, pl.ds(EBD * ix, EBD)] = own

        def send(to, y):
            pltpu.make_async_remote_copy(
                XO, XA.at[it, pl.ds(EBD * ix, EBD)], xsend.at[it], xrecv.at[it],
                device_id=(to, y, iz), device_id_type=MESH,
            ).start()

        def group(step, carry):
            for to, home_y in owners_at(step):
                send(to, home_y)
            return carry

        lax.fori_loop(0, RING_Z - 1, group, 0)
        for to, home_y in near_owners:
            send(to, home_y)

    def respond(it):
        rest = XA.at[it, pl.ds(0, (NFX - 1) * EBD)]
        pltpu.make_async_copy(rest, rest, xrecv.at[it]).wait()
        high, low = split(XA[it])
        both = jnp.concatenate([high, low], axis=1)
        for m in range(AROUND):
            found = jnp.dot(G[m], both, preferred_element_type=F32)
            GW[m] = found[:, :CY] + found[:, CY:]

        def chunk(n, carry):
            at = pl.ds(pl.multiple_of(n * CX, CX), CX)
            centre = {d: GW[d + 2, at] for d in range(-2, 3)}
            beyond = {d: jnp.where(lane >= CY // 2, GW[d + 6, at], GW[d + 9, at]) for d in range(-1, 2)}
            coeff = {d: RC[d + 2, at] for d in range(-1, 2)}

            def wide_sum(d):
                total = centre[d - 1] + centre[d + 1] - 4.0 * centre[d]
                total += jnp.where(lane == 0, pltpu.roll(beyond[d], 1, 1), pltpu.roll(centre[d], 1, 1))
                return total + jnp.where(
                    lane == CY - 1, pltpu.roll(beyond[d], CY - 1, 1), pltpu.roll(centre[d], CY - 1, 1)
                )

            sums = {d: wide_sum(d) for d in range(-1, 2)}
            slopes = {d: coeff[d] * (sums[d] + first_jump * centre[d]) for d in range(-1, 2)}
            above = RC[4, at] * ((NZ - 1.0) / NZ * sums[0])
            facts = RC[0, at]
            edge_coeff = jnp.where(lane >= CY // 2, facts[:, AROUND : AROUND + 1], facts[:, AROUND + 1 : AROUND + 2])
            edge_sum = beyond[-1] + beyond[1] - 4.0 * beyond[0]
            edge_sum += jnp.where(
                lane >= CY // 2,
                pltpu.roll(beyond[0], 1, 1) + pltpu.roll(centre[0], CY - 1, 1),
                pltpu.roll(beyond[0], CY - 1, 1) + pltpu.roll(centre[0], 1, 1),
            )
            edges = edge_coeff * (edge_sum + first_jump * beyond[0])
            bend = slopes[-1] + slopes[1] + above - 6.0 * slopes[0]
            bend += jnp.where(lane == 0, pltpu.roll(edges, 1, 1), pltpu.roll(slopes[0], 1, 1))
            bend += jnp.where(lane == CY - 1, pltpu.roll(edges, CY - 1, 1), pltpu.roll(slopes[0], CY - 1, 1))
            IN[at] = press_twice * centre[0] + 2.0 * press_once * slopes[0] + press_source * coeff[0] * bend
            return carry

        lax.fori_loop(0, FACES // CX, chunk, 0)

    def answer(it):
        heard_from_faces(it)
        if it:
            sent_to_faces(it - 1)
        rows_in = RF[it] + IN[...] if it else RF[it]
        FR[...] = pick(FP[...].astype(BF16), rows_in)
        solve()
        facing = lax.dot_general(XV[...], interp[...], NT, precision=HIGHEST, preferred_element_type=F32)
        if 0 < it < ITERS - 1:
            tell_solvers(it, facing)
        SD[...] = pick(FPT[...].astype(BF16), facing)
        send_to_faces(it)
        if it == 0:
            tell_solvers(it, facing)

    def hear_wall(it):
        whole = RD.at[it]
        pltpu.make_async_copy(whole, whole, drecv.at[it]).wait()
        WN[it, 1, inner] = pick(AT[...].astype(BF16), RD[it])

    def relay(it, part):
        return pltpu.make_async_remote_copy(
            part, part, rsend.at[it], rrecv.at[it], device_id=other_core, device_id_type=MESH
        )

    last = ITERS - 1

    def disp_copy(t):
        return pltpu.make_async_remote_copy(
            DV, DR, osend.at[t], orecv.at[1], device_id=(ix, (iy + t) % NFY, iz), device_id_type=MESH
        )

    def answer_last():
        answer(last)
        back = lax.dot_general(placed, XV[...], (((0,), (0,)), ((), ())), precision=HIGHEST, preferred_element_type=F32)
        DV[...] = back[:EBD]
        for t in range(1, NFY):
            disp_copy(t).start()
        disp_out[...] = back[:EBD]

    for it in range(ITERS - 1):
        n = 2 * it + 2
        pack(S.at[0])
        start_halo(n, S.at[0])
        if it == 0:

            @pl.when(on_wall)
            def _():
                each(around_wall, lambda pair: pair[1].wait_recv())
                tell_faces()
                each(around_wall, lambda pair: pair[0].wait_send())

            send_facts()
        else:

            @pl.when(is_solver)
            def _():
                answer(it)

        finish_halo(n, S.at[0])
        sweep(n, S.at[0], S.at[1])
        pack(S.at[1])
        start_halo(n + 1, S.at[1])
        if it == 0:
            sent_facts()

            @pl.when(is_solver)
            def _():
                answer(it)
                pass_facts()

        finish_halo(n + 1, S.at[1])
        sweep(n + 1, S.at[1], S.at[0], 0, 1)
        wall_base()
        sent_to_solvers(it)
        send_pressure(it + 1)
        sweep(n + 1, S.at[1], S.at[0], 1, NZL)
        if it == 0:

            @pl.when(is_solver)
            def _():
                hear_facts()

        copies = wall_copies(it)

        @pl.when(on_wall)
        def _():
            hear_wall(it)
            each(copies, lambda pair: pair[0].start())

        @pl.when(is_solver)
        def _():
            respond(it)
            if it == last - 1:
                answer_last()

        beside_wall = relay(it, WN.at[it])

        @pl.when(on_wall)
        def _():
            each(copies, lambda pair: pair[1].wait_recv())
            beside_wall.start()

        @pl.when(off_wall)
        def _():
            beside_wall.wait_recv()

        spread(it)
        update()

        @pl.when(on_wall)
        def _():
            each(copies, lambda pair: pair[0].wait_send())
            beside_wall.wait_send()

    out = pltpu.make_async_copy(S.at[0, :, pl.ds(1, NZL)], state_out, load_sem.at[0])
    out.start()

    beside_wall = relay(last, WN.at[last, 1, pl.ds(PAD, CX)])

    @pl.when(on_wall)
    def _():
        sent_to_solvers(last)
        hear_wall(last)
        beside_wall.start()

    @pl.when(off_wall)
    def _():
        beside_wall.wait_recv()

    for z in range(NZL):
        share, _ = profile(z + 1)
        raised_out[z] = share * WN[last, 1, inner]

    @pl.when(on_wall)
    def _():
        beside_wall.wait_send()

    @pl.when(is_solver)
    def _():
        sent_to_faces(last)
        rest = XA.at[0, pl.ds(0, (NFX - 1) * EBD)]
        pltpu.make_async_copy(rest, rest, xsend.at[last - 1]).wait()
        for t in range(1, NFY):
            disp_copy(t).wait_send()

    @pl.when(not_solver)
    def _():
        disp_copy(1).wait_recv()
        disp_out[...] = DR[...]

    out.wait()


def last_add(before, raised, source_in, displacement, state_out, disp_out, T, A, D, source_weight, load_sem, out_sem):
    weights = pltpu.make_async_copy(source_in, source_weight, load_sem.at[NV])
    heights = pltpu.make_async_copy(raised, A, load_sem.at[NV + 1])
    small_in = pltpu.make_async_copy(displacement, D, load_sem.at[NV + 2])
    loads = [pltpu.make_async_copy(before.at[c], T.at[c], load_sem.at[c]) for c in range(NV)]
    stores = [pltpu.make_async_copy(T.at[c], state_out.at[c], out_sem.at[c]) for c in range(NV)]
    small_out = pltpu.make_async_copy(D, disp_out, out_sem.at[NV])
    for copy in [weights, heights] + loads + [small_in]:
        copy.start()
    weights.wait()
    heights.wait()
    for c in range(NV):
        loads[c].wait()

        def plane(z, carry):
            T[c, z] += source_weight[c] * A[z]
            return carry

        lax.fori_loop(0, NZL, plane, 0)
        stores[c].start()
    small_in.wait()
    small_out.start()
    for copy in stores + [small_out]:
        copy.wait()


def on_device(
    state, kappa, mix, press_weight, source_weight, interp, block_inverse, coupling, front_order, face_owner, face_slot
):
    hbm = pl.BlockSpec(memory_space=pltpu.HBM)
    vmem = pl.BlockSpec(memory_space=pltpu.VMEM)
    dma = pltpu.SemaphoreType.DMA
    sweeps = 2 * ITERS
    before, raised, displacement = pl.pallas_call(
        kernel,
        out_shape=(
            jax.ShapeDtypeStruct(state.shape, F32),
            jax.ShapeDtypeStruct(kappa.shape, F32),
            jax.ShapeDtypeStruct((EBD, EB), F32),
        ),
        in_specs=[hbm] * 11,
        out_specs=(hbm, vmem, vmem),
        scratch_shapes=[
            pltpu.SMEM((NV, NV), F32),
            pltpu.SMEM((NV,), F32),
            pltpu.SMEM((NV,), F32),
            pltpu.VMEM((CY, EB), F32),
            pltpu.SMEM((1, EBD), jnp.int32),
            pltpu.VMEM((1, CX), jnp.int32),
            pltpu.VMEM((1, CX), jnp.int32),
            pltpu.VMEM((2, NV, NZL + 2, CX, CY), F32),
            pltpu.VMEM((NZL, CX, CY), F32),
            pltpu.VMEM((NZL + 2, CXE, CY), F32),
            pltpu.VMEM((NZL, CX, CY), F32),
            pltpu.VMEM((EBD, EB, EB), F32),
            pltpu.VMEM((EBD, EB, EB), F32),
            pltpu.VMEM((PAIRS, 2 * EB, 2 * EB), BF16),
            pltpu.VMEM((PAIRS, 2 * EB, 2 * EB), BF16),
            pltpu.VMEM((PAIRS, EB, 2 * EB), BF16),
            pltpu.VMEM((2, NV + 1, NZL, CY), F32),
            pltpu.VMEM((sweeps, 2, NV + 1, NZL, CY), F32),
            pltpu.VMEM((CX, CY), F32),
            pltpu.VMEM((sweeps, 2, CX, CY), F32),
            pltpu.VMEM((CX, CY), F32),
            pltpu.VMEM((sweeps, NV, CX, CY), F32),
            pltpu.VMEM((CXE, CY), F32),
            pltpu.VMEM((CAP * NFX, CY), F32),
            pltpu.VMEM((CAP * NFX, CY), F32),
            pltpu.VMEM((5, CAP * NFX, CY), F32),
            pltpu.VMEM((ITERS + 1, FACES, CY), F32),
            pltpu.VMEM((5, FACES, CY), F32),
            pltpu.VMEM((FACES, CY), F32),
            pltpu.VMEM((ITERS, CAP * NFX, CY), F32),
            pltpu.VMEM((EBD, FACES), F32),
            pltpu.VMEM((FACES, EBD), F32),
            pltpu.VMEM((CAP * NFX, CX), F32),
            pltpu.VMEM((CX, CAP * NFX), F32),
            pltpu.VMEM((EBD, EB), F32),
            pltpu.VMEM((EBD, EB), F32),
            pltpu.VMEM((EBD, EB), F32),
            pltpu.VMEM((EBD, EB), F32),
            pltpu.VMEM((ITERS + 1, 3, CXE, CY), F32),
            pltpu.VMEM((2, CXE, CY), F32),
            pltpu.VMEM((2, CX, CY), F32),
            pltpu.VMEM((NZL + 2, CXE, CY), F32),
            pltpu.VMEM((CX, CY), F32),
            pltpu.VMEM((AROUND, FACES, NFX * EBD), BF16),
            pltpu.VMEM((AROUND, FACES, CY), F32),
            pltpu.VMEM((FACES, CY), F32),
            pltpu.VMEM((EBD, EB), F32),
            pltpu.VMEM((ITERS - 1, NFX * EBD, EB), F32),
            dma((11,)),
            dma((sweeps, 5)),
            dma((sweeps, 5)),
            dma((ITERS + 1,)),
            dma((ITERS + 1,)),
            dma((ITERS,)),
            dma((ITERS,)),
            dma((NFY,)),
            dma((2,)),
            dma((ITERS + 1, 8)),
            dma((ITERS + 1, 8)),
            dma((ITERS,)),
            dma((ITERS,)),
            dma,
            dma((2,)),
            dma((ITERS - 1,)),
            dma((ITERS - 1,)),
        ],
        compiler_params=pltpu.CompilerParams(
            collective_id=0, has_side_effects=True, vmem_limit_bytes=60 * 1024 * 1024
        ),
    )(
        state, kappa, mix, press_weight, source_weight, interp, block_inverse, coupling, front_order,
        face_owner.reshape(1, -1), face_slot.reshape(1, -1),
    )
    return pl.pallas_call(
        last_add,
        out_shape=(
            jax.ShapeDtypeStruct(state.shape, F32),
            jax.ShapeDtypeStruct((EBD, EB), F32),
        ),
        in_specs=[hbm] * 4,
        out_specs=(hbm, hbm),
        scratch_shapes=[
            pltpu.VMEM((NV, NZL, CX, CY), F32),
            pltpu.VMEM((NZL, CX, CY), F32),
            pltpu.VMEM((EBD, EB), F32),
            pltpu.SMEM((NV,), F32),
            dma((NV + 3,)),
            dma((NV + 1,)),
        ],
        compiler_params=pltpu.CompilerParams(vmem_limit_bytes=60 * 1024 * 1024),
    )(before, raised, source_weight, displacement)


def solution(mesh):
    return jax.shard_map(
        on_device,
        mesh=mesh,
        in_specs=(
            P(None, "fz", "fx", "fy"),
            P("fz", "fx", "fy"),
            P(),
            P(),
            P(),
            P(),
            P("fx", None, None),
            P("fx", None, None),
            P("fx", None),
            P(("fx", "fy"), None),
            P(("fx", "fy")),
        ),
        out_specs=(P(None, "fz", "fx", "fy"), P("fx", None)),
        check_vma=False,
    )
```

```python
import jax
import jax.numpy as jnp
from jax import lax
from jax.experimental import pallas as pl
from jax.experimental.pallas import tpu as pltpu
from jax.sharding import PartitionSpec as P

ITERS = 3
DIFFUSION = 0.16
HIGHEST = lax.Precision.HIGHEST
MESH = pl.DeviceIdType.MESH
F32 = jnp.float32
BF16 = jnp.bfloat16

NV, NZL, CX, CY = 5, 8, 32, 128
NZ = 16
NFX, NFY = 32, 4
RING_Z, RING_Y = 8, 4
EB, EBD, CAP = 128, 16, 2
PAIRS = EBD // 2
FACES = NFX * NFY * CAP
PAD = 8
CXE = CX + 2 * PAD
NT = (((1,), (1,)), ((), ()))
FAR_Y = (2, 1, 3, 0)
AROUND = 11


def far_first(step, ring):
    return ring // 2 + (1 - 2 * (step % 2)) * ((step + 1) // 2)


def split(values):
    high = values.astype(BF16)
    return high, (values - high.astype(F32)).astype(BF16)


def pick(selector, values):
    high, low = split(values)
    return jnp.dot(selector, high, preferred_element_type=F32) + jnp.dot(selector, low, preferred_element_type=F32)


def kernel(
    state_in, kappa_in, mix_in, press_in, source_in, interp_in, inverse_in, coupling_in, order_in, owner_in, slot_in,
    state_out, raised_out, disp_out,
    mix, press_weight, source_weight, interp, order, owner, slot,
    S, K, KX, KE, BI, CO, R, RO, RN, XS, XR, YS, YR, YK, ZR, KZ, SL, SF, CS, RF, RC, SD, RD, FP, FPT, AM, AT, FR, XV, DV, DR,
    WN, LP, LE, QB, PB, G, GW, IN, XO, XA,
    load_sem, hsend, hrecv, fsend, frecv, dsend, drecv, osend, orecv, wsend, wrecv, rsend, rrecv, csend, crecv, xsend, xrecv,
):
    ix, iy, iz = lax.axis_index("fx"), lax.axis_index("fy"), lax.axis_index("fz")
    ring_z, ring_y = ix // RING_Y, ix % RING_Y
    on_wall = iz == 0
    off_wall = iz == 1
    home = (ring_y + ring_z) % NFY
    is_solver = iy == home
    not_solver = jnp.logical_not(is_solver)
    turned_y = {d: (ring_y + d) % RING_Y for d in FAR_Y}
    turned_x = {d: (iy + d) % NFY for d in FAR_Y}
    answer_x = ((iy + 2 - iz) % NFY, (iy + 3 * iz) % NFY)

    def row_base(step):
        return ((ring_z + far_first(step, RING_Z)) % RING_Z) * RING_Y

    def homes(z):
        return {d: (turned_y[d] + z) % NFY for d in FAR_Y}

    def owners_at(step):
        z = (ring_z + far_first(step, RING_Z)) % RING_Z
        return [(z * RING_Y + turned_y[d], home_y) for d, home_y in homes(z).items()]

    near_owners = [(ring_z * RING_Y + turned_y[d], home_y) for d, home_y in homes(ring_z).items()][:3]

    def signal(barrier, device):
        pl.semaphore_signal(barrier, inc=1, device_id=device, device_id_type=MESH)

    loads = [
        pltpu.make_async_copy(source, target, load_sem.at[n])
        for n, (source, target) in enumerate(
            (
                (owner_in, owner),
                (slot_in, slot),
                (order_in, order),
                (kappa_in, K),
                (state_in, S.at[0, :, pl.ds(1, NZL)]),
                (inverse_in, BI),
                (coupling_in, CO),
                (interp_in, interp),
                (mix_in, mix),
                (press_in, press_weight),
                (source_in, source_weight),
            )
        )
    ]
    for load in loads:
        load.start()

    barrier = pltpu.get_barrier_semaphore()
    has_left, has_right, has_front, has_back = ix > 0, ix < NFX - 1, iy > 0, iy < NFY - 1
    sides = (
        (has_left, (ix - 1, iy, iz)),
        (has_right, (ix + 1, iy, iz)),
        (has_front, (ix, iy - 1, iz)),
        (has_back, (ix, iy + 1, iz)),
    )
    corners = (
        (jnp.logical_and(has_left, has_front), (ix - 1, iy - 1, iz)),
        (jnp.logical_and(has_left, has_back), (ix - 1, iy + 1, iz)),
        (jnp.logical_and(has_right, has_front), (ix + 1, iy - 1, iz)),
        (jnp.logical_and(has_right, has_back), (ix + 1, iy + 1, iz)),
    )
    other_core = (ix, iy, 1 - iz)

    @pl.when(is_solver)
    def _():
        def greet(step, carry):
            base = row_base(step)
            for dy in FAR_Y:
                for dx in FAR_Y:
                    signal(barrier, (base + turned_y[dy], turned_x[dx], 0))
            return carry

        lax.fori_loop(0, RING_Z - 1, greet, 0)
        for dy in FAR_Y:
            for dx in FAR_Y:
                if dy or dx:
                    signal(barrier, (ring_z * RING_Y + turned_y[dy], turned_x[dx], 0))

        @pl.when(off_wall)
        def _():
            signal(barrier, (ix, iy, 0))

        def greet_solvers(step, carry):
            for to, home_y in owners_at(step):
                signal(barrier, (to, home_y, iz))
            return carry

        lax.fori_loop(0, RING_Z - 1, greet_solvers, 0)
        for to, home_y in near_owners:
            signal(barrier, (to, home_y, iz))

    @pl.when(on_wall)
    def _():
        def greet(step, carry):
            for to, home_y in owners_at(step):
                signal(barrier, (to, home_y, (iy + home_y) % 2))
            return carry

        lax.fori_loop(0, RING_Z - 1, greet, 0)
        for to, home_y in near_owners:
            signal(barrier, (to, home_y, (iy + home_y) % 2))

        @pl.when(not_solver)
        def _():
            signal(barrier, (ix, home, (iy + home) % 2))

    @pl.when(not_solver)
    def _():
        signal(barrier, (ix, home, iz))

    for ref in (XR, YR, WN):
        ref[...] = jnp.zeros_like(ref)

    signal(barrier, other_core)
    solver_count = is_solver.astype(jnp.int32)
    wall_count = on_wall.astype(jnp.int32)
    expected = 1 + wall_count * (2 * NFX - solver_count) + solver_count * (2 * NFX - wall_count + NFY - 1 + NFX - 1)
    for present, device in sides + corners:
        expected = expected + present.astype(jnp.int32)

        @pl.when(present)
        def _():
            signal(barrier, device)

    zero_plane = jnp.zeros((NV, CX, CY), F32)
    for buffer in range(2):
        S[buffer, :, 0] = zero_plane
        S[buffer, :, NZL + 1] = zero_plane

    for load in loads[:3]:
        load.wait()
    rows = lax.broadcasted_iota(jnp.int32, (CAP * NFX, CX), 0)
    named = (owner[...] == rows // CAP).astype(F32)
    earlier = (
        lax.broadcasted_iota(jnp.int32, (CX, CX), 0) < lax.broadcasted_iota(jnp.int32, (CX, CX), 1)
    ).astype(BF16)
    rank = jnp.dot(named.astype(BF16), earlier, preferred_element_type=F32)
    chosen = jnp.where(rank == (rows % CAP).astype(F32), named, 0.0)
    AM[...] = chosen
    unit = (lax.broadcasted_iota(jnp.int32, (CX, CX), 0) == lax.broadcasted_iota(jnp.int32, (CX, CX), 1)).astype(F32)
    AT[...] = lax.dot_general(unit, chosen, NT, preferred_element_type=F32)
    slot_rows = jnp.sum(chosen * (slot[...] + 1).astype(F32), axis=1, keepdims=True)
    SL[...] = jnp.broadcast_to(slot_rows, (CAP * NFX, CY))
    target_of = jnp.sum(unit * (EBD * owner[...] + slot[...] + 1).astype(F32), axis=1, keepdims=True)
    WN[ITERS, 1, PAD : PAD + CX] = jnp.broadcast_to(target_of, (CX, CY))
    block_rows = lax.broadcasted_iota(jnp.int32, (EBD, EB), 0)
    block_lanes = lax.broadcasted_iota(jnp.int32, (EBD, EB), 1)
    placed = jnp.zeros((EBD, EB), F32)
    for k in range(EBD):
        placed = jnp.where(jnp.logical_and(block_rows == k, block_lanes == order[0, k]), 1.0, placed)

    lane = lax.broadcasted_iota(jnp.int32, (CX, CY), 1)
    row = lax.broadcasted_iota(jnp.int32, (CX, CY), 0)
    for load in loads[3:5]:
        load.wait()

    pair = lane // 2

    def put_ends(ends, centre, at):
        return jnp.where(pair == at, pltpu.roll(centre, 2 * at + 1, 1), ends)

    def take_ends(n):
        return jnp.where(lane % 2 == 0, pltpu.roll(YR[n, 1], CY - 1, 1), pltpu.roll(YR[n, 0], 1, 1))

    def kappa_faces(z, ends):
        coeff = DIFFUSION * K[z]
        KX[z + 1, PAD : PAD + CX] = coeff
        XS[0, NV, pl.ds(z, 1), :] = coeff[0:1]
        XS[1, NV, pl.ds(z, 1), :] = coeff[CX - 1 : CX]
        return put_ends(ends, coeff, NV * NZL + z)

    YK[...] = lax.fori_loop(0, NZL, kappa_faces, jnp.zeros((CX, CY), F32))

    def pack(src):
        def plane(z, ends):
            for c in range(NV):
                centre = src[c, z + 1]
                XS[0, c, pl.ds(z, 1), :] = centre[0:1]
                XS[1, c, pl.ds(z, 1), :] = centre[CX - 1 : CX]
                ends = put_ends(ends, centre, c * NZL + z)
            return ends

        YS[...] = lax.fori_loop(0, NZL, plane, YK[...])

    edge = NZL - (NZL - 1) * iz

    def halo_copies(n, src):
        def remote(source, target, at, there, device):
            return pltpu.make_async_remote_copy(
                source, target, hsend.at[n, at], hrecv.at[n, there], device_id=device, device_id_type=MESH
            )

        (_, left), (_, right), (_, front), (_, back) = sides
        always = iz >= 0
        plane = src.at[:, edge]
        sends = (
            (has_left, remote(XS.at[0], XR.at[n, 1], 0, 1, left)),
            (has_right, remote(XS.at[1], XR.at[n, 0], 1, 0, right)),
            (has_front, remote(YS, YR.at[n, 1], 2, 3, front)),
            (has_back, remote(YS, YR.at[n, 0], 3, 2, back)),
            (always, remote(plane, ZR.at[n], 4, 4, other_core)),
        )
        waits = (
            (has_left, remote(XS.at[0], XR.at[n, 0], 0, 0, left)),
            (has_right, remote(XS.at[1], XR.at[n, 1], 1, 1, right)),
            (has_front, remote(YS, YR.at[n, 0], 2, 2, front)),
            (has_back, remote(YS, YR.at[n, 1], 3, 3, back)),
            (always, remote(plane, ZR.at[n], 4, 4, other_core)),
        )
        return sends, waits

    def each(copies, action):
        for present, copy in copies:

            @pl.when(present)
            def _():
                action(copy)

    def start_halo(n, src):
        each(halo_copies(n, src)[0], lambda copy: copy.start())

    def finish_halo(n, src):
        _, waits = halo_copies(n, src)
        each(waits, lambda copy: copy.wait_recv())
        src[:, (NZL + 1) * (1 - iz)] = ZR[n]

    def sweep(n, src, dst, first=0, end=NZL):
        outer = take_ends(n)

        def plane(z, carry):
            coeff = KX[z + 1, PAD : PAD + CX]
            centres = [src[c, z + 1] for c in range(NV)]
            for c in range(NV):
                centre = centres[c]
                at = c * NZL + z
                beside = src[c, z] + src[c, z + 2]
                beside += jnp.where(row == 0, XR[n, 0, c, pl.ds(z, 1), :], pltpu.roll(centre, 1, 0))
                beside += jnp.where(row == CX - 1, XR[n, 1, c, pl.ds(z, 1), :], pltpu.roll(centre, CX - 1, 0))
                ends = pltpu.roll(outer, CY - 1 - 2 * at, 1)
                beside += jnp.where(lane == 0, ends, pltpu.roll(centre, 1, 1))
                beside += jnp.where(lane == CY - 1, ends, pltpu.roll(centre, CY - 1, 1))
                total = centre + coeff * (beside - 6.0 * centre)
                for d in range(NV):
                    total += mix[c, d] * centres[d]
                dst[c, z + 1] = total
            return carry

        lax.fori_loop(first, end, plane, 0)
        if end == NZL:
            each(halo_copies(n, src)[0], lambda copy: copy.wait_send())

    kappa_plane = pltpu.make_async_remote_copy(
        KX.at[edge], KZ, osend.at[0], orecv.at[0], device_id=other_core, device_id_type=MESH
    )

    def send_to_solvers(rows_of, target, sent, heard):
        def send(to, y, core):
            pltpu.make_async_remote_copy(
                rows_of(to), target, sent, heard, device_id=(to, y, core), device_id_type=MESH
            ).start()

        def group(step, carry):
            for to, home_y in owners_at(step):
                for core in range(2):
                    send(to, home_y, core)
            return carry

        @pl.when(on_wall)
        def _():
            lax.fori_loop(0, RING_Z - 1, group, 0)
            for to, home_y in near_owners:
                for core in range(2):
                    send(to, home_y, core)
            send(ix, home, 1)

            @pl.when(not_solver)
            def _():
                send(ix, home, 0)

            @pl.when(is_solver)
            def _():
                pltpu.make_async_copy(rows_of(ix), target, heard).start()

    own_rows = pl.ds(CAP * (ix * NFY + iy), CAP)

    def send_rows(turn, rows_out):
        send_to_solvers(
            lambda to: rows_out.at[pl.ds(CAP * to, CAP)], RF.at[turn, own_rows], fsend.at[turn], frecv.at[turn]
        )

    def send_pressure(turn):
        @pl.when(on_wall)
        def _():
            SF[...] = pick(AM[...].astype(BF16), PB[...])

        send_rows(turn, SF)

    def sent_to_solvers(turn):
        @pl.when(on_wall)
        def _():
            @pl.when(is_solver)
            def _():
                rest = RF.at[turn, pl.ds(0, CAP * (2 * NFX - 1))]
                pltpu.make_async_copy(rest, rest, fsend.at[turn]).wait()

            @pl.when(not_solver)
            def _():
                rest = RF.at[turn, pl.ds(0, CAP * 2 * NFX)]
                pltpu.make_async_copy(rest, rest, fsend.at[turn]).wait()

    def heard_from_faces(turn):
        whole = RF.at[turn]
        pltpu.make_async_copy(whole, whole, frecv.at[turn]).wait()

    def send_to_faces(turn):
        target = RD.at[turn, pl.ds(CAP * ix, CAP)]

        def send(to_x, to_y):
            pltpu.make_async_remote_copy(
                SD.at[pl.ds(CAP * (to_x * NFY + to_y), CAP)], target, dsend.at[turn], drecv.at[turn],
                device_id=(to_x, to_y, 0), device_id_type=MESH,
            ).start()

        def group(step, carry):
            base = row_base(step)
            for dy in FAR_Y:
                for x in answer_x:
                    send(base + turned_y[dy], x)
            return carry

        lax.fori_loop(0, RING_Z - 1, group, 0)
        for dy in FAR_Y[:3]:
            for x in answer_x:
                send(ring_z * RING_Y + turned_y[dy], x)
        send(ix, answer_x[0])

        @pl.when(off_wall)
        def _():
            send(ix, answer_x[1])

        @pl.when(on_wall)
        def _():
            pltpu.make_async_copy(SD.at[pl.ds(CAP * (ix * NFY + iy), CAP)], target, drecv.at[turn]).start()

    def sent_to_faces(turn):
        @pl.when(on_wall)
        def _():
            rest = RF.at[turn, pl.ds(0, CAP * (2 * NFX - 1))]
            pltpu.make_async_copy(rest, rest, dsend.at[turn]).wait()

        @pl.when(off_wall)
        def _():
            rest = RF.at[turn, pl.ds(0, CAP * 2 * NFX)]
            pltpu.make_async_copy(rest, rest, dsend.at[turn]).wait()

    for load in loads[5:]:
        load.wait()

    def parts(k):
        block = order[0, k]
        inverse = BI[block]
        force_part = lax.dot_general(interp[...], inverse, NT, precision=HIGHEST, preferred_element_type=F32)
        chain = jnp.dot(inverse, CO[block], precision=HIGHEST, preferred_element_type=F32)
        return force_part, -chain.T

    def both_parts(matrix):
        high, low = split(matrix)
        return jnp.concatenate([high, low], axis=1)

    def products(m, carry):
        force, chain = parts(2 * m)
        next_force, next_chain = parts(2 * m + 1)
        passed = jnp.dot(force, next_chain, precision=HIGHEST, preferred_element_type=F32)
        leap = jnp.dot(chain, next_chain, precision=HIGHEST, preferred_element_type=F32)
        R[m] = both_parts(jnp.concatenate([force, chain], axis=0))
        RO[m] = both_parts(jnp.concatenate([next_force, passed], axis=0))
        RN[m] = both_parts(leap)
        return carry

    def multiply(first, end):
        @pl.when(is_solver)
        def _():
            lax.fori_loop(first, end, products, 0)

    multiply(0, PAIRS // 2)

    numbers = range(NV)
    source = [source_weight[c] for c in numbers]
    once = [source[c] + sum(mix[c, d] * source[d] for d in numbers) for c in numbers]
    twice = [once[c] + sum(mix[c, d] * once[d] for d in numbers) for c in numbers]
    press_source = sum(press_weight[c] * source[c] for c in numbers)
    press_once = sum(press_weight[c] * once[c] for c in numbers)
    press_twice = sum(press_weight[c] * twice[c] for c in numbers)

    inner = slice(PAD, PAD + CX)

    def wall_copies(it):
        def remote(n, opposite, source_row, side, target_row, count, device):
            copy = lambda here, there: pltpu.make_async_remote_copy(
                WN.at[it, 1, pl.ds(source_row, count)], WN.at[it, side, pl.ds(target_row, count)],
                wsend.at[it, here], wrecv.at[it, there], device_id=device, device_id_type=MESH,
            )
            return copy(n, opposite), copy(n, n)

        low, high = PAD, PAD + CX - 8
        (_, left), (_, right), (_, front), (_, back) = sides
        (lf, left_front), (lb, left_back), (rf, right_front), (rb, right_back) = corners
        return (
            (has_left, remote(0, 1, low, 1, PAD + CX, 8, left)),
            (has_right, remote(1, 0, high, 1, 0, 8, right)),
            (has_front, remote(2, 3, PAD, 2, PAD, CX, front)),
            (has_back, remote(3, 2, PAD, 0, PAD, CX, back)),
            (lf, remote(4, 7, low, 2, PAD + CX, 8, left_front)),
            (lb, remote(5, 6, low, 0, PAD + CX, 8, left_back)),
            (rf, remote(6, 5, high, 2, 0, 8, right_front)),
            (rb, remote(7, 4, high, 0, 0, 8, right_back)),
        )

    def tell_faces():
        targets = (
            [pltpu.roll(WN[ITERS, 1], (CXE - d) % CXE, 0)[inner] for d in range(-2, 3)]
            + [pltpu.roll(WN[ITERS, 0], (CXE - d) % CXE, 0)[inner] for d in range(-1, 2)]
            + [pltpu.roll(WN[ITERS, 2], (CXE - d) % CXE, 0)[inner] for d in range(-1, 2)]
        )
        facts = targets + [
            jnp.broadcast_to(KE[0, :, CY - 1 : CY], (CX, CY)), jnp.broadcast_to(KE[0, :, 0:1], (CX, CY)),
        ]
        table = jnp.zeros((CX, CY), F32)
        for n, fact in enumerate(facts):
            table = jnp.where(lane == n, fact, table)
        wall_coeff = KX[1]
        selector = AM[...].astype(BF16)
        CS[0] = pick(selector, table)
        for n, d in enumerate((-1, 0, 1)):
            CS[n + 1] = pick(selector, pltpu.roll(wall_coeff, (CXE - d) % CXE, 0)[inner])
        CS[4] = pick(selector, KX[2, inner])

    half = FACES // 2
    facts_core = ix // (NFX // 2)
    facts_here = jnp.logical_and(is_solver, facts_core == iz)

    def send_facts():
        def send(to, home_y):
            pltpu.make_async_remote_copy(
                CS.at[:, pl.ds(CAP * to, CAP)], RC.at[:, own_rows], csend, crecv.at[0],
                device_id=(to, home_y, facts_core), device_id_type=MESH,
            ).start()

        def group(step, carry):
            for to, home_y in owners_at(step):
                send(to, home_y)
            return carry

        @pl.when(on_wall)
        def _():
            lax.fori_loop(0, RING_Z - 1, group, 0)
            for to, home_y in near_owners:
                send(to, home_y)

            @pl.when(facts_here)
            def _():
                pltpu.make_async_copy(CS.at[:, pl.ds(CAP * ix, CAP)], RC.at[:, own_rows], crecv.at[0]).start()

            @pl.when(jnp.logical_not(facts_here))
            def _():
                send(ix, home)

    share_facts = pltpu.make_async_remote_copy(
        RC.at[:, pl.ds(half * iz, half)], RC.at[:, pl.ds(half * iz, half)], csend, crecv.at[1],
        device_id=other_core, device_id_type=MESH,
    )

    around_wall = wall_copies(ITERS)
    pack(S.at[0])
    pl.semaphore_wait(barrier, expected)
    start_halo(0, S.at[0])

    @pl.when(on_wall)
    def _():
        each(around_wall, lambda pair: pair[0].start())

    kappa_plane.start()
    send_rows(ITERS, SL)
    multiply(PAIRS // 2, PAIRS)
    finish_halo(0, S.at[0])
    sweep(0, S.at[0], S.at[1])
    pack(S.at[1])
    start_halo(1, S.at[1])

    kappa_plane.wait()
    KX[(NZL + 1) * (1 - iz)] = KZ[...]
    KX[(NZL + 1) * iz] = jnp.zeros((CXE, CY), F32)
    tile_row = lax.broadcasted_iota(jnp.int32, (PAD, CY), 0)

    ends = take_ends(0)

    def kappa_edges(z, carry):
        KX[z + 1, 0:PAD] = jnp.where(tile_row == PAD - 1, XR[0, 0, NV, pl.ds(z, 1), :], 0.0)
        KX[z + 1, PAD + CX : CXE] = jnp.where(tile_row == 0, XR[0, 1, NV, pl.ds(z, 1), :], 0.0)
        at = 2 * (NV * NZL + z)
        front = pltpu.roll(ends, CY - 2 - at, 1)
        back = pltpu.roll(ends, CY - at, 1)
        KE[z] = jnp.where(lane >= CY // 2, front, back)
        return carry

    lax.fori_loop(0, NZL, kappa_edges, 0)

    def wall_base():
        @pl.when(on_wall)
        def _():
            pressure = press_weight[0] * S[0, 0, 1]
            for c in range(1, NV):
                pressure += press_weight[c] * S[0, c, 1]
            PB[...] = pressure

    finish_halo(1, S.at[1])
    sweep(1, S.at[1], S.at[0], 0, 1)
    wall_base()
    send_pressure(0)
    sweep(1, S.at[1], S.at[0], 1, NZL)
    sent_to_solvers(ITERS)


    @pl.when(is_solver)
    def _():
        heard_from_faces(ITERS)
        face_lanes = lax.broadcasted_iota(jnp.int32, (FACES, EB), 1) + 1
        slot_of = (RF[ITERS] == face_lanes.astype(F32)).astype(F32)
        FP[...] = lax.dot_general(placed, slot_of, NT, preferred_element_type=F32)
        FPT[...] = lax.dot_general(slot_of, placed, NT, preferred_element_type=F32)

    def times(row_in, matrix):
        width = row_in.shape[1]
        high = row_in.astype(BF16).astype(F32)
        at = lax.broadcasted_iota(jnp.int32, (8, width), 0)
        left = jnp.where(at == 0, high, jnp.where(at == 1, row_in - high, 0.0)).astype(BF16)
        result = jnp.dot(left, matrix, preferred_element_type=F32)
        summed = result[:, :EB] + result[:, EB:]
        return summed[0:1] + summed[1:2]

    def solve():
        force = [FR[pl.ds(k, 1), :] for k in range(EBD)]
        odd = [times(jnp.concatenate([force[2 * m + 1], force[2 * m]], axis=1), RO[m]) for m in range(PAIRS)]
        for m in range(PAIRS):
            if m:
                odd[m] += times(odd[m - 1], RN[m])
            XV[pl.ds(2 * m + 1, 1), :] = odd[m]
            previous = odd[m - 1] if m else jnp.zeros((1, EB), F32)
            XV[pl.ds(2 * m, 1), :] = times(jnp.concatenate([force[2 * m], previous], axis=1), R[m])

    lane_e = lax.broadcasted_iota(jnp.int32, (CXE, CY), 1)

    def spread(it):
        centre = WN[it, 1]
        beyond = jnp.where(lane_e >= CY // 2, WN[it, 0], WN[it, 2])
        up, down = pltpu.roll(centre, 1, 1), pltpu.roll(centre, CY - 1, 1)
        out_up, out_down = pltpu.roll(beyond, 1, 1), pltpu.roll(beyond, CY - 1, 1)
        lap = pltpu.roll(centre, 1, 0) + pltpu.roll(centre, CXE - 1, 0) - 4.0 * centre
        lap += jnp.where(lane_e == 0, out_up, up) + jnp.where(lane_e == CY - 1, out_down, down)
        lap_e = pltpu.roll(beyond, 1, 0) + pltpu.roll(beyond, CXE - 1, 0) - 4.0 * beyond
        lap_e += jnp.where(lane_e >= CY // 2, out_up + down, out_down + up)
        LP[0], LP[1] = lap, centre
        LE[0], LE[1] = lap_e[inner], beyond[inner]

    def ring_sum(wide, edge_columns, below, above, coeff):
        own = wide[inner]
        total = pltpu.roll(wide, 1, 0)[inner] + pltpu.roll(wide, CXE - 1, 0)[inner] + below + above - 6.0 * own
        total += jnp.where(lane == 0, pltpu.roll(edge_columns, 1, 1), pltpu.roll(own, 1, 1))
        total += jnp.where(lane == CY - 1, pltpu.roll(edge_columns, CY - 1, 1), pltpu.roll(own, CY - 1, 1))
        return coeff * total

    first_jump = (NZ - 1.0) / NZ - 2.0

    def profile(plane):
        height = iz * NZL + plane - 1
        return 1.0 - height.astype(F32) / NZ, jnp.where(height == 0, first_jump, 0.0)

    def update():
        def first(plane, carry):
            share, jump = profile(plane)
            QB[plane] = KX[plane] * (share * LP[0] + jump * LP[1])
            return carry

        lax.fori_loop(0, NZL + 2, first, 0)

        def second(z, carry):
            share, jump = profile(z + 1)
            edges = KE[z] * (share * LE[0] + jump * LE[1])
            wide = QB[z + 1]
            bend = ring_sum(wide, edges, QB[z, inner], QB[z + 2, inner], KX[z + 1, inner])
            raised, slope = share * LP[1, inner], wide[inner]
            for c in range(NV):
                S[0, c, z + 1] += twice[c] * raised + 2.0 * once[c] * slope + source[c] * bend
            return carry

        lax.fori_loop(0, NZL, second, 0)

    def sent_facts():
        @pl.when(on_wall)
        def _():
            @pl.when(facts_here)
            def _():
                rest = RC.at[:, pl.ds(0, CAP * (NFX - 1))]
                pltpu.make_async_copy(rest, rest, csend).wait()

            @pl.when(jnp.logical_not(facts_here))
            def _():
                rest = RC.at[:, pl.ds(0, CAP * NFX)]
                pltpu.make_async_copy(rest, rest, csend).wait()

    def pass_facts():
        mine = RC.at[:, pl.ds(half * iz, half)]
        pltpu.make_async_copy(mine, mine, crecv.at[0]).wait()
        share_facts.start()

    def hear_facts():
        share_facts.wait()
        names = lax.broadcasted_iota(jnp.int32, (FACES, NFX * EBD), 1) + 1
        names = names.astype(F32)
        for m in range(AROUND):
            G[m] = jnp.where(names == RC[0, :, m : m + 1], 1.0, 0.0).astype(BF16)

    def tell_solvers(it, facing):
        if it:
            rest = XA.at[0, pl.ds(0, (NFX - 1) * EBD)]
            pltpu.make_async_copy(rest, rest, xsend.at[it - 1]).wait()
        own = pick(placed.T[:EBD].astype(BF16), facing)
        XO[...] = own
        XA[it, pl.ds(EBD * ix, EBD)] = own

        def send(to, y):
            pltpu.make_async_remote_copy(
                XO, XA.at[it, pl.ds(EBD * ix, EBD)], xsend.at[it], xrecv.at[it],
                device_id=(to, y, iz), device_id_type=MESH,
            ).start()

        def group(step, carry):
            for to, home_y in owners_at(step):
                send(to, home_y)
            return carry

        lax.fori_loop(0, RING_Z - 1, group, 0)
        for to, home_y in near_owners:
            send(to, home_y)

    def respond(it):
        rest = XA.at[it, pl.ds(0, (NFX - 1) * EBD)]
        pltpu.make_async_copy(rest, rest, xrecv.at[it]).wait()
        high, low = split(XA[it])
        both = jnp.concatenate([high, low], axis=1)
        for m in range(AROUND):
            found = jnp.dot(G[m], both, preferred_element_type=F32)
            GW[m] = found[:, :CY] + found[:, CY:]

        def chunk(n, carry):
            at = pl.ds(pl.multiple_of(n * CX, CX), CX)
            centre = {d: GW[d + 2, at] for d in range(-2, 3)}
            beyond = {d: jnp.where(lane >= CY // 2, GW[d + 6, at], GW[d + 9, at]) for d in range(-1, 2)}
            coeff = {d: RC[d + 2, at] for d in range(-1, 2)}

            def wide_sum(d):
                total = centre[d - 1] + centre[d + 1] - 4.0 * centre[d]
                total += jnp.where(lane == 0, pltpu.roll(beyond[d], 1, 1), pltpu.roll(centre[d], 1, 1))
                return total + jnp.where(
                    lane == CY - 1, pltpu.roll(beyond[d], CY - 1, 1), pltpu.roll(centre[d], CY - 1, 1)
                )

            sums = {d: wide_sum(d) for d in range(-1, 2)}
            slopes = {d: coeff[d] * (sums[d] + first_jump * centre[d]) for d in range(-1, 2)}
            above = RC[4, at] * ((NZ - 1.0) / NZ * sums[0])
            facts = RC[0, at]
            edge_coeff = jnp.where(lane >= CY // 2, facts[:, AROUND : AROUND + 1], facts[:, AROUND + 1 : AROUND + 2])
            edge_sum = beyond[-1] + beyond[1] - 4.0 * beyond[0]
            edge_sum += jnp.where(
                lane >= CY // 2,
                pltpu.roll(beyond[0], 1, 1) + pltpu.roll(centre[0], CY - 1, 1),
                pltpu.roll(beyond[0], CY - 1, 1) + pltpu.roll(centre[0], 1, 1),
            )
            edges = edge_coeff * (edge_sum + first_jump * beyond[0])
            bend = slopes[-1] + slopes[1] + above - 6.0 * slopes[0]
            bend += jnp.where(lane == 0, pltpu.roll(edges, 1, 1), pltpu.roll(slopes[0], 1, 1))
            bend += jnp.where(lane == CY - 1, pltpu.roll(edges, CY - 1, 1), pltpu.roll(slopes[0], CY - 1, 1))
            IN[at] = press_twice * centre[0] + 2.0 * press_once * slopes[0] + press_source * coeff[0] * bend
            return carry

        lax.fori_loop(0, FACES // CX, chunk, 0)

    def answer(it):
        heard_from_faces(it)
        if it:
            sent_to_faces(it - 1)
        rows_in = RF[it] + IN[...] if it else RF[it]
        FR[...] = pick(FP[...].astype(BF16), rows_in)
        solve()
        facing = lax.dot_general(XV[...], interp[...], NT, precision=HIGHEST, preferred_element_type=F32)
        if 0 < it < ITERS - 1:
            tell_solvers(it, facing)
        SD[...] = pick(FPT[...].astype(BF16), facing)
        send_to_faces(it)
        if it == 0:
            tell_solvers(it, facing)

    def hear_wall(it):
        whole = RD.at[it]
        pltpu.make_async_copy(whole, whole, drecv.at[it]).wait()
        WN[it, 1, inner] = pick(AT[...].astype(BF16), RD[it])

    def relay(it, part):
        return pltpu.make_async_remote_copy(
            part, part, rsend.at[it], rrecv.at[it], device_id=other_core, device_id_type=MESH
        )

    last = ITERS - 1

    def disp_copy(t):
        return pltpu.make_async_remote_copy(
            DV, DR, osend.at[t], orecv.at[1], device_id=(ix, (iy + t) % NFY, iz), device_id_type=MESH
        )

    def answer_last():
        answer(last)
        back = lax.dot_general(placed, XV[...], (((0,), (0,)), ((), ())), precision=HIGHEST, preferred_element_type=F32)
        DV[...] = back[:EBD]
        for t in range(1, NFY):
            disp_copy(t).start()
        disp_out[...] = back[:EBD]

    for it in range(ITERS - 1):
        n = 2 * it + 2
        pack(S.at[0])
        start_halo(n, S.at[0])
        if it == 0:

            @pl.when(on_wall)
            def _():
                each(around_wall, lambda pair: pair[1].wait_recv())
                tell_faces()
                each(around_wall, lambda pair: pair[0].wait_send())

            send_facts()
        else:

            @pl.when(is_solver)
            def _():
                answer(it)

        finish_halo(n, S.at[0])
        sweep(n, S.at[0], S.at[1])
        pack(S.at[1])
        start_halo(n + 1, S.at[1])
        if it == 0:
            sent_facts()

            @pl.when(is_solver)
            def _():
                answer(it)
                pass_facts()

        finish_halo(n + 1, S.at[1])
        sweep(n + 1, S.at[1], S.at[0], 0, 1)
        wall_base()
        sent_to_solvers(it)
        send_pressure(it + 1)
        sweep(n + 1, S.at[1], S.at[0], 1, NZL)
        if it == 0:

            @pl.when(is_solver)
            def _():
                hear_facts()

        copies = wall_copies(it)

        @pl.when(on_wall)
        def _():
            hear_wall(it)
            each(copies, lambda pair: pair[0].start())

        @pl.when(is_solver)
        def _():
            respond(it)
            if it == last - 1:
                answer_last()

        beside_wall = relay(it, WN.at[it])

        @pl.when(on_wall)
        def _():
            each(copies, lambda pair: pair[1].wait_recv())
            beside_wall.start()

        @pl.when(off_wall)
        def _():
            beside_wall.wait_recv()

        spread(it)
        update()

        @pl.when(on_wall)
        def _():
            each(copies, lambda pair: pair[0].wait_send())
            beside_wall.wait_send()

    out = pltpu.make_async_copy(S.at[0, :, pl.ds(1, NZL)], state_out, load_sem.at[0])
    out.start()

    beside_wall = relay(last, WN.at[last, 1, pl.ds(PAD, CX)])

    @pl.when(on_wall)
    def _():
        sent_to_solvers(last)
        hear_wall(last)
        beside_wall.start()

    @pl.when(off_wall)
    def _():
        beside_wall.wait_recv()

    for z in range(NZL):
        share, _ = profile(z + 1)
        raised_out[z] = share * WN[last, 1, inner]

    @pl.when(on_wall)
    def _():
        beside_wall.wait_send()

    @pl.when(is_solver)
    def _():
        sent_to_faces(last)
        rest = XA.at[0, pl.ds(0, (NFX - 1) * EBD)]
        pltpu.make_async_copy(rest, rest, xsend.at[last - 1]).wait()
        for t in range(1, NFY):
            disp_copy(t).wait_send()

    @pl.when(not_solver)
    def _():
        disp_copy(1).wait_recv()
        disp_out[...] = DR[...]

    out.wait()


def last_add(before, raised, source_in, displacement, state_out, disp_out, T, A, D, source_weight, load_sem, out_sem):
    weights = pltpu.make_async_copy(source_in, source_weight, load_sem.at[NV])
    heights = pltpu.make_async_copy(raised, A, load_sem.at[NV + 1])
    small_in = pltpu.make_async_copy(displacement, D, load_sem.at[NV + 2])
    loads = [pltpu.make_async_copy(before.at[c], T.at[c], load_sem.at[c]) for c in range(NV)]
    stores = [pltpu.make_async_copy(T.at[c], state_out.at[c], out_sem.at[c]) for c in range(NV)]
    small_out = pltpu.make_async_copy(D, disp_out, out_sem.at[NV])
    for copy in [weights, heights] + loads + [small_in]:
        copy.start()
    weights.wait()
    heights.wait()
    for c in range(NV):
        loads[c].wait()

        def plane(z, carry):
            T[c, z] += source_weight[c] * A[z]
            return carry

        lax.fori_loop(0, NZL, plane, 0)
        stores[c].start()
    small_in.wait()
    small_out.start()
    for copy in stores + [small_out]:
        copy.wait()


def on_device(
    state, kappa, mix, press_weight, source_weight, interp, block_inverse, coupling, front_order, face_owner, face_slot
):
    hbm = pl.BlockSpec(memory_space=pltpu.HBM)
    vmem = pl.BlockSpec(memory_space=pltpu.VMEM)
    dma = pltpu.SemaphoreType.DMA
    sweeps = 2 * ITERS
    before, raised, displacement = pl.pallas_call(
        kernel,
        out_shape=(
            jax.ShapeDtypeStruct(state.shape, F32),
            jax.ShapeDtypeStruct(kappa.shape, F32),
            jax.ShapeDtypeStruct((EBD, EB), F32),
        ),
        in_specs=[hbm] * 11,
        out_specs=(hbm, vmem, vmem),
        scratch_shapes=[
            pltpu.SMEM((NV, NV), F32),
            pltpu.SMEM((NV,), F32),
            pltpu.SMEM((NV,), F32),
            pltpu.VMEM((CY, EB), F32),
            pltpu.SMEM((1, EBD), jnp.int32),
            pltpu.VMEM((1, CX), jnp.int32),
            pltpu.VMEM((1, CX), jnp.int32),
            pltpu.VMEM((2, NV, NZL + 2, CX, CY), F32),
            pltpu.VMEM((NZL, CX, CY), F32),
            pltpu.VMEM((NZL + 2, CXE, CY), F32),
            pltpu.VMEM((NZL, CX, CY), F32),
            pltpu.VMEM((EBD, EB, EB), F32),
            pltpu.VMEM((EBD, EB, EB), F32),
            pltpu.VMEM((PAIRS, 2 * EB, 2 * EB), BF16),
            pltpu.VMEM((PAIRS, 2 * EB, 2 * EB), BF16),
            pltpu.VMEM((PAIRS, EB, 2 * EB), BF16),
            pltpu.VMEM((2, NV + 1, NZL, CY), F32),
            pltpu.VMEM((sweeps, 2, NV + 1, NZL, CY), F32),
            pltpu.VMEM((CX, CY), F32),
            pltpu.VMEM((sweeps, 2, CX, CY), F32),
            pltpu.VMEM((CX, CY), F32),
            pltpu.VMEM((sweeps, NV, CX, CY), F32),
            pltpu.VMEM((CXE, CY), F32),
            pltpu.VMEM((CAP * NFX, CY), F32),
            pltpu.VMEM((CAP * NFX, CY), F32),
            pltpu.VMEM((5, CAP * NFX, CY), F32),
            pltpu.VMEM((ITERS + 1, FACES, CY), F32),
            pltpu.VMEM((5, FACES, CY), F32),
            pltpu.VMEM((FACES, CY), F32),
            pltpu.VMEM((ITERS, CAP * NFX, CY), F32),
            pltpu.VMEM((EBD, FACES), F32),
            pltpu.VMEM((FACES, EBD), F32),
            pltpu.VMEM((CAP * NFX, CX), F32),
            pltpu.VMEM((CX, CAP * NFX), F32),
            pltpu.VMEM((EBD, EB), F32),
            pltpu.VMEM((EBD, EB), F32),
            pltpu.VMEM((EBD, EB), F32),
            pltpu.VMEM((EBD, EB), F32),
            pltpu.VMEM((ITERS + 1, 3, CXE, CY), F32),
            pltpu.VMEM((2, CXE, CY), F32),
            pltpu.VMEM((2, CX, CY), F32),
            pltpu.VMEM((NZL + 2, CXE, CY), F32),
            pltpu.VMEM((CX, CY), F32),
            pltpu.VMEM((AROUND, FACES, NFX * EBD), BF16),
            pltpu.VMEM((AROUND, FACES, CY), F32),
            pltpu.VMEM((FACES, CY), F32),
            pltpu.VMEM((EBD, EB), F32),
            pltpu.VMEM((ITERS - 1, NFX * EBD, EB), F32),
            dma((11,)),
            dma((sweeps, 5)),
            dma((sweeps, 5)),
            dma((ITERS + 1,)),
            dma((ITERS + 1,)),
            dma((ITERS,)),
            dma((ITERS,)),
            dma((NFY,)),
            dma((2,)),
            dma((ITERS + 1, 8)),
            dma((ITERS + 1, 8)),
            dma((ITERS,)),
            dma((ITERS,)),
            dma,
            dma((2,)),
            dma((ITERS - 1,)),
            dma((ITERS - 1,)),
        ],
        compiler_params=pltpu.CompilerParams(
            collective_id=0, has_side_effects=True, vmem_limit_bytes=60 * 1024 * 1024
        ),
    )(
        state, kappa, mix, press_weight, source_weight, interp, block_inverse, coupling, front_order,
        face_owner.reshape(1, -1), face_slot.reshape(1, -1),
    )
    return pl.pallas_call(
        last_add,
        out_shape=(
            jax.ShapeDtypeStruct(state.shape, F32),
            jax.ShapeDtypeStruct((EBD, EB), F32),
        ),
        in_specs=[hbm] * 4,
        out_specs=(hbm, hbm),
        scratch_shapes=[
            pltpu.VMEM((NV, NZL, CX, CY), F32),
            pltpu.VMEM((NZL, CX, CY), F32),
            pltpu.VMEM((EBD, EB), F32),
            pltpu.SMEM((NV,), F32),
            dma((NV + 3,)),
            dma((NV + 1,)),
        ],
        compiler_params=pltpu.CompilerParams(vmem_limit_bytes=60 * 1024 * 1024),
    )(before, raised, source_weight, displacement)


def solution(mesh):
    return jax.shard_map(
        on_device,
        mesh=mesh,
        in_specs=(
            P(None, "fz", "fx", "fy"),
            P("fz", "fx", "fy"),
            P(),
            P(),
            P(),
            P(),
            P("fx", None, None),
            P("fx", None, None),
            P("fx", None),
            P(("fx", "fy"), None),
            P(("fx", "fy")),
        ),
        out_specs=(P(None, "fz", "fx", "fy"), P("fx", None)),
        check_vma=False,
    )
```
